32 devices in a mesh: shard: 8 (over z, y), rep: 4 (over x, core).
Axes of the slice: x: 2, y: 2, z: 4, core: 2. Of those that a mesh axis runs over, the one named last changes fastest.
Arguments:
- block_input: bfloat16 [4096, 1024], P(('shard', 'rep')), may hold values from -6 to 6
- out_cotangent: bfloat16 [4096, 1024], P(('shard', 'rep')), may hold values from -6 to 6
- w_query: bfloat16 [1024, 1024], P('shard'), may hold values from -0.1875 to 0.1875
- w_key: bfloat16 [1024, 1024], P('shard'), may hold values from -0.1875 to 0.1875
- w_value: bfloat16 [1024, 1024], P('shard'), may hold values from -0.1875 to 0.1875
- w_output: bfloat16 [1024, 1024], P('shard'), may hold values from -0.75 to 0.75
- bias_query: float32 [1024], P('shard'), may hold values from -3 to 3
- bias_value: float32 [1024], P('shard'), may hold values from -3 to 3
- bias_output: float32 [1024], P('shard'), may hold values from -3 to 3
- gain_first: float32 [1024], P('shard'), may hold values from 0.5 to 1.5
- shift_first: float32 [1024], P('shard'), may hold values from -3 to 3
- w_inner: bfloat16 [1024, 4096], P('shard'), may hold values from -0.1875 to 0.1875
- bias_inner: float32 [4096], P('shard'), may hold values from -3 to 3
- w_down: bfloat16 [4096, 1024], P('shard'), may hold values from -0.09375 to 0.09375
- bias_down: float32 [1024], P('shard'), may hold values from -3 to 3
- gain_second: float32 [1024], P('shard'), may hold values from 0.5 to 1.5
- shift_second: float32 [1024], P('shard'), may hold values from -3 to 3
Outputs:
- block_output: bfloat16 [4096, 1024], P(('shard', 'rep'))
- grad_input: bfloat16 [4096, 1024], P(('shard', 'rep'))
- grad_w_query: float32 [1024, 1024], P('shard')
- grad_w_key: float32 [1024, 1024], P('shard')
- grad_w_value: float32 [1024, 1024], P('shard')
- grad_w_output: float32 [1024, 1024], P('shard')
- grad_bias_query: float32 [1024], P('shard')
- grad_bias_value: float32 [1024], P('shard')
- grad_bias_output: float32 [1024], P('shard')
- grad_gain_first: float32 [1024], P('shard')
- grad_shift_first: float32 [1024], P('shard')
- grad_w_inner: float32 [1024, 4096], P('shard')
- grad_bias_inner: float32 [4096], P('shard')
- grad_w_down: float32 [4096, 1024], P('shard')
- grad_bias_down: float32 [1024], P('shard')
- grad_gain_second: float32 [1024], P('shard')
- grad_shift_second: float32 [1024], P('shard')
The draws below stay inside these ranges and needn't reach their ends.
All inputs are finite; a program needn't handle non-finite values.
Results may differ from the reference program's by a relative error of at most 0.025.
Values may be sent and summed in bfloat16 or wider, within the bound.
A program may use at most 192 MiB of HBM per device.

```python
import math
import jax
import jax.numpy as jnp
from jax import lax

D = 1024
FF = 4096
HEADS = 16
HEAD_DIM = 64
SEQ = 128
TOKENS = 4096


def draw_block_input(key, part):
    values = jnp.clip(jax.random.normal(key, (TOKENS, D), jnp.float32), -6.0, 6.0)
    return values.astype(jnp.bfloat16)


def levels(key, dims, pieces, least, top_value):
    def one(position, parts):
        steps = jax.random.uniform(jax.random.fold_in(jax.random.fold_in(key, 6), position), (parts,), jnp.float32, least / len(pieces), top_value / len(pieces))
        return jnp.repeat(jnp.exp(steps), dims[position] // parts).reshape((-1,) + (1,) * (len(dims) - position - 1))

    level = one(*pieces[0])
    for cut in pieces[1:]:
        level = level * one(*cut)
    return level


def scatter_about(key, extent, deviation, most, shards=(), dtype=jnp.bfloat16):
    gain = levels(key, extent, shards, -0.22, 0.18) if shards else 1.0
    result = jax.random.normal(key, extent, jnp.float32) * deviation * gain
    return jnp.minimum(jnp.maximum(result, -most), most).astype(dtype)


def setup_inputs(seed: int = 0) -> dict:
    seeds = jax.random.split(jax.random.key(seed), 18)
    block_input = draw_block_input(jax.random.fold_in(seeds[17], 71), 0)
    out_cotangent = scatter_about(seeds[1], (TOKENS, D), 1.0, 6.0, ((0, 32),))
    w_query = scatter_about(seeds[2], (D, D), D ** -0.5, 0.1875, ((0, 8),))
    w_key = scatter_about(seeds[3], (D, D), D ** -0.5, 0.1875, ((0, 8),))
    w_value = scatter_about(seeds[4], (D, D), D ** -0.5, 0.1875, ((0, 8),))
    w_output = scatter_about(seeds[5], (D, D), (D // 16) ** -0.5, 0.75, ((0, 8),))
    bias_query = scatter_about(seeds[6], (D,), 0.5, 3.0, ((0, 8),), jnp.float32)
    bias_value = scatter_about(seeds[7], (D,), 0.5, 3.0, ((0, 8),), jnp.float32)
    bias_output = scatter_about(seeds[8], (D,), 0.5, 3.0, ((0, 8),), jnp.float32)
    gain_first = jnp.clip(1.0 + 0.1 * jax.random.normal(seeds[9], (D,), jnp.float32), 0.5, 1.5)
    shift_first = scatter_about(seeds[10], (D,), 0.5, 3.0, ((0, 8),), jnp.float32)
    w_inner = scatter_about(seeds[11], (D, FF), D ** -0.5, 0.1875, ((0, 8),))
    bias_inner = scatter_about(seeds[12], (FF,), 0.5, 3.0, ((0, 8),), jnp.float32)
    w_down = scatter_about(seeds[13], (FF, D), FF ** -0.5, 0.09375, ((0, 8),))
    bias_down = scatter_about(seeds[14], (D,), 0.5, 3.0, ((0, 8),), jnp.float32)
    gain_second = jnp.clip(1.0 + 0.1 * jax.random.normal(seeds[15], (D,), jnp.float32), 0.5, 1.5)
    shift_second = scatter_about(seeds[16], (D,), 0.5, 3.0, ((0, 8),), jnp.float32)
    return dict(block_input=block_input, out_cotangent=out_cotangent, w_query=w_query, w_key=w_key, w_value=w_value, w_output=w_output, bias_query=bias_query, bias_value=bias_value, bias_output=bias_output, gain_first=gain_first, shift_first=shift_first, w_inner=w_inner, bias_inner=bias_inner, w_down=w_down, bias_down=bias_down, gain_second=gain_second, shift_second=shift_second)


EPS = 1e-06
INV_ROOT_TWO = 0.7071067811865476
INV_ROOT_TWO_PI = 0.3989422804014327

def norm_parts(resid):
    centre = resid - lax.optimization_barrier(jnp.mean(resid, axis=-1, keepdims=True))
    variance = lax.optimization_barrier(jnp.mean(centre * centre, axis=-1, keepdims=True))
    rstd = lax.rsqrt(variance + EPS)
    return (centre * rstd, rstd)

def norm_back(upstream, normed, rstd):
    return rstd * (upstream - lax.optimization_barrier(jnp.mean(upstream, axis=-1, keepdims=True)) - normed * lax.optimization_barrier(jnp.mean(upstream * normed, axis=-1, keepdims=True)))

def gelu_value(inner):
    return 0.5 * inner * (1.0 + lax.erf(inner * INV_ROOT_TWO))

def gelu_slope(inner):
    return 0.5 * (1.0 + lax.erf(inner * INV_ROOT_TWO)) + inner * jnp.exp(-0.5 * inner * inner) * INV_ROOT_TWO_PI

def score_table(query4, keyed4):
    return jnp.einsum('bqhe,bkhe->bhqk', query4.astype(jnp.float32), keyed4.astype(jnp.float32)) * 0.125

def layer_pass(inputs, cotan, params):
    w_query, w_key, w_value, w_output, bias_query, bias_value, bias_output, gain_first, shift_first, w_inner, bias_inner, w_down, bias_down, gain_second, shift_second = params
    rows = inputs.shape[0]
    shape4 = (rows // SEQ, SEQ, HEADS, HEAD_DIM)
    query = (jnp.dot(inputs, w_query, preferred_element_type=jnp.float32) + bias_query).astype(jnp.bfloat16)
    keyed = jnp.dot(inputs, w_key, preferred_element_type=jnp.float32).astype(jnp.bfloat16)
    valued = (jnp.dot(inputs, w_value, preferred_element_type=jnp.float32) + bias_value).astype(jnp.bfloat16)
    query4 = query.reshape(shape4)
    keyed4 = keyed.reshape(shape4)
    valued4 = valued.reshape(shape4)
    scores = score_table(query4, keyed4)
    top = lax.optimization_barrier(jnp.max(scores, axis=-1, keepdims=True))
    logsum = top + jnp.log(lax.optimization_barrier(jnp.sum(jnp.exp(scores - top), axis=-1, keepdims=True)))
    probs_b = jnp.exp(scores - logsum).astype(jnp.bfloat16)
    context4 = jnp.einsum('bhqk,bkhe->bqhe', probs_b.astype(jnp.float32), valued4.astype(jnp.float32)).astype(jnp.bfloat16)
    context = context4.reshape(rows, D)
    resid_one = inputs.astype(jnp.float32) + jnp.dot(context, w_output, preferred_element_type=jnp.float32) + bias_output
    normed_one, rstd_one = norm_parts(resid_one)
    hidden = normed_one * gain_first + shift_first
    hidden_b = hidden.astype(jnp.bfloat16)
    inner = jnp.dot(hidden_b, w_inner, preferred_element_type=jnp.float32) + bias_inner
    acted = gelu_value(inner).astype(jnp.bfloat16)
    resid_two = hidden + jnp.dot(acted, w_down, preferred_element_type=jnp.float32) + bias_down
    normed_two, rstd_two = norm_parts(resid_two)
    output = (normed_two * gain_second + shift_second).astype(jnp.bfloat16)
    dout = cotan.astype(jnp.float32)
    g_gain_second = lax.optimization_barrier(jnp.sum(dout * normed_two, axis=0))
    g_shift_second = lax.optimization_barrier(jnp.sum(dout, axis=0))
    d_two = norm_back(dout * gain_second, normed_two, rstd_two)
    d_two_b = d_two.astype(jnp.bfloat16)
    g_bias_down = lax.optimization_barrier(jnp.sum(d_two, axis=0))
    g_w_down = jnp.dot(acted.T, d_two_b, preferred_element_type=jnp.float32)
    d_inner = jnp.dot(d_two_b, w_down.T, preferred_element_type=jnp.float32) * gelu_slope(inner)
    g_bias_inner = lax.optimization_barrier(jnp.sum(d_inner, axis=0))
    d_inner_b = d_inner.astype(jnp.bfloat16)
    g_w_inner = jnp.dot(hidden_b.T, d_inner_b, preferred_element_type=jnp.float32)
    d_hidden = d_two + jnp.dot(d_inner_b, w_inner.T, preferred_element_type=jnp.float32)
    g_gain_first = lax.optimization_barrier(jnp.sum(d_hidden * normed_one, axis=0))
    g_shift_first = lax.optimization_barrier(jnp.sum(d_hidden, axis=0))
    d_one = norm_back(d_hidden * gain_first, normed_one, rstd_one)
    g_bias_output = lax.optimization_barrier(jnp.sum(d_one, axis=0))
    d_one_b = d_one.astype(jnp.bfloat16)
    g_w_output = jnp.dot(context.T, d_one_b, preferred_element_type=jnp.float32)
    d_context = jnp.dot(d_one_b, w_output.T, preferred_element_type=jnp.float32).astype(jnp.bfloat16)
    d_context4 = d_context.reshape(shape4).astype(jnp.float32)
    probs = jnp.exp(score_table(query4, keyed4) - logsum)
    probs_again = probs.astype(jnp.bfloat16)
    d_probs = jnp.einsum('bqhe,bkhe->bhqk', d_context4, valued4.astype(jnp.float32))
    delta = lax.optimization_barrier(jnp.sum(probs * d_probs, axis=-1, keepdims=True))
    d_scores = (probs * (d_probs - delta) * 0.125).astype(jnp.bfloat16).astype(jnp.float32)
    d_query = jnp.einsum('bhqk,bkhe->bqhe', d_scores, keyed4.astype(jnp.float32)).reshape(rows, D)
    d_keyed = jnp.einsum('bhqk,bqhe->bkhe', d_scores, query4.astype(jnp.float32)).reshape(rows, D)
    d_valued = jnp.einsum('bhqk,bqhe->bkhe', probs_again.astype(jnp.float32), d_context4).reshape(rows, D)
    g_bias_query = lax.optimization_barrier(jnp.sum(d_query, axis=0))
    g_bias_value = lax.optimization_barrier(jnp.sum(d_valued, axis=0))
    dq_b = d_query.astype(jnp.bfloat16)
    dk_b = d_keyed.astype(jnp.bfloat16)
    dv_b = d_valued.astype(jnp.bfloat16)
    g_w_query = jnp.dot(inputs.T, dq_b, preferred_element_type=jnp.float32)
    g_w_key = jnp.dot(inputs.T, dk_b, preferred_element_type=jnp.float32)
    g_w_value = jnp.dot(inputs.T, dv_b, preferred_element_type=jnp.float32)
    d_input = d_one + jnp.dot(dq_b, w_query.T, preferred_element_type=jnp.float32)
    d_input = d_input + jnp.dot(dk_b, w_key.T, preferred_element_type=jnp.float32)
    d_input = d_input + jnp.dot(dv_b, w_value.T, preferred_element_type=jnp.float32)
    grads = (g_w_query, g_w_key, g_w_value, g_w_output, g_bias_query, g_bias_value, g_bias_output, g_gain_first, g_shift_first, g_w_inner, g_bias_inner, g_w_down, g_bias_down, g_gain_second, g_shift_second)
    return (output, d_input.astype(jnp.bfloat16), grads)

def reference(block_input, out_cotangent, w_query, w_key, w_value, w_output, bias_query, bias_value, bias_output, gain_first, shift_first, w_inner, bias_inner, w_down, bias_down, gain_second, shift_second):
    params = (w_query, w_key, w_value, w_output, bias_query, bias_value, bias_output, gain_first, shift_first, w_inner, bias_inner, w_down, bias_down, gain_second, shift_second)
    block_rows = math.gcd(TOKENS, 4096)
    blocks = TOKENS // block_rows
    inputs = block_input.reshape(blocks, block_rows, D)
    cotans = out_cotangent.reshape(blocks, block_rows, D)
    zeros = tuple((jnp.zeros(p.shape, jnp.float32) for p in params))

    def advance(carry, pair):
        output, d_input, grads = layer_pass(pair[0], pair[1], params)
        return (tuple((c + g for c, g in zip(carry, grads))), (output, d_input))
    totals, (outputs, d_inputs) = lax.scan(advance, zeros, (inputs, cotans))
    return (outputs.reshape(TOKENS, D), d_inputs.reshape(TOKENS, D), totals[0], totals[1], totals[2], totals[3], totals[4], totals[5], totals[6], totals[7], totals[8], totals[9], totals[10], totals[11], totals[12], totals[13], totals[14])
```

```python
import jax
import jax.numpy as jnp
from jax import lax
from jax.experimental import pallas as pl
from jax.experimental.pallas import tpu as pltpu
from jax.sharding import PartitionSpec as P

HEAD_DIM = 64
SEQ = 128
PAD = 16


EPS = 1e-06
INV_ROOT_TWO = 0.7071067811865476
INV_ROOT_TWO_PI = 0.3989422804014327
BF = jnp.bfloat16
F32 = jnp.float32


def norm_parts(resid):
    centre = resid - jnp.mean(resid, axis=-1, keepdims=True)
    variance = jnp.mean(centre * centre, axis=-1, keepdims=True)
    rstd = lax.rsqrt(variance + EPS)
    return (centre * rstd, rstd)


def norm_back(upstream, normed, rstd):
    return rstd * (
        upstream
        - jnp.mean(upstream, axis=-1, keepdims=True)
        - normed * jnp.mean(upstream * normed, axis=-1, keepdims=True)
    )


def mm(a, b):
    return jnp.dot(a, b, preferred_element_type=F32)


def mm_nt(a, b):
    return lax.dot_general(a, b, (((1,), (1,)), ((), ())), preferred_element_type=F32)


def mm_tn(a, b):
    return lax.dot_general(a, b, (((0,), (0,)), ((), ())), preferred_element_type=F32)


def ein(spec, a, b):
    return jnp.einsum(spec, a, b, preferred_element_type=F32)


MESH = pl.DeviceIdType.MESH
CHUNK = 16


class Peers:
    def __init__(self, R):
        self.R, self.A = R, R // 2
        self.me = lax.axis_index("rep")
        self.c = lax.rem(self.me, 2)
        self.a = lax.div(self.me, 2)
        self.partner = self.me + 1 - 2 * self.c

    def chip(self, k):
        return lax.rem(self.a + k, self.A)

    def same(self, k):
        return 2 * self.chip(k) + self.c

    def other(self, k):
        return 2 * self.chip(k) + 1 - self.c

    def meet(self):
        barrier = pltpu.get_barrier_semaphore()
        for dev in [self.partner] + [self.same(k) for k in range(1, self.A)]:
            pl.semaphore_signal(barrier, inc=1, device_id={"rep": dev}, device_id_type=MESH)
        pl.semaphore_wait(barrier, self.A)


def rows_of(index, T):
    return pl.ds(pl.multiple_of(index * T, T), T)


def chunk_rows(i, base=None):
    start = i * CHUNK if base is None else base + i * CHUNK
    return pl.ds(pl.multiple_of(start, CHUNK), CHUNK)


def remote(src, dst, send, recv, dev):
    return pltpu.make_async_remote_copy(
        src_ref=src,
        dst_ref=dst,
        send_sem=send,
        recv_sem=recv,
        device_id={"rep": dev},
        device_id_type=MESH,
    )


def scatter_sum(p, part, T, near, far, out, sems):
    near_s, near_r, far_s, far_r = sems
    order = list(range(1, p.A)) + [0]
    first = {
        k: remote(
            part.at[rows_of(p.other(k), T)], near.at[k], near_s.at[k], near_r.at[k], p.partner
        )
        for k in order
    }
    for k in order:
        first[k].start()
    second = []
    for k in range(1, p.A):
        first[k].wait_recv()
        base = p.same(k) * T

        def add(i, _, k=k, base=base):
            mine = part[chunk_rows(i, base), :].astype(F32)
            out[k - 1, chunk_rows(i), :] = (mine + near[k, chunk_rows(i), :].astype(F32)).astype(BF)
            return 0

        lax.fori_loop(0, T // CHUNK, add, 0)
        copy = remote(out.at[k - 1], far.at[k - 1], far_s.at[k - 1], far_r.at[k - 1], p.same(k))
        copy.start()
        second.append(copy)
    first[0].wait_recv()
    for copy in second:
        copy.wait_recv()

    def read(i):
        total = part[chunk_rows(i, p.me * T), :].astype(F32) + near[0, chunk_rows(i), :].astype(F32)
        for k in range(1, p.A):
            total = total + far[k - 1, chunk_rows(i), :].astype(F32)
        return total

    return read, list(first.values()) + second


def spread(p, src, full, T, sems):
    dir_s, dir_r, fwd_s, fwd_r = sems
    mine = full.at[rows_of(p.me, T)]
    direct = {}
    for k in list(range(1, p.A)) + [0]:
        dev = p.partner if k == 0 else p.same(k)
        direct[k] = remote(src, mine, dir_s.at[k], dir_r.at[k], dev)
        direct[k].start()
    passed = []
    for k in range(1, p.A):
        direct[k].wait_recv()
        block = full.at[rows_of(p.same(p.A - k), T)]
        copy = remote(block, block, fwd_s.at[k - 1], fwd_r.at[k - 1], p.partner)
        copy.start()
        passed.append(copy)
    direct[0].wait_recv()
    for copy in passed:
        copy.wait_recv()
    return list(direct.values()) + passed


def drain(copies):
    for copy in copies:
        copy.wait_send()


def run_kernel(kernel, cid, T, D, R, ins, outs, scatter, gather):
    A = R // 2
    few = max(A - 1, 1)
    scratch = []
    if scatter:
        scratch += [
            pltpu.VMEM((A, T, D), BF),
            pltpu.VMEM((few, T, D), BF),
            pltpu.VMEM((few, T, D), BF),
        ]
        scratch += [pltpu.SemaphoreType.DMA((n,)) for n in (A, A, few, few)]
    if gather:
        scratch += [pltpu.SemaphoreType.DMA((n,)) for n in (A, A, few, few)]
    vmem = pl.BlockSpec(memory_space=pltpu.VMEM)
    return pl.pallas_call(
        kernel,
        out_shape=[jax.ShapeDtypeStruct(*o) for o in outs],
        in_specs=[vmem] * len(ins),
        out_specs=[vmem] * len(outs),
        scratch_shapes=scratch,
        compiler_params=pltpu.CompilerParams(collective_id=cid, has_side_effects=True),
        cost_estimate=pl.CostEstimate(flops=0, bytes_accessed=24 << 20, transcendentals=0),
    )(*ins)


def gather_kernel(block, R, cid):
    T, D = block.shape

    def kernel(src, full, *sems):
        p = Peers(R)
        p.meet()

        def put(i, _):
            full[chunk_rows(i, p.me * T), :] = src[chunk_rows(i), :]
            return 0

        lax.fori_loop(0, T // CHUNK, put, 0)
        drain(spread(p, src, full, T, sems))

    return run_kernel(kernel, cid, T, D, R, [block], [((R * T, D), BF)], False, True)[0]


def norm_one_step(partial, x, bo, gone, sone):
    T, D = x.shape
    R = partial.shape[0] // T

    def kernel(part, xr, bor, gr, sr, normed_o, rstd_o, hidden_o, full, near, far, out, *sems):
        p = Peers(R)
        p.meet()
        read, sent = scatter_sum(p, part, T, near, far, out, sems[:4])

        def step(i, _):
            normed, rstd = norm_parts(xr[chunk_rows(i), :].astype(F32) + read(i) + bor[...])
            hidden = normed * gr[...] + sr[...]
            normed_o[chunk_rows(i), :] = normed
            rstd_o[chunk_rows(i), :] = rstd
            hidden_o[chunk_rows(i), :] = hidden
            full[chunk_rows(i, p.me * T), :] = hidden.astype(BF)
            return 0

        lax.fori_loop(0, T // CHUNK, step, 0)
        drain(sent + spread(p, full.at[rows_of(p.me, T)], full, T, sems[4:]))

    ins = [partial, x, bo[None], gone[None], sone[None]]
    outs = [((T, D), F32), ((T, 1), F32), ((T, D), F32), ((R * T, D), BF)]
    return run_kernel(kernel, 1, T, D, R, ins, outs, True, True)


def add_sums(ref, values):
    for n, v in enumerate(values):
        ref[n : n + 1, :] += jnp.sum(v, axis=0, keepdims=True)


def norm_two_step(partial, hidden, bd, gtwo, stwo, cot):
    T, D = hidden.shape
    R = partial.shape[0] // T

    def kernel(part, hr, br, gr, sr, cr, out_o, d_o, sums, full, near, far, out, *sems):
        p = Peers(R)
        p.meet()
        sums[...] = jnp.zeros_like(sums)
        read, sent = scatter_sum(p, part, T, near, far, out, sems[:4])

        def step(i, _):
            normed, rstd = norm_parts(hr[chunk_rows(i), :] + read(i) + br[...])
            out_o[chunk_rows(i), :] = (normed * gr[...] + sr[...]).astype(BF)
            dout = cr[chunk_rows(i), :].astype(F32)
            d_two = norm_back(dout * gr[...], normed, rstd)
            add_sums(sums, (d_two, dout * normed, dout))
            d_o[chunk_rows(i), :] = d_two
            full[chunk_rows(i, p.me * T), :] = d_two.astype(BF)
            return 0

        lax.fori_loop(0, T // CHUNK, step, 0)
        drain(sent + spread(p, full.at[rows_of(p.me, T)], full, T, sems[4:]))

    ins = [partial, hidden, bd[None], gtwo[None], stwo[None], cot]
    outs = [((T, D), BF), ((T, D), F32), ((8, D), F32), ((R * T, D), BF)]
    return run_kernel(kernel, 2, T, D, R, ins, outs, True, True)


def back_one_step(partial, d_two, normed, rstd, gone):
    T, D = d_two.shape
    R = partial.shape[0] // T

    def kernel(part, dr, nr, rr, gr, d_o, sums, full, near, far, out, *sems):
        p = Peers(R)
        p.meet()
        sums[...] = jnp.zeros_like(sums)
        read, sent = scatter_sum(p, part, T, near, far, out, sems[:4])

        def step(i, _):
            d_hidden = dr[chunk_rows(i), :] + read(i)
            normed = nr[chunk_rows(i), :]
            d_one = norm_back(d_hidden * gr[...], normed, rr[chunk_rows(i), :])
            add_sums(sums, (d_one, d_hidden * normed, d_hidden))
            d_o[chunk_rows(i), :] = d_one
            full[chunk_rows(i, p.me * T), :] = d_one.astype(BF)
            return 0

        lax.fori_loop(0, T // CHUNK, step, 0)
        drain(sent + spread(p, full.at[rows_of(p.me, T)], full, T, sems[4:]))

    ins = [partial, d_two, normed, rstd, gone[None]]
    outs = [((T, D), F32), ((8, D), F32), ((R * T, D), BF)]
    return run_kernel(kernel, 3, T, D, R, ins, outs, True, True)


def input_step(partial, d_one):
    T, D = d_one.shape
    R = partial.shape[0] // T

    def kernel(part, dr, grad, near, far, out, *sems):
        p = Peers(R)
        p.meet()
        read, sent = scatter_sum(p, part, T, near, far, out, sems)

        def step(i, _):
            grad[chunk_rows(i), :] = (dr[chunk_rows(i), :] + read(i)).astype(BF)
            return 0

        lax.fori_loop(0, T // CHUNK, step, 0)
        drain(sent)

    return run_kernel(kernel, 4, T, D, R, [partial, d_one], [((T, D), BF)], True, False)[0]


def body(
    block_input,
    out_cotangent,
    w_query,
    w_key,
    w_value,
    w_output,
    bias_query,
    bias_value,
    bias_output,
    gain_first,
    shift_first,
    w_inner,
    bias_inner,
    w_down,
    bias_down,
    gain_second,
    shift_second,
):
    S = lax.axis_size("shard")
    R = lax.axis_size("rep")
    r = lax.axis_index("rep")
    T = block_input.shape[0]
    D = w_query.shape[1]
    ds = w_query.shape[0]
    dr = D // R
    fs = w_down.shape[0]
    fr = fs // R
    W = 4 * dr

    def cols(w):
        return lax.dynamic_slice(w, (0, r * dr), (ds, dr))

    small = jnp.concatenate(
        [
            v.astype(BF)
            for v in (
                bias_query,
                bias_value,
                bias_output,
                gain_first,
                shift_first,
                bias_down,
                gain_second,
                shift_second,
                bias_inner,
            )
        ]
    )
    n_small = small.shape[0]
    small = jnp.pad(small, (0, PAD * W - n_small)).reshape(PAD, W)
    pack = jnp.concatenate(
        [jnp.concatenate([cols(w_query), cols(w_key), cols(w_value), cols(w_output)], 1), small], 0
    )
    got = lax.all_gather(pack, "shard", axis=0)
    x_all = gather_kernel(block_input, R, 0)
    wi_r = lax.dynamic_index_in_dim(w_inner.reshape(ds, S, R, fr), r, 2, keepdims=False)
    V = S * fr
    dv = fr * D // V
    wd_r = lax.dynamic_slice(w_down, (r * fr, 0), (fr, D)).reshape(dv, V)
    mlp = lax.all_gather(jnp.concatenate([wi_r.reshape(ds, V), wd_r], 0), "shard", axis=0)
    wi = mlp[:, :ds].reshape(D, V)
    wd = mlp[:, ds:].reshape(V, D)
    wqkv = got[:, :ds, : 3 * dr].reshape(D, 3 * dr)
    wo = lax.all_to_all(
        got[:, :ds, 3 * dr :].reshape(D, dr), "rep", split_axis=0, concat_axis=1, tiled=True
    )
    flat = got[:, ds:, :].reshape(S, PAD * W)[:, :n_small].astype(F32)
    bq, bv, bo, gone, sone, bd, gtwo, stwo = (
        flat[:, i * ds : (i + 1) * ds].reshape(D) for i in range(8)
    )
    bi = lax.dynamic_index_in_dim(flat[:, 8 * ds :].reshape(S, R, fr), r, 1, keepdims=False)
    bi = bi.reshape(S * fr)
    bq = lax.dynamic_slice(bq, (r * dr,), (dr,))
    bv = lax.dynamic_slice(bv, (r * dr,), (dr,))

    N = R * T
    shape4 = (N // SEQ, SEQ, dr // HEAD_DIM, HEAD_DIM)
    qkv = mm(x_all, wqkv)
    query = (qkv[:, :dr] + bq).astype(BF).reshape(shape4)
    keyed = qkv[:, dr : 2 * dr].astype(BF).reshape(shape4)
    valued = (qkv[:, 2 * dr :] + bv).astype(BF).reshape(shape4)
    scores = ein("bqhe,bkhe->bhqk", query, keyed) * 0.125
    top = jnp.max(scores, axis=-1, keepdims=True)
    logsum = top + jnp.log(jnp.sum(jnp.exp(scores - top), axis=-1, keepdims=True))
    probs = jnp.exp(scores - logsum)
    probs_b = probs.astype(BF)
    context = ein("bhqk,bkhe->bqhe", probs_b, valued).astype(BF).reshape(N, dr)
    attn_part = mm(context, wo).astype(BF)

    normed_one, rstd_one, hidden, hidden_all = norm_one_step(attn_part, block_input, bo, gone, sone)
    inner = mm(hidden_all, wi) + bi
    phi = 0.5 * (1.0 + lax.erf(inner * INV_ROOT_TWO))
    acted = (inner * phi).astype(BF)
    slope = phi + inner * jnp.exp(-0.5 * inner * inner) * INV_ROOT_TWO_PI
    down_part = mm(acted, wd).astype(BF)

    output, d_two, sums_two, d_two_all = norm_two_step(
        down_part, hidden, bd, gtwo, stwo, out_cotangent
    )
    d_inner = mm_nt(d_two_all, wd) * slope
    g_bias_inner = jnp.sum(d_inner, axis=0)
    d_inner_b = d_inner.astype(BF)
    hid_part = mm_nt(d_inner_b, wi).astype(BF)
    g_wd = mm_tn(acted, d_two_all).astype(BF).reshape(S, dv, V)
    g_wi = mm_tn(hidden_all, d_inner_b).astype(BF).reshape(S, ds, V)
    g_mlp = lax.psum_scatter(
        jnp.concatenate([g_wi, g_wd], 1), "shard", scatter_dimension=0, tiled=True
    )[0]

    d_one, sums_one, d_one_all = back_one_step(hid_part, d_two, normed_one, rstd_one, gone)
    g_wo = mm_tn(context, d_one_all).astype(BF)
    g_wo = lax.all_to_all(g_wo, "rep", split_axis=1, concat_axis=0, tiled=True)
    d_context = mm_nt(d_one_all, wo).astype(BF).reshape(shape4)
    d_probs = ein("bqhe,bkhe->bhqk", d_context, valued)
    delta = jnp.sum(probs * d_probs, axis=-1, keepdims=True)
    d_scores = (probs * (d_probs - delta) * 0.125).astype(BF)
    d_query = ein("bhqk,bkhe->bqhe", d_scores, keyed).reshape(N, dr)
    d_keyed = ein("bhqk,bqhe->bkhe", d_scores, query).reshape(N, dr)
    d_valued = ein("bhqk,bqhe->bkhe", probs_b, d_context).reshape(N, dr)
    g_bias_query = jnp.sum(d_query, axis=0)
    g_bias_value = jnp.sum(d_valued, axis=0)
    d_qkv = jnp.concatenate([d_query.astype(BF), d_keyed.astype(BF), d_valued.astype(BF)], 1)
    in_part = mm_nt(d_qkv, wqkv).astype(BF)

    def placed(v):
        return lax.dynamic_update_slice(jnp.zeros((D,), F32), v, (r * dr,)).reshape(S, ds)

    g_small = jnp.concatenate(
        [
            placed(g_bias_query),
            placed(g_bias_value),
            sums_one[0].reshape(S, ds),
            sums_one[1].reshape(S, ds),
            sums_one[2].reshape(S, ds),
            sums_two[0].reshape(S, ds),
            sums_two[1].reshape(S, ds),
            sums_two[2].reshape(S, ds),
            g_bias_inner.reshape(S, fr),
        ],
        1,
    ).astype(BF)
    n_g = g_small.shape[1]
    g_small = jnp.pad(g_small, ((0, 0), (0, PAD * W - n_g))).reshape(S, PAD, W)
    g_pack = jnp.concatenate([mm_tn(x_all, d_qkv).astype(BF), g_wo], 1).reshape(S, ds, W)
    g_pack = jnp.concatenate([g_pack, g_small], 1)
    g_pack = lax.psum_scatter(g_pack, "shard", scatter_dimension=0, tiled=True)[0]

    grad_input = input_step(in_part, d_one)

    mlps = gather_kernel(g_mlp, R, 5).reshape(R, ds + dv, V).astype(F32)
    wd_out = mlps[:, ds:].reshape(R * fr, D)
    wi_out = mlps[:, :ds].reshape(R, ds, S, fr).transpose(1, 2, 0, 3).reshape(ds, S * R * fr)
    packs = gather_kernel(g_pack, R, 6).reshape(R, ds + PAD, W).astype(F32)
    main = packs[:, :ds].reshape(R, ds, 4, dr).transpose(2, 1, 0, 3).reshape(4, ds, D)
    tail = packs[:, ds:].reshape(R, PAD * W)
    summed = jnp.sum(tail[:, : 8 * ds], axis=0)
    gbq, gbv, gbo, ggone, gsone, gbd, ggtwo, gstwo = (
        summed[i * ds : (i + 1) * ds] for i in range(8)
    )
    gbi = tail[:, 8 * ds : n_g].reshape(fs)
    return (
        output,
        grad_input,
        main[0],
        main[1],
        main[2],
        main[3],
        gbq,
        gbv,
        gbo,
        ggone,
        gsone,
        wi_out,
        gbi,
        wd_out,
        gbd,
        ggtwo,
        gstwo,
    )

VMEM_SPEC = pl.BlockSpec(memory_space=pltpu.VMEM)
ANY_SPEC = pl.BlockSpec(memory_space=pl.ANY)
LIMIT = 56 << 20
NVEC = 16


def dma_sems(*counts):
    return [pltpu.SemaphoreType.DMA((n,)) for n in counts]


class Place(Peers):
    def __init__(self, S, R):
        super().__init__(R)
        self.S, self.Z = S, S // 2
        self.s = lax.axis_index("shard")
        self.z = lax.div(self.s, 2)
        self.y = lax.rem(self.s, 2)
        self.across = self.s + 1 - 2 * self.y

    def up(self, k):
        return 2 * lax.rem(self.z + k, self.Z) + self.y

    def down(self, k):
        return 2 * lax.rem(self.z + self.Z - k, self.Z) + self.y

    def flip(self, s):
        return s + 1 - 2 * self.y

    def meet_all(self):
        barrier = pltpu.get_barrier_semaphore()
        for dev in [self.partner] + [self.same(k) for k in range(1, self.A)]:
            pl.semaphore_signal(barrier, inc=1, device_id={"rep": dev}, device_id_type=MESH)
        for dev in [self.across] + [self.up(k) for k in range(1, self.Z)]:
            pl.semaphore_signal(barrier, inc=1, device_id={"shard": dev}, device_id_type=MESH)
        pl.semaphore_wait(barrier, self.A + self.Z)


def to_shard(src, dst, send, recv, dev):
    return pltpu.make_async_remote_copy(
        src_ref=src,
        dst_ref=dst,
        send_sem=send,
        recv_sem=recv,
        device_id={"shard": dev},
        device_id_type=MESH,
    )


class RowGather:
    def __init__(self, p, full, T, sems):
        self.p, self.full, self.T = p, full, T
        self.zs, self.zr, self.ys, self.yr = sems
        self.far = {k: self.copy(p.s, self.zs, self.zr, k - 1, p.up(k)) for k in range(1, p.Z)}
        self.near = {0: self.copy(p.s, self.ys, self.yr, 0, p.across)}
        for k in range(1, p.Z):
            self.near[k] = self.copy(p.down(k), self.ys, self.yr, k, p.across)

    @staticmethod
    def sems(Z):
        return dma_sems(Z - 1, Z - 1, Z, Z)

    def copy(self, block, send, recv, i, dev):
        rows = self.full.at[rows_of(block, self.T)]
        return to_shard(rows, rows, send.at[i], recv.at[i], dev)

    def start(self):
        for k in range(1, self.p.Z):
            self.far[k].start()
        self.near[0].start()

    def forward(self, k):
        self.far[k].wait_recv()
        self.near[k].start()

    def finish(self):
        for k in range(self.p.Z):
            self.near[k].wait_recv()

    def drain(self):
        for copy in list(self.far.values()) + list(self.near.values()):
            copy.wait_send()


class PlaneGather:
    def __init__(self, p, full, T, sems):
        self.p = p
        self.zs, self.zr, self.ys, self.yr = sems
        rows = full.at[rows_of(p.y, T)]
        self.far = {
            k: to_shard(rows, rows, self.zs.at[k - 1], self.zr.at[0], p.up(k))
            for k in range(1, p.Z)
        }
        self.near = to_shard(rows, rows, self.ys.at[0], self.yr.at[0], p.across)
        self.mine = p.z == p.me

    @staticmethod
    def sems(Z):
        return dma_sems(Z - 1, 1, 1, 1)

    def start(self):
        @pl.when(self.mine)
        def _():
            for k in range(1, self.p.Z):
                self.far[k].start()
            self.near.start()

    def forward(self):
        @pl.when(jnp.logical_not(self.mine))
        def _():
            self.far[1].wait_recv()
            self.near.start()

    def finish(self):
        self.near.wait_recv()

    def drain(self):
        @pl.when(self.mine)
        def _():
            for k in range(1, self.p.Z):
                self.far[k].wait_send()

        self.near.wait_send()


def fetch_all(x, wq, wk, wv, wo, wi, wd, vectors, S, R):
    T, D = x.shape
    ds, fs = wq.shape[0], wd.shape[0]
    dr, fr = D // R, fs // R
    Z, A = S // 2, R // 2
    few = A - 1
    nv = len(vectors)
    nq = [4, 4, 4, 4, 4]

    def kernel(*refs):
        x, wq, wk, wv, wo, wi, wd = refs[:7]
        vecs = refs[7 : 7 + nv]
        x_all, wqkv, wor, wir, wdr, flat, small = refs[7 + nv : 14 + nv]
        sems = list(refs[14 + nv :])
        here = sems.pop(0)
        p = Place(S, R)
        mine = rows_of(p.s, ds)
        cols = pl.ds(pl.multiple_of(p.me * dr, dr), dr)
        local = []

        def bring(src, dst):
            copy = pltpu.make_async_copy(src, dst, here.at[len(local)])
            copy.start()
            local.append(copy)

        for i, w in enumerate((wq, wk, wv)):
            bring(w.at[:, cols], wqkv.at[mine, pl.ds(i * dr, dr)])
        bring(x, x_all.at[rows_of(p.me, T)])
        for c in range(S):
            part = pl.ds(pl.multiple_of(c * fs + p.me * fr, fr), fr)
            bring(wi.at[:, part], wir.at[mine, pl.ds(c * fr, fr)])
        bring(wd.at[rows_of(p.me, fr)], wdr.at[mine])
        own = pltpu.make_async_copy(wo, wor.at[rows_of(p.y, ds)], here.at[len(local)])

        @pl.when(p.z == p.me)
        def _():
            own.start()

        part = pl.ds(pl.multiple_of(p.me * fr, fr), fr)
        pieces = [v[...] for v in vecs[:-1]] + [vecs[-1][:, part]]
        pieces.append(jnp.zeros((NVEC - nv, ds), F32))
        small[rows_of(p.s, NVEC), :] = jnp.concatenate(pieces, 0)
        p.meet_all()

        def take(n):
            got = sems[:n]
            del sems[:n]
            return got

        smalls = RowGather(p, small, NVEC, take(4))
        qkv = RowGather(p, wqkv, ds, take(4))
        inner = RowGather(p, wir, ds, take(4))
        down = RowGather(p, wdr, fr, take(4))
        out = PlaneGather(p, wor, ds, take(4))
        smalls.start()
        for copy in local[:3]:
            copy.wait()
        qkv.start()
        local[3].wait()
        dir_s, dir_r, fwd_s, fwd_r = take(4)
        sent = spread(p, x_all.at[rows_of(p.me, T)], x_all, T, (dir_s, dir_r, fwd_s, fwd_r))
        for copy in local[4:]:
            copy.wait()

        @pl.when(p.z == p.me)
        def _():
            own.wait()

        out.start()
        for k in range(1, Z):
            smalls.forward(k)
        for k in range(1, Z):
            qkv.forward(k)
        inner.start()
        out.forward()
        down.start()
        for k in range(1, Z):
            inner.forward(k)
        for k in range(1, Z):
            down.forward(k)
        smalls.finish()
        for i in range(nv):
            row = [small[s * NVEC + i : s * NVEC + i + 1, :] for s in range(S)]
            flat[i : i + 1, :] = jnp.concatenate(row, 1)
        flat[nv:, :] = jnp.zeros((NVEC - nv, D), F32)
        for g in (qkv, out, inner, down):
            g.finish()
        drain(sent)
        for g in (smalls, qkv, out, inner, down):
            g.drain()

    ins = [x, wq, wk, wv, wo, wi, wd] + [v[None] for v in vectors]
    outs = [
        ((R * T, D), BF),
        ((D, 3 * dr), BF),
        ((dr, D), BF),
        ((D, S * fr), BF),
        ((S * fr, D), BF),
        ((NVEC, D), F32),
    ]
    scratch = [pltpu.VMEM((S * NVEC, ds), F32), pltpu.SemaphoreType.DMA((S + 6,))]
    for _ in range(4):
        scratch += RowGather.sems(Z)
    scratch += PlaneGather.sems(Z)
    scratch += dma_sems(A, A, few, few)
    return pl.pallas_call(
        kernel,
        out_shape=[jax.ShapeDtypeStruct(*o) for o in outs],
        in_specs=[ANY_SPEC] * 7 + [VMEM_SPEC] * nv,
        out_specs=[VMEM_SPEC] * len(outs),
        scratch_shapes=scratch,
        compiler_params=pltpu.CompilerParams(
            collective_id=10, has_side_effects=True, vmem_limit_bytes=LIMIT
        ),
        cost_estimate=pl.CostEstimate(flops=0, bytes_accessed=24 << 20, transcendentals=0),
    )(*ins)


def add_rows(dst, terms, n, step, finish=None):
    def add(i, _):
        at = pl.ds(pl.multiple_of(i * step, step), step)
        total = terms[0](at)
        for t in terms[1:]:
            total = total + t(at)
        dst(at, total)
        return 0

    lax.fori_loop(0, n // step, add, 0)


class RowScatter:
    def __init__(self, p, part, T, bufs, sems):
        self.p, self.part, self.T = p, part, T
        self.close, self.out, self.far = bufs
        ys, yr, zs, zr = sems
        self.first = {}
        for k in range(p.Z):
            to = p.up(k)
            self.first[k] = to_shard(
                part.at[rows_of(p.flip(to), T)], self.close.at[k], ys.at[k], yr.at[k], p.across
            )
        self.second = {
            k: to_shard(
                self.out.at[k - 1], self.far.at[k - 1], zs.at[k - 1], zr.at[k - 1], p.up(k)
            )
            for k in range(1, p.Z)
        }

    @staticmethod
    def bufs(Z, T, C, dtype):
        return [pltpu.VMEM((n, T, C), dtype) for n in (Z, Z - 1, Z - 1)]

    @staticmethod
    def sems(Z):
        return dma_sems(Z, Z, Z - 1, Z - 1)

    def start(self):
        for k in list(range(1, self.p.Z)) + [0]:
            self.first[k].start()

    def pass_on(self, k):
        self.first[k].wait_recv()
        base = self.p.up(k) * self.T
        dtype = self.out.dtype

        def add(i, _):
            mine = self.part[chunk_rows(i, base), :].astype(F32)
            near = self.close[k, chunk_rows(i), :].astype(F32)
            self.out[k - 1, chunk_rows(i), :] = (mine + near).astype(dtype)
            return 0

        lax.fori_loop(0, self.T // CHUNK, add, 0)
        self.second[k].start()

    def total(self, dst, at=None):
        p = self.p
        self.first[0].wait_recv()
        for k in range(1, p.Z):
            self.second[k].wait_recv()

        def add(i, _):
            total = self.part[chunk_rows(i, p.s * self.T), :].astype(F32)
            total = total + self.close[0, chunk_rows(i), :].astype(F32)
            for k in range(1, p.Z):
                total = total + self.far[k - 1, chunk_rows(i), :].astype(F32)
            dst[p.me, chunk_rows(i), :] = total.astype(dst.dtype)
            return 0

        lax.fori_loop(0, self.T // CHUNK, add, 0)

    def drain(self):
        for copy in list(self.first.values()) + list(self.second.values()):
            copy.wait_send()


class PlaneScatter:
    def __init__(self, p, part, T, bufs, sems):
        self.p, self.part, self.T = p, part, T
        self.close, self.out, self.far = bufs
        ys, yr, zs, zr = sems
        self.first = to_shard(
            part.at[rows_of(1 - p.y, T)], self.close, ys.at[0], yr.at[0], p.across
        )
        self.mine = p.z == p.me
        self.hop = lax.rem(p.z + p.Z - p.me, p.Z)
        self.sends = to_shard(
            self.out,
            self.far.at[jnp.maximum(self.hop - 1, 0)],
            zs.at[0],
            zr.at[jnp.maximum(self.hop - 1, 0)],
            2 * p.me + p.y,
        )
        self.gets = [
            to_shard(self.out, self.far.at[k], zs.at[0], zr.at[k], p.up(k + 1))
            for k in range(p.Z - 1)
        ]

    @staticmethod
    def bufs(Z, T, C, dtype):
        return [pltpu.VMEM((T, C), dtype), pltpu.VMEM((T, C), dtype), pltpu.VMEM((Z - 1, T, C), dtype)]

    @staticmethod
    def sems(Z):
        return dma_sems(1, 1, 1, Z - 1)

    def start(self):
        self.first.start()

    def pass_on(self):
        self.first.wait_recv()

        def add(i, _):
            mine = self.part[chunk_rows(i, self.p.y * self.T), :].astype(F32)
            self.out[chunk_rows(i), :] = (mine + self.close[chunk_rows(i), :].astype(F32)).astype(BF)
            return 0

        lax.fori_loop(0, self.T // CHUNK, add, 0)

        @pl.when(jnp.logical_not(self.mine))
        def _():
            self.sends.start()

    def total(self, dst):
        @pl.when(self.mine)
        def _():
            for copy in self.gets:
                copy.wait_recv()

            def add(i, _):
                total = self.part[chunk_rows(i, self.p.y * self.T), :].astype(F32)
                total = total + self.close[chunk_rows(i), :].astype(F32)
                for k in range(self.p.Z - 1):
                    total = total + self.far[k, chunk_rows(i), :].astype(F32)
                dst[chunk_rows(i), :] = total.astype(BF)
                return 0

            lax.fori_loop(0, self.T // CHUNK, add, 0)

    def drain(self):
        self.first.wait_send()

        @pl.when(jnp.logical_not(self.mine))
        def _():
            self.sends.wait_send()


class RepSpread:
    def __init__(self, p, full, sems):
        self.p = p
        dir_s, dir_r, fwd_s, fwd_r = sems
        own = full.at[p.me]
        self.direct = {0: remote(own, own, dir_s.at[0], dir_r.at[0], p.partner)}
        self.passed = {}
        for k in range(1, p.A):
            self.direct[k] = remote(own, own, dir_s.at[k], dir_r.at[k], p.same(k))
            block = full.at[p.same(p.A - k)]
            self.passed[k] = remote(block, block, fwd_s.at[k - 1], fwd_r.at[k - 1], p.partner)

    @staticmethod
    def sems(A):
        return dma_sems(A, A, A - 1, A - 1)

    def start(self):
        for k in list(range(1, self.p.A)) + [0]:
            self.direct[k].start()

    def forward(self):
        for k in range(1, self.p.A):
            self.direct[k].wait_recv()
            self.passed[k].start()

    def finish(self):
        self.direct[0].wait_recv()
        for copy in self.passed.values():
            copy.wait_recv()

    def drain(self):
        drain(list(self.direct.values()) + list(self.passed.values()))


class OwnerSpread:
    def __init__(self, p, block, sems):
        self.p = p
        s0, s1, rx, rp = sems
        self.across = remote(block, block, s0.at[0], rx.at[0], p.same(1))
        self.beside = remote(block, block, s1.at[0], rp.at[0], p.partner)
        self.mine = p.z == p.me
        self.relay = p.z == p.same(1)
        self.other = jnp.logical_not(jnp.logical_or(self.mine, self.relay))

    @staticmethod
    def sems():
        return dma_sems(1, 1, 1, 1)

    def start(self):
        @pl.when(self.mine)
        def _():
            self.across.start()
            self.beside.start()

    def forward(self):
        @pl.when(self.relay)
        def _():
            self.across.wait_recv()
            self.beside.start()

    def finish(self):
        @pl.when(self.other)
        def _():
            self.beside.wait_recv()

    def drain(self):
        @pl.when(self.mine)
        def _():
            self.across.wait_send()

        @pl.when(jnp.logical_not(self.other))
        def _():
            self.beside.wait_send()


def store_all(g_qkv, g_wo, g_wi, g_wd, g_small, S, R):
    D, W = g_qkv.shape
    dr = W // 3
    ds = D // S
    V = g_wi.shape[1]
    fr = g_wd.shape[0] // S
    Z, A = S // 2, R // 2
    fs = fr * R

    def kernel(gq, go, gi, gd, gs, oq, ok, ov, oo, oi, od, *rest):
        vec_o, rest = rest[:9], list(rest[9:])

        def take(n):
            got = rest[:n]
            del rest[:n]
            return got

        p = Place(S, R)
        tq, ti, td, ts, to = take(5)
        wd = RowScatter(p, gd, fr, take(3), take(4))
        wi = RowScatter(p, gi, ds, take(3), take(4))
        qkv = RowScatter(p, gq, ds, take(3), take(4))
        sm = RowScatter(p, gs, NVEC, take(3), take(4))
        wo = PlaneScatter(p, go, ds, take(3), take(4))
        sq = RepSpread(p, tq, take(4))
        si = RepSpread(p, ti, take(4))
        sd = RepSpread(p, td, take(4))
        ss = RepSpread(p, ts, take(4))
        so = OwnerSpread(p, to, take(4))
        p.meet_all()
        groups = ((wd, sd, td), (wi, si, ti), (qkv, sq, tq), (sm, ss, ts))
        for g, _, _ in groups:
            g.start()
        wo.start()
        for g, _, _ in groups[:2]:
            for k in range(1, Z):
                g.pass_on(k)
        wo.pass_on()
        for g, _, _ in groups[2:]:
            for k in range(1, Z):
                g.pass_on(k)
        for g, spr, dst in groups[:2]:
            g.total(dst)
            spr.start()
        wo.total(to)
        so.start()
        for g, spr, dst in groups[2:]:
            g.total(dst)
            spr.start()
        for _, spr, _ in groups[:2]:
            spr.forward()
        so.forward()
        for _, spr, _ in groups[2:]:
            spr.forward()
        sd.finish()
        for r in range(R):

            def put_d(i, _, r=r):
                od[chunk_rows(i, r * fr), :] = td[r, chunk_rows(i), :].astype(F32)
                return 0

            lax.fori_loop(0, fr // CHUNK, put_d, 0)
        si.finish()

        def put_i(i, _):
            for r in range(R):
                for c in range(S):
                    lo = c * fs + r * fr
                    oi[chunk_rows(i), lo : lo + fr] = ti[
                        r, chunk_rows(i), c * fr : (c + 1) * fr
                    ].astype(F32)
            return 0

        lax.fori_loop(0, ds // CHUNK, put_i, 0)
        so.finish()
        sq.finish()

        def put_q(i, _):
            oo[chunk_rows(i), :] = to[chunk_rows(i), :].astype(F32)
            for r in range(R):
                for n, o in enumerate((oq, ok, ov)):
                    o[chunk_rows(i), r * dr : (r + 1) * dr] = tq[
                        r, chunk_rows(i), n * dr : (n + 1) * dr
                    ].astype(F32)
            return 0

        lax.fori_loop(0, ds // CHUNK, put_q, 0)
        ss.finish()
        total = ts[0]
        for r in range(1, R):
            total = total + ts[r]
        for i in range(8):
            vec_o[i][...] = total[i : i + 1, :]
        for r in range(R):
            vec_o[8][:, r * fr : (r + 1) * fr] = ts[r, 8:9, :]
        for g, spr, _ in groups:
            g.drain()
            spr.drain()
        wo.drain()
        so.drain()

    outs = [((ds, D), F32)] * 4 + [((ds, S * fs), F32), ((fs, D), F32)]
    outs += [((1, ds), F32)] * 8 + [((1, fs), F32)]
    scratch = [
        pltpu.VMEM((R, ds, W), BF),
        pltpu.VMEM((R, ds, V), BF),
        pltpu.VMEM((R, fr, D), BF),
        pltpu.VMEM((R, NVEC, ds), F32),
        pltpu.VMEM((ds, D), BF),
    ]
    for T, C, t in ((fr, D, BF), (ds, V, BF), (ds, W, BF), (NVEC, ds, F32)):
        scratch += RowScatter.bufs(Z, T, C, t) + RowScatter.sems(Z)
    scratch += PlaneScatter.bufs(Z, ds, D, BF) + PlaneScatter.sems(Z)
    for _ in range(4):
        scratch += RepSpread.sems(A)
    scratch += OwnerSpread.sems()
    return pl.pallas_call(
        kernel,
        out_shape=[jax.ShapeDtypeStruct(*o) for o in outs],
        in_specs=[VMEM_SPEC] * 5,
        out_specs=[VMEM_SPEC] * len(outs),
        scratch_shapes=scratch,
        compiler_params=pltpu.CompilerParams(
            collective_id=11, has_side_effects=True, vmem_limit_bytes=LIMIT
        ),
        cost_estimate=pl.CostEstimate(flops=0, bytes_accessed=24 << 20, transcendentals=0),
    )(g_qkv, g_wo, g_wi, g_wd, g_small)


def fast_body(
    block_input,
    out_cotangent,
    w_query,
    w_key,
    w_value,
    w_output,
    bias_query,
    bias_value,
    bias_output,
    gain_first,
    shift_first,
    w_inner,
    bias_inner,
    w_down,
    bias_down,
    gain_second,
    shift_second,
):
    S = lax.axis_size("shard")
    R = lax.axis_size("rep")
    r = lax.axis_index("rep")
    T = block_input.shape[0]
    D = w_query.shape[1]
    ds = w_query.shape[0]
    dr = D // R
    vectors = (
        bias_query,
        bias_value,
        bias_output,
        gain_first,
        shift_first,
        bias_down,
        gain_second,
        shift_second,
        bias_inner,
    )
    x_all, wqkv, wo, wi, wd, flat = fetch_all(
        block_input, w_query, w_key, w_value, w_output, w_inner, w_down, vectors, S, R
    )
    bo, gone, sone, bd, gtwo, stwo, bi = (flat[i] for i in range(2, 9))
    bqv = lax.dynamic_slice(flat[:2], (0, r * dr), (2, dr))
    bq, bv = bqv[0], bqv[1]

    N = R * T
    shape4 = (N // SEQ, SEQ, dr // HEAD_DIM, HEAD_DIM)
    qkv = mm(x_all, wqkv)
    query = (qkv[:, :dr] + bq).astype(BF).reshape(shape4)
    keyed = qkv[:, dr : 2 * dr].astype(BF).reshape(shape4)
    valued = (qkv[:, 2 * dr :] + bv).astype(BF).reshape(shape4)
    scores = ein("bqhe,bkhe->bhqk", query, keyed) * 0.125
    top = jnp.max(scores, axis=-1, keepdims=True)
    logsum = top + jnp.log(jnp.sum(jnp.exp(scores - top), axis=-1, keepdims=True))
    probs = jnp.exp(scores - logsum)
    probs_b = probs.astype(BF)
    context = ein("bhqk,bkhe->bqhe", probs_b, valued).astype(BF).reshape(N, dr)
    attn_part = mm(context, wo).astype(BF)

    normed_one, rstd_one, hidden, hidden_all = norm_one_step(attn_part, block_input, bo, gone, sone)
    inner = mm(hidden_all, wi) + bi
    phi = 0.5 * (1.0 + lax.erf(inner * INV_ROOT_TWO))
    acted = (inner * phi).astype(BF)
    slope = phi + inner * jnp.exp(-0.5 * inner * inner) * INV_ROOT_TWO_PI
    down_part = mm(acted, wd).astype(BF)

    output, d_two, sums_two, d_two_all = norm_two_step(
        down_part, hidden, bd, gtwo, stwo, out_cotangent
    )
    d_inner = mm_nt(d_two_all, wd) * slope
    g_bias_inner = jnp.sum(d_inner, axis=0)
    d_inner_b = d_inner.astype(BF)
    hid_part = mm_nt(d_inner_b, wi).astype(BF)
    g_wd = mm_tn(acted, d_two_all).astype(BF)
    g_wi = mm_tn(hidden_all, d_inner_b).astype(BF)

    d_one, sums_one, d_one_all = back_one_step(hid_part, d_two, normed_one, rstd_one, gone)
    g_wo = mm_tn(context, d_one_all).astype(BF)
    d_context = mm_nt(d_one_all, wo).astype(BF).reshape(shape4)
    d_probs = ein("bqhe,bkhe->bhqk", d_context, valued)
    delta = jnp.sum(probs * d_probs, axis=-1, keepdims=True)
    d_scores = (probs * (d_probs - delta) * 0.125).astype(BF)
    d_query = ein("bhqk,bkhe->bqhe", d_scores, keyed).reshape(N, dr)
    d_keyed = ein("bhqk,bqhe->bkhe", d_scores, query).reshape(N, dr)
    d_valued = ein("bhqk,bqhe->bkhe", probs_b, d_context).reshape(N, dr)
    g_bias_query = jnp.sum(d_query, axis=0)
    g_bias_value = jnp.sum(d_valued, axis=0)
    d_qkv = jnp.concatenate([d_query.astype(BF), d_keyed.astype(BF), d_valued.astype(BF)], 1)
    in_part = mm_nt(d_qkv, wqkv).astype(BF)
    g_qkv = mm_tn(x_all, d_qkv).astype(BF)

    def placed(v):
        return lax.dynamic_update_slice(jnp.zeros((D,), F32), v, (r * dr,))[None]

    g_small = jnp.concatenate(
        [
            placed(g_bias_query),
            placed(g_bias_value),
            sums_one[:3],
            sums_two[:3],
            g_bias_inner[None],
            jnp.zeros((NVEC - 9, D), F32),
        ],
        0,
    )
    g_small = g_small.reshape(NVEC, S, ds).transpose(1, 0, 2).reshape(S * NVEC, ds)
    grad_input = input_step(in_part, d_one)
    got = store_all(g_qkv, g_wo, g_wi, g_wd, g_small, S, R)
    gq, gk, gv, go, gi, gd = got[:6]
    gbq, gbv, gbo, ggone, gsone, gbd, ggtwo, gstwo, gbi = (v.reshape(-1) for v in got[6:])
    return (
        output,
        grad_input,
        gq,
        gk,
        gv,
        go,
        gbq,
        gbv,
        gbo,
        ggone,
        gsone,
        gi,
        gbi,
        gd,
        gbd,
        ggtwo,
        gstwo,
    )


def fits_fast(mesh):
    S, R = mesh.shape["shard"], mesh.shape["rep"]
    return R == 4 and S == 2 * R


def solution(mesh):
    tokens = P(("shard", "rep"), None)
    mat = P("shard", None)
    vec = P("shard")
    params = (mat, mat, mat, mat, vec, vec, vec, vec, vec, mat, vec, mat, vec, vec, vec)
    return jax.shard_map(
        fast_body if fits_fast(mesh) else body,
        mesh=mesh,
        in_specs=(tokens, tokens) + params,
        out_specs=(tokens, tokens) + params,
        check_vma=False,
    )
```

```python
import jax
import jax.numpy as jnp
from jax import lax
from jax.experimental import pallas as pl
from jax.experimental.pallas import tpu as pltpu
from jax.sharding import PartitionSpec as P

HEAD_DIM = 64
SEQ = 128
PAD = 16


EPS = 1e-06
INV_ROOT_TWO = 0.7071067811865476
INV_ROOT_TWO_PI = 0.3989422804014327
BF = jnp.bfloat16
F32 = jnp.float32


def norm_parts(resid):
    centre = resid - jnp.mean(resid, axis=-1, keepdims=True)
    variance = jnp.mean(centre * centre, axis=-1, keepdims=True)
    rstd = lax.rsqrt(variance + EPS)
    return (centre * rstd, rstd)


def norm_back(upstream, normed, rstd):
    return rstd * (
        upstream
        - jnp.mean(upstream, axis=-1, keepdims=True)
        - normed * jnp.mean(upstream * normed, axis=-1, keepdims=True)
    )


def mm(a, b):
    return jnp.dot(a, b, preferred_element_type=F32)


def mm_nt(a, b):
    return lax.dot_general(a, b, (((1,), (1,)), ((), ())), preferred_element_type=F32)


def mm_tn(a, b):
    return lax.dot_general(a, b, (((0,), (0,)), ((), ())), preferred_element_type=F32)


def ein(spec, a, b):
    return jnp.einsum(spec, a, b, preferred_element_type=F32)


MESH = pl.DeviceIdType.MESH
CHUNK = 16


class Peers:
    def __init__(self, R):
        self.R, self.A = R, R // 2
        self.me = lax.axis_index("rep")
        self.c = lax.rem(self.me, 2)
        self.a = lax.div(self.me, 2)
        self.partner = self.me + 1 - 2 * self.c

    def chip(self, k):
        return lax.rem(self.a + k, self.A)

    def same(self, k):
        return 2 * self.chip(k) + self.c

    def other(self, k):
        return 2 * self.chip(k) + 1 - self.c

    def meet(self):
        barrier = pltpu.get_barrier_semaphore()
        for dev in [self.partner] + [self.same(k) for k in range(1, self.A)]:
            pl.semaphore_signal(barrier, inc=1, device_id={"rep": dev}, device_id_type=MESH)
        pl.semaphore_wait(barrier, self.A)


def rows_of(index, T):
    return pl.ds(pl.multiple_of(index * T, T), T)


def chunk_rows(i, base=None):
    start = i * CHUNK if base is None else base + i * CHUNK
    return pl.ds(pl.multiple_of(start, CHUNK), CHUNK)


def remote(src, dst, send, recv, dev):
    return pltpu.make_async_remote_copy(
        src_ref=src,
        dst_ref=dst,
        send_sem=send,
        recv_sem=recv,
        device_id={"rep": dev},
        device_id_type=MESH,
    )


def scatter_sum(p, part, T, near, far, out, sems):
    near_s, near_r, far_s, far_r = sems
    order = list(range(1, p.A)) + [0]
    first = {
        k: remote(
            part.at[rows_of(p.other(k), T)], near.at[k], near_s.at[k], near_r.at[k], p.partner
        )
        for k in order
    }
    for k in order:
        first[k].start()
    second = []
    for k in range(1, p.A):
        first[k].wait_recv()
        base = p.same(k) * T

        def add(i, _, k=k, base=base):
            mine = part[chunk_rows(i, base), :].astype(F32)
            out[k - 1, chunk_rows(i), :] = (mine + near[k, chunk_rows(i), :].astype(F32)).astype(BF)
            return 0

        lax.fori_loop(0, T // CHUNK, add, 0)
        copy = remote(out.at[k - 1], far.at[k - 1], far_s.at[k - 1], far_r.at[k - 1], p.same(k))
        copy.start()
        second.append(copy)
    first[0].wait_recv()
    for copy in second:
        copy.wait_recv()

    def read(i):
        total = part[chunk_rows(i, p.me * T), :].astype(F32) + near[0, chunk_rows(i), :].astype(F32)
        for k in range(1, p.A):
            total = total + far[k - 1, chunk_rows(i), :].astype(F32)
        return total

    return read, list(first.values()) + second


def spread(p, src, full, T, sems):
    dir_s, dir_r, fwd_s, fwd_r = sems
    mine = full.at[rows_of(p.me, T)]
    direct = {}
    for k in list(range(1, p.A)) + [0]:
        dev = p.partner if k == 0 else p.same(k)
        direct[k] = remote(src, mine, dir_s.at[k], dir_r.at[k], dev)
        direct[k].start()
    passed = []
    for k in range(1, p.A):
        direct[k].wait_recv()
        block = full.at[rows_of(p.same(p.A - k), T)]
        copy = remote(block, block, fwd_s.at[k - 1], fwd_r.at[k - 1], p.partner)
        copy.start()
        passed.append(copy)
    direct[0].wait_recv()
    for copy in passed:
        copy.wait_recv()
    return list(direct.values()) + passed


def drain(copies):
    for copy in copies:
        copy.wait_send()


def run_kernel(kernel, cid, T, D, R, ins, outs, scatter, gather):
    A = R // 2
    few = max(A - 1, 1)
    scratch = []
    if scatter:
        scratch += [
            pltpu.VMEM((A, T, D), BF),
            pltpu.VMEM((few, T, D), BF),
            pltpu.VMEM((few, T, D), BF),
        ]
        scratch += [pltpu.SemaphoreType.DMA((n,)) for n in (A, A, few, few)]
    if gather:
        scratch += [pltpu.SemaphoreType.DMA((n,)) for n in (A, A, few, few)]
    vmem = pl.BlockSpec(memory_space=pltpu.VMEM)
    return pl.pallas_call(
        kernel,
        out_shape=[jax.ShapeDtypeStruct(*o) for o in outs],
        in_specs=[vmem] * len(ins),
        out_specs=[vmem] * len(outs),
        scratch_shapes=scratch,
        compiler_params=pltpu.CompilerParams(collective_id=cid, has_side_effects=True),
        cost_estimate=pl.CostEstimate(flops=0, bytes_accessed=24 << 20, transcendentals=0),
    )(*ins)


def gather_kernel(block, R, cid):
    T, D = block.shape

    def kernel(src, full, *sems):
        p = Peers(R)
        p.meet()

        def put(i, _):
            full[chunk_rows(i, p.me * T), :] = src[chunk_rows(i), :]
            return 0

        lax.fori_loop(0, T // CHUNK, put, 0)
        drain(spread(p, src, full, T, sems))

    return run_kernel(kernel, cid, T, D, R, [block], [((R * T, D), BF)], False, True)[0]


def norm_one_step(partial, x, bo, gone, sone):
    T, D = x.shape
    R = partial.shape[0] // T

    def kernel(part, xr, bor, gr, sr, normed_o, rstd_o, hidden_o, full, near, far, out, *sems):
        p = Peers(R)
        p.meet()
        read, sent = scatter_sum(p, part, T, near, far, out, sems[:4])

        def step(i, _):
            normed, rstd = norm_parts(xr[chunk_rows(i), :].astype(F32) + read(i) + bor[...])
            hidden = normed * gr[...] + sr[...]
            normed_o[chunk_rows(i), :] = normed
            rstd_o[chunk_rows(i), :] = rstd
            hidden_o[chunk_rows(i), :] = hidden
            full[chunk_rows(i, p.me * T), :] = hidden.astype(BF)
            return 0

        lax.fori_loop(0, T // CHUNK, step, 0)
        drain(sent + spread(p, full.at[rows_of(p.me, T)], full, T, sems[4:]))

    ins = [partial, x, bo[None], gone[None], sone[None]]
    outs = [((T, D), F32), ((T, 1), F32), ((T, D), F32), ((R * T, D), BF)]
    return run_kernel(kernel, 1, T, D, R, ins, outs, True, True)


def add_sums(ref, values):
    for n, v in enumerate(values):
        ref[n : n + 1, :] += jnp.sum(v, axis=0, keepdims=True)


def norm_two_step(partial, hidden, bd, gtwo, stwo, cot):
    T, D = hidden.shape
    R = partial.shape[0] // T

    def kernel(part, hr, br, gr, sr, cr, out_o, d_o, sums, full, near, far, out, *sems):
        p = Peers(R)
        p.meet()
        sums[...] = jnp.zeros_like(sums)
        read, sent = scatter_sum(p, part, T, near, far, out, sems[:4])

        def step(i, _):
            normed, rstd = norm_parts(hr[chunk_rows(i), :] + read(i) + br[...])
            out_o[chunk_rows(i), :] = (normed * gr[...] + sr[...]).astype(BF)
            dout = cr[chunk_rows(i), :].astype(F32)
            d_two = norm_back(dout * gr[...], normed, rstd)
            add_sums(sums, (d_two, dout * normed, dout))
            d_o[chunk_rows(i), :] = d_two
            full[chunk_rows(i, p.me * T), :] = d_two.astype(BF)
            return 0

        lax.fori_loop(0, T // CHUNK, step, 0)
        drain(sent + spread(p, full.at[rows_of(p.me, T)], full, T, sems[4:]))

    ins = [partial, hidden, bd[None], gtwo[None], stwo[None], cot]
    outs = [((T, D), BF), ((T, D), F32), ((8, D), F32), ((R * T, D), BF)]
    return run_kernel(kernel, 2, T, D, R, ins, outs, True, True)


def back_one_step(partial, d_two, normed, rstd, gone):
    T, D = d_two.shape
    R = partial.shape[0] // T

    def kernel(part, dr, nr, rr, gr, d_o, sums, full, near, far, out, *sems):
        p = Peers(R)
        p.meet()
        sums[...] = jnp.zeros_like(sums)
        read, sent = scatter_sum(p, part, T, near, far, out, sems[:4])

        def step(i, _):
            d_hidden = dr[chunk_rows(i), :] + read(i)
            normed = nr[chunk_rows(i), :]
            d_one = norm_back(d_hidden * gr[...], normed, rr[chunk_rows(i), :])
            add_sums(sums, (d_one, d_hidden * normed, d_hidden))
            d_o[chunk_rows(i), :] = d_one
            full[chunk_rows(i, p.me * T), :] = d_one.astype(BF)
            return 0

        lax.fori_loop(0, T // CHUNK, step, 0)
        drain(sent + spread(p, full.at[rows_of(p.me, T)], full, T, sems[4:]))

    ins = [partial, d_two, normed, rstd, gone[None]]
    outs = [((T, D), F32), ((8, D), F32), ((R * T, D), BF)]
    return run_kernel(kernel, 3, T, D, R, ins, outs, True, True)


def input_step(partial, d_one):
    T, D = d_one.shape
    R = partial.shape[0] // T

    def kernel(part, dr, grad, near, far, out, *sems):
        p = Peers(R)
        p.meet()
        read, sent = scatter_sum(p, part, T, near, far, out, sems)

        def step(i, _):
            grad[chunk_rows(i), :] = (dr[chunk_rows(i), :] + read(i)).astype(BF)
            return 0

        lax.fori_loop(0, T // CHUNK, step, 0)
        drain(sent)

    return run_kernel(kernel, 4, T, D, R, [partial, d_one], [((T, D), BF)], True, False)[0]


def body(
    block_input,
    out_cotangent,
    w_query,
    w_key,
    w_value,
    w_output,
    bias_query,
    bias_value,
    bias_output,
    gain_first,
    shift_first,
    w_inner,
    bias_inner,
    w_down,
    bias_down,
    gain_second,
    shift_second,
):
    S = lax.axis_size("shard")
    R = lax.axis_size("rep")
    r = lax.axis_index("rep")
    T = block_input.shape[0]
    D = w_query.shape[1]
    ds = w_query.shape[0]
    dr = D // R
    fs = w_down.shape[0]
    fr = fs // R
    W = 4 * dr

    def cols(w):
        return lax.dynamic_slice(w, (0, r * dr), (ds, dr))

    small = jnp.concatenate(
        [
            v.astype(BF)
            for v in (
                bias_query,
                bias_value,
                bias_output,
                gain_first,
                shift_first,
                bias_down,
                gain_second,
                shift_second,
                bias_inner,
            )
        ]
    )
    n_small = small.shape[0]
    small = jnp.pad(small, (0, PAD * W - n_small)).reshape(PAD, W)
    pack = jnp.concatenate(
        [jnp.concatenate([cols(w_query), cols(w_key), cols(w_value), cols(w_output)], 1), small], 0
    )
    got = lax.all_gather(pack, "shard", axis=0)
    x_all = gather_kernel(block_input, R, 0)
    wi_r = lax.dynamic_index_in_dim(w_inner.reshape(ds, S, R, fr), r, 2, keepdims=False)
    V = S * fr
    dv = fr * D // V
    wd_r = lax.dynamic_slice(w_down, (r * fr, 0), (fr, D)).reshape(dv, V)
    mlp = lax.all_gather(jnp.concatenate([wi_r.reshape(ds, V), wd_r], 0), "shard", axis=0)
    wi = mlp[:, :ds].reshape(D, V)
    wd = mlp[:, ds:].reshape(V, D)
    wqkv = got[:, :ds, : 3 * dr].reshape(D, 3 * dr)
    wo = lax.all_to_all(
        got[:, :ds, 3 * dr :].reshape(D, dr), "rep", split_axis=0, concat_axis=1, tiled=True
    )
    flat = got[:, ds:, :].reshape(S, PAD * W)[:, :n_small].astype(F32)
    bq, bv, bo, gone, sone, bd, gtwo, stwo = (
        flat[:, i * ds : (i + 1) * ds].reshape(D) for i in range(8)
    )
    bi = lax.dynamic_index_in_dim(flat[:, 8 * ds :].reshape(S, R, fr), r, 1, keepdims=False)
    bi = bi.reshape(S * fr)
    bq = lax.dynamic_slice(bq, (r * dr,), (dr,))
    bv = lax.dynamic_slice(bv, (r * dr,), (dr,))

    N = R * T
    shape4 = (N // SEQ, SEQ, dr // HEAD_DIM, HEAD_DIM)
    qkv = mm(x_all, wqkv)
    query = (qkv[:, :dr] + bq).astype(BF).reshape(shape4)
    keyed = qkv[:, dr : 2 * dr].astype(BF).reshape(shape4)
    valued = (qkv[:, 2 * dr :] + bv).astype(BF).reshape(shape4)
    scores = ein("bqhe,bkhe->bhqk", query, keyed) * 0.125
    top = jnp.max(scores, axis=-1, keepdims=True)
    logsum = top + jnp.log(jnp.sum(jnp.exp(scores - top), axis=-1, keepdims=True))
    probs = jnp.exp(scores - logsum)
    probs_b = probs.astype(BF)
    context = ein("bhqk,bkhe->bqhe", probs_b, valued).astype(BF).reshape(N, dr)
    attn_part = mm(context, wo).astype(BF)

    normed_one, rstd_one, hidden, hidden_all = norm_one_step(attn_part, block_input, bo, gone, sone)
    inner = mm(hidden_all, wi) + bi
    phi = 0.5 * (1.0 + lax.erf(inner * INV_ROOT_TWO))
    acted = (inner * phi).astype(BF)
    slope = phi + inner * jnp.exp(-0.5 * inner * inner) * INV_ROOT_TWO_PI
    down_part = mm(acted, wd).astype(BF)

    output, d_two, sums_two, d_two_all = norm_two_step(
        down_part, hidden, bd, gtwo, stwo, out_cotangent
    )
    d_inner = mm_nt(d_two_all, wd) * slope
    g_bias_inner = jnp.sum(d_inner, axis=0)
    d_inner_b = d_inner.astype(BF)
    hid_part = mm_nt(d_inner_b, wi).astype(BF)
    g_wd = mm_tn(acted, d_two_all).astype(BF).reshape(S, dv, V)
    g_wi = mm_tn(hidden_all, d_inner_b).astype(BF).reshape(S, ds, V)
    g_mlp = lax.psum_scatter(
        jnp.concatenate([g_wi, g_wd], 1), "shard", scatter_dimension=0, tiled=True
    )[0]

    d_one, sums_one, d_one_all = back_one_step(hid_part, d_two, normed_one, rstd_one, gone)
    g_wo = mm_tn(context, d_one_all).astype(BF)
    g_wo = lax.all_to_all(g_wo, "rep", split_axis=1, concat_axis=0, tiled=True)
    d_context = mm_nt(d_one_all, wo).astype(BF).reshape(shape4)
    d_probs = ein("bqhe,bkhe->bhqk", d_context, valued)
    delta = jnp.sum(probs * d_probs, axis=-1, keepdims=True)
    d_scores = (probs * (d_probs - delta) * 0.125).astype(BF)
    d_query = ein("bhqk,bkhe->bqhe", d_scores, keyed).reshape(N, dr)
    d_keyed = ein("bhqk,bqhe->bkhe", d_scores, query).reshape(N, dr)
    d_valued = ein("bhqk,bqhe->bkhe", probs_b, d_context).reshape(N, dr)
    g_bias_query = jnp.sum(d_query, axis=0)
    g_bias_value = jnp.sum(d_valued, axis=0)
    d_qkv = jnp.concatenate([d_query.astype(BF), d_keyed.astype(BF), d_valued.astype(BF)], 1)
    in_part = mm_nt(d_qkv, wqkv).astype(BF)

    def placed(v):
        return lax.dynamic_update_slice(jnp.zeros((D,), F32), v, (r * dr,)).reshape(S, ds)

    g_small = jnp.concatenate(
        [
            placed(g_bias_query),
            placed(g_bias_value),
            sums_one[0].reshape(S, ds),
            sums_one[1].reshape(S, ds),
            sums_one[2].reshape(S, ds),
            sums_two[0].reshape(S, ds),
            sums_two[1].reshape(S, ds),
            sums_two[2].reshape(S, ds),
            g_bias_inner.reshape(S, fr),
        ],
        1,
    ).astype(BF)
    n_g = g_small.shape[1]
    g_small = jnp.pad(g_small, ((0, 0), (0, PAD * W - n_g))).reshape(S, PAD, W)
    g_pack = jnp.concatenate([mm_tn(x_all, d_qkv).astype(BF), g_wo], 1).reshape(S, ds, W)
    g_pack = jnp.concatenate([g_pack, g_small], 1)
    g_pack = lax.psum_scatter(g_pack, "shard", scatter_dimension=0, tiled=True)[0]

    grad_input = input_step(in_part, d_one)

    mlps = gather_kernel(g_mlp, R, 5).reshape(R, ds + dv, V).astype(F32)
    wd_out = mlps[:, ds:].reshape(R * fr, D)
    wi_out = mlps[:, :ds].reshape(R, ds, S, fr).transpose(1, 2, 0, 3).reshape(ds, S * R * fr)
    packs = gather_kernel(g_pack, R, 6).reshape(R, ds + PAD, W).astype(F32)
    main = packs[:, :ds].reshape(R, ds, 4, dr).transpose(2, 1, 0, 3).reshape(4, ds, D)
    tail = packs[:, ds:].reshape(R, PAD * W)
    summed = jnp.sum(tail[:, : 8 * ds], axis=0)
    gbq, gbv, gbo, ggone, gsone, gbd, ggtwo, gstwo = (
        summed[i * ds : (i + 1) * ds] for i in range(8)
    )
    gbi = tail[:, 8 * ds : n_g].reshape(fs)
    return (
        output,
        grad_input,
        main[0],
        main[1],
        main[2],
        main[3],
        gbq,
        gbv,
        gbo,
        ggone,
        gsone,
        wi_out,
        gbi,
        wd_out,
        gbd,
        ggtwo,
        gstwo,
    )

VMEM_SPEC = pl.BlockSpec(memory_space=pltpu.VMEM)
ANY_SPEC = pl.BlockSpec(memory_space=pl.ANY)
LIMIT = 56 << 20
NVEC = 16


def dma_sems(*counts):
    return [pltpu.SemaphoreType.DMA((n,)) for n in counts]


class Place(Peers):
    def __init__(self, S, R):
        super().__init__(R)
        self.S, self.Z = S, S // 2
        self.s = lax.axis_index("shard")
        self.z = lax.div(self.s, 2)
        self.y = lax.rem(self.s, 2)
        self.across = self.s + 1 - 2 * self.y

    def up(self, k):
        return 2 * lax.rem(self.z + k, self.Z) + self.y

    def down(self, k):
        return 2 * lax.rem(self.z + self.Z - k, self.Z) + self.y

    def flip(self, s):
        return s + 1 - 2 * self.y

    def meet_all(self):
        barrier = pltpu.get_barrier_semaphore()
        for dev in [self.partner] + [self.same(k) for k in range(1, self.A)]:
            pl.semaphore_signal(barrier, inc=1, device_id={"rep": dev}, device_id_type=MESH)
        for dev in [self.across] + [self.up(k) for k in range(1, self.Z)]:
            pl.semaphore_signal(barrier, inc=1, device_id={"shard": dev}, device_id_type=MESH)
        pl.semaphore_wait(barrier, self.A + self.Z)


def to_shard(src, dst, send, recv, dev):
    return pltpu.make_async_remote_copy(
        src_ref=src,
        dst_ref=dst,
        send_sem=send,
        recv_sem=recv,
        device_id={"shard": dev},
        device_id_type=MESH,
    )


class RowGather:
    def __init__(self, p, full, T, sems, cols=None):
        self.p, self.full, self.T, self.cols = p, full, T, cols
        self.zs, self.zr, self.ys, self.yr = sems
        self.far = {k: self.copy(p.s, self.zs, self.zr, k - 1, p.up(k)) for k in range(1, p.Z)}
        self.near = {0: self.copy(p.s, self.ys, self.yr, 0, p.across)}
        for k in range(1, p.Z):
            self.near[k] = self.copy(p.down(k), self.ys, self.yr, k, p.across)

    @staticmethod
    def sems(Z):
        return dma_sems(Z - 1, Z - 1, Z, Z)

    def copy(self, block, send, recv, i, dev):
        rows = rows_of(block, self.T)
        rows = self.full.at[rows] if self.cols is None else self.full.at[rows, self.cols]
        return to_shard(rows, rows, send.at[i], recv.at[i], dev)

    def start(self):
        for k in range(1, self.p.Z):
            self.far[k].start()
        self.near[0].start()

    def forward(self, k):
        self.far[k].wait_recv()
        self.near[k].start()

    def finish(self):
        for k in range(self.p.Z):
            self.near[k].wait_recv()

    def drain(self):
        for copy in list(self.far.values()) + list(self.near.values()):
            copy.wait_send()


class PlaneGather:
    def __init__(self, p, full, T, sems):
        self.p = p
        self.zs, self.zr, self.ys, self.yr = sems
        rows = full.at[rows_of(p.y, T)]
        self.far = {
            k: to_shard(rows, rows, self.zs.at[k - 1], self.zr.at[0], p.up(k))
            for k in range(1, p.Z)
        }
        self.near = to_shard(rows, rows, self.ys.at[0], self.yr.at[0], p.across)
        self.mine = p.z == p.me

    @staticmethod
    def sems(Z):
        return dma_sems(Z - 1, 1, 1, 1)

    def start(self):
        @pl.when(self.mine)
        def _():
            for k in range(1, self.p.Z):
                self.far[k].start()
            self.near.start()

    def forward(self):
        @pl.when(jnp.logical_not(self.mine))
        def _():
            self.far[1].wait_recv()
            self.near.start()

    def finish(self):
        self.near.wait_recv()

    def drain(self):
        @pl.when(self.mine)
        def _():
            for k in range(1, self.p.Z):
                self.far[k].wait_send()

        self.near.wait_send()


class RowScatter:
    def __init__(self, p, part, T, bufs, sems):
        self.p, self.part, self.T = p, part, T
        self.close, self.out, self.far = bufs
        ys, yr, zs, zr = sems
        self.first = {}
        for k in range(p.Z):
            to = p.up(k)
            self.first[k] = to_shard(
                part.at[rows_of(p.flip(to), T)], self.close.at[k], ys.at[k], yr.at[k], p.across
            )
        self.second = {
            k: to_shard(
                self.out.at[k - 1], self.far.at[k - 1], zs.at[k - 1], zr.at[k - 1], p.up(k)
            )
            for k in range(1, p.Z)
        }

    @staticmethod
    def bufs(Z, T, C, dtype):
        return [pltpu.VMEM((n, T, C), dtype) for n in (Z, Z - 1, Z - 1)]

    @staticmethod
    def sems(Z):
        return dma_sems(Z, Z, Z - 1, Z - 1)

    def start(self):
        for k in list(range(1, self.p.Z)) + [0]:
            self.first[k].start()

    def pass_on(self, k):
        self.first[k].wait_recv()
        base = self.p.up(k) * self.T
        dtype = self.out.dtype

        def add(i, _):
            mine = self.part[chunk_rows(i, base), :].astype(F32)
            near = self.close[k, chunk_rows(i), :].astype(F32)
            self.out[k - 1, chunk_rows(i), :] = (mine + near).astype(dtype)
            return 0

        lax.fori_loop(0, self.T // CHUNK, add, 0)
        self.second[k].start()

    def total(self, dst, at=None):
        p = self.p
        self.first[0].wait_recv()
        for k in range(1, p.Z):
            self.second[k].wait_recv()

        def add(i, _):
            total = self.part[chunk_rows(i, p.s * self.T), :].astype(F32)
            total = total + self.close[0, chunk_rows(i), :].astype(F32)
            for k in range(1, p.Z):
                total = total + self.far[k - 1, chunk_rows(i), :].astype(F32)
            dst[p.me, chunk_rows(i), :] = total.astype(dst.dtype)
            return 0

        lax.fori_loop(0, self.T // CHUNK, add, 0)

    def drain(self):
        for copy in list(self.first.values()) + list(self.second.values()):
            copy.wait_send()


class PlaneScatter:
    def __init__(self, p, part, T, bufs, sems):
        self.p, self.part, self.T = p, part, T
        self.close, self.out, self.far = bufs
        ys, yr, zs, zr = sems
        self.first = to_shard(
            part.at[rows_of(1 - p.y, T)], self.close, ys.at[0], yr.at[0], p.across
        )
        self.mine = p.z == p.me
        self.hop = lax.rem(p.z + p.Z - p.me, p.Z)
        self.sends = to_shard(
            self.out,
            self.far.at[jnp.maximum(self.hop - 1, 0)],
            zs.at[0],
            zr.at[jnp.maximum(self.hop - 1, 0)],
            2 * p.me + p.y,
        )
        self.gets = [
            to_shard(self.out, self.far.at[k], zs.at[0], zr.at[k], p.up(k + 1))
            for k in range(p.Z - 1)
        ]

    @staticmethod
    def bufs(Z, T, C, dtype):
        return [pltpu.VMEM((T, C), dtype), pltpu.VMEM((T, C), dtype), pltpu.VMEM((Z - 1, T, C), dtype)]

    @staticmethod
    def sems(Z):
        return dma_sems(1, 1, 1, Z - 1)

    def start(self):
        self.first.start()

    def pass_on(self):
        self.first.wait_recv()

        def add(i, _):
            mine = self.part[chunk_rows(i, self.p.y * self.T), :].astype(F32)
            self.out[chunk_rows(i), :] = (mine + self.close[chunk_rows(i), :].astype(F32)).astype(BF)
            return 0

        lax.fori_loop(0, self.T // CHUNK, add, 0)

        @pl.when(jnp.logical_not(self.mine))
        def _():
            self.sends.start()

    def total(self, dst):
        @pl.when(self.mine)
        def _():
            for copy in self.gets:
                copy.wait_recv()

            def add(i, _):
                total = self.part[chunk_rows(i, self.p.y * self.T), :].astype(F32)
                total = total + self.close[chunk_rows(i), :].astype(F32)
                for k in range(self.p.Z - 1):
                    total = total + self.far[k, chunk_rows(i), :].astype(F32)
                dst[chunk_rows(i), :] = total.astype(BF)
                return 0

            lax.fori_loop(0, self.T // CHUNK, add, 0)

    def drain(self):
        self.first.wait_send()

        @pl.when(jnp.logical_not(self.mine))
        def _():
            self.sends.wait_send()


class RepSpread:
    def __init__(self, p, full, sems):
        self.p = p
        dir_s, dir_r, fwd_s, fwd_r = sems
        own = full.at[p.me]
        self.direct = {0: remote(own, own, dir_s.at[0], dir_r.at[0], p.partner)}
        self.passed = {}
        for k in range(1, p.A):
            self.direct[k] = remote(own, own, dir_s.at[k], dir_r.at[k], p.same(k))
            block = full.at[p.same(p.A - k)]
            self.passed[k] = remote(block, block, fwd_s.at[k - 1], fwd_r.at[k - 1], p.partner)

    @staticmethod
    def sems(A):
        return dma_sems(A, A, A - 1, A - 1)

    def start(self):
        for k in list(range(1, self.p.A)) + [0]:
            self.direct[k].start()

    def forward(self):
        for k in range(1, self.p.A):
            self.direct[k].wait_recv()
            self.passed[k].start()

    def finish(self):
        self.direct[0].wait_recv()
        for copy in self.passed.values():
            copy.wait_recv()

    def drain(self):
        drain(list(self.direct.values()) + list(self.passed.values()))


class OwnerSpread:
    def __init__(self, p, block, sems):
        self.p = p
        s0, s1, rx, rp = sems
        self.across = remote(block, block, s0.at[0], rx.at[0], p.same(1))
        self.beside = remote(block, block, s1.at[0], rp.at[0], p.partner)
        self.mine = p.z == p.me
        self.relay = p.z == p.same(1)
        self.other = jnp.logical_not(jnp.logical_or(self.mine, self.relay))

    @staticmethod
    def sems():
        return dma_sems(1, 1, 1, 1)

    def start(self):
        @pl.when(self.mine)
        def _():
            self.across.start()
            self.beside.start()

    def forward(self):
        @pl.when(self.relay)
        def _():
            self.across.wait_recv()
            self.beside.start()

    def finish(self):
        @pl.when(self.other)
        def _():
            self.beside.wait_recv()

    def drain(self):
        @pl.when(self.mine)
        def _():
            self.across.wait_send()

        @pl.when(jnp.logical_not(self.other))
        def _():
            self.beside.wait_send()

class RepScatter:
    def __init__(self, p, part, T, bufs, sems):
        self.p, self.part, self.T = p, part, T
        self.near, self.out, self.far = bufs
        near_s, near_r, far_s, far_r = sems
        self.first = {
            k: remote(
                part.at[rows_of(p.other(k), T)],
                self.near.at[k],
                near_s.at[k],
                near_r.at[k],
                p.partner,
            )
            for k in range(p.A)
        }
        self.second = {
            k: remote(
                self.out.at[k - 1], self.far.at[k - 1], far_s.at[k - 1], far_r.at[k - 1], p.same(k)
            )
            for k in range(1, p.A)
        }

    @staticmethod
    def bufs(A, T, D):
        return [pltpu.VMEM((n, T, D), BF) for n in (A, A - 1, A - 1)]

    @staticmethod
    def sems(A):
        return dma_sems(A, A, A - 1, A - 1)

    def start_far(self):
        for k in range(1, self.p.A):
            self.first[k].start()

    def start_near(self):
        self.first[0].start()

    def pass_on(self):
        for k in range(1, self.p.A):
            self.first[k].wait_recv()
            base = self.p.same(k) * self.T

            def add(i, _, k=k, base=base):
                mine = self.part[step_rows(i, base), :].astype(F32)
                near = self.near[k, step_rows(i), :].astype(F32)
                self.out[k - 1, step_rows(i), :] = (mine + near).astype(BF)
                return 0

            lax.fori_loop(0, self.T // STEP, add, 0)
            self.second[k].start()

    def finish(self):
        self.first[0].wait_recv()
        for copy in self.second.values():
            copy.wait_recv()

    def read(self, i):
        total = self.part[step_rows(i, self.p.me * self.T), :].astype(F32)
        total = total + self.near[0, step_rows(i), :].astype(F32)
        for k in range(1, self.p.A):
            total = total + self.far[k - 1, step_rows(i), :].astype(F32)
        return total

    def drain(self):
        drain(list(self.first.values()) + list(self.second.values()))


STEP = 32


def step_rows(i, base=None):
    start = i * STEP if base is None else base + i * STEP
    return pl.ds(pl.multiple_of(start, STEP), STEP)


class TokenSpread:
    def __init__(self, p, full, T, sems):
        self.p = p
        dir_s, dir_r, fwd_s, fwd_r = sems
        own = full.at[rows_of(p.me, T)]
        self.direct = {0: remote(own, own, dir_s.at[0], dir_r.at[0], p.partner)}
        self.passed = {}
        for k in range(1, p.A):
            self.direct[k] = remote(own, own, dir_s.at[k], dir_r.at[k], p.same(k))
            block = full.at[rows_of(p.same(p.A - k), T)]
            self.passed[k] = remote(block, block, fwd_s.at[k - 1], fwd_r.at[k - 1], p.partner)

    @staticmethod
    def sems(A):
        return dma_sems(A, A, A - 1, A - 1)

    def start(self):
        for k in list(range(1, self.p.A)) + [0]:
            self.direct[k].start()

    def beside(self):
        self.direct[0].wait_recv()

    def across(self):
        for k in range(1, self.p.A):
            self.direct[k].wait_recv()
            self.passed[k].start()
        for copy in self.passed.values():
            copy.wait_recv()

    def drain(self):
        drain(list(self.direct.values()) + list(self.passed.values()))


class Bag:
    def __init__(self):
        self.names, self.specs = [], []

    def want(self, name, specs):
        specs = specs if isinstance(specs, list) else [specs]
        self.names.append((name, len(specs)))
        self.specs += specs

    def hand_out(self, refs):
        got, at = {}, 0
        for name, n in self.names:
            got[name] = refs[at] if n == 1 else list(refs[at : at + n])
            at += n
        return got


def fold(v):
    return jnp.sum(v.reshape(v.shape[0] // 8, 8, v.shape[1]), axis=0)


TILE = 256


def tiles(n, body):
    def step(i, _):
        body(pl.ds(pl.multiple_of(i * TILE, TILE), TILE))
        return 0

    lax.fori_loop(0, n // TILE, step, 0)


def layer(x, cot, wq, wk, wv, wo, wi, wd, vectors, S, R):
    T, D = x.shape
    ds, fs = wq.shape[0], wd.shape[0]
    dr, fr = D // R, fs // R
    V = S * fr
    W = 3 * dr
    Z, A = S // 2, R // 2
    nv = len(vectors)
    N = R * T
    C = N // A
    pairs = dr // 128
    half = V // 2

    bag = Bag()
    bag.want("here", pltpu.SemaphoreType.DMA((S + 6,)))
    bag.want("small", pltpu.VMEM((S * NVEC, ds), F32))
    bag.want("flat", pltpu.VMEM((NVEC, D), F32))
    for name, shape, t in (
        ("x_all", (N, D), BF),
        ("wqkv", (D, W), BF),
        ("wor", (dr, D), BF),
        ("wir", (D, V), BF),
        ("wdr", (V, D), BF),
        ("qkv", (N, W), BF),
        ("probs", (N * dr // HEAD_DIM, SEQ), F32),
        ("ctx", (N, dr), BF),
        ("part", (N, D), BF),
        ("normed", (T, D), F32),
        ("rstd", (T, 128), F32),
        ("hidden", (T, D), F32),
        ("hid_all", (N, D), BF),
        ("acted", (N, V), BF),
        ("slope", (N, V), F32),
        ("d_two", (T, D), F32),
        ("d2_all", (N, D), BF),
        ("d_in", (N, V), BF),
        ("d_one", (T, D), F32),
        ("d1_all", (N, D), BF),
        ("dctx", (N, dr), BF),
        ("dqkv", (N, W), BF),
        ("sums", (48, D), F32),
        ("gbi8", (8, V), F32),
        ("gqv8", (8, 2 * dr), F32),
        ("gflat", (NVEC, D), F32),
        ("gs", (S * NVEC, ds), F32),
        ("gwd", (V, D), BF),
        ("gwi", (D, V), BF),
        ("gqkv", (D, W), BF),
        ("gwo", (dr, D), BF),
        ("tq", (R, ds, W), BF),
        ("ti", (R, ds, V), BF),
        ("td", (R, fr, D), BF),
        ("ts", (R, NVEC, ds), F32),
        ("to", (ds, D), BF),
    ):
        bag.want(name, pltpu.VMEM(shape, t))
    for name in ("smalls", "g_qkv", "g_wia", "g_wib", "g_wda", "g_wdb"):
        bag.want(name, RowGather.sems(Z))
    bag.want("g_wo", PlaneGather.sems(Z))
    for name in ("ax", "a1", "a2", "a3"):
        bag.want(name, TokenSpread.sems(A))
    for name in ("t1", "t2", "t3", "t4"):
        bag.want(name + "b", RepScatter.bufs(A, T, D))
        bag.want(name + "s", RepScatter.sems(A))
    for name, n, c, t in (
        ("rwd", fr, D, BF),
        ("rwi", ds, V, BF),
        ("rqkv", ds, W, BF),
        ("rsm", NVEC, ds, F32),
    ):
        bag.want(name + "b", RowScatter.bufs(Z, n, c, t))
        bag.want(name + "s", RowScatter.sems(Z))
        bag.want(name + "p", RepSpread.sems(A))
    bag.want("rwob", PlaneScatter.bufs(Z, ds, D, BF))
    bag.want("rwos", PlaneScatter.sems(Z))
    bag.want("rwop", OwnerSpread.sems())

    def kernel(*refs):
        x, cot, wq, wk, wv, wo, wi, wd = refs[:8]
        vecs = refs[8 : 8 + nv]
        at = 8 + nv
        out_o, gin_o, oq, ok, ov, oo, oi, od = refs[at : at + 8]
        vec_o = refs[at + 8 : at + 17]
        b = bag.hand_out(refs[at + 17 :])
        x_all, wqkv, wor, wir, wdr = b["x_all"], b["wqkv"], b["wor"], b["wir"], b["wdr"]
        qkv, probs, ctx, part = b["qkv"], b["probs"], b["ctx"], b["part"]
        flat, small, here = b["flat"], b["small"], b["here"]
        normed_r, rstd_r, hidden_r = b["normed"], b["rstd"], b["hidden"]
        hid_all, acted, slope, d_two_r, d2_all = (
            b["hid_all"],
            b["acted"],
            b["slope"],
            b["d_two"],
            b["d2_all"],
        )
        d_in, d_one_r, d1_all, dctx, dqkv = b["d_in"], b["d_one"], b["d1_all"], b["dctx"], b["dqkv"]
        sums, gbi8, gqv8, gflat, gs = b["sums"], b["gbi8"], b["gqv8"], b["gflat"], b["gs"]
        gwd, gwi, gqkv, gwo = b["gwd"], b["gwi"], b["gqkv"], b["gwo"]
        tq, ti, td, ts, to = b["tq"], b["ti"], b["td"], b["ts"], b["to"]

        p = Place(S, R)
        mine = rows_of(p.s, ds)
        own_tok = rows_of(p.me, T)
        own_chip = rows_of(p.a, C)
        far_chip = rows_of(p.chip(1), C)
        cols = pl.ds(pl.multiple_of(p.me * dr, dr), dr)
        local = []

        def bring(src, dst):
            copy = pltpu.make_async_copy(src, dst, here.at[len(local)])
            copy.start()
            local.append(copy)

        for i, w in enumerate((wq, wk, wv)):
            bring(w.at[:, cols], wqkv.at[mine, pl.ds(i * dr, dr)])
        for c in range(S):
            piece = pl.ds(pl.multiple_of(c * fs + p.me * fr, fr), fr)
            bring(wi.at[:, piece], wir.at[mine, pl.ds(c * fr, fr)])
        bring(wd.at[rows_of(p.me, fr)], wdr.at[mine])
        own_wo = pltpu.make_async_copy(wo, wor.at[rows_of(p.y, ds)], here.at[len(local)])

        @pl.when(p.z == p.me)
        def _():
            own_wo.start()

        piece = pl.ds(pl.multiple_of(p.me * fr, fr), fr)
        pieces = [v[...] for v in vecs[:-1]] + [vecs[-1][:, piece]]
        pieces.append(jnp.zeros((NVEC - nv, ds), F32))
        small[rows_of(p.s, NVEC), :] = jnp.concatenate(pieces, 0)
        x_all[own_tok, :] = x[...]
        p.meet_all()

        smalls = RowGather(p, small, NVEC, b["smalls"])
        g_qkv = RowGather(p, wqkv, ds, b["g_qkv"])
        left, right = pl.ds(0, half), pl.ds(half, half)
        g_wia = RowGather(p, wir, ds, b["g_wia"], left)
        g_wib = RowGather(p, wir, ds, b["g_wib"], right)
        dleft, dright = pl.ds(0, D // 2), pl.ds(D // 2, D // 2)
        g_wda = RowGather(p, wdr, fr, b["g_wda"], dleft)
        g_wdb = RowGather(p, wdr, fr, b["g_wdb"], dright)
        g_wo = PlaneGather(p, wor, ds, b["g_wo"])
        ax = TokenSpread(p, x_all, T, b["ax"])
        a1 = TokenSpread(p, hid_all, T, b["a1"])
        a2 = TokenSpread(p, d2_all, T, b["a2"])
        a3 = TokenSpread(p, d1_all, T, b["a3"])
        t1 = RepScatter(p, part, T, b["t1b"], b["t1s"])
        t2 = RepScatter(p, part, T, b["t2b"], b["t2s"])
        t3 = RepScatter(p, part, T, b["t3b"], b["t3s"])
        t4 = RepScatter(p, part, T, b["t4b"], b["t4s"])
        rwd = RowScatter(p, gwd, fr, b["rwdb"], b["rwds"])
        rwi = RowScatter(p, gwi, ds, b["rwib"], b["rwis"])
        rqkv = RowScatter(p, gqkv, ds, b["rqkvb"], b["rqkvs"])
        rsm = RowScatter(p, gs, NVEC, b["rsmb"], b["rsms"])
        rwo = PlaneScatter(p, gwo, ds, b["rwob"], b["rwos"])
        sd = RepSpread(p, td, b["rwdp"])
        si = RepSpread(p, ti, b["rwip"])
        sq = RepSpread(p, tq, b["rqkvp"])
        ss = RepSpread(p, ts, b["rsmp"])
        so = OwnerSpread(p, to, b["rwop"])

        smalls.start()
        for copy in local[:3]:
            copy.wait()
        g_qkv.start()
        ax.start()
        for copy in local[3:]:
            copy.wait()

        @pl.when(p.z == p.me)
        def _():
            own_wo.wait()

        g_wo.start()
        sums[...] = jnp.zeros_like(sums)
        gbi8[...] = jnp.zeros_like(gbi8)
        gqv8[...] = jnp.zeros_like(gqv8)
        gflat[...] = jnp.zeros_like(gflat)
        for k in range(1, Z):
            smalls.forward(k)
        for k in range(1, Z):
            g_qkv.forward(k)
        g_wia.start()
        g_wo.forward()
        smalls.finish()
        for i in range(nv):
            row = [small[s * NVEC + i : s * NVEC + i + 1, :] for s in range(S)]
            flat[i : i + 1, :] = jnp.concatenate(row, 1)
        ax.beside()
        ax.across()
        g_qkv.finish()

        low = lax.broadcasted_iota(jnp.int32, (SEQ, 128), 1) < HEAD_DIM
        keep = (low, jnp.logical_not(low))

        def project(rows):
            for n in range(3):
                c = pl.ds(n * dr, dr)
                z = mm(x_all[rows, :], wqkv[:, c])
                if n == 0:
                    z = z + flat[0:1, cols]
                if n == 2:
                    z = z + flat[1:2, cols]
                qkv[rows, c] = z.astype(BF)

        def pick(v, h):
            return jnp.where(keep[h], v, jnp.zeros_like(v))

        def attend(chip):
            def one(j, _):
                seq = chip * (C // SEQ) + j
                rows = rows_of(seq, SEQ)
                for n in range(pairs):
                    q2 = qkv[rows, n * 128 : n * 128 + 128]
                    k2 = qkv[rows, dr + n * 128 : dr + n * 128 + 128]
                    v2 = qkv[rows, 2 * dr + n * 128 : 2 * dr + n * 128 + 128]
                    got = []
                    for h in range(2):
                        scores = mm_nt(pick(q2, h), k2) * 0.125
                        e = jnp.exp(scores - jnp.max(scores, axis=-1, keepdims=True))
                        pr = e / jnp.sum(e, axis=-1, keepdims=True)
                        probs[rows_of(seq * 2 * pairs + 2 * n + h, SEQ), :] = pr
                        got.append(mm(pr.astype(BF), v2))
                    ctx[rows, n * 128 : n * 128 + 128] = jnp.where(low, got[0], got[1]).astype(BF)
                return 0

            lax.fori_loop(0, C // SEQ, one, 0)

        def attn_part(rows):
            def tile(c):
                part[rows, c] = mm(ctx[rows, :], wor[:, c]).astype(BF)

            tiles(D, tile)

        def inner(rows):
            def tile(c):
                z = mm(hid_all[rows, :], wir[:, c]) + flat[8:9, c]
                phi = 0.5 * (1.0 + lax.erf(z * INV_ROOT_TWO))
                acted[rows, c] = (z * phi).astype(BF)
                slope[rows, c] = phi + z * jnp.exp(-0.5 * z * z) * INV_ROOT_TWO_PI

            tiles(V, tile)

        def down(rows):
            def tile(c):
                part[rows, c] = mm(acted[rows, :], wdr[:, c]).astype(BF)

            tiles(D, tile)

        def d_inner(rows):
            def tile(c):
                d = mm_nt(d2_all[rows, :], wdr[c, :]) * slope[rows, c]
                gbi8[:, c] += fold(d)
                d_in[rows, c] = d.astype(BF)

            tiles(V, tile)

        def hid_part(rows):
            def tile(c):
                part[rows, c] = mm_nt(d_in[rows, :], wir[c, :]).astype(BF)

            tiles(D, tile)

        def d_attend(chip):
            rows = rows_of(chip, C)
            dctx[rows, :] = mm_nt(d1_all[rows, :], wor[...]).astype(BF)

            def one(j, _):
                seq = chip * (C // SEQ) + j
                rows = rows_of(seq, SEQ)
                for n in range(pairs):
                    lanes = [slice(m * dr + n * 128, m * dr + n * 128 + 128) for m in range(3)]
                    q2, k2, v2 = (qkv[rows, c] for c in lanes)
                    dc2 = dctx[rows, lanes[0]]
                    got = []
                    for h in range(2):
                        pr = probs[rows_of(seq * 2 * pairs + 2 * n + h, SEQ), :]
                        dp = mm_nt(pick(dc2, h), v2)
                        delta = jnp.sum(pr * dp, axis=-1, keepdims=True)
                        dsc = (pr * (dp - delta) * 0.125).astype(BF)
                        got.append((mm(dsc, k2), mm_tn(dsc, q2), mm_tn(pr.astype(BF), dc2)))
                    dq, dk, dv = (jnp.where(low, u, w) for u, w in zip(*got))
                    gqv8[:, lanes[0]] += fold(dq)
                    gqv8[:, lanes[1]] += fold(dv)
                    for v, c in zip((dq, dk, dv), lanes):
                        dqkv[rows, c] = v.astype(BF)
                return 0

            lax.fori_loop(0, C // SEQ, one, 0)

        def in_part(rows):
            def tile(c):
                part[rows, c] = mm_nt(dqkv[rows, :], wqkv[c, :]).astype(BF)

            tiles(D, tile)

        def grad_plane(lhs, rhs, dst, z):
            both = pl.ds(pl.multiple_of(z * 2 * ds, 2 * ds), 2 * ds)
            dst[both, :] = mm_tn(lhs[:, both], rhs[...]).astype(BF)

        def grad_all(lhs, rhs, dst, scatter):
            for k in list(range(1, Z)) + [0]:
                grad_plane(lhs, rhs, dst, lax.rem(p.z + k, Z))
                scatter.first[k].start()

        project(far_chip)
        project(own_chip)
        attend(p.chip(1))
        g_wo.finish()
        attn_part(far_chip)
        t1.start_far()
        for k in range(1, Z):
            g_wia.forward(k)
        g_wib.start()
        attend(p.a)
        attn_part(own_chip)
        t1.start_near()
        t1.pass_on()
        for k in range(1, Z):
            g_wib.forward(k)
        g_wda.start()
        t1.finish()

        def norm_one(i, _):
            at = step_rows(i)
            normed, rstd = norm_parts(x[at, :].astype(F32) + t1.read(i) + flat[2:3, :])
            hidden = normed * flat[3:4, :] + flat[4:5, :]
            normed_r[at, :] = normed
            rstd_r[at, :] = jnp.broadcast_to(rstd, (STEP, 128))
            hidden_r[at, :] = hidden
            hid_all[step_rows(i, p.me * T), :] = hidden.astype(BF)
            return 0

        lax.fori_loop(0, T // STEP, norm_one, 0)
        a1.start()
        t1.drain()
        g_wia.finish()
        g_wib.finish()
        a1.beside()
        inner(own_chip)
        a1.across()
        for k in range(1, Z):
            g_wda.forward(k)
        g_wdb.start()
        inner(far_chip)
        for k in range(1, Z):
            g_wdb.forward(k)
        g_wda.finish()
        g_wdb.finish()
        down(far_chip)
        t2.start_far()
        down(own_chip)
        t2.start_near()
        t2.pass_on()
        t2.finish()

        def norm_two(i, _):
            at = step_rows(i)
            normed, rstd = norm_parts(hidden_r[at, :] + t2.read(i) + flat[5:6, :])
            out_o[at, :] = (normed * flat[6:7, :] + flat[7:8, :]).astype(BF)
            dout = cot[at, :].astype(F32)
            d_two = norm_back(dout * flat[6:7, :], normed, rstd)
            sums[24:32, :] += fold(d_two)
            sums[32:40, :] += fold(dout * normed)
            sums[40:48, :] += fold(dout)
            d_two_r[at, :] = d_two
            d2_all[step_rows(i, p.me * T), :] = d_two.astype(BF)
            return 0

        lax.fori_loop(0, T // STEP, norm_two, 0)
        a2.start()
        t2.drain()
        a2.beside()
        d_inner(own_chip)
        a2.across()
        d_inner(far_chip)
        hid_part(far_chip)
        t3.start_far()
        hid_part(own_chip)
        t3.start_near()
        t3.pass_on()
        grad_all(acted, d2_all, gwd, rwd)
        t3.finish()

        def back_one(i, _):
            at = step_rows(i)
            d_hidden = d_two_r[at, :] + t3.read(i)
            normed = normed_r[at, :]
            d_one = norm_back(d_hidden * flat[3:4, :], normed, rstd_r[at, 0:1])
            sums[0:8, :] += fold(d_one)
            sums[8:16, :] += fold(d_hidden * normed)
            sums[16:24, :] += fold(d_hidden)
            d_one_r[at, :] = d_one
            d1_all[step_rows(i, p.me * T), :] = d_one.astype(BF)
            return 0

        lax.fori_loop(0, T // STEP, back_one, 0)
        a3.start()
        t3.drain()
        grad_all(hid_all, d_in, gwi, rwi)
        a3.beside()
        d_attend(p.a)
        a3.across()
        d_attend(p.chip(1))
        grad_all(x_all, dqkv, gqkv, rqkv)
        gwo[...] = mm_tn(ctx[...], d1_all[...]).astype(BF)
        rwo.start()
        for k in range(1, Z):
            rwd.pass_on(k)
        in_part(far_chip)
        t4.start_far()
        in_part(own_chip)
        t4.start_near()
        t4.pass_on()
        gflat[0:1, cols] = jnp.sum(gqv8[:, :dr], axis=0, keepdims=True)
        gflat[1:2, cols] = jnp.sum(gqv8[:, dr:], axis=0, keepdims=True)
        for i in range(6):
            gflat[i + 2 : i + 3, :] = jnp.sum(sums[8 * i : 8 * i + 8, :], axis=0, keepdims=True)
        gflat[8:9, :] = jnp.sum(gbi8[...], axis=0, keepdims=True)
        for s in range(S):
            gs[s * NVEC : (s + 1) * NVEC, :] = gflat[:, s * ds : (s + 1) * ds]
        rsm.start()
        for k in range(1, Z):
            rwi.pass_on(k)
        t4.finish()

        def last(i, _):
            at = step_rows(i)
            gin_o[at, :] = (d_one_r[at, :] + t4.read(i)).astype(BF)
            return 0

        lax.fori_loop(0, T // STEP, last, 0)
        rwo.pass_on()
        for k in range(1, Z):
            rqkv.pass_on(k)
        for k in range(1, Z):
            rsm.pass_on(k)
        rwd.total(td)
        sd.start()
        rwi.total(ti)
        si.start()
        rwo.total(to)
        so.start()
        sd.forward()
        rqkv.total(tq)
        sq.start()
        rsm.total(ts)
        ss.start()
        si.forward()
        so.forward()
        sd.finish()
        for r in range(R):

            def put_d(i, _, r=r):
                od[chunk_rows(i, r * fr), :] = td[r, chunk_rows(i), :].astype(F32)
                return 0

            lax.fori_loop(0, fr // CHUNK, put_d, 0)
        si.finish()

        def put_i(i, _):
            for r in range(R):
                for c in range(S):
                    lo = c * fs + r * fr
                    oi[chunk_rows(i), lo : lo + fr] = ti[
                        r, chunk_rows(i), c * fr : (c + 1) * fr
                    ].astype(F32)
            return 0

        lax.fori_loop(0, ds // CHUNK, put_i, 0)
        sq.forward()
        ss.forward()
        so.finish()
        sq.finish()

        def put_q(i, _):
            oo[chunk_rows(i), :] = to[chunk_rows(i), :].astype(F32)
            for r in range(R):
                for n, o in enumerate((oq, ok, ov)):
                    o[chunk_rows(i), r * dr : (r + 1) * dr] = tq[
                        r, chunk_rows(i), n * dr : (n + 1) * dr
                    ].astype(F32)
            return 0

        lax.fori_loop(0, ds // CHUNK, put_q, 0)
        ss.finish()
        total = ts[0]
        for r in range(1, R):
            total = total + ts[r]
        for i in range(8):
            vec_o[i][...] = total[i : i + 1, :]
        for r in range(R):
            vec_o[8][:, r * fr : (r + 1) * fr] = ts[r, 8:9, :]
        for g in (smalls, g_qkv, g_wo, g_wia, g_wib, g_wda, g_wdb, ax, a1, a2, a3, t4):
            g.drain()
        for g in (rwd, rwi, rqkv, rsm, rwo, sd, si, sq, ss, so):
            g.drain()

    ins = [x, cot, wq, wk, wv, wo, wi, wd] + [v[None] for v in vectors]
    outs = [((T, D), BF)] * 2 + [((ds, D), F32)] * 4 + [((ds, S * fs), F32), ((fs, D), F32)]
    outs += [((1, ds), F32)] * 8 + [((1, fs), F32)]
    return pl.pallas_call(
        kernel,
        out_shape=[jax.ShapeDtypeStruct(*o) for o in outs],
        in_specs=[VMEM_SPEC] * 2 + [ANY_SPEC] * 6 + [VMEM_SPEC] * nv,
        out_specs=[VMEM_SPEC] * len(outs),
        scratch_shapes=bag.specs,
        compiler_params=pltpu.CompilerParams(
            collective_id=12, has_side_effects=True, vmem_limit_bytes=LIMIT
        ),
        cost_estimate=pl.CostEstimate(
            flops=10 * 10**9, bytes_accessed=24 << 20, transcendentals=4 << 20
        ),
    )(*ins)


def fast_body(
    block_input,
    out_cotangent,
    w_query,
    w_key,
    w_value,
    w_output,
    bias_query,
    bias_value,
    bias_output,
    gain_first,
    shift_first,
    w_inner,
    bias_inner,
    w_down,
    bias_down,
    gain_second,
    shift_second,
):
    vectors = (
        bias_query,
        bias_value,
        bias_output,
        gain_first,
        shift_first,
        bias_down,
        gain_second,
        shift_second,
        bias_inner,
    )
    got = layer(
        block_input,
        out_cotangent,
        w_query,
        w_key,
        w_value,
        w_output,
        w_inner,
        w_down,
        vectors,
        lax.axis_size("shard"),
        lax.axis_size("rep"),
    )
    output, grad_input, gq, gk, gv, go, gi, gd = got[:8]
    gbq, gbv, gbo, ggone, gsone, gbd, ggtwo, gstwo, gbi = (v.reshape(-1) for v in got[8:])
    return (
        output,
        grad_input,
        gq,
        gk,
        gv,
        go,
        gbq,
        gbv,
        gbo,
        ggone,
        gsone,
        gi,
        gbi,
        gd,
        gbd,
        ggtwo,
        gstwo,
    )


def fits_fast(mesh):
    S, R = mesh.shape["shard"], mesh.shape["rep"]
    return R == 4 and S == 2 * R


def solution(mesh):
    tokens = P(("shard", "rep"), None)
    mat = P("shard", None)
    vec = P("shard")
    params = (mat, mat, mat, mat, vec, vec, vec, vec, vec, mat, vec, mat, vec, vec, vec)
    return jax.shard_map(
        fast_body if fits_fast(mesh) else body,
        mesh=mesh,
        in_specs=(tokens, tokens) + params,
        out_specs=(tokens, tokens) + params,
        check_vma=False,
    )
```

```python
import jax
import jax.numpy as jnp
from jax import lax
from jax.experimental import pallas as pl
from jax.experimental.pallas import tpu as pltpu
from jax.sharding import PartitionSpec as P

HEAD_DIM = 64
SEQ = 128
PAD = 16


EPS = 1e-06
INV_ROOT_TWO = 0.7071067811865476
INV_ROOT_TWO_PI = 0.3989422804014327
BF = jnp.bfloat16
F32 = jnp.float32


def norm_parts(resid):
    centre = resid - jnp.mean(resid, axis=-1, keepdims=True)
    variance = jnp.mean(centre * centre, axis=-1, keepdims=True)
    rstd = lax.rsqrt(variance + EPS)
    return (centre * rstd, rstd)


def norm_back(upstream, normed, rstd):
    return rstd * (
        upstream
        - jnp.mean(upstream, axis=-1, keepdims=True)
        - normed * jnp.mean(upstream * normed, axis=-1, keepdims=True)
    )


def mm(a, b):
    return jnp.dot(a, b, preferred_element_type=F32)


def mm_nt(a, b):
    return lax.dot_general(a, b, (((1,), (1,)), ((), ())), preferred_element_type=F32)


def mm_tn(a, b):
    return lax.dot_general(a, b, (((0,), (0,)), ((), ())), preferred_element_type=F32)


def ein(spec, a, b):
    return jnp.einsum(spec, a, b, preferred_element_type=F32)


MESH = pl.DeviceIdType.MESH
CHUNK = 16


class Peers:
    def __init__(self, R):
        self.R, self.A = R, R // 2
        self.me = lax.axis_index("rep")
        self.c = lax.rem(self.me, 2)
        self.a = lax.div(self.me, 2)
        self.partner = self.me + 1 - 2 * self.c

    def chip(self, k):
        return lax.rem(self.a + k, self.A)

    def same(self, k):
        return 2 * self.chip(k) + self.c

    def other(self, k):
        return 2 * self.chip(k) + 1 - self.c

    def meet(self):
        barrier = pltpu.get_barrier_semaphore()
        for dev in [self.partner] + [self.same(k) for k in range(1, self.A)]:
            pl.semaphore_signal(barrier, inc=1, device_id={"rep": dev}, device_id_type=MESH)
        pl.semaphore_wait(barrier, self.A)


def rows_of(index, T):
    return pl.ds(pl.multiple_of(index * T, T), T)


def chunk_rows(i, base=None):
    start = i * CHUNK if base is None else base + i * CHUNK
    return pl.ds(pl.multiple_of(start, CHUNK), CHUNK)


def remote(src, dst, send, recv, dev):
    return pltpu.make_async_remote_copy(
        src_ref=src,
        dst_ref=dst,
        send_sem=send,
        recv_sem=recv,
        device_id={"rep": dev},
        device_id_type=MESH,
    )


def scatter_sum(p, part, T, near, far, out, sems):
    near_s, near_r, far_s, far_r = sems
    order = list(range(1, p.A)) + [0]
    first = {
        k: remote(
            part.at[rows_of(p.other(k), T)], near.at[k], near_s.at[k], near_r.at[k], p.partner
        )
        for k in order
    }
    for k in order:
        first[k].start()
    second = []
    for k in range(1, p.A):
        first[k].wait_recv()
        base = p.same(k) * T

        def add(i, _, k=k, base=base):
            mine = part[chunk_rows(i, base), :].astype(F32)
            out[k - 1, chunk_rows(i), :] = (mine + near[k, chunk_rows(i), :].astype(F32)).astype(BF)
            return 0

        lax.fori_loop(0, T // CHUNK, add, 0)
        copy = remote(out.at[k - 1], far.at[k - 1], far_s.at[k - 1], far_r.at[k - 1], p.same(k))
        copy.start()
        second.append(copy)
    first[0].wait_recv()
    for copy in second:
        copy.wait_recv()

    def read(i):
        total = part[chunk_rows(i, p.me * T), :].astype(F32) + near[0, chunk_rows(i), :].astype(F32)
        for k in range(1, p.A):
            total = total + far[k - 1, chunk_rows(i), :].astype(F32)
        return total

    return read, list(first.values()) + second


def spread(p, src, full, T, sems):
    dir_s, dir_r, fwd_s, fwd_r = sems
    mine = full.at[rows_of(p.me, T)]
    direct = {}
    for k in list(range(1, p.A)) + [0]:
        dev = p.partner if k == 0 else p.same(k)
        direct[k] = remote(src, mine, dir_s.at[k], dir_r.at[k], dev)
        direct[k].start()
    passed = []
    for k in range(1, p.A):
        direct[k].wait_recv()
        block = full.at[rows_of(p.same(p.A - k), T)]
        copy = remote(block, block, fwd_s.at[k - 1], fwd_r.at[k - 1], p.partner)
        copy.start()
        passed.append(copy)
    direct[0].wait_recv()
    for copy in passed:
        copy.wait_recv()
    return list(direct.values()) + passed


def drain(copies):
    for copy in copies:
        copy.wait_send()


def run_kernel(kernel, cid, T, D, R, ins, outs, scatter, gather):
    A = R // 2
    few = max(A - 1, 1)
    scratch = []
    if scatter:
        scratch += [
            pltpu.VMEM((A, T, D), BF),
            pltpu.VMEM((few, T, D), BF),
            pltpu.VMEM((few, T, D), BF),
        ]
        scratch += [pltpu.SemaphoreType.DMA((n,)) for n in (A, A, few, few)]
    if gather:
        scratch += [pltpu.SemaphoreType.DMA((n,)) for n in (A, A, few, few)]
    vmem = pl.BlockSpec(memory_space=pltpu.VMEM)
    return pl.pallas_call(
        kernel,
        out_shape=[jax.ShapeDtypeStruct(*o) for o in outs],
        in_specs=[vmem] * len(ins),
        out_specs=[vmem] * len(outs),
        scratch_shapes=scratch,
        compiler_params=pltpu.CompilerParams(collective_id=cid, has_side_effects=True),
        cost_estimate=pl.CostEstimate(flops=0, bytes_accessed=24 << 20, transcendentals=0),
    )(*ins)


def gather_kernel(block, R, cid):
    T, D = block.shape

    def kernel(src, full, *sems):
        p = Peers(R)
        p.meet()

        def put(i, _):
            full[chunk_rows(i, p.me * T), :] = src[chunk_rows(i), :]
            return 0

        lax.fori_loop(0, T // CHUNK, put, 0)
        drain(spread(p, src, full, T, sems))

    return run_kernel(kernel, cid, T, D, R, [block], [((R * T, D), BF)], False, True)[0]


def norm_one_step(partial, x, bo, gone, sone):
    T, D = x.shape
    R = partial.shape[0] // T

    def kernel(part, xr, bor, gr, sr, normed_o, rstd_o, hidden_o, full, near, far, out, *sems):
        p = Peers(R)
        p.meet()
        read, sent = scatter_sum(p, part, T, near, far, out, sems[:4])

        def step(i, _):
            normed, rstd = norm_parts(xr[chunk_rows(i), :].astype(F32) + read(i) + bor[...])
            hidden = normed * gr[...] + sr[...]
            normed_o[chunk_rows(i), :] = normed
            rstd_o[chunk_rows(i), :] = rstd
            hidden_o[chunk_rows(i), :] = hidden
            full[chunk_rows(i, p.me * T), :] = hidden.astype(BF)
            return 0

        lax.fori_loop(0, T // CHUNK, step, 0)
        drain(sent + spread(p, full.at[rows_of(p.me, T)], full, T, sems[4:]))

    ins = [partial, x, bo[None], gone[None], sone[None]]
    outs = [((T, D), F32), ((T, 1), F32), ((T, D), F32), ((R * T, D), BF)]
    return run_kernel(kernel, 1, T, D, R, ins, outs, True, True)


def add_sums(ref, values):
    for n, v in enumerate(values):
        ref[n : n + 1, :] += jnp.sum(v, axis=0, keepdims=True)


def norm_two_step(partial, hidden, bd, gtwo, stwo, cot):
    T, D = hidden.shape
    R = partial.shape[0] // T

    def kernel(part, hr, br, gr, sr, cr, out_o, d_o, sums, full, near, far, out, *sems):
        p = Peers(R)
        p.meet()
        sums[...] = jnp.zeros_like(sums)
        read, sent = scatter_sum(p, part, T, near, far, out, sems[:4])

        def step(i, _):
            normed, rstd = norm_parts(hr[chunk_rows(i), :] + read(i) + br[...])
            out_o[chunk_rows(i), :] = (normed * gr[...] + sr[...]).astype(BF)
            dout = cr[chunk_rows(i), :].astype(F32)
            d_two = norm_back(dout * gr[...], normed, rstd)
            add_sums(sums, (d_two, dout * normed, dout))
            d_o[chunk_rows(i), :] = d_two
            full[chunk_rows(i, p.me * T), :] = d_two.astype(BF)
            return 0

        lax.fori_loop(0, T // CHUNK, step, 0)
        drain(sent + spread(p, full.at[rows_of(p.me, T)], full, T, sems[4:]))

    ins = [partial, hidden, bd[None], gtwo[None], stwo[None], cot]
    outs = [((T, D), BF), ((T, D), F32), ((8, D), F32), ((R * T, D), BF)]
    return run_kernel(kernel, 2, T, D, R, ins, outs, True, True)


def back_one_step(partial, d_two, normed, rstd, gone):
    T, D = d_two.shape
    R = partial.shape[0] // T

    def kernel(part, dr, nr, rr, gr, d_o, sums, full, near, far, out, *sems):
        p = Peers(R)
        p.meet()
        sums[...] = jnp.zeros_like(sums)
        read, sent = scatter_sum(p, part, T, near, far, out, sems[:4])

        def step(i, _):
            d_hidden = dr[chunk_rows(i), :] + read(i)
            normed = nr[chunk_rows(i), :]
            d_one = norm_back(d_hidden * gr[...], normed, rr[chunk_rows(i), :])
            add_sums(sums, (d_one, d_hidden * normed, d_hidden))
            d_o[chunk_rows(i), :] = d_one
            full[chunk_rows(i, p.me * T), :] = d_one.astype(BF)
            return 0

        lax.fori_loop(0, T // CHUNK, step, 0)
        drain(sent + spread(p, full.at[rows_of(p.me, T)], full, T, sems[4:]))

    ins = [partial, d_two, normed, rstd, gone[None]]
    outs = [((T, D), F32), ((8, D), F32), ((R * T, D), BF)]
    return run_kernel(kernel, 3, T, D, R, ins, outs, True, True)


def input_step(partial, d_one):
    T, D = d_one.shape
    R = partial.shape[0] // T

    def kernel(part, dr, grad, near, far, out, *sems):
        p = Peers(R)
        p.meet()
        read, sent = scatter_sum(p, part, T, near, far, out, sems)

        def step(i, _):
            grad[chunk_rows(i), :] = (dr[chunk_rows(i), :] + read(i)).astype(BF)
            return 0

        lax.fori_loop(0, T // CHUNK, step, 0)
        drain(sent)

    return run_kernel(kernel, 4, T, D, R, [partial, d_one], [((T, D), BF)], True, False)[0]


def body(
    block_input,
    out_cotangent,
    w_query,
    w_key,
    w_value,
    w_output,
    bias_query,
    bias_value,
    bias_output,
    gain_first,
    shift_first,
    w_inner,
    bias_inner,
    w_down,
    bias_down,
    gain_second,
    shift_second,
):
    S = lax.axis_size("shard")
    R = lax.axis_size("rep")
    r = lax.axis_index("rep")
    T = block_input.shape[0]
    D = w_query.shape[1]
    ds = w_query.shape[0]
    dr = D // R
    fs = w_down.shape[0]
    fr = fs // R
    W = 4 * dr

    def cols(w):
        return lax.dynamic_slice(w, (0, r * dr), (ds, dr))

    small = jnp.concatenate(
        [
            v.astype(BF)
            for v in (
                bias_query,
                bias_value,
                bias_output,
                gain_first,
                shift_first,
                bias_down,
                gain_second,
                shift_second,
                bias_inner,
            )
        ]
    )
    n_small = small.shape[0]
    small = jnp.pad(small, (0, PAD * W - n_small)).reshape(PAD, W)
    pack = jnp.concatenate(
        [jnp.concatenate([cols(w_query), cols(w_key), cols(w_value), cols(w_output)], 1), small], 0
    )
    got = lax.all_gather(pack, "shard", axis=0)
    x_all = gather_kernel(block_input, R, 0)
    wi_r = lax.dynamic_index_in_dim(w_inner.reshape(ds, S, R, fr), r, 2, keepdims=False)
    V = S * fr
    dv = fr * D // V
    wd_r = lax.dynamic_slice(w_down, (r * fr, 0), (fr, D)).reshape(dv, V)
    mlp = lax.all_gather(jnp.concatenate([wi_r.reshape(ds, V), wd_r], 0), "shard", axis=0)
    wi = mlp[:, :ds].reshape(D, V)
    wd = mlp[:, ds:].reshape(V, D)
    wqkv = got[:, :ds, : 3 * dr].reshape(D, 3 * dr)
    wo = lax.all_to_all(
        got[:, :ds, 3 * dr :].reshape(D, dr), "rep", split_axis=0, concat_axis=1, tiled=True
    )
    flat = got[:, ds:, :].reshape(S, PAD * W)[:, :n_small].astype(F32)
    bq, bv, bo, gone, sone, bd, gtwo, stwo = (
        flat[:, i * ds : (i + 1) * ds].reshape(D) for i in range(8)
    )
    bi = lax.dynamic_index_in_dim(flat[:, 8 * ds :].reshape(S, R, fr), r, 1, keepdims=False)
    bi = bi.reshape(S * fr)
    bq = lax.dynamic_slice(bq, (r * dr,), (dr,))
    bv = lax.dynamic_slice(bv, (r * dr,), (dr,))

    N = R * T
    shape4 = (N // SEQ, SEQ, dr // HEAD_DIM, HEAD_DIM)
    qkv = mm(x_all, wqkv)
    query = (qkv[:, :dr] + bq).astype(BF).reshape(shape4)
    keyed = qkv[:, dr : 2 * dr].astype(BF).reshape(shape4)
    valued = (qkv[:, 2 * dr :] + bv).astype(BF).reshape(shape4)
    scores = ein("bqhe,bkhe->bhqk", query, keyed) * 0.125
    top = jnp.max(scores, axis=-1, keepdims=True)
    logsum = top + jnp.log(jnp.sum(jnp.exp(scores - top), axis=-1, keepdims=True))
    probs = jnp.exp(scores - logsum)
    probs_b = probs.astype(BF)
    context = ein("bhqk,bkhe->bqhe", probs_b, valued).astype(BF).reshape(N, dr)
    attn_part = mm(context, wo).astype(BF)

    normed_one, rstd_one, hidden, hidden_all = norm_one_step(attn_part, block_input, bo, gone, sone)
    inner = mm(hidden_all, wi) + bi
    phi = 0.5 * (1.0 + lax.erf(inner * INV_ROOT_TWO))
    acted = (inner * phi).astype(BF)
    slope = phi + inner * jnp.exp(-0.5 * inner * inner) * INV_ROOT_TWO_PI
    down_part = mm(acted, wd).astype(BF)

    output, d_two, sums_two, d_two_all = norm_two_step(
        down_part, hidden, bd, gtwo, stwo, out_cotangent
    )
    d_inner = mm_nt(d_two_all, wd) * slope
    g_bias_inner = jnp.sum(d_inner, axis=0)
    d_inner_b = d_inner.astype(BF)
    hid_part = mm_nt(d_inner_b, wi).astype(BF)
    g_wd = mm_tn(acted, d_two_all).astype(BF).reshape(S, dv, V)
    g_wi = mm_tn(hidden_all, d_inner_b).astype(BF).reshape(S, ds, V)
    g_mlp = lax.psum_scatter(
        jnp.concatenate([g_wi, g_wd], 1), "shard", scatter_dimension=0, tiled=True
    )[0]

    d_one, sums_one, d_one_all = back_one_step(hid_part, d_two, normed_one, rstd_one, gone)
    g_wo = mm_tn(context, d_one_all).astype(BF)
    g_wo = lax.all_to_all(g_wo, "rep", split_axis=1, concat_axis=0, tiled=True)
    d_context = mm_nt(d_one_all, wo).astype(BF).reshape(shape4)
    d_probs = ein("bqhe,bkhe->bhqk", d_context, valued)
    delta = jnp.sum(probs * d_probs, axis=-1, keepdims=True)
    d_scores = (probs * (d_probs - delta) * 0.125).astype(BF)
    d_query = ein("bhqk,bkhe->bqhe", d_scores, keyed).reshape(N, dr)
    d_keyed = ein("bhqk,bqhe->bkhe", d_scores, query).reshape(N, dr)
    d_valued = ein("bhqk,bqhe->bkhe", probs_b, d_context).reshape(N, dr)
    g_bias_query = jnp.sum(d_query, axis=0)
    g_bias_value = jnp.sum(d_valued, axis=0)
    d_qkv = jnp.concatenate([d_query.astype(BF), d_keyed.astype(BF), d_valued.astype(BF)], 1)
    in_part = mm_nt(d_qkv, wqkv).astype(BF)

    def placed(v):
        return lax.dynamic_update_slice(jnp.zeros((D,), F32), v, (r * dr,)).reshape(S, ds)

    g_small = jnp.concatenate(
        [
            placed(g_bias_query),
            placed(g_bias_value),
            sums_one[0].reshape(S, ds),
            sums_one[1].reshape(S, ds),
            sums_one[2].reshape(S, ds),
            sums_two[0].reshape(S, ds),
            sums_two[1].reshape(S, ds),
            sums_two[2].reshape(S, ds),
            g_bias_inner.reshape(S, fr),
        ],
        1,
    ).astype(BF)
    n_g = g_small.shape[1]
    g_small = jnp.pad(g_small, ((0, 0), (0, PAD * W - n_g))).reshape(S, PAD, W)
    g_pack = jnp.concatenate([mm_tn(x_all, d_qkv).astype(BF), g_wo], 1).reshape(S, ds, W)
    g_pack = jnp.concatenate([g_pack, g_small], 1)
    g_pack = lax.psum_scatter(g_pack, "shard", scatter_dimension=0, tiled=True)[0]

    grad_input = input_step(in_part, d_one)

    mlps = gather_kernel(g_mlp, R, 5).reshape(R, ds + dv, V).astype(F32)
    wd_out = mlps[:, ds:].reshape(R * fr, D)
    wi_out = mlps[:, :ds].reshape(R, ds, S, fr).transpose(1, 2, 0, 3).reshape(ds, S * R * fr)
    packs = gather_kernel(g_pack, R, 6).reshape(R, ds + PAD, W).astype(F32)
    main = packs[:, :ds].reshape(R, ds, 4, dr).transpose(2, 1, 0, 3).reshape(4, ds, D)
    tail = packs[:, ds:].reshape(R, PAD * W)
    summed = jnp.sum(tail[:, : 8 * ds], axis=0)
    gbq, gbv, gbo, ggone, gsone, gbd, ggtwo, gstwo = (
        summed[i * ds : (i + 1) * ds] for i in range(8)
    )
    gbi = tail[:, 8 * ds : n_g].reshape(fs)
    return (
        output,
        grad_input,
        main[0],
        main[1],
        main[2],
        main[3],
        gbq,
        gbv,
        gbo,
        ggone,
        gsone,
        wi_out,
        gbi,
        wd_out,
        gbd,
        ggtwo,
        gstwo,
    )

VMEM_SPEC = pl.BlockSpec(memory_space=pltpu.VMEM)
ANY_SPEC = pl.BlockSpec(memory_space=pl.ANY)
LIMIT = 56 << 20
NVEC = 16


def dma_sems(*counts):
    return [pltpu.SemaphoreType.DMA((n,)) for n in counts]


class Place(Peers):
    def __init__(self, S, R):
        super().__init__(R)
        self.S, self.Z = S, S // 2
        self.s = lax.axis_index("shard")
        self.z = lax.div(self.s, 2)
        self.y = lax.rem(self.s, 2)
        self.across = self.s + 1 - 2 * self.y

    def up(self, k):
        return 2 * lax.rem(self.z + k, self.Z) + self.y

    def down(self, k):
        return 2 * lax.rem(self.z + self.Z - k, self.Z) + self.y

    def flip(self, s):
        return s + 1 - 2 * self.y

    def meet_all(self):
        barrier = pltpu.get_barrier_semaphore()
        for dev in [self.partner] + [self.same(k) for k in range(1, self.A)]:
            pl.semaphore_signal(barrier, inc=1, device_id={"rep": dev}, device_id_type=MESH)
        for dev in [self.across] + [self.up(k) for k in range(1, self.Z)]:
            pl.semaphore_signal(barrier, inc=1, device_id={"shard": dev}, device_id_type=MESH)
        pl.semaphore_wait(barrier, self.A + self.Z)


def to_shard(src, dst, send, recv, dev):
    return pltpu.make_async_remote_copy(
        src_ref=src,
        dst_ref=dst,
        send_sem=send,
        recv_sem=recv,
        device_id={"shard": dev},
        device_id_type=MESH,
    )


class RowGather:
    def __init__(self, p, full, T, sems, cols=None):
        self.p, self.full, self.T, self.cols = p, full, T, cols
        self.zs, self.zr, self.ys, self.yr = sems
        self.far = {k: self.copy(p.s, self.zs, self.zr, k - 1, p.up(k)) for k in range(1, p.Z)}
        self.near = {0: self.copy(p.s, self.ys, self.yr, 0, p.across)}
        for k in range(1, p.Z):
            self.near[k] = self.copy(p.down(k), self.ys, self.yr, k, p.across)

    @staticmethod
    def sems(Z):
        return dma_sems(Z - 1, Z - 1, Z, Z)

    def copy(self, block, send, recv, i, dev):
        rows = rows_of(block, self.T)
        rows = self.full.at[rows] if self.cols is None else self.full.at[rows, self.cols]
        return to_shard(rows, rows, send.at[i], recv.at[i], dev)

    def start(self):
        for k in range(1, self.p.Z):
            self.far[k].start()
        self.near[0].start()

    def forward(self, k):
        self.far[k].wait_recv()
        self.near[k].start()

    def finish(self):
        for k in range(self.p.Z):
            self.near[k].wait_recv()

    def drain(self):
        for copy in list(self.far.values()) + list(self.near.values()):
            copy.wait_send()


class PlaneGather:
    def __init__(self, p, full, T, sems):
        self.p = p
        self.zs, self.zr, self.ys, self.yr = sems
        rows = full.at[rows_of(p.y, T)]
        self.far = {
            k: to_shard(rows, rows, self.zs.at[k - 1], self.zr.at[0], p.up(k))
            for k in range(1, p.Z)
        }
        self.near = to_shard(rows, rows, self.ys.at[0], self.yr.at[0], p.across)
        self.mine = p.z == p.me

    @staticmethod
    def sems(Z):
        return dma_sems(Z - 1, 1, 1, 1)

    def start(self):
        @pl.when(self.mine)
        def _():
            for k in range(1, self.p.Z):
                self.far[k].start()
            self.near.start()

    def forward(self):
        @pl.when(jnp.logical_not(self.mine))
        def _():
            self.far[1].wait_recv()
            self.near.start()

    def finish(self):
        self.near.wait_recv()

    def drain(self):
        @pl.when(self.mine)
        def _():
            for k in range(1, self.p.Z):
                self.far[k].wait_send()

        self.near.wait_send()


class RowScatter:
    def __init__(self, p, part, T, bufs, sems):
        self.p, self.part, self.T = p, part, T
        self.close, self.out, self.far = bufs
        ys, yr, zs, zr = sems
        self.first = {}
        for k in range(p.Z):
            to = p.up(k)
            self.first[k] = to_shard(
                part.at[rows_of(p.flip(to), T)], self.close.at[k], ys.at[k], yr.at[k], p.across
            )
        self.second = {
            k: to_shard(
                self.out.at[k - 1], self.far.at[k - 1], zs.at[k - 1], zr.at[k - 1], p.up(k)
            )
            for k in range(1, p.Z)
        }

    @staticmethod
    def bufs(Z, T, C, dtype):
        return [pltpu.VMEM((n, T, C), dtype) for n in (Z, Z - 1, Z - 1)]

    @staticmethod
    def sems(Z):
        return dma_sems(Z, Z, Z - 1, Z - 1)

    def start(self):
        for k in list(range(1, self.p.Z)) + [0]:
            self.first[k].start()

    def pass_on(self, k):
        self.first[k].wait_recv()
        base = self.p.up(k) * self.T
        dtype = self.out.dtype

        def add(i, _):
            mine = self.part[chunk_rows(i, base), :].astype(F32)
            near = self.close[k, chunk_rows(i), :].astype(F32)
            self.out[k - 1, chunk_rows(i), :] = (mine + near).astype(dtype)
            return 0

        lax.fori_loop(0, self.T // CHUNK, add, 0)
        self.second[k].start()

    def total(self, dst, at=None):
        p = self.p
        self.first[0].wait_recv()
        for k in range(1, p.Z):
            self.second[k].wait_recv()

        def add(i, _):
            total = self.part[chunk_rows(i, p.s * self.T), :].astype(F32)
            total = total + self.close[0, chunk_rows(i), :].astype(F32)
            for k in range(1, p.Z):
                total = total + self.far[k - 1, chunk_rows(i), :].astype(F32)
            dst[p.me, chunk_rows(i), :] = total.astype(dst.dtype)
            return 0

        lax.fori_loop(0, self.T // CHUNK, add, 0)

    def drain(self):
        for copy in list(self.first.values()) + list(self.second.values()):
            copy.wait_send()


class PlaneScatter:
    def __init__(self, p, part, T, bufs, sems):
        self.p, self.part, self.T = p, part, T
        self.close, self.out, self.far = bufs
        ys, yr, zs, zr = sems
        self.first = to_shard(
            part.at[rows_of(1 - p.y, T)], self.close, ys.at[0], yr.at[0], p.across
        )
        self.mine = p.z == p.me
        self.hop = lax.rem(p.z + p.Z - p.me, p.Z)
        self.sends = to_shard(
            self.out,
            self.far.at[jnp.maximum(self.hop - 1, 0)],
            zs.at[0],
            zr.at[jnp.maximum(self.hop - 1, 0)],
            2 * p.me + p.y,
        )
        self.gets = [
            to_shard(self.out, self.far.at[k], zs.at[0], zr.at[k], p.up(k + 1))
            for k in range(p.Z - 1)
        ]

    @staticmethod
    def bufs(Z, T, C, dtype):
        return [pltpu.VMEM((T, C), dtype), pltpu.VMEM((T, C), dtype), pltpu.VMEM((Z - 1, T, C), dtype)]

    @staticmethod
    def sems(Z):
        return dma_sems(1, 1, 1, Z - 1)

    def start(self):
        self.first.start()

    def pass_on(self):
        self.first.wait_recv()

        def add(i, _):
            mine = self.part[chunk_rows(i, self.p.y * self.T), :].astype(F32)
            self.out[chunk_rows(i), :] = (mine + self.close[chunk_rows(i), :].astype(F32)).astype(BF)
            return 0

        lax.fori_loop(0, self.T // CHUNK, add, 0)

        @pl.when(jnp.logical_not(self.mine))
        def _():
            self.sends.start()

    def total(self, dst):
        @pl.when(self.mine)
        def _():
            for copy in self.gets:
                copy.wait_recv()

            def add(i, _):
                total = self.part[chunk_rows(i, self.p.y * self.T), :].astype(F32)
                total = total + self.close[chunk_rows(i), :].astype(F32)
                for k in range(self.p.Z - 1):
                    total = total + self.far[k, chunk_rows(i), :].astype(F32)
                dst[chunk_rows(i), :] = total.astype(BF)
                return 0

            lax.fori_loop(0, self.T // CHUNK, add, 0)

    def drain(self):
        self.first.wait_send()

        @pl.when(jnp.logical_not(self.mine))
        def _():
            self.sends.wait_send()


class RepSpread:
    def __init__(self, p, full, sems):
        self.p = p
        dir_s, dir_r, fwd_s, fwd_r = sems
        own = full.at[p.me]
        self.direct = {0: remote(own, own, dir_s.at[0], dir_r.at[0], p.partner)}
        self.passed = {}
        for k in range(1, p.A):
            self.direct[k] = remote(own, own, dir_s.at[k], dir_r.at[k], p.same(k))
            block = full.at[p.same(p.A - k)]
            self.passed[k] = remote(block, block, fwd_s.at[k - 1], fwd_r.at[k - 1], p.partner)

    @staticmethod
    def sems(A):
        return dma_sems(A, A, A - 1, A - 1)

    def start(self):
        for k in list(range(1, self.p.A)) + [0]:
            self.direct[k].start()

    def forward(self):
        for k in range(1, self.p.A):
            self.direct[k].wait_recv()
            self.passed[k].start()

    def finish(self):
        self.direct[0].wait_recv()
        for copy in self.passed.values():
            copy.wait_recv()

    def drain(self):
        drain(list(self.direct.values()) + list(self.passed.values()))


class OwnerSpread:
    def __init__(self, p, block, sems):
        self.p = p
        s0, s1, rx, rp = sems
        self.across = remote(block, block, s0.at[0], rx.at[0], p.same(1))
        self.beside = remote(block, block, s1.at[0], rp.at[0], p.partner)
        self.mine = p.z == p.me
        self.relay = p.z == p.same(1)
        self.other = jnp.logical_not(jnp.logical_or(self.mine, self.relay))

    @staticmethod
    def sems():
        return dma_sems(1, 1, 1, 1)

    def start(self):
        @pl.when(self.mine)
        def _():
            self.across.start()
            self.beside.start()

    def forward(self):
        @pl.when(self.relay)
        def _():
            self.across.wait_recv()
            self.beside.start()

    def finish(self):
        @pl.when(self.other)
        def _():
            self.beside.wait_recv()

    def drain(self):
        @pl.when(self.mine)
        def _():
            self.across.wait_send()

        @pl.when(jnp.logical_not(self.other))
        def _():
            self.beside.wait_send()

class RepScatter:
    def __init__(self, p, part, T, bufs, sems):
        self.p, self.part, self.T = p, part, T
        self.near, self.out, self.far = bufs
        near_s, near_r, far_s, far_r = sems
        self.first = {
            k: remote(
                part.at[rows_of(p.other(k), T)],
                self.near.at[k],
                near_s.at[k],
                near_r.at[k],
                p.partner,
            )
            for k in range(p.A)
        }
        self.second = {
            k: remote(
                self.out.at[k - 1], self.far.at[k - 1], far_s.at[k - 1], far_r.at[k - 1], p.same(k)
            )
            for k in range(1, p.A)
        }

    @staticmethod
    def bufs(A, T, D):
        return [pltpu.VMEM((n, T, D), BF) for n in (A, A - 1, A - 1)]

    @staticmethod
    def sems(A):
        return dma_sems(A, A, A - 1, A - 1)

    def start_far(self):
        for k in range(1, self.p.A):
            self.first[k].start()

    def start_near(self):
        self.first[0].start()

    def pass_on(self):
        for k in range(1, self.p.A):
            self.first[k].wait_recv()
            base = self.p.same(k) * self.T

            def add(i, _, k=k, base=base):
                mine = self.part[step_rows(i, base), :].astype(F32)
                near = self.near[k, step_rows(i), :].astype(F32)
                self.out[k - 1, step_rows(i), :] = (mine + near).astype(BF)
                return 0

            lax.fori_loop(0, self.T // STEP, add, 0)
            self.second[k].start()

    def finish(self):
        self.first[0].wait_recv()
        for copy in self.second.values():
            copy.wait_recv()

    def read(self, i):
        total = self.part[step_rows(i, self.p.me * self.T), :].astype(F32)
        total = total + self.near[0, step_rows(i), :].astype(F32)
        for k in range(1, self.p.A):
            total = total + self.far[k - 1, step_rows(i), :].astype(F32)
        return total

    def drain(self):
        drain(list(self.first.values()) + list(self.second.values()))


STEP = 32


def step_rows(i, base=None):
    start = i * STEP if base is None else base + i * STEP
    return pl.ds(pl.multiple_of(start, STEP), STEP)


class TokenSpread:
    def __init__(self, p, full, T, sems):
        self.p = p
        dir_s, dir_r, fwd_s, fwd_r = sems
        own = full.at[rows_of(p.me, T)]
        self.direct = {0: remote(own, own, dir_s.at[0], dir_r.at[0], p.partner)}
        self.passed = {}
        for k in range(1, p.A):
            self.direct[k] = remote(own, own, dir_s.at[k], dir_r.at[k], p.same(k))
            block = full.at[rows_of(p.same(p.A - k), T)]
            self.passed[k] = remote(block, block, fwd_s.at[k - 1], fwd_r.at[k - 1], p.partner)

    @staticmethod
    def sems(A):
        return dma_sems(A, A, A - 1, A - 1)

    def start(self):
        for k in list(range(1, self.p.A)) + [0]:
            self.direct[k].start()

    def beside(self):
        self.direct[0].wait_recv()

    def across(self):
        for k in range(1, self.p.A):
            self.direct[k].wait_recv()
            self.passed[k].start()
        for copy in self.passed.values():
            copy.wait_recv()

    def drain(self):
        drain(list(self.direct.values()) + list(self.passed.values()))


class Bag:
    def __init__(self):
        self.names, self.specs = [], []

    def want(self, name, specs):
        specs = specs if isinstance(specs, list) else [specs]
        self.names.append((name, len(specs)))
        self.specs += specs

    def hand_out(self, refs):
        got, at = {}, 0
        for name, n in self.names:
            got[name] = refs[at] if n == 1 else list(refs[at : at + n])
            at += n
        return got


def fold(v):
    return jnp.sum(v.reshape(v.shape[0] // 8, 8, v.shape[1]), axis=0)


TILE = 256
QUARTERS = 4


def tiles(n, body):
    def step(i, _):
        body(pl.ds(pl.multiple_of(i * TILE, TILE), TILE))
        return 0

    lax.fori_loop(0, n // TILE, step, 0)


def layer(x, cot, wq, wk, wv, wo, wi, wd, vectors, S, R):
    T, D = x.shape
    ds, fs = wq.shape[0], wd.shape[0]
    dr, fr = D // R, fs // R
    V = S * fr
    W = 3 * dr
    Z, A = S // 2, R // 2
    nv = len(vectors)
    N = R * T
    C = N // A
    pairs = dr // 128
    half = V // 2
    wide = D // QUARTERS

    bag = Bag()
    bag.want("here", pltpu.SemaphoreType.DMA((S + 6,)))
    bag.want("small", pltpu.VMEM((S * NVEC, ds), F32))
    bag.want("flat", pltpu.VMEM((NVEC, D), F32))
    for name, shape, t in (
        ("x_all", (N, D), BF),
        ("wqkv", (D, W), BF),
        ("wor", (dr, D), BF),
        ("wir", (D, V), BF),
        ("wdr", (V, D), BF),
        ("qkv", (N, W), BF),
        ("probs", (N * dr // HEAD_DIM, SEQ), F32),
        ("ctx", (N, dr), BF),
        ("part", (N, D), BF),
        ("normed", (T, D), F32),
        ("rstd", (T, 128), F32),
        ("hidden", (T, D), F32),
        ("hid_all", (N, D), BF),
        ("acted", (N, V), BF),
        ("slope", (N, V), F32),
        ("d_two", (T, D), F32),
        ("d2_all", (N, D), BF),
        ("d_in", (N, V), BF),
        ("d_one", (T, D), F32),
        ("d1_all", (N, D), BF),
        ("dctx", (N, dr), BF),
        ("dqkv", (N, W), BF),
        ("sums", (48, D), F32),
        ("gbi8", (8, V), F32),
        ("gqv8", (8, 2 * dr), F32),
        ("gflat", (NVEC, D), F32),
        ("gs", (S * NVEC, ds), F32),
        ("gwd", (V, D), BF),
        ("gwi", (D, V), BF),
        ("gqkv", (D, W), BF),
        ("gwo", (dr, D), BF),
    ):
        bag.want(name, pltpu.VMEM(shape, t))
    for name in ["smalls", "g_qkv", "g_wia", "g_wib"] + ["g_wd%d" % q for q in range(QUARTERS)]:
        bag.want(name, RowGather.sems(Z))
    bag.want("g_wo", PlaneGather.sems(Z))
    for name in ("ax", "a1", "a2", "a3"):
        bag.want(name, TokenSpread.sems(A))
    for name in ("t1", "t2", "t3", "t4"):
        bag.want(name + "b", RepScatter.bufs(A, T, D))
        bag.want(name + "s", RepScatter.sems(A))
    for name, n, c, t in (
        ("rwd", fr, D, BF),
        ("rwi", ds, V, BF),
        ("rqkv", ds, W, BF),
        ("rsm", NVEC, ds, F32),
    ):
        bag.want(name + "b", RowScatter.bufs(Z, n, c, t))
        bag.want(name + "s", RowScatter.sems(Z))
        bag.want(name + "p", RepSpread.sems(A))
    bag.want("rwob", PlaneScatter.bufs(Z, ds, D, BF))
    bag.want("rwos", PlaneScatter.sems(Z))
    bag.want("rwop", OwnerSpread.sems())

    def kernel(*refs):
        x, cot, wq, wk, wv, wo, wi, wd = refs[:8]
        vecs = refs[8 : 8 + nv]
        at = 8 + nv
        out_o, gin_o, tq, ti, td, to, ts = refs[at : at + 7]
        b = bag.hand_out(refs[at + 7 :])
        x_all, wqkv, wor, wir, wdr = b["x_all"], b["wqkv"], b["wor"], b["wir"], b["wdr"]
        qkv, probs, ctx, part = b["qkv"], b["probs"], b["ctx"], b["part"]
        flat, small, here = b["flat"], b["small"], b["here"]
        normed_r, rstd_r, hidden_r = b["normed"], b["rstd"], b["hidden"]
        hid_all, acted, slope, d_two_r, d2_all = (
            b["hid_all"],
            b["acted"],
            b["slope"],
            b["d_two"],
            b["d2_all"],
        )
        d_in, d_one_r, d1_all, dctx, dqkv = b["d_in"], b["d_one"], b["d1_all"], b["dctx"], b["dqkv"]
        sums, gbi8, gqv8, gflat, gs = b["sums"], b["gbi8"], b["gqv8"], b["gflat"], b["gs"]
        gwd, gwi, gqkv, gwo = b["gwd"], b["gwi"], b["gqkv"], b["gwo"]

        p = Place(S, R)
        mine = rows_of(p.s, ds)
        own_tok = rows_of(p.me, T)
        own_chip = rows_of(p.a, C)
        far_chip = rows_of(p.chip(1), C)
        cols = pl.ds(pl.multiple_of(p.me * dr, dr), dr)
        local = []

        def bring(src, dst):
            copy = pltpu.make_async_copy(src, dst, here.at[len(local)])
            copy.start()
            local.append(copy)

        for i, w in enumerate((wq, wk, wv)):
            bring(w.at[:, cols], wqkv.at[mine, pl.ds(i * dr, dr)])
        for c in range(S):
            piece = pl.ds(pl.multiple_of(c * fs + p.me * fr, fr), fr)
            bring(wi.at[:, piece], wir.at[mine, pl.ds(c * fr, fr)])
        bring(wd.at[rows_of(p.me, fr)], wdr.at[mine])
        own_wo = pltpu.make_async_copy(wo, wor.at[rows_of(p.y, ds)], here.at[len(local)])

        @pl.when(p.z == p.me)
        def _():
            own_wo.start()

        piece = pl.ds(pl.multiple_of(p.me * fr, fr), fr)
        pieces = [v[...] for v in vecs[:-1]] + [vecs[-1][:, piece]]
        pieces.append(jnp.zeros((NVEC - nv, ds), F32))
        small[rows_of(p.s, NVEC), :] = jnp.concatenate(pieces, 0)
        x_all[own_tok, :] = x[...]
        p.meet_all()

        smalls = RowGather(p, small, NVEC, b["smalls"])
        g_qkv = RowGather(p, wqkv, ds, b["g_qkv"])
        left, right = pl.ds(0, half), pl.ds(half, half)
        g_wia = RowGather(p, wir, ds, b["g_wia"], left)
        g_wib = RowGather(p, wir, ds, b["g_wib"], right)
        g_wd = [
            RowGather(p, wdr, fr, b["g_wd%d" % q], pl.ds(q * wide, wide)) for q in range(QUARTERS)
        ]
        g_wo = PlaneGather(p, wor, ds, b["g_wo"])
        ax = TokenSpread(p, x_all, T, b["ax"])
        a1 = TokenSpread(p, hid_all, T, b["a1"])
        a2 = TokenSpread(p, d2_all, T, b["a2"])
        a3 = TokenSpread(p, d1_all, T, b["a3"])
        t1 = RepScatter(p, part, T, b["t1b"], b["t1s"])
        t2 = RepScatter(p, part, T, b["t2b"], b["t2s"])
        t3 = RepScatter(p, part, T, b["t3b"], b["t3s"])
        t4 = RepScatter(p, part, T, b["t4b"], b["t4s"])
        rwd = RowScatter(p, gwd, fr, b["rwdb"], b["rwds"])
        rwi = RowScatter(p, gwi, ds, b["rwib"], b["rwis"])
        rqkv = RowScatter(p, gqkv, ds, b["rqkvb"], b["rqkvs"])
        rsm = RowScatter(p, gs, NVEC, b["rsmb"], b["rsms"])
        rwo = PlaneScatter(p, gwo, ds, b["rwob"], b["rwos"])
        sd = RepSpread(p, td, b["rwdp"])
        si = RepSpread(p, ti, b["rwip"])
        sq = RepSpread(p, tq, b["rqkvp"])
        ss = RepSpread(p, ts, b["rsmp"])
        so = OwnerSpread(p, to, b["rwop"])

        smalls.start()
        for copy in local[:3]:
            copy.wait()
        g_qkv.start()
        ax.start()
        for copy in local[3:]:
            copy.wait()

        @pl.when(p.z == p.me)
        def _():
            own_wo.wait()

        g_wo.start()
        for g in [g_wia, g_wib] + g_wd:
            g.start()
        sums[...] = jnp.zeros_like(sums)
        gbi8[...] = jnp.zeros_like(gbi8)
        gqv8[...] = jnp.zeros_like(gqv8)
        gflat[...] = jnp.zeros_like(gflat)
        for k in range(1, Z):
            smalls.forward(k)
        for k in range(1, Z):
            g_qkv.forward(k)
        g_wo.forward()
        smalls.finish()
        for i in range(nv):
            row = [small[s * NVEC + i : s * NVEC + i + 1, :] for s in range(S)]
            flat[i : i + 1, :] = jnp.concatenate(row, 1)
        ax.beside()
        ax.across()
        g_qkv.finish()

        low = lax.broadcasted_iota(jnp.int32, (SEQ, 128), 1) < HEAD_DIM
        keep = (low, jnp.logical_not(low))

        def project(rows):
            for n in range(3):
                c = pl.ds(n * dr, dr)
                z = mm(x_all[rows, :], wqkv[:, c])
                if n == 0:
                    z = z + flat[0:1, cols]
                if n == 2:
                    z = z + flat[1:2, cols]
                qkv[rows, c] = z.astype(BF)

        def pick(v, h):
            return jnp.where(keep[h], v, jnp.zeros_like(v))

        def attend(chip):
            def one(j, _):
                seq = chip * (C // SEQ) + j
                rows = rows_of(seq, SEQ)
                for n in range(pairs):
                    q2 = qkv[rows, n * 128 : n * 128 + 128]
                    k2 = qkv[rows, dr + n * 128 : dr + n * 128 + 128]
                    v2 = qkv[rows, 2 * dr + n * 128 : 2 * dr + n * 128 + 128]
                    got = []
                    for h in range(2):
                        scores = mm_nt(pick(q2, h), k2) * 0.125
                        e = jnp.exp(scores - jnp.max(scores, axis=-1, keepdims=True))
                        pr = e / jnp.sum(e, axis=-1, keepdims=True)
                        probs[rows_of(seq * 2 * pairs + 2 * n + h, SEQ), :] = pr
                        got.append(mm(pr.astype(BF), v2))
                    ctx[rows, n * 128 : n * 128 + 128] = jnp.where(low, got[0], got[1]).astype(BF)
                return 0

            lax.fori_loop(0, C // SEQ, one, 0)

        def attn_part(rows):
            def tile(c):
                part[rows, c] = mm(ctx[rows, :], wor[:, c]).astype(BF)

            tiles(D, tile)

        def inner(rows):
            def tile(c):
                z = mm(hid_all[rows, :], wir[:, c]) + flat[8:9, c]
                phi = 0.5 * (1.0 + lax.erf(z * INV_ROOT_TWO))
                acted[rows, c] = (z * phi).astype(BF)
                slope[rows, c] = phi + z * jnp.exp(-0.5 * z * z) * INV_ROOT_TWO_PI

            tiles(V, tile)

        def down(rows, q):
            c = pl.ds(q * wide, wide)
            part[rows, c] = mm(acted[rows, :], wdr[:, c]).astype(BF)

        def d_inner(rows):
            def tile(c):
                d = mm_nt(d2_all[rows, :], wdr[c, :]) * slope[rows, c]
                gbi8[:, c] += fold(d)
                d_in[rows, c] = d.astype(BF)

            tiles(V, tile)

        def hid_part(rows):
            def tile(c):
                part[rows, c] = mm_nt(d_in[rows, :], wir[c, :]).astype(BF)

            tiles(D, tile)

        def d_attend(chip):
            rows = rows_of(chip, C)
            dctx[rows, :] = mm_nt(d1_all[rows, :], wor[...]).astype(BF)

            def one(j, _):
                seq = chip * (C // SEQ) + j
                rows = rows_of(seq, SEQ)
                for n in range(pairs):
                    lanes = [slice(m * dr + n * 128, m * dr + n * 128 + 128) for m in range(3)]
                    q2, k2, v2 = (qkv[rows, c] for c in lanes)
                    dc2 = dctx[rows, lanes[0]]
                    got = []
                    for h in range(2):
                        pr = probs[rows_of(seq * 2 * pairs + 2 * n + h, SEQ), :]
                        dp = mm_nt(pick(dc2, h), v2)
                        delta = jnp.sum(pr * dp, axis=-1, keepdims=True)
                        dsc = (pr * (dp - delta) * 0.125).astype(BF)
                        got.append((mm(dsc, k2), mm_tn(dsc, q2), mm_tn(pr.astype(BF), dc2)))
                    dq, dk, dv = (jnp.where(low, u, w) for u, w in zip(*got))
                    gqv8[:, lanes[0]] += fold(dq)
                    gqv8[:, lanes[1]] += fold(dv)
                    for v, c in zip((dq, dk, dv), lanes):
                        dqkv[rows, c] = v.astype(BF)
                return 0

            lax.fori_loop(0, C // SEQ, one, 0)

        def in_part(rows):
            def tile(c):
                part[rows, c] = mm_nt(dqkv[rows, :], wqkv[c, :]).astype(BF)

            tiles(D, tile)

        def grad_plane(lhs, rhs, dst, z):
            both = pl.ds(pl.multiple_of(z * 2 * ds, 2 * ds), 2 * ds)
            dst[both, :] = mm_tn(lhs[:, both], rhs[...]).astype(BF)

        def grad_all(lhs, rhs, dst, scatter):
            for k in list(range(1, Z)) + [0]:
                grad_plane(lhs, rhs, dst, lax.rem(p.z + k, Z))
                scatter.first[k].start()

        def forward(g):
            for k in range(1, Z):
                g.forward(k)

        project(far_chip)
        project(own_chip)
        attend(p.chip(1))
        g_wo.finish()
        attn_part(far_chip)
        t1.start_far()
        attend(p.a)
        attn_part(own_chip)
        t1.start_near()
        t1.pass_on()
        t1.finish()
        forward(g_wia)

        def norm_one(i, _):
            at = step_rows(i)
            normed, rstd = norm_parts(x[at, :].astype(F32) + t1.read(i) + flat[2:3, :])
            hidden = normed * flat[3:4, :] + flat[4:5, :]
            normed_r[at, :] = normed
            rstd_r[at, :] = jnp.broadcast_to(rstd, (STEP, 128))
            hidden_r[at, :] = hidden
            hid_all[step_rows(i, p.me * T), :] = hidden.astype(BF)
            return 0

        lax.fori_loop(0, T // STEP, norm_one, 0)
        a1.start()
        t1.drain()
        a1.beside()
        a1.across()
        forward(g_wib)
        g_wia.finish()
        g_wib.finish()
        inner(own_chip)
        forward(g_wd[0])
        inner(far_chip)
        forward(g_wd[1])
        for q in range(QUARTERS):
            g_wd[q].finish()
            down(far_chip, q)
            if q == QUARTERS - 1:
                t2.start_far()
            down(own_chip, q)
            if q + 2 < QUARTERS:
                forward(g_wd[q + 2])
        t2.start_near()
        t2.pass_on()
        t2.finish()

        def norm_two(i, _):
            at = step_rows(i)
            normed, rstd = norm_parts(hidden_r[at, :] + t2.read(i) + flat[5:6, :])
            out_o[at, :] = (normed * flat[6:7, :] + flat[7:8, :]).astype(BF)
            dout = cot[at, :].astype(F32)
            d_two = norm_back(dout * flat[6:7, :], normed, rstd)
            sums[24:32, :] += fold(d_two)
            sums[32:40, :] += fold(dout * normed)
            sums[40:48, :] += fold(dout)
            d_two_r[at, :] = d_two
            d2_all[step_rows(i, p.me * T), :] = d_two.astype(BF)
            return 0

        lax.fori_loop(0, T // STEP, norm_two, 0)
        a2.start()
        t2.drain()
        a2.beside()
        d_inner(own_chip)
        a2.across()
        grad_all(acted, d2_all, gwd, rwd)
        d_inner(far_chip)
        hid_part(far_chip)
        t3.start_far()
        hid_part(own_chip)
        t3.start_near()
        t3.pass_on()
        grad_all(hid_all, d_in, gwi, rwi)
        rwd.pass_on(1)
        t3.finish()

        def back_one(i, _):
            at = step_rows(i)
            d_hidden = d_two_r[at, :] + t3.read(i)
            normed = normed_r[at, :]
            d_one = norm_back(d_hidden * flat[3:4, :], normed, rstd_r[at, 0:1])
            sums[0:8, :] += fold(d_one)
            sums[8:16, :] += fold(d_hidden * normed)
            sums[16:24, :] += fold(d_hidden)
            d_one_r[at, :] = d_one
            d1_all[step_rows(i, p.me * T), :] = d_one.astype(BF)
            return 0

        lax.fori_loop(0, T // STEP, back_one, 0)
        a3.start()
        t3.drain()
        rwd.pass_on(2)
        a3.beside()
        d_attend(p.a)
        a3.across()
        rwd.pass_on(3)
        gwo[...] = mm_tn(ctx[...], d1_all[...]).astype(BF)
        rwo.start()
        d_attend(p.chip(1))
        gflat[0:1, cols] = jnp.sum(gqv8[:, :dr], axis=0, keepdims=True)
        gflat[1:2, cols] = jnp.sum(gqv8[:, dr:], axis=0, keepdims=True)
        for i in range(6):
            gflat[i + 2 : i + 3, :] = jnp.sum(sums[8 * i : 8 * i + 8, :], axis=0, keepdims=True)
        gflat[8:9, :] = jnp.sum(gbi8[...], axis=0, keepdims=True)
        for s in range(S):
            gs[s * NVEC : (s + 1) * NVEC, :] = gflat[:, s * ds : (s + 1) * ds]
        rsm.start()
        rwi.pass_on(1)
        grad_all(x_all, dqkv, gqkv, rqkv)
        in_part(far_chip)
        t4.start_far()
        in_part(own_chip)
        t4.start_near()
        t4.pass_on()
        rwi.pass_on(2)
        t4.finish()

        def last(i, _):
            at = step_rows(i)
            gin_o[at, :] = (d_one_r[at, :] + t4.read(i)).astype(BF)
            return 0

        lax.fori_loop(0, T // STEP, last, 0)
        rwd.total(td)
        sd.start()
        rwi.pass_on(3)
        rwo.pass_on()
        for k in range(1, Z):
            rsm.pass_on(k)
        sd.forward()
        rqkv.pass_on(1)
        rwi.total(ti)
        si.start()
        rqkv.pass_on(2)
        rwo.total(to)
        so.start()
        rqkv.pass_on(3)
        si.forward()
        rsm.total(ts)
        ss.start()
        so.forward()
        rqkv.total(tq)
        sq.start()
        ss.forward()
        sd.finish()
        si.finish()
        so.finish()
        sq.forward()
        sq.finish()
        ss.finish()
        for g in [smalls, g_qkv, g_wo, g_wia, g_wib] + g_wd + [ax, a1, a2, a3, t4]:
            g.drain()
        for g in (rwd, rwi, rqkv, rsm, rwo, sd, si, sq, ss, so):
            g.drain()

    ins = [x, cot, wq, wk, wv, wo, wi, wd] + [v[None] for v in vectors]
    outs = [((T, D), BF)] * 2
    outs += [((R, ds, W), BF), ((R, ds, V), BF), ((R, fr, D), BF), ((ds, D), BF)]
    outs += [((R, NVEC, ds), F32)]
    return pl.pallas_call(
        kernel,
        out_shape=[jax.ShapeDtypeStruct(*o) for o in outs],
        in_specs=[VMEM_SPEC] * 2 + [ANY_SPEC] * 6 + [VMEM_SPEC] * nv,
        out_specs=[VMEM_SPEC] * len(outs),
        scratch_shapes=bag.specs,
        compiler_params=pltpu.CompilerParams(
            collective_id=12, has_side_effects=True, vmem_limit_bytes=LIMIT
        ),
        cost_estimate=pl.CostEstimate(
            flops=10 * 10**9, bytes_accessed=24 << 20, transcendentals=4 << 20
        ),
    )(*ins)


def widen(out, gin, tq, ti, td, to, ts, S):
    R, ds, W = tq.shape
    D, dr = R * W // 3, W // 3
    fr, V = td.shape[1], ti.shape[2]
    fs = fr * R
    T = out.shape[0]
    few, tok = ds // R, T // R

    def kernel(out, gin, tq, ti, td, to, ts, out_o, gin_o, oq, ok, ov, oo, oi, od, *vec_o):
        out_o[...] = out[...]
        gin_o[...] = gin[...]
        od[...] = td[0].astype(F32)
        oo[...] = to[...].astype(F32)
        for r in range(R):
            for n, o in enumerate((oq, ok, ov)):
                o[:, r * dr : (r + 1) * dr] = tq[r, :, n * dr : (n + 1) * dr].astype(F32)
            for c in range(S):
                lo = c * fs + r * fr
                oi[:, lo : lo + fr] = ti[r, :, c * fr : (c + 1) * fr].astype(F32)

        @pl.when(pl.program_id(0) == 0)
        def _():
            total = ts[0]
            for r in range(1, R):
                total = total + ts[r]
            for i in range(8):
                vec_o[i][...] = total[i : i + 1, :]
            for r in range(R):
                vec_o[8][:, r * fr : (r + 1) * fr] = ts[r, 8:9, :]

    def rows(n, c):
        return pl.BlockSpec((n, c), lambda i: (i, 0))

    def slab(n, c):
        return pl.BlockSpec((R, n, c), lambda i: (0, i, 0))

    def whole(*shape):
        return pl.BlockSpec(shape, lambda i: (0,) * len(shape))

    outs = [((T, D), BF)] * 2 + [((ds, D), F32)] * 4 + [((ds, S * fs), F32), ((fs, D), F32)]
    outs += [((1, ds), F32)] * 8 + [((1, fs), F32)]
    return pl.pallas_call(
        kernel,
        grid=(R,),
        out_shape=[jax.ShapeDtypeStruct(*o) for o in outs],
        in_specs=[
            rows(tok, D),
            rows(tok, D),
            slab(few, W),
            slab(few, V),
            pl.BlockSpec((1, fr, D), lambda i: (i, 0, 0)),
            rows(few, D),
            whole(R, NVEC, ds),
        ],
        out_specs=[rows(tok, D)] * 2
        + [rows(few, D)] * 4
        + [rows(few, S * fs), rows(fr, D)]
        + [whole(1, ds)] * 8
        + [whole(1, fs)],
        compiler_params=pltpu.CompilerParams(vmem_limit_bytes=24 << 20),
    )(out, gin, tq, ti, td, to, ts)


def fast_body(
    block_input,
    out_cotangent,
    w_query,
    w_key,
    w_value,
    w_output,
    bias_query,
    bias_value,
    bias_output,
    gain_first,
    shift_first,
    w_inner,
    bias_inner,
    w_down,
    bias_down,
    gain_second,
    shift_second,
):
    vectors = (
        bias_query,
        bias_value,
        bias_output,
        gain_first,
        shift_first,
        bias_down,
        gain_second,
        shift_second,
        bias_inner,
    )
    S = lax.axis_size("shard")
    got = layer(
        block_input,
        out_cotangent,
        w_query,
        w_key,
        w_value,
        w_output,
        w_inner,
        w_down,
        vectors,
        S,
        lax.axis_size("rep"),
    )
    got = widen(*got, S)
    output, grad_input, gq, gk, gv, go, gi, gd = got[:8]
    gbq, gbv, gbo, ggone, gsone, gbd, ggtwo, gstwo, gbi = (v.reshape(-1) for v in got[8:])
    return (
        output,
        grad_input,
        gq,
        gk,
        gv,
        go,
        gbq,
        gbv,
        gbo,
        ggone,
        gsone,
        gi,
        gbi,
        gd,
        gbd,
        ggtwo,
        gstwo,
    )


def fits_fast(mesh):
    S, R = mesh.shape["shard"], mesh.shape["rep"]
    return R == 4 and S == 2 * R


def solution(mesh):
    tokens = P(("shard", "rep"), None)
    mat = P("shard", None)
    vec = P("shard")
    params = (mat, mat, mat, mat, vec, vec, vec, vec, vec, mat, vec, mat, vec, vec, vec)
    return jax.shard_map(
        fast_body if fits_fast(mesh) else body,
        mesh=mesh,
        in_specs=(tokens, tokens) + params,
        out_specs=(tokens, tokens) + params,
        check_vma=False,
    )
```

```python
import jax
import jax.numpy as jnp
from jax import lax
from jax.experimental import pallas as pl
from jax.experimental.pallas import tpu as pltpu
from jax.sharding import PartitionSpec as P

HEAD_DIM = 64
SEQ = 128
PAD = 16


EPS = 1e-06
INV_ROOT_TWO = 0.7071067811865476
INV_ROOT_TWO_PI = 0.3989422804014327
BF = jnp.bfloat16
F32 = jnp.float32


def norm_parts(resid):
    centre = resid - jnp.mean(resid, axis=-1, keepdims=True)
    variance = jnp.mean(centre * centre, axis=-1, keepdims=True)
    rstd = lax.rsqrt(variance + EPS)
    return (centre * rstd, rstd)


def norm_back(upstream, normed, rstd):
    return rstd * (
        upstream
        - jnp.mean(upstream, axis=-1, keepdims=True)
        - normed * jnp.mean(upstream * normed, axis=-1, keepdims=True)
    )


def mm(a, b):
    return jnp.dot(a, b, preferred_element_type=F32)


def mm_nt(a, b):
    return lax.dot_general(a, b, (((1,), (1,)), ((), ())), preferred_element_type=F32)


def mm_tn(a, b):
    return lax.dot_general(a, b, (((0,), (0,)), ((), ())), preferred_element_type=F32)


def ein(spec, a, b):
    return jnp.einsum(spec, a, b, preferred_element_type=F32)


MESH = pl.DeviceIdType.MESH
CHUNK = 16


class Peers:
    def __init__(self, R):
        self.R, self.A = R, R // 2
        self.me = lax.axis_index("rep")
        self.c = lax.rem(self.me, 2)
        self.a = lax.div(self.me, 2)
        self.partner = self.me + 1 - 2 * self.c

    def chip(self, k):
        return lax.rem(self.a + k, self.A)

    def same(self, k):
        return 2 * self.chip(k) + self.c

    def other(self, k):
        return 2 * self.chip(k) + 1 - self.c

    def meet(self):
        barrier = pltpu.get_barrier_semaphore()
        for dev in [self.partner] + [self.same(k) for k in range(1, self.A)]:
            pl.semaphore_signal(barrier, inc=1, device_id={"rep": dev}, device_id_type=MESH)
        pl.semaphore_wait(barrier, self.A)


def rows_of(index, T):
    return pl.ds(pl.multiple_of(index * T, T), T)


def chunk_rows(i, base=None):
    start = i * CHUNK if base is None else base + i * CHUNK
    return pl.ds(pl.multiple_of(start, CHUNK), CHUNK)


def remote(src, dst, send, recv, dev):
    return pltpu.make_async_remote_copy(
        src_ref=src,
        dst_ref=dst,
        send_sem=send,
        recv_sem=recv,
        device_id={"rep": dev},
        device_id_type=MESH,
    )


def scatter_sum(p, part, T, near, far, out, sems):
    near_s, near_r, far_s, far_r = sems
    order = list(range(1, p.A)) + [0]
    first = {
        k: remote(
            part.at[rows_of(p.other(k), T)], near.at[k], near_s.at[k], near_r.at[k], p.partner
        )
        for k in order
    }
    for k in order:
        first[k].start()
    second = []
    for k in range(1, p.A):
        first[k].wait_recv()
        base = p.same(k) * T

        def add(i, _, k=k, base=base):
            mine = part[chunk_rows(i, base), :].astype(F32)
            out[k - 1, chunk_rows(i), :] = (mine + near[k, chunk_rows(i), :].astype(F32)).astype(BF)
            return 0

        lax.fori_loop(0, T // CHUNK, add, 0)
        copy = remote(out.at[k - 1], far.at[k - 1], far_s.at[k - 1], far_r.at[k - 1], p.same(k))
        copy.start()
        second.append(copy)
    first[0].wait_recv()
    for copy in second:
        copy.wait_recv()

    def read(i):
        total = part[chunk_rows(i, p.me * T), :].astype(F32) + near[0, chunk_rows(i), :].astype(F32)
        for k in range(1, p.A):
            total = total + far[k - 1, chunk_rows(i), :].astype(F32)
        return total

    return read, list(first.values()) + second


def spread(p, src, full, T, sems):
    dir_s, dir_r, fwd_s, fwd_r = sems
    mine = full.at[rows_of(p.me, T)]
    direct = {}
    for k in list(range(1, p.A)) + [0]:
        dev = p.partner if k == 0 else p.same(k)
        direct[k] = remote(src, mine, dir_s.at[k], dir_r.at[k], dev)
        direct[k].start()
    passed = []
    for k in range(1, p.A):
        direct[k].wait_recv()
        block = full.at[rows_of(p.same(p.A - k), T)]
        copy = remote(block, block, fwd_s.at[k - 1], fwd_r.at[k - 1], p.partner)
        copy.start()
        passed.append(copy)
    direct[0].wait_recv()
    for copy in passed:
        copy.wait_recv()
    return list(direct.values()) + passed


def drain(copies):
    for copy in copies:
        copy.wait_send()


def run_kernel(kernel, cid, T, D, R, ins, outs, scatter, gather):
    A = R // 2
    few = max(A - 1, 1)
    scratch = []
    if scatter:
        scratch += [
            pltpu.VMEM((A, T, D), BF),
            pltpu.VMEM((few, T, D), BF),
            pltpu.VMEM((few, T, D), BF),
        ]
        scratch += [pltpu.SemaphoreType.DMA((n,)) for n in (A, A, few, few)]
    if gather:
        scratch += [pltpu.SemaphoreType.DMA((n,)) for n in (A, A, few, few)]
    vmem = pl.BlockSpec(memory_space=pltpu.VMEM)
    return pl.pallas_call(
        kernel,
        out_shape=[jax.ShapeDtypeStruct(*o) for o in outs],
        in_specs=[vmem] * len(ins),
        out_specs=[vmem] * len(outs),
        scratch_shapes=scratch,
        compiler_params=pltpu.CompilerParams(collective_id=cid, has_side_effects=True),
        cost_estimate=pl.CostEstimate(flops=0, bytes_accessed=24 << 20, transcendentals=0),
    )(*ins)


def gather_kernel(block, R, cid):
    T, D = block.shape

    def kernel(src, full, *sems):
        p = Peers(R)
        p.meet()

        def put(i, _):
            full[chunk_rows(i, p.me * T), :] = src[chunk_rows(i), :]
            return 0

        lax.fori_loop(0, T // CHUNK, put, 0)
        drain(spread(p, src, full, T, sems))

    return run_kernel(kernel, cid, T, D, R, [block], [((R * T, D), BF)], False, True)[0]


def norm_one_step(partial, x, bo, gone, sone):
    T, D = x.shape
    R = partial.shape[0] // T

    def kernel(part, xr, bor, gr, sr, normed_o, rstd_o, hidden_o, full, near, far, out, *sems):
        p = Peers(R)
        p.meet()
        read, sent = scatter_sum(p, part, T, near, far, out, sems[:4])

        def step(i, _):
            normed, rstd = norm_parts(xr[chunk_rows(i), :].astype(F32) + read(i) + bor[...])
            hidden = normed * gr[...] + sr[...]
            normed_o[chunk_rows(i), :] = normed
            rstd_o[chunk_rows(i), :] = rstd
            hidden_o[chunk_rows(i), :] = hidden
            full[chunk_rows(i, p.me * T), :] = hidden.astype(BF)
            return 0

        lax.fori_loop(0, T // CHUNK, step, 0)
        drain(sent + spread(p, full.at[rows_of(p.me, T)], full, T, sems[4:]))

    ins = [partial, x, bo[None], gone[None], sone[None]]
    outs = [((T, D), F32), ((T, 1), F32), ((T, D), F32), ((R * T, D), BF)]
    return run_kernel(kernel, 1, T, D, R, ins, outs, True, True)


def add_sums(ref, values):
    for n, v in enumerate(values):
        ref[n : n + 1, :] += jnp.sum(v, axis=0, keepdims=True)


def norm_two_step(partial, hidden, bd, gtwo, stwo, cot):
    T, D = hidden.shape
    R = partial.shape[0] // T

    def kernel(part, hr, br, gr, sr, cr, out_o, d_o, sums, full, near, far, out, *sems):
        p = Peers(R)
        p.meet()
        sums[...] = jnp.zeros_like(sums)
        read, sent = scatter_sum(p, part, T, near, far, out, sems[:4])

        def step(i, _):
            normed, rstd = norm_parts(hr[chunk_rows(i), :] + read(i) + br[...])
            out_o[chunk_rows(i), :] = (normed * gr[...] + sr[...]).astype(BF)
            dout = cr[chunk_rows(i), :].astype(F32)
            d_two = norm_back(dout * gr[...], normed, rstd)
            add_sums(sums, (d_two, dout * normed, dout))
            d_o[chunk_rows(i), :] = d_two
            full[chunk_rows(i, p.me * T), :] = d_two.astype(BF)
            return 0

        lax.fori_loop(0, T // CHUNK, step, 0)
        drain(sent + spread(p, full.at[rows_of(p.me, T)], full, T, sems[4:]))

    ins = [partial, hidden, bd[None], gtwo[None], stwo[None], cot]
    outs = [((T, D), BF), ((T, D), F32), ((8, D), F32), ((R * T, D), BF)]
    return run_kernel(kernel, 2, T, D, R, ins, outs, True, True)


def back_one_step(partial, d_two, normed, rstd, gone):
    T, D = d_two.shape
    R = partial.shape[0] // T

    def kernel(part, dr, nr, rr, gr, d_o, sums, full, near, far, out, *sems):
        p = Peers(R)
        p.meet()
        sums[...] = jnp.zeros_like(sums)
        read, sent = scatter_sum(p, part, T, near, far, out, sems[:4])

        def step(i, _):
            d_hidden = dr[chunk_rows(i), :] + read(i)
            normed = nr[chunk_rows(i), :]
            d_one = norm_back(d_hidden * gr[...], normed, rr[chunk_rows(i), :])
            add_sums(sums, (d_one, d_hidden * normed, d_hidden))
            d_o[chunk_rows(i), :] = d_one
            full[chunk_rows(i, p.me * T), :] = d_one.astype(BF)
            return 0

        lax.fori_loop(0, T // CHUNK, step, 0)
        drain(sent + spread(p, full.at[rows_of(p.me, T)], full, T, sems[4:]))

    ins = [partial, d_two, normed, rstd, gone[None]]
    outs = [((T, D), F32), ((8, D), F32), ((R * T, D), BF)]
    return run_kernel(kernel, 3, T, D, R, ins, outs, True, True)


def input_step(partial, d_one):
    T, D = d_one.shape
    R = partial.shape[0] // T

    def kernel(part, dr, grad, near, far, out, *sems):
        p = Peers(R)
        p.meet()
        read, sent = scatter_sum(p, part, T, near, far, out, sems)

        def step(i, _):
            grad[chunk_rows(i), :] = (dr[chunk_rows(i), :] + read(i)).astype(BF)
            return 0

        lax.fori_loop(0, T // CHUNK, step, 0)
        drain(sent)

    return run_kernel(kernel, 4, T, D, R, [partial, d_one], [((T, D), BF)], True, False)[0]


def body(
    block_input,
    out_cotangent,
    w_query,
    w_key,
    w_value,
    w_output,
    bias_query,
    bias_value,
    bias_output,
    gain_first,
    shift_first,
    w_inner,
    bias_inner,
    w_down,
    bias_down,
    gain_second,
    shift_second,
):
    S = lax.axis_size("shard")
    R = lax.axis_size("rep")
    r = lax.axis_index("rep")
    T = block_input.shape[0]
    D = w_query.shape[1]
    ds = w_query.shape[0]
    dr = D // R
    fs = w_down.shape[0]
    fr = fs // R
    W = 4 * dr

    def cols(w):
        return lax.dynamic_slice(w, (0, r * dr), (ds, dr))

    small = jnp.concatenate(
        [
            v.astype(BF)
            for v in (
                bias_query,
                bias_value,
                bias_output,
                gain_first,
                shift_first,
                bias_down,
                gain_second,
                shift_second,
                bias_inner,
            )
        ]
    )
    n_small = small.shape[0]
    small = jnp.pad(small, (0, PAD * W - n_small)).reshape(PAD, W)
    pack = jnp.concatenate(
        [jnp.concatenate([cols(w_query), cols(w_key), cols(w_value), cols(w_output)], 1), small], 0
    )
    got = lax.all_gather(pack, "shard", axis=0)
    x_all = gather_kernel(block_input, R, 0)
    wi_r = lax.dynamic_index_in_dim(w_inner.reshape(ds, S, R, fr), r, 2, keepdims=False)
    V = S * fr
    dv = fr * D // V
    wd_r = lax.dynamic_slice(w_down, (r * fr, 0), (fr, D)).reshape(dv, V)
    mlp = lax.all_gather(jnp.concatenate([wi_r.reshape(ds, V), wd_r], 0), "shard", axis=0)
    wi = mlp[:, :ds].reshape(D, V)
    wd = mlp[:, ds:].reshape(V, D)
    wqkv = got[:, :ds, : 3 * dr].reshape(D, 3 * dr)
    wo = lax.all_to_all(
        got[:, :ds, 3 * dr :].reshape(D, dr), "rep", split_axis=0, concat_axis=1, tiled=True
    )
    flat = got[:, ds:, :].reshape(S, PAD * W)[:, :n_small].astype(F32)
    bq, bv, bo, gone, sone, bd, gtwo, stwo = (
        flat[:, i * ds : (i + 1) * ds].reshape(D) for i in range(8)
    )
    bi = lax.dynamic_index_in_dim(flat[:, 8 * ds :].reshape(S, R, fr), r, 1, keepdims=False)
    bi = bi.reshape(S * fr)
    bq = lax.dynamic_slice(bq, (r * dr,), (dr,))
    bv = lax.dynamic_slice(bv, (r * dr,), (dr,))

    N = R * T
    shape4 = (N // SEQ, SEQ, dr // HEAD_DIM, HEAD_DIM)
    qkv = mm(x_all, wqkv)
    query = (qkv[:, :dr] + bq).astype(BF).reshape(shape4)
    keyed = qkv[:, dr : 2 * dr].astype(BF).reshape(shape4)
    valued = (qkv[:, 2 * dr :] + bv).astype(BF).reshape(shape4)
    scores = ein("bqhe,bkhe->bhqk", query, keyed) * 0.125
    top = jnp.max(scores, axis=-1, keepdims=True)
    logsum = top + jnp.log(jnp.sum(jnp.exp(scores - top), axis=-1, keepdims=True))
    probs = jnp.exp(scores - logsum)
    probs_b = probs.astype(BF)
    context = ein("bhqk,bkhe->bqhe", probs_b, valued).astype(BF).reshape(N, dr)
    attn_part = mm(context, wo).astype(BF)

    normed_one, rstd_one, hidden, hidden_all = norm_one_step(attn_part, block_input, bo, gone, sone)
    inner = mm(hidden_all, wi) + bi
    phi = 0.5 * (1.0 + lax.erf(inner * INV_ROOT_TWO))
    acted = (inner * phi).astype(BF)
    slope = phi + inner * jnp.exp(-0.5 * inner * inner) * INV_ROOT_TWO_PI
    down_part = mm(acted, wd).astype(BF)

    output, d_two, sums_two, d_two_all = norm_two_step(
        down_part, hidden, bd, gtwo, stwo, out_cotangent
    )
    d_inner = mm_nt(d_two_all, wd) * slope
    g_bias_inner = jnp.sum(d_inner, axis=0)
    d_inner_b = d_inner.astype(BF)
    hid_part = mm_nt(d_inner_b, wi).astype(BF)
    g_wd = mm_tn(acted, d_two_all).astype(BF).reshape(S, dv, V)
    g_wi = mm_tn(hidden_all, d_inner_b).astype(BF).reshape(S, ds, V)
    g_mlp = lax.psum_scatter(
        jnp.concatenate([g_wi, g_wd], 1), "shard", scatter_dimension=0, tiled=True
    )[0]

    d_one, sums_one, d_one_all = back_one_step(hid_part, d_two, normed_one, rstd_one, gone)
    g_wo = mm_tn(context, d_one_all).astype(BF)
    g_wo = lax.all_to_all(g_wo, "rep", split_axis=1, concat_axis=0, tiled=True)
    d_context = mm_nt(d_one_all, wo).astype(BF).reshape(shape4)
    d_probs = ein("bqhe,bkhe->bhqk", d_context, valued)
    delta = jnp.sum(probs * d_probs, axis=-1, keepdims=True)
    d_scores = (probs * (d_probs - delta) * 0.125).astype(BF)
    d_query = ein("bhqk,bkhe->bqhe", d_scores, keyed).reshape(N, dr)
    d_keyed = ein("bhqk,bqhe->bkhe", d_scores, query).reshape(N, dr)
    d_valued = ein("bhqk,bqhe->bkhe", probs_b, d_context).reshape(N, dr)
    g_bias_query = jnp.sum(d_query, axis=0)
    g_bias_value = jnp.sum(d_valued, axis=0)
    d_qkv = jnp.concatenate([d_query.astype(BF), d_keyed.astype(BF), d_valued.astype(BF)], 1)
    in_part = mm_nt(d_qkv, wqkv).astype(BF)

    def placed(v):
        return lax.dynamic_update_slice(jnp.zeros((D,), F32), v, (r * dr,)).reshape(S, ds)

    g_small = jnp.concatenate(
        [
            placed(g_bias_query),
            placed(g_bias_value),
            sums_one[0].reshape(S, ds),
            sums_one[1].reshape(S, ds),
            sums_one[2].reshape(S, ds),
            sums_two[0].reshape(S, ds),
            sums_two[1].reshape(S, ds),
            sums_two[2].reshape(S, ds),
            g_bias_inner.reshape(S, fr),
        ],
        1,
    ).astype(BF)
    n_g = g_small.shape[1]
    g_small = jnp.pad(g_small, ((0, 0), (0, PAD * W - n_g))).reshape(S, PAD, W)
    g_pack = jnp.concatenate([mm_tn(x_all, d_qkv).astype(BF), g_wo], 1).reshape(S, ds, W)
    g_pack = jnp.concatenate([g_pack, g_small], 1)
    g_pack = lax.psum_scatter(g_pack, "shard", scatter_dimension=0, tiled=True)[0]

    grad_input = input_step(in_part, d_one)

    mlps = gather_kernel(g_mlp, R, 5).reshape(R, ds + dv, V).astype(F32)
    wd_out = mlps[:, ds:].reshape(R * fr, D)
    wi_out = mlps[:, :ds].reshape(R, ds, S, fr).transpose(1, 2, 0, 3).reshape(ds, S * R * fr)
    packs = gather_kernel(g_pack, R, 6).reshape(R, ds + PAD, W).astype(F32)
    main = packs[:, :ds].reshape(R, ds, 4, dr).transpose(2, 1, 0, 3).reshape(4, ds, D)
    tail = packs[:, ds:].reshape(R, PAD * W)
    summed = jnp.sum(tail[:, : 8 * ds], axis=0)
    gbq, gbv, gbo, ggone, gsone, gbd, ggtwo, gstwo = (
        summed[i * ds : (i + 1) * ds] for i in range(8)
    )
    gbi = tail[:, 8 * ds : n_g].reshape(fs)
    return (
        output,
        grad_input,
        main[0],
        main[1],
        main[2],
        main[3],
        gbq,
        gbv,
        gbo,
        ggone,
        gsone,
        wi_out,
        gbi,
        wd_out,
        gbd,
        ggtwo,
        gstwo,
    )

VMEM_SPEC = pl.BlockSpec(memory_space=pltpu.VMEM)
ANY_SPEC = pl.BlockSpec(memory_space=pl.ANY)
LIMIT = 56 << 20
NVEC = 16


def dma_sems(*counts):
    return [pltpu.SemaphoreType.DMA((n,)) for n in counts]


class Place(Peers):
    def __init__(self, S, R):
        super().__init__(R)
        self.S, self.Z = S, S // 2
        self.s = lax.axis_index("shard")
        self.z = lax.div(self.s, 2)
        self.y = lax.rem(self.s, 2)
        self.across = self.s + 1 - 2 * self.y

    def up(self, k):
        return 2 * lax.rem(self.z + k, self.Z) + self.y

    def down(self, k):
        return 2 * lax.rem(self.z + self.Z - k, self.Z) + self.y

    def flip(self, s):
        return s + 1 - 2 * self.y

    def meet_all(self):
        barrier = pltpu.get_barrier_semaphore()
        for dev in [self.partner] + [self.same(k) for k in range(1, self.A)]:
            pl.semaphore_signal(barrier, inc=1, device_id={"rep": dev}, device_id_type=MESH)
        for dev in [self.across] + [self.up(k) for k in range(1, self.Z)]:
            pl.semaphore_signal(barrier, inc=1, device_id={"shard": dev}, device_id_type=MESH)
        pl.semaphore_wait(barrier, self.A + self.Z)


def to_shard(src, dst, send, recv, dev):
    return pltpu.make_async_remote_copy(
        src_ref=src,
        dst_ref=dst,
        send_sem=send,
        recv_sem=recv,
        device_id={"shard": dev},
        device_id_type=MESH,
    )


class LineGather:
    def __init__(self, p, full, T, row, sems, cols=None):
        self.p, self.full, self.T, self.row, self.cols = p, full, T, row, cols
        a_s, a_r, b_s, b_r, f_s, f_r = sems
        half = lax.div(p.z, 2)
        self.inner = p.z == 1 + half
        self.outer = jnp.logical_not(self.inner)
        beside = 4 * half + 1 - p.z
        turn = jnp.where(self.inner, 1, 0)
        self.zs = [beside, 3 - 3 * half, 2 - half]
        self.near = self.copy(p.z, a_s.at[0], a_r.at[0], beside)
        self.over = self.copy(p.z, b_s.at[0], b_r.at[turn], 2 - half)
        self.on = [self.copy(self.zs[j + 1], f_s.at[j], b_r.at[j], beside) for j in range(2)]

    @staticmethod
    def sems():
        return dma_sems(1, 1, 1, 2, 2, 1)

    def block(self, z):
        rows = rows_of(2 * z + self.row, self.T)
        return self.full.at[rows] if self.cols is None else self.full.at[rows, self.cols]

    def copy(self, z, send, recv, to):
        return to_shard(self.block(z), self.block(z), send, recv, 2 * to + self.p.y)

    def start(self):
        self.near.start()
        self.over.start()

    def push(self, then=(None, None, None)):
        self.near.wait_recv()
        if then[0] is not None:
            then[0].start()

        @pl.when(self.inner)
        def _():
            for j in range(2):
                self.on[j].wait_recv()
                self.on[j].start()
                if then[j + 1] is not None:
                    then[j + 1].start()

    def pull(self, then=(None, None, None)):
        @pl.when(self.outer)
        def _():
            for j in range(2):
                self.on[j].wait_recv()
                if then[j + 1] is not None:
                    then[j + 1].start()

    def drain(self):
        self.near.wait_send()
        self.over.wait_send()

        @pl.when(self.inner)
        def _():
            for copy in self.on:
                copy.wait_send()


class RowGather:
    def __init__(self, p, full, T, sems, cols=None):
        self.line = LineGather(p, full, T, p.y, sems[:6], cols)
        ys, yr = sems[6:]
        self.side = []
        for i, z in enumerate([p.z] + self.line.zs):
            block = self.line.block(z)
            self.side.append(to_shard(block, block, ys.at[i], yr.at[i], p.across))

    @staticmethod
    def sems(Z):
        return LineGather.sems() + dma_sems(Z, Z)

    def start(self):
        self.line.start()
        self.side[0].start()

    def push(self):
        self.line.push(self.side[1:])

    def pull(self):
        self.line.pull(self.side[1:])

    def finish(self):
        for copy in self.side:
            copy.wait_recv()

    def drain(self):
        self.line.drain()
        drain(self.side)


class SideGather:
    def __init__(self, p, full, T, sems, cols=None):
        self.lines = [
            LineGather(p, full, T, row, sems[6 * i : 6 * i + 6], cols)
            for i, row in enumerate((p.y, 1 - p.y))
        ]
        block = self.lines[0].block(p.z)
        self.side = to_shard(block, block, sems[12].at[0], sems[13].at[0], p.across)

    @staticmethod
    def sems(Z):
        return LineGather.sems() * 2 + dma_sems(1, 1)

    def begin(self):
        self.side.start()

    def start(self):
        self.lines[0].start()
        self.side.wait_recv()
        self.lines[1].start()

    def push(self):
        for line in self.lines:
            line.push()

    def pull(self):
        for line in self.lines:
            line.pull()

    def finish(self):
        pass

    def drain(self):
        for line in self.lines:
            line.drain()
        self.side.wait_send()


class PlaneGather:
    def __init__(self, p, full, T, sems):
        self.p = p
        self.zs, self.zr, self.ys, self.yr = sems
        rows = full.at[rows_of(p.y, T)]
        self.far = {
            k: to_shard(rows, rows, self.zs.at[k - 1], self.zr.at[0], p.up(k))
            for k in range(1, p.Z)
        }
        self.near = to_shard(rows, rows, self.ys.at[0], self.yr.at[0], p.across)
        self.mine = p.z == p.me

    @staticmethod
    def sems(Z):
        return dma_sems(Z - 1, 1, 1, 1)

    def start(self):
        @pl.when(self.mine)
        def _():
            for k in range(1, self.p.Z):
                self.far[k].start()
            self.near.start()

    def forward(self):
        @pl.when(jnp.logical_not(self.mine))
        def _():
            self.far[1].wait_recv()
            self.near.start()

    def finish(self):
        self.near.wait_recv()

    def drain(self):
        @pl.when(self.mine)
        def _():
            for k in range(1, self.p.Z):
                self.far[k].wait_send()

        self.near.wait_send()


class RowScatter:
    def __init__(self, p, part, T, bufs, sems):
        self.p, self.part, self.T = p, part, T
        self.close, self.out, self.far = bufs
        ys, yr, zs, zr = sems
        self.first = {}
        for k in range(p.Z):
            to = p.up(k)
            self.first[k] = to_shard(
                part.at[rows_of(p.flip(to), T)], self.close.at[k], ys.at[k], yr.at[k], p.across
            )
        self.second = {
            k: to_shard(
                self.out.at[k - 1], self.far.at[k - 1], zs.at[k - 1], zr.at[k - 1], p.up(k)
            )
            for k in range(1, p.Z)
        }

    @staticmethod
    def bufs(Z, T, C, dtype):
        return [pltpu.VMEM((n, T, C), dtype) for n in (Z, Z - 1, Z - 1)]

    @staticmethod
    def sems(Z):
        return dma_sems(Z, Z, Z - 1, Z - 1)

    def start(self):
        for k in list(range(1, self.p.Z)) + [0]:
            self.first[k].start()

    def pass_on(self, k):
        self.first[k].wait_recv()
        base = self.p.up(k) * self.T
        dtype = self.out.dtype

        def add(i, _):
            mine = self.part[chunk_rows(i, base), :].astype(F32)
            near = self.close[k, chunk_rows(i), :].astype(F32)
            self.out[k - 1, chunk_rows(i), :] = (mine + near).astype(dtype)
            return 0

        lax.fori_loop(0, self.T // CHUNK, add, 0)
        self.second[k].start()

    def total(self, dst, at=None):
        p = self.p
        self.first[0].wait_recv()
        for k in range(1, p.Z):
            self.second[k].wait_recv()

        def add(i, _):
            total = self.part[chunk_rows(i, p.s * self.T), :].astype(F32)
            total = total + self.close[0, chunk_rows(i), :].astype(F32)
            for k in range(1, p.Z):
                total = total + self.far[k - 1, chunk_rows(i), :].astype(F32)
            dst[p.me, chunk_rows(i), :] = total.astype(dst.dtype)
            return 0

        lax.fori_loop(0, self.T // CHUNK, add, 0)

    def drain(self):
        for copy in list(self.first.values()) + list(self.second.values()):
            copy.wait_send()


class PlaneScatter:
    def __init__(self, p, part, T, bufs, sems):
        self.p, self.part, self.T = p, part, T
        self.close, self.out, self.far = bufs
        ys, yr, zs, zr = sems
        self.first = to_shard(
            part.at[rows_of(1 - p.y, T)], self.close, ys.at[0], yr.at[0], p.across
        )
        self.mine = p.z == p.me
        self.hop = lax.rem(p.z + p.Z - p.me, p.Z)
        self.sends = to_shard(
            self.out,
            self.far.at[jnp.maximum(self.hop - 1, 0)],
            zs.at[0],
            zr.at[jnp.maximum(self.hop - 1, 0)],
            2 * p.me + p.y,
        )
        self.gets = [
            to_shard(self.out, self.far.at[k], zs.at[0], zr.at[k], p.up(k + 1))
            for k in range(p.Z - 1)
        ]

    @staticmethod
    def bufs(Z, T, C, dtype):
        return [pltpu.VMEM((T, C), dtype), pltpu.VMEM((T, C), dtype), pltpu.VMEM((Z - 1, T, C), dtype)]

    @staticmethod
    def sems(Z):
        return dma_sems(1, 1, 1, Z - 1)

    def start(self):
        self.first.start()

    def pass_on(self):
        self.first.wait_recv()

        def add(i, _):
            mine = self.part[chunk_rows(i, self.p.y * self.T), :].astype(F32)
            self.out[chunk_rows(i), :] = (mine + self.close[chunk_rows(i), :].astype(F32)).astype(BF)
            return 0

        lax.fori_loop(0, self.T // CHUNK, add, 0)

        @pl.when(jnp.logical_not(self.mine))
        def _():
            self.sends.start()

    def total(self, dst):
        @pl.when(self.mine)
        def _():
            for copy in self.gets:
                copy.wait_recv()

            def add(i, _):
                total = self.part[chunk_rows(i, self.p.y * self.T), :].astype(F32)
                total = total + self.close[chunk_rows(i), :].astype(F32)
                for k in range(self.p.Z - 1):
                    total = total + self.far[k, chunk_rows(i), :].astype(F32)
                dst[chunk_rows(i), :] = total.astype(BF)
                return 0

            lax.fori_loop(0, self.T // CHUNK, add, 0)

    def drain(self):
        self.first.wait_send()

        @pl.when(jnp.logical_not(self.mine))
        def _():
            self.sends.wait_send()


class RepSpread:
    def __init__(self, p, full, sems):
        self.p = p
        dir_s, dir_r, fwd_s, fwd_r = sems
        own = full.at[p.me]
        self.direct = {0: remote(own, own, dir_s.at[0], dir_r.at[0], p.partner)}
        self.passed = {}
        for k in range(1, p.A):
            self.direct[k] = remote(own, own, dir_s.at[k], dir_r.at[k], p.same(k))
            block = full.at[p.same(p.A - k)]
            self.passed[k] = remote(block, block, fwd_s.at[k - 1], fwd_r.at[k - 1], p.partner)

    @staticmethod
    def sems(A):
        return dma_sems(A, A, A - 1, A - 1)

    def start(self):
        for k in list(range(1, self.p.A)) + [0]:
            self.direct[k].start()

    def forward(self):
        for k in range(1, self.p.A):
            self.direct[k].wait_recv()
            self.passed[k].start()

    def finish(self):
        self.direct[0].wait_recv()
        for copy in self.passed.values():
            copy.wait_recv()

    def drain(self):
        drain(list(self.direct.values()) + list(self.passed.values()))


class OwnerSpread:
    def __init__(self, p, block, sems):
        self.p = p
        s0, s1, rx, rp = sems
        self.across = remote(block, block, s0.at[0], rx.at[0], p.same(1))
        self.beside = remote(block, block, s1.at[0], rp.at[0], p.partner)
        self.mine = p.z == p.me
        self.relay = p.z == p.same(1)
        self.other = jnp.logical_not(jnp.logical_or(self.mine, self.relay))

    @staticmethod
    def sems():
        return dma_sems(1, 1, 1, 1)

    def start(self):
        @pl.when(self.mine)
        def _():
            self.across.start()
            self.beside.start()

    def forward(self):
        @pl.when(self.relay)
        def _():
            self.across.wait_recv()
            self.beside.start()

    def finish(self):
        @pl.when(self.other)
        def _():
            self.beside.wait_recv()

    def drain(self):
        @pl.when(self.mine)
        def _():
            self.across.wait_send()

        @pl.when(jnp.logical_not(self.other))
        def _():
            self.beside.wait_send()

class RepScatter:
    def __init__(self, p, part, T, bufs, sems):
        self.p, self.part, self.T = p, part, T
        self.near, self.out, self.far = bufs
        near_s, near_r, far_s, far_r = sems
        self.first = {
            k: remote(
                part.at[rows_of(p.other(k), T)],
                self.near.at[k],
                near_s.at[k],
                near_r.at[k],
                p.partner,
            )
            for k in range(p.A)
        }
        self.second = {
            k: remote(
                self.out.at[k - 1], self.far.at[k - 1], far_s.at[k - 1], far_r.at[k - 1], p.same(k)
            )
            for k in range(1, p.A)
        }

    @staticmethod
    def bufs(A, T, D):
        return [pltpu.VMEM((n, T, D), BF) for n in (A, A - 1, A - 1)]

    @staticmethod
    def sems(A):
        return dma_sems(A, A, A - 1, A - 1)

    def start_far(self):
        for k in range(1, self.p.A):
            self.first[k].start()

    def start_near(self):
        self.first[0].start()

    def pass_on(self):
        for k in range(1, self.p.A):
            self.first[k].wait_recv()
            base = self.p.same(k) * self.T

            def add(i, _, k=k, base=base):
                mine = self.part[step_rows(i, base), :].astype(F32)
                near = self.near[k, step_rows(i), :].astype(F32)
                self.out[k - 1, step_rows(i), :] = (mine + near).astype(BF)
                return 0

            lax.fori_loop(0, self.T // STEP, add, 0)
            self.second[k].start()

    def finish(self):
        self.first[0].wait_recv()
        for copy in self.second.values():
            copy.wait_recv()

    def read(self, i):
        total = self.part[step_rows(i, self.p.me * self.T), :].astype(F32)
        total = total + self.near[0, step_rows(i), :].astype(F32)
        for k in range(1, self.p.A):
            total = total + self.far[k - 1, step_rows(i), :].astype(F32)
        return total

    def drain(self):
        drain(list(self.first.values()) + list(self.second.values()))


STEP = 32


def step_rows(i, base=None):
    start = i * STEP if base is None else base + i * STEP
    return pl.ds(pl.multiple_of(start, STEP), STEP)


class TokenSpread:
    def __init__(self, p, full, T, sems):
        self.p = p
        dir_s, dir_r, fwd_s, fwd_r = sems
        own = full.at[rows_of(p.me, T)]
        self.direct = {0: remote(own, own, dir_s.at[0], dir_r.at[0], p.partner)}
        self.passed = {}
        for k in range(1, p.A):
            self.direct[k] = remote(own, own, dir_s.at[k], dir_r.at[k], p.same(k))
            block = full.at[rows_of(p.same(p.A - k), T)]
            self.passed[k] = remote(block, block, fwd_s.at[k - 1], fwd_r.at[k - 1], p.partner)

    @staticmethod
    def sems(A):
        return dma_sems(A, A, A - 1, A - 1)

    def start(self):
        for k in list(range(1, self.p.A)) + [0]:
            self.direct[k].start()

    def beside(self):
        self.direct[0].wait_recv()

    def across(self):
        for k in range(1, self.p.A):
            self.direct[k].wait_recv()
            self.passed[k].start()
        for copy in self.passed.values():
            copy.wait_recv()

    def drain(self):
        drain(list(self.direct.values()) + list(self.passed.values()))


class Bag:
    def __init__(self):
        self.names, self.specs = [], []

    def want(self, name, specs):
        specs = specs if isinstance(specs, list) else [specs]
        self.names.append((name, len(specs)))
        self.specs += specs

    def hand_out(self, refs):
        got, at = {}, 0
        for name, n in self.names:
            got[name] = refs[at] if n == 1 else list(refs[at : at + n])
            at += n
        return got


def fold(v):
    return jnp.sum(v.reshape(v.shape[0] // 8, 8, v.shape[1]), axis=0)


TILE = 256
QUARTERS = 4


def tiles(n, body):
    def step(i, _):
        body(pl.ds(pl.multiple_of(i * TILE, TILE), TILE))
        return 0

    lax.fori_loop(0, n // TILE, step, 0)


def layer(x, cot, wq, wk, wv, wo, wi, wd, vectors, S, R):
    T, D = x.shape
    ds, fs = wq.shape[0], wd.shape[0]
    dr, fr = D // R, fs // R
    V = S * fr
    W = 3 * dr
    Z, A = S // 2, R // 2
    nv = len(vectors)
    N = R * T
    C = N // A
    pairs = dr // 128
    half = V // 2
    wide = D // QUARTERS

    bag = Bag()
    bag.want("here", pltpu.SemaphoreType.DMA((S + 6,)))
    bag.want("small", pltpu.VMEM((S * NVEC, ds), F32))
    bag.want("flat", pltpu.VMEM((NVEC, D), F32))
    for name, shape, t in (
        ("x_all", (N, D), BF),
        ("wqkv", (D, W), BF),
        ("wor", (dr, D), BF),
        ("wir", (D, V), BF),
        ("wdr", (V, D), BF),
        ("qkv", (N, W), BF),
        ("probs", (N * dr // HEAD_DIM, SEQ), F32),
        ("ctx", (N, dr), BF),
        ("part", (N, D), BF),
        ("normed", (T, D), F32),
        ("rstd", (T, 128), F32),
        ("hidden", (T, D), F32),
        ("hid_all", (N, D), BF),
        ("acted", (N, V), BF),
        ("slope", (N, V), F32),
        ("d_two", (T, D), F32),
        ("d2_all", (N, D), BF),
        ("d_in", (N, V), BF),
        ("d_one", (T, D), F32),
        ("d1_all", (N, D), BF),
        ("dctx", (N, dr), BF),
        ("dqkv", (N, W), BF),
        ("sums", (48, D), F32),
        ("gbi8", (8, V), F32),
        ("gqv8", (8, 2 * dr), F32),
        ("gflat", (NVEC, D), F32),
        ("gs", (S * NVEC, ds), F32),
        ("gwd", (V, D), BF),
        ("gwi", (D, V), BF),
        ("gqkv", (D, W), BF),
        ("gwo", (dr, D), BF),
    ):
        bag.want(name, pltpu.VMEM(shape, t))
    for name in ("smalls", "g_qkv", "g_wia", "g_wib", "g_wd0", "g_wd1"):
        bag.want(name, RowGather.sems(Z))
    bag.want("g_wd2", SideGather.sems(Z))
    bag.want("g_wo", PlaneGather.sems(Z))
    for name in ("ax", "a1", "a2", "a3"):
        bag.want(name, TokenSpread.sems(A))
    for name in ("t1", "t2", "t3", "t4"):
        bag.want(name + "b", RepScatter.bufs(A, T, D))
        bag.want(name + "s", RepScatter.sems(A))
    for name, n, c, t in (
        ("rwd", fr, D, BF),
        ("rwi", ds, V, BF),
        ("rqkv", ds, W, BF),
        ("rsm", NVEC, ds, F32),
    ):
        bag.want(name + "b", RowScatter.bufs(Z, n, c, t))
        bag.want(name + "s", RowScatter.sems(Z))
        bag.want(name + "p", RepSpread.sems(A))
    bag.want("rwob", PlaneScatter.bufs(Z, ds, D, BF))
    bag.want("rwos", PlaneScatter.sems(Z))
    bag.want("rwop", OwnerSpread.sems())

    def kernel(*refs):
        x, cot, wq, wk, wv, wo, wi, wd = refs[:8]
        vecs = refs[8 : 8 + nv]
        at = 8 + nv
        out_o, gin_o, tq, ti, td, to, ts = refs[at : at + 7]
        b = bag.hand_out(refs[at + 7 :])
        x_all, wqkv, wor, wir, wdr = b["x_all"], b["wqkv"], b["wor"], b["wir"], b["wdr"]
        qkv, probs, ctx, part = b["qkv"], b["probs"], b["ctx"], b["part"]
        flat, small, here = b["flat"], b["small"], b["here"]
        normed_r, rstd_r, hidden_r = b["normed"], b["rstd"], b["hidden"]
        hid_all, acted, slope, d_two_r, d2_all = (
            b["hid_all"],
            b["acted"],
            b["slope"],
            b["d_two"],
            b["d2_all"],
        )
        d_in, d_one_r, d1_all, dctx, dqkv = b["d_in"], b["d_one"], b["d1_all"], b["dctx"], b["dqkv"]
        sums, gbi8, gqv8, gflat, gs = b["sums"], b["gbi8"], b["gqv8"], b["gflat"], b["gs"]
        gwd, gwi, gqkv, gwo = b["gwd"], b["gwi"], b["gqkv"], b["gwo"]

        p = Place(S, R)
        mine = rows_of(p.s, ds)
        own_tok = rows_of(p.me, T)
        own_chip = rows_of(p.a, C)
        far_chip = rows_of(p.chip(1), C)
        cols = pl.ds(pl.multiple_of(p.me * dr, dr), dr)
        local = []

        def bring(src, dst):
            copy = pltpu.make_async_copy(src, dst, here.at[len(local)])
            copy.start()
            local.append(copy)

        for i, w in enumerate((wq, wk, wv)):
            bring(w.at[:, cols], wqkv.at[mine, pl.ds(i * dr, dr)])
        for c in range(S):
            piece = pl.ds(pl.multiple_of(c * fs + p.me * fr, fr), fr)
            bring(wi.at[:, piece], wir.at[mine, pl.ds(c * fr, fr)])
        bring(wd.at[rows_of(p.me, fr)], wdr.at[mine])
        own_wo = pltpu.make_async_copy(wo, wor.at[rows_of(p.y, ds)], here.at[len(local)])

        @pl.when(p.z == p.me)
        def _():
            own_wo.start()

        piece = pl.ds(pl.multiple_of(p.me * fr, fr), fr)
        pieces = [v[...] for v in vecs[:-1]] + [vecs[-1][:, piece]]
        pieces.append(jnp.zeros((NVEC - nv, ds), F32))
        small[rows_of(p.s, NVEC), :] = jnp.concatenate(pieces, 0)
        x_all[own_tok, :] = x[...]
        p.meet_all()

        smalls = RowGather(p, small, NVEC, b["smalls"])
        g_qkv = RowGather(p, wqkv, ds, b["g_qkv"])
        left, right = pl.ds(0, half), pl.ds(half, half)
        g_wia = RowGather(p, wir, ds, b["g_wia"], left)
        g_wib = RowGather(p, wir, ds, b["g_wib"], right)
        g_wd0 = RowGather(p, wdr, fr, b["g_wd0"], pl.ds(0, wide))
        g_wd1 = RowGather(p, wdr, fr, b["g_wd1"], pl.ds(wide, wide))
        g_wd2 = SideGather(p, wdr, fr, b["g_wd2"], pl.ds(2 * wide, 2 * wide))
        g_wo = PlaneGather(p, wor, ds, b["g_wo"])
        ax = TokenSpread(p, x_all, T, b["ax"])
        a1 = TokenSpread(p, hid_all, T, b["a1"])
        a2 = TokenSpread(p, d2_all, T, b["a2"])
        a3 = TokenSpread(p, d1_all, T, b["a3"])
        t1 = RepScatter(p, part, T, b["t1b"], b["t1s"])
        t2 = RepScatter(p, part, T, b["t2b"], b["t2s"])
        t3 = RepScatter(p, part, T, b["t3b"], b["t3s"])
        t4 = RepScatter(p, part, T, b["t4b"], b["t4s"])
        rwd = RowScatter(p, gwd, fr, b["rwdb"], b["rwds"])
        rwi = RowScatter(p, gwi, ds, b["rwib"], b["rwis"])
        rqkv = RowScatter(p, gqkv, ds, b["rqkvb"], b["rqkvs"])
        rsm = RowScatter(p, gs, NVEC, b["rsmb"], b["rsms"])
        rwo = PlaneScatter(p, gwo, ds, b["rwob"], b["rwos"])
        sd = RepSpread(p, td, b["rwdp"])
        si = RepSpread(p, ti, b["rwip"])
        sq = RepSpread(p, tq, b["rqkvp"])
        ss = RepSpread(p, ts, b["rsmp"])
        so = OwnerSpread(p, to, b["rwop"])

        smalls.start()
        for copy in local[:3]:
            copy.wait()
        g_qkv.start()
        ax.start()
        for copy in local[3:]:
            copy.wait()

        @pl.when(p.z == p.me)
        def _():
            own_wo.wait()

        g_wo.start()
        g_wia.start()
        sums[...] = jnp.zeros_like(sums)
        gbi8[...] = jnp.zeros_like(gbi8)
        gqv8[...] = jnp.zeros_like(gqv8)
        gflat[...] = jnp.zeros_like(gflat)
        smalls.push()
        g_qkv.push()
        smalls.pull()
        g_wo.forward()
        g_qkv.pull()
        g_wib.start()
        g_wd2.begin()
        g_wd0.start()
        g_wd1.start()
        smalls.finish()
        for i in range(nv):
            row = [small[s * NVEC + i : s * NVEC + i + 1, :] for s in range(S)]
            flat[i : i + 1, :] = jnp.concatenate(row, 1)
        ax.beside()
        ax.across()
        g_wia.push()
        g_qkv.finish()

        low = lax.broadcasted_iota(jnp.int32, (SEQ, 128), 1) < HEAD_DIM
        keep = (low, jnp.logical_not(low))

        def project(rows):
            for n in range(3):
                c = pl.ds(n * dr, dr)
                z = mm(x_all[rows, :], wqkv[:, c])
                if n == 0:
                    z = z + flat[0:1, cols]
                if n == 2:
                    z = z + flat[1:2, cols]
                qkv[rows, c] = z.astype(BF)

        def pick(v, h):
            return jnp.where(keep[h], v, jnp.zeros_like(v))

        def attend(chip):
            def one(j, _):
                seq = chip * (C // SEQ) + j
                rows = rows_of(seq, SEQ)
                for n in range(pairs):
                    q2 = qkv[rows, n * 128 : n * 128 + 128]
                    k2 = qkv[rows, dr + n * 128 : dr + n * 128 + 128]
                    v2 = qkv[rows, 2 * dr + n * 128 : 2 * dr + n * 128 + 128]
                    got = []
                    for h in range(2):
                        scores = mm_nt(pick(q2, h), k2) * 0.125
                        e = jnp.exp(scores - jnp.max(scores, axis=-1, keepdims=True))
                        pr = e / jnp.sum(e, axis=-1, keepdims=True)
                        probs[rows_of(seq * 2 * pairs + 2 * n + h, SEQ), :] = pr
                        got.append(mm(pr.astype(BF), v2))
                    ctx[rows, n * 128 : n * 128 + 128] = jnp.where(low, got[0], got[1]).astype(BF)
                return 0

            lax.fori_loop(0, C // SEQ, one, 0)

        def attn_part(rows):
            def tile(c):
                part[rows, c] = mm(ctx[rows, :], wor[:, c]).astype(BF)

            tiles(D, tile)

        def inner(rows):
            def tile(c):
                z = mm(hid_all[rows, :], wir[:, c]) + flat[8:9, c]
                phi = 0.5 * (1.0 + lax.erf(z * INV_ROOT_TWO))
                acted[rows, c] = (z * phi).astype(BF)
                slope[rows, c] = phi + z * jnp.exp(-0.5 * z * z) * INV_ROOT_TWO_PI

            tiles(V, tile)

        def down(rows, q):
            c = pl.ds(q * wide, wide)
            part[rows, c] = mm(acted[rows, :], wdr[:, c]).astype(BF)

        def d_inner(rows):
            def tile(c):
                d = mm_nt(d2_all[rows, :], wdr[c, :]) * slope[rows, c]
                gbi8[:, c] += fold(d)
                d_in[rows, c] = d.astype(BF)

            tiles(V, tile)

        def hid_part(rows):
            def tile(c):
                part[rows, c] = mm_nt(d_in[rows, :], wir[c, :]).astype(BF)

            tiles(D, tile)

        def d_attend(chip):
            rows = rows_of(chip, C)
            dctx[rows, :] = mm_nt(d1_all[rows, :], wor[...]).astype(BF)

            def one(j, _):
                seq = chip * (C // SEQ) + j
                rows = rows_of(seq, SEQ)
                for n in range(pairs):
                    lanes = [slice(m * dr + n * 128, m * dr + n * 128 + 128) for m in range(3)]
                    q2, k2, v2 = (qkv[rows, c] for c in lanes)
                    dc2 = dctx[rows, lanes[0]]
                    got = []
                    for h in range(2):
                        pr = probs[rows_of(seq * 2 * pairs + 2 * n + h, SEQ), :]
                        dp = mm_nt(pick(dc2, h), v2)
                        delta = jnp.sum(pr * dp, axis=-1, keepdims=True)
                        dsc = (pr * (dp - delta) * 0.125).astype(BF)
                        got.append((mm(dsc, k2), mm_tn(dsc, q2), mm_tn(pr.astype(BF), dc2)))
                    dq, dk, dv = (jnp.where(low, u, w) for u, w in zip(*got))
                    gqv8[:, lanes[0]] += fold(dq)
                    gqv8[:, lanes[1]] += fold(dv)
                    for v, c in zip((dq, dk, dv), lanes):
                        dqkv[rows, c] = v.astype(BF)
                return 0

            lax.fori_loop(0, C // SEQ, one, 0)

        def in_part(rows):
            def tile(c):
                part[rows, c] = mm_nt(dqkv[rows, :], wqkv[c, :]).astype(BF)

            tiles(D, tile)

        def grad_plane(lhs, rhs, dst, z):
            both = pl.ds(pl.multiple_of(z * 2 * ds, 2 * ds), 2 * ds)
            dst[both, :] = mm_tn(lhs[:, both], rhs[...]).astype(BF)

        def grad_all(lhs, rhs, dst, scatter):
            for k in list(range(1, Z)) + [0]:
                grad_plane(lhs, rhs, dst, lax.rem(p.z + k, Z))
                scatter.first[k].start()

        project(far_chip)
        project(own_chip)
        attend(p.chip(1))
        g_wia.pull()
        g_wo.finish()
        attn_part(far_chip)
        t1.start_far()
        g_wib.push()
        attend(p.a)
        attn_part(own_chip)
        t1.start_near()
        t1.pass_on()
        g_wib.pull()
        g_wd0.push()
        g_wd2.start()
        t1.finish()

        def norm_one(i, _):
            at = step_rows(i)
            normed, rstd = norm_parts(x[at, :].astype(F32) + t1.read(i) + flat[2:3, :])
            hidden = normed * flat[3:4, :] + flat[4:5, :]
            normed_r[at, :] = normed
            rstd_r[at, :] = jnp.broadcast_to(rstd, (STEP, 128))
            hidden_r[at, :] = hidden
            hid_all[step_rows(i, p.me * T), :] = hidden.astype(BF)
            return 0

        lax.fori_loop(0, T // STEP, norm_one, 0)
        a1.start()
        t1.drain()
        g_wd0.pull()
        g_wd1.push()
        a1.beside()
        a1.across()
        g_wd1.pull()
        g_wd2.push()
        g_wia.finish()
        g_wib.finish()
        inner(own_chip)
        inner(far_chip)
        g_wd0.finish()
        down(far_chip, 0)
        down(own_chip, 0)
        g_wd1.finish()
        down(far_chip, 1)
        down(own_chip, 1)
        g_wd2.pull()
        down(far_chip, 2)
        down(far_chip, 3)
        t2.start_far()
        down(own_chip, 2)
        down(own_chip, 3)
        t2.start_near()
        t2.pass_on()
        t2.finish()

        def norm_two(i, _):
            at = step_rows(i)
            normed, rstd = norm_parts(hidden_r[at, :] + t2.read(i) + flat[5:6, :])
            out_o[at, :] = (normed * flat[6:7, :] + flat[7:8, :]).astype(BF)
            dout = cot[at, :].astype(F32)
            d_two = norm_back(dout * flat[6:7, :], normed, rstd)
            sums[24:32, :] += fold(d_two)
            sums[32:40, :] += fold(dout * normed)
            sums[40:48, :] += fold(dout)
            d_two_r[at, :] = d_two
            d2_all[step_rows(i, p.me * T), :] = d_two.astype(BF)
            return 0

        lax.fori_loop(0, T // STEP, norm_two, 0)
        a2.start()
        t2.drain()
        a2.beside()
        d_inner(own_chip)
        a2.across()
        grad_all(acted, d2_all, gwd, rwd)
        d_inner(far_chip)
        hid_part(far_chip)
        t3.start_far()
        hid_part(own_chip)
        t3.start_near()
        t3.pass_on()
        grad_all(hid_all, d_in, gwi, rwi)
        rwd.pass_on(1)
        t3.finish()

        def back_one(i, _):
            at = step_rows(i)
            d_hidden = d_two_r[at, :] + t3.read(i)
            normed = normed_r[at, :]
            d_one = norm_back(d_hidden * flat[3:4, :], normed, rstd_r[at, 0:1])
            sums[0:8, :] += fold(d_one)
            sums[8:16, :] += fold(d_hidden * normed)
            sums[16:24, :] += fold(d_hidden)
            d_one_r[at, :] = d_one
            d1_all[step_rows(i, p.me * T), :] = d_one.astype(BF)
            return 0

        lax.fori_loop(0, T // STEP, back_one, 0)
        a3.start()
        t3.drain()
        rwd.pass_on(2)
        a3.beside()
        d_attend(p.a)
        a3.across()
        rwd.pass_on(3)
        gwo[...] = mm_tn(ctx[...], d1_all[...]).astype(BF)
        rwo.start()
        d_attend(p.chip(1))
        gflat[0:1, cols] = jnp.sum(gqv8[:, :dr], axis=0, keepdims=True)
        gflat[1:2, cols] = jnp.sum(gqv8[:, dr:], axis=0, keepdims=True)
        for i in range(6):
            gflat[i + 2 : i + 3, :] = jnp.sum(sums[8 * i : 8 * i + 8, :], axis=0, keepdims=True)
        gflat[8:9, :] = jnp.sum(gbi8[...], axis=0, keepdims=True)
        for s in range(S):
            gs[s * NVEC : (s + 1) * NVEC, :] = gflat[:, s * ds : (s + 1) * ds]
        rsm.start()
        rwi.pass_on(1)
        grad_all(x_all, dqkv, gqkv, rqkv)
        in_part(far_chip)
        t4.start_far()
        in_part(own_chip)
        t4.start_near()
        t4.pass_on()
        rwi.pass_on(2)
        t4.finish()

        def last(i, _):
            at = step_rows(i)
            gin_o[at, :] = (d_one_r[at, :] + t4.read(i)).astype(BF)
            return 0

        lax.fori_loop(0, T // STEP, last, 0)
        rwd.total(td)
        sd.start()
        rwi.pass_on(3)
        rwo.pass_on()
        for k in range(1, Z):
            rsm.pass_on(k)
        sd.forward()
        rqkv.pass_on(1)
        rwi.total(ti)
        si.start()
        rqkv.pass_on(2)
        rwo.total(to)
        so.start()
        rqkv.pass_on(3)
        si.forward()
        rsm.total(ts)
        ss.start()
        so.forward()
        rqkv.total(tq)
        sq.start()
        ss.forward()
        sd.finish()
        si.finish()
        so.finish()
        sq.forward()
        sq.finish()
        ss.finish()
        for g in (smalls, g_qkv, g_wo, g_wia, g_wib, g_wd0, g_wd1, g_wd2, ax, a1, a2, a3, t4):
            g.drain()
        for g in (rwd, rwi, rqkv, rsm, rwo, sd, si, sq, ss, so):
            g.drain()

    ins = [x, cot, wq, wk, wv, wo, wi, wd] + [v[None] for v in vectors]
    outs = [((T, D), BF)] * 2
    outs += [((R, ds, W), BF), ((R, ds, V), BF), ((R, fr, D), BF), ((ds, D), BF)]
    outs += [((R, NVEC, ds), F32)]
    return pl.pallas_call(
        kernel,
        out_shape=[jax.ShapeDtypeStruct(*o) for o in outs],
        in_specs=[VMEM_SPEC] * 2 + [ANY_SPEC] * 6 + [VMEM_SPEC] * nv,
        out_specs=[VMEM_SPEC] * len(outs),
        scratch_shapes=bag.specs,
        compiler_params=pltpu.CompilerParams(
            collective_id=12, has_side_effects=True, vmem_limit_bytes=LIMIT
        ),
        cost_estimate=pl.CostEstimate(
            flops=10 * 10**9, bytes_accessed=24 << 20, transcendentals=4 << 20
        ),
    )(*ins)


def widen(out, gin, tq, ti, td, to, ts, S):
    R, ds, W = tq.shape
    D, dr = R * W // 3, W // 3
    fr, V = td.shape[1], ti.shape[2]
    fs = fr * R
    T = out.shape[0]
    few, tok = ds // R, T // R

    def kernel(out, gin, tq, ti, td, to, ts, out_o, gin_o, oq, ok, ov, oo, oi, od, *vec_o):
        out_o[...] = out[...]
        gin_o[...] = gin[...]
        od[...] = td[0].astype(F32)
        oo[...] = to[...].astype(F32)
        for r in range(R):
            for n, o in enumerate((oq, ok, ov)):
                o[:, r * dr : (r + 1) * dr] = tq[r, :, n * dr : (n + 1) * dr].astype(F32)
            for c in range(S):
                lo = c * fs + r * fr
                oi[:, lo : lo + fr] = ti[r, :, c * fr : (c + 1) * fr].astype(F32)

        @pl.when(pl.program_id(0) == 0)
        def _():
            total = ts[0]
            for r in range(1, R):
                total = total + ts[r]
            for i in range(8):
                vec_o[i][...] = total[i : i + 1, :]
            for r in range(R):
                vec_o[8][:, r * fr : (r + 1) * fr] = ts[r, 8:9, :]

    def rows(n, c):
        return pl.BlockSpec((n, c), lambda i: (i, 0))

    def slab(n, c):
        return pl.BlockSpec((R, n, c), lambda i: (0, i, 0))

    def whole(*shape):
        return pl.BlockSpec(shape, lambda i: (0,) * len(shape))

    outs = [((T, D), BF)] * 2 + [((ds, D), F32)] * 4 + [((ds, S * fs), F32), ((fs, D), F32)]
    outs += [((1, ds), F32)] * 8 + [((1, fs), F32)]
    return pl.pallas_call(
        kernel,
        grid=(R,),
        out_shape=[jax.ShapeDtypeStruct(*o) for o in outs],
        in_specs=[
            rows(tok, D),
            rows(tok, D),
            slab(few, W),
            slab(few, V),
            pl.BlockSpec((1, fr, D), lambda i: (i, 0, 0)),
            rows(few, D),
            whole(R, NVEC, ds),
        ],
        out_specs=[rows(tok, D)] * 2
        + [rows(few, D)] * 4
        + [rows(few, S * fs), rows(fr, D)]
        + [whole(1, ds)] * 8
        + [whole(1, fs)],
        compiler_params=pltpu.CompilerParams(vmem_limit_bytes=LIMIT),
    )(out, gin, tq, ti, td, to, ts)


def fast_body(
    block_input,
    out_cotangent,
    w_query,
    w_key,
    w_value,
    w_output,
    bias_query,
    bias_value,
    bias_output,
    gain_first,
    shift_first,
    w_inner,
    bias_inner,
    w_down,
    bias_down,
    gain_second,
    shift_second,
):
    vectors = (
        bias_query,
        bias_value,
        bias_output,
        gain_first,
        shift_first,
        bias_down,
        gain_second,
        shift_second,
        bias_inner,
    )
    S = lax.axis_size("shard")
    got = layer(
        block_input,
        out_cotangent,
        w_query,
        w_key,
        w_value,
        w_output,
        w_inner,
        w_down,
        vectors,
        S,
        lax.axis_size("rep"),
    )
    got = widen(*got, S)
    output, grad_input, gq, gk, gv, go, gi, gd = got[:8]
    gbq, gbv, gbo, ggone, gsone, gbd, ggtwo, gstwo, gbi = (v.reshape(-1) for v in got[8:])
    return (
        output,
        grad_input,
        gq,
        gk,
        gv,
        go,
        gbq,
        gbv,
        gbo,
        ggone,
        gsone,
        gi,
        gbi,
        gd,
        gbd,
        ggtwo,
        gstwo,
    )


def fits_fast(mesh):
    S, R = mesh.shape["shard"], mesh.shape["rep"]
    return R == 4 and S == 8


def solution(mesh):
    tokens = P(("shard", "rep"), None)
    mat = P("shard", None)
    vec = P("shard")
    params = (mat, mat, mat, mat, vec, vec, vec, vec, vec, mat, vec, mat, vec, vec, vec)
    return jax.shard_map(
        fast_body if fits_fast(mesh) else body,
        mesh=mesh,
        in_specs=(tokens, tokens) + params,
        out_specs=(tokens, tokens) + params,
        check_vma=False,
    )
```

```python
import jax
import jax.numpy as jnp
from jax import lax
from jax.experimental import pallas as pl
from jax.experimental.pallas import tpu as pltpu
from jax.sharding import PartitionSpec as P

HEAD_DIM = 64
SEQ = 128
PAD = 16


EPS = 1e-06
INV_ROOT_TWO = 0.7071067811865476
INV_ROOT_TWO_PI = 0.3989422804014327
BF = jnp.bfloat16
F32 = jnp.float32


def norm_parts(resid):
    centre = resid - jnp.mean(resid, axis=-1, keepdims=True)
    variance = jnp.mean(centre * centre, axis=-1, keepdims=True)
    rstd = lax.rsqrt(variance + EPS)
    return (centre * rstd, rstd)


def norm_back(upstream, normed, rstd):
    return rstd * (
        upstream
        - jnp.mean(upstream, axis=-1, keepdims=True)
        - normed * jnp.mean(upstream * normed, axis=-1, keepdims=True)
    )


def mm(a, b):
    return jnp.dot(a, b, preferred_element_type=F32)


def mm_nt(a, b):
    return lax.dot_general(a, b, (((1,), (1,)), ((), ())), preferred_element_type=F32)


def mm_tn(a, b):
    return lax.dot_general(a, b, (((0,), (0,)), ((), ())), preferred_element_type=F32)


def ein(spec, a, b):
    return jnp.einsum(spec, a, b, preferred_element_type=F32)


MESH = pl.DeviceIdType.MESH
CHUNK = 16


class Peers:
    def __init__(self, R):
        self.R, self.A = R, R // 2
        self.me = lax.axis_index("rep")
        self.c = lax.rem(self.me, 2)
        self.a = lax.div(self.me, 2)
        self.partner = self.me + 1 - 2 * self.c

    def chip(self, k):
        return lax.rem(self.a + k, self.A)

    def same(self, k):
        return 2 * self.chip(k) + self.c

    def other(self, k):
        return 2 * self.chip(k) + 1 - self.c

    def meet(self):
        barrier = pltpu.get_barrier_semaphore()
        for dev in [self.partner] + [self.same(k) for k in range(1, self.A)]:
            pl.semaphore_signal(barrier, inc=1, device_id={"rep": dev}, device_id_type=MESH)
        pl.semaphore_wait(barrier, self.A)


def rows_of(index, T):
    return pl.ds(pl.multiple_of(index * T, T), T)


def chunk_rows(i, base=None):
    start = i * CHUNK if base is None else base + i * CHUNK
    return pl.ds(pl.multiple_of(start, CHUNK), CHUNK)


def remote(src, dst, send, recv, dev):
    return pltpu.make_async_remote_copy(
        src_ref=src,
        dst_ref=dst,
        send_sem=send,
        recv_sem=recv,
        device_id={"rep": dev},
        device_id_type=MESH,
    )


def scatter_sum(p, part, T, near, far, out, sems):
    near_s, near_r, far_s, far_r = sems
    order = list(range(1, p.A)) + [0]
    first = {
        k: remote(
            part.at[rows_of(p.other(k), T)], near.at[k], near_s.at[k], near_r.at[k], p.partner
        )
        for k in order
    }
    for k in order:
        first[k].start()
    second = []
    for k in range(1, p.A):
        first[k].wait_recv()
        base = p.same(k) * T

        def add(i, _, k=k, base=base):
            mine = part[chunk_rows(i, base), :].astype(F32)
            out[k - 1, chunk_rows(i), :] = (mine + near[k, chunk_rows(i), :].astype(F32)).astype(BF)
            return 0

        lax.fori_loop(0, T // CHUNK, add, 0)
        copy = remote(out.at[k - 1], far.at[k - 1], far_s.at[k - 1], far_r.at[k - 1], p.same(k))
        copy.start()
        second.append(copy)
    first[0].wait_recv()
    for copy in second:
        copy.wait_recv()

    def read(i):
        total = part[chunk_rows(i, p.me * T), :].astype(F32) + near[0, chunk_rows(i), :].astype(F32)
        for k in range(1, p.A):
            total = total + far[k - 1, chunk_rows(i), :].astype(F32)
        return total

    return read, list(first.values()) + second


def spread(p, src, full, T, sems):
    dir_s, dir_r, fwd_s, fwd_r = sems
    mine = full.at[rows_of(p.me, T)]
    direct = {}
    for k in list(range(1, p.A)) + [0]:
        dev = p.partner if k == 0 else p.same(k)
        direct[k] = remote(src, mine, dir_s.at[k], dir_r.at[k], dev)
        direct[k].start()
    passed = []
    for k in range(1, p.A):
        direct[k].wait_recv()
        block = full.at[rows_of(p.same(p.A - k), T)]
        copy = remote(block, block, fwd_s.at[k - 1], fwd_r.at[k - 1], p.partner)
        copy.start()
        passed.append(copy)
    direct[0].wait_recv()
    for copy in passed:
        copy.wait_recv()
    return list(direct.values()) + passed


def drain(copies):
    for copy in copies:
        copy.wait_send()


def run_kernel(kernel, cid, T, D, R, ins, outs, scatter, gather):
    A = R // 2
    few = max(A - 1, 1)
    scratch = []
    if scatter:
        scratch += [
            pltpu.VMEM((A, T, D), BF),
            pltpu.VMEM((few, T, D), BF),
            pltpu.VMEM((few, T, D), BF),
        ]
        scratch += [pltpu.SemaphoreType.DMA((n,)) for n in (A, A, few, few)]
    if gather:
        scratch += [pltpu.SemaphoreType.DMA((n,)) for n in (A, A, few, few)]
    vmem = pl.BlockSpec(memory_space=pltpu.VMEM)
    return pl.pallas_call(
        kernel,
        out_shape=[jax.ShapeDtypeStruct(*o) for o in outs],
        in_specs=[vmem] * len(ins),
        out_specs=[vmem] * len(outs),
        scratch_shapes=scratch,
        compiler_params=pltpu.CompilerParams(collective_id=cid, has_side_effects=True),
        cost_estimate=pl.CostEstimate(flops=0, bytes_accessed=24 << 20, transcendentals=0),
    )(*ins)


def gather_kernel(block, R, cid):
    T, D = block.shape

    def kernel(src, full, *sems):
        p = Peers(R)
        p.meet()

        def put(i, _):
            full[chunk_rows(i, p.me * T), :] = src[chunk_rows(i), :]
            return 0

        lax.fori_loop(0, T // CHUNK, put, 0)
        drain(spread(p, src, full, T, sems))

    return run_kernel(kernel, cid, T, D, R, [block], [((R * T, D), BF)], False, True)[0]


def norm_one_step(partial, x, bo, gone, sone):
    T, D = x.shape
    R = partial.shape[0] // T

    def kernel(part, xr, bor, gr, sr, normed_o, rstd_o, hidden_o, full, near, far, out, *sems):
        p = Peers(R)
        p.meet()
        read, sent = scatter_sum(p, part, T, near, far, out, sems[:4])

        def step(i, _):
            normed, rstd = norm_parts(xr[chunk_rows(i), :].astype(F32) + read(i) + bor[...])
            hidden = normed * gr[...] + sr[...]
            normed_o[chunk_rows(i), :] = normed
            rstd_o[chunk_rows(i), :] = rstd
            hidden_o[chunk_rows(i), :] = hidden
            full[chunk_rows(i, p.me * T), :] = hidden.astype(BF)
            return 0

        lax.fori_loop(0, T // CHUNK, step, 0)
        drain(sent + spread(p, full.at[rows_of(p.me, T)], full, T, sems[4:]))

    ins = [partial, x, bo[None], gone[None], sone[None]]
    outs = [((T, D), F32), ((T, 1), F32), ((T, D), F32), ((R * T, D), BF)]
    return run_kernel(kernel, 1, T, D, R, ins, outs, True, True)


def add_sums(ref, values):
    for n, v in enumerate(values):
        ref[n : n + 1, :] += jnp.sum(v, axis=0, keepdims=True)


def norm_two_step(partial, hidden, bd, gtwo, stwo, cot):
    T, D = hidden.shape
    R = partial.shape[0] // T

    def kernel(part, hr, br, gr, sr, cr, out_o, d_o, sums, full, near, far, out, *sems):
        p = Peers(R)
        p.meet()
        sums[...] = jnp.zeros_like(sums)
        read, sent = scatter_sum(p, part, T, near, far, out, sems[:4])

        def step(i, _):
            normed, rstd = norm_parts(hr[chunk_rows(i), :] + read(i) + br[...])
            out_o[chunk_rows(i), :] = (normed * gr[...] + sr[...]).astype(BF)
            dout = cr[chunk_rows(i), :].astype(F32)
            d_two = norm_back(dout * gr[...], normed, rstd)
            add_sums(sums, (d_two, dout * normed, dout))
            d_o[chunk_rows(i), :] = d_two
            full[chunk_rows(i, p.me * T), :] = d_two.astype(BF)
            return 0

        lax.fori_loop(0, T // CHUNK, step, 0)
        drain(sent + spread(p, full.at[rows_of(p.me, T)], full, T, sems[4:]))

    ins = [partial, hidden, bd[None], gtwo[None], stwo[None], cot]
    outs = [((T, D), BF), ((T, D), F32), ((8, D), F32), ((R * T, D), BF)]
    return run_kernel(kernel, 2, T, D, R, ins, outs, True, True)


def back_one_step(partial, d_two, normed, rstd, gone):
    T, D = d_two.shape
    R = partial.shape[0] // T

    def kernel(part, dr, nr, rr, gr, d_o, sums, full, near, far, out, *sems):
        p = Peers(R)
        p.meet()
        sums[...] = jnp.zeros_like(sums)
        read, sent = scatter_sum(p, part, T, near, far, out, sems[:4])

        def step(i, _):
            d_hidden = dr[chunk_rows(i), :] + read(i)
            normed = nr[chunk_rows(i), :]
            d_one = norm_back(d_hidden * gr[...], normed, rr[chunk_rows(i), :])
            add_sums(sums, (d_one, d_hidden * normed, d_hidden))
            d_o[chunk_rows(i), :] = d_one
            full[chunk_rows(i, p.me * T), :] = d_one.astype(BF)
            return 0

        lax.fori_loop(0, T // CHUNK, step, 0)
        drain(sent + spread(p, full.at[rows_of(p.me, T)], full, T, sems[4:]))

    ins = [partial, d_two, normed, rstd, gone[None]]
    outs = [((T, D), F32), ((8, D), F32), ((R * T, D), BF)]
    return run_kernel(kernel, 3, T, D, R, ins, outs, True, True)


def input_step(partial, d_one):
    T, D = d_one.shape
    R = partial.shape[0] // T

    def kernel(part, dr, grad, near, far, out, *sems):
        p = Peers(R)
        p.meet()
        read, sent = scatter_sum(p, part, T, near, far, out, sems)

        def step(i, _):
            grad[chunk_rows(i), :] = (dr[chunk_rows(i), :] + read(i)).astype(BF)
            return 0

        lax.fori_loop(0, T // CHUNK, step, 0)
        drain(sent)

    return run_kernel(kernel, 4, T, D, R, [partial, d_one], [((T, D), BF)], True, False)[0]


def body(
    block_input,
    out_cotangent,
    w_query,
    w_key,
    w_value,
    w_output,
    bias_query,
    bias_value,
    bias_output,
    gain_first,
    shift_first,
    w_inner,
    bias_inner,
    w_down,
    bias_down,
    gain_second,
    shift_second,
):
    S = lax.axis_size("shard")
    R = lax.axis_size("rep")
    r = lax.axis_index("rep")
    T = block_input.shape[0]
    D = w_query.shape[1]
    ds = w_query.shape[0]
    dr = D // R
    fs = w_down.shape[0]
    fr = fs // R
    W = 4 * dr

    def cols(w):
        return lax.dynamic_slice(w, (0, r * dr), (ds, dr))

    small = jnp.concatenate(
        [
            v.astype(BF)
            for v in (
                bias_query,
                bias_value,
                bias_output,
                gain_first,
                shift_first,
                bias_down,
                gain_second,
                shift_second,
                bias_inner,
            )
        ]
    )
    n_small = small.shape[0]
    small = jnp.pad(small, (0, PAD * W - n_small)).reshape(PAD, W)
    pack = jnp.concatenate(
        [jnp.concatenate([cols(w_query), cols(w_key), cols(w_value), cols(w_output)], 1), small], 0
    )
    got = lax.all_gather(pack, "shard", axis=0)
    x_all = gather_kernel(block_input, R, 0)
    wi_r = lax.dynamic_index_in_dim(w_inner.reshape(ds, S, R, fr), r, 2, keepdims=False)
    V = S * fr
    dv = fr * D // V
    wd_r = lax.dynamic_slice(w_down, (r * fr, 0), (fr, D)).reshape(dv, V)
    mlp = lax.all_gather(jnp.concatenate([wi_r.reshape(ds, V), wd_r], 0), "shard", axis=0)
    wi = mlp[:, :ds].reshape(D, V)
    wd = mlp[:, ds:].reshape(V, D)
    wqkv = got[:, :ds, : 3 * dr].reshape(D, 3 * dr)
    wo = lax.all_to_all(
        got[:, :ds, 3 * dr :].reshape(D, dr), "rep", split_axis=0, concat_axis=1, tiled=True
    )
    flat = got[:, ds:, :].reshape(S, PAD * W)[:, :n_small].astype(F32)
    bq, bv, bo, gone, sone, bd, gtwo, stwo = (
        flat[:, i * ds : (i + 1) * ds].reshape(D) for i in range(8)
    )
    bi = lax.dynamic_index_in_dim(flat[:, 8 * ds :].reshape(S, R, fr), r, 1, keepdims=False)
    bi = bi.reshape(S * fr)
    bq = lax.dynamic_slice(bq, (r * dr,), (dr,))
    bv = lax.dynamic_slice(bv, (r * dr,), (dr,))

    N = R * T
    shape4 = (N // SEQ, SEQ, dr // HEAD_DIM, HEAD_DIM)
    qkv = mm(x_all, wqkv)
    query = (qkv[:, :dr] + bq).astype(BF).reshape(shape4)
    keyed = qkv[:, dr : 2 * dr].astype(BF).reshape(shape4)
    valued = (qkv[:, 2 * dr :] + bv).astype(BF).reshape(shape4)
    scores = ein("bqhe,bkhe->bhqk", query, keyed) * 0.125
    top = jnp.max(scores, axis=-1, keepdims=True)
    logsum = top + jnp.log(jnp.sum(jnp.exp(scores - top), axis=-1, keepdims=True))
    probs = jnp.exp(scores - logsum)
    probs_b = probs.astype(BF)
    context = ein("bhqk,bkhe->bqhe", probs_b, valued).astype(BF).reshape(N, dr)
    attn_part = mm(context, wo).astype(BF)

    normed_one, rstd_one, hidden, hidden_all = norm_one_step(attn_part, block_input, bo, gone, sone)
    inner = mm(hidden_all, wi) + bi
    phi = 0.5 * (1.0 + lax.erf(inner * INV_ROOT_TWO))
    acted = (inner * phi).astype(BF)
    slope = phi + inner * jnp.exp(-0.5 * inner * inner) * INV_ROOT_TWO_PI
    down_part = mm(acted, wd).astype(BF)

    output, d_two, sums_two, d_two_all = norm_two_step(
        down_part, hidden, bd, gtwo, stwo, out_cotangent
    )
    d_inner = mm_nt(d_two_all, wd) * slope
    g_bias_inner = jnp.sum(d_inner, axis=0)
    d_inner_b = d_inner.astype(BF)
    hid_part = mm_nt(d_inner_b, wi).astype(BF)
    g_wd = mm_tn(acted, d_two_all).astype(BF).reshape(S, dv, V)
    g_wi = mm_tn(hidden_all, d_inner_b).astype(BF).reshape(S, ds, V)
    g_mlp = lax.psum_scatter(
        jnp.concatenate([g_wi, g_wd], 1), "shard", scatter_dimension=0, tiled=True
    )[0]

    d_one, sums_one, d_one_all = back_one_step(hid_part, d_two, normed_one, rstd_one, gone)
    g_wo = mm_tn(context, d_one_all).astype(BF)
    g_wo = lax.all_to_all(g_wo, "rep", split_axis=1, concat_axis=0, tiled=True)
    d_context = mm_nt(d_one_all, wo).astype(BF).reshape(shape4)
    d_probs = ein("bqhe,bkhe->bhqk", d_context, valued)
    delta = jnp.sum(probs * d_probs, axis=-1, keepdims=True)
    d_scores = (probs * (d_probs - delta) * 0.125).astype(BF)
    d_query = ein("bhqk,bkhe->bqhe", d_scores, keyed).reshape(N, dr)
    d_keyed = ein("bhqk,bqhe->bkhe", d_scores, query).reshape(N, dr)
    d_valued = ein("bhqk,bqhe->bkhe", probs_b, d_context).reshape(N, dr)
    g_bias_query = jnp.sum(d_query, axis=0)
    g_bias_value = jnp.sum(d_valued, axis=0)
    d_qkv = jnp.concatenate([d_query.astype(BF), d_keyed.astype(BF), d_valued.astype(BF)], 1)
    in_part = mm_nt(d_qkv, wqkv).astype(BF)

    def placed(v):
        return lax.dynamic_update_slice(jnp.zeros((D,), F32), v, (r * dr,)).reshape(S, ds)

    g_small = jnp.concatenate(
        [
            placed(g_bias_query),
            placed(g_bias_value),
            sums_one[0].reshape(S, ds),
            sums_one[1].reshape(S, ds),
            sums_one[2].reshape(S, ds),
            sums_two[0].reshape(S, ds),
            sums_two[1].reshape(S, ds),
            sums_two[2].reshape(S, ds),
            g_bias_inner.reshape(S, fr),
        ],
        1,
    ).astype(BF)
    n_g = g_small.shape[1]
    g_small = jnp.pad(g_small, ((0, 0), (0, PAD * W - n_g))).reshape(S, PAD, W)
    g_pack = jnp.concatenate([mm_tn(x_all, d_qkv).astype(BF), g_wo], 1).reshape(S, ds, W)
    g_pack = jnp.concatenate([g_pack, g_small], 1)
    g_pack = lax.psum_scatter(g_pack, "shard", scatter_dimension=0, tiled=True)[0]

    grad_input = input_step(in_part, d_one)

    mlps = gather_kernel(g_mlp, R, 5).reshape(R, ds + dv, V).astype(F32)
    wd_out = mlps[:, ds:].reshape(R * fr, D)
    wi_out = mlps[:, :ds].reshape(R, ds, S, fr).transpose(1, 2, 0, 3).reshape(ds, S * R * fr)
    packs = gather_kernel(g_pack, R, 6).reshape(R, ds + PAD, W).astype(F32)
    main = packs[:, :ds].reshape(R, ds, 4, dr).transpose(2, 1, 0, 3).reshape(4, ds, D)
    tail = packs[:, ds:].reshape(R, PAD * W)
    summed = jnp.sum(tail[:, : 8 * ds], axis=0)
    gbq, gbv, gbo, ggone, gsone, gbd, ggtwo, gstwo = (
        summed[i * ds : (i + 1) * ds] for i in range(8)
    )
    gbi = tail[:, 8 * ds : n_g].reshape(fs)
    return (
        output,
        grad_input,
        main[0],
        main[1],
        main[2],
        main[3],
        gbq,
        gbv,
        gbo,
        ggone,
        gsone,
        wi_out,
        gbi,
        wd_out,
        gbd,
        ggtwo,
        gstwo,
    )

VMEM_SPEC = pl.BlockSpec(memory_space=pltpu.VMEM)
ANY_SPEC = pl.BlockSpec(memory_space=pl.ANY)
LIMIT = 56 << 20
NVEC = 16


def dma_sems(*counts):
    return [pltpu.SemaphoreType.DMA((n,)) for n in counts]


class Place(Peers):
    def __init__(self, S, R):
        super().__init__(R)
        self.S, self.Z = S, S // 2
        self.s = lax.axis_index("shard")
        self.z = lax.div(self.s, 2)
        self.y = lax.rem(self.s, 2)
        self.across = self.s + 1 - 2 * self.y

    def up(self, k):
        return 2 * lax.rem(self.z + k, self.Z) + self.y

    def down(self, k):
        return 2 * lax.rem(self.z + self.Z - k, self.Z) + self.y

    def flip(self, s):
        return s + 1 - 2 * self.y

    def meet_all(self):
        barrier = pltpu.get_barrier_semaphore()
        for dev in [self.partner] + [self.same(k) for k in range(1, self.A)]:
            pl.semaphore_signal(barrier, inc=1, device_id={"rep": dev}, device_id_type=MESH)
        for dev in [self.across] + [self.up(k) for k in range(1, self.Z)]:
            pl.semaphore_signal(barrier, inc=1, device_id={"shard": dev}, device_id_type=MESH)
        pl.semaphore_wait(barrier, self.A + self.Z)


def to_shard(src, dst, send, recv, dev):
    return pltpu.make_async_remote_copy(
        src_ref=src,
        dst_ref=dst,
        send_sem=send,
        recv_sem=recv,
        device_id={"shard": dev},
        device_id_type=MESH,
    )


class LineGather:
    def __init__(self, p, full, T, row, sems, cols=None):
        self.p, self.full, self.T, self.row, self.cols = p, full, T, row, cols
        a_s, a_r, b_s, b_r, f_s, f_r = sems
        half = lax.div(p.z, 2)
        self.inner = p.z == 1 + half
        self.outer = jnp.logical_not(self.inner)
        beside = 4 * half + 1 - p.z
        turn = jnp.where(self.inner, 1, 0)
        self.zs = [beside, 3 - 3 * half, 2 - half]
        self.near = self.copy(p.z, a_s.at[0], a_r.at[0], beside)
        self.over = self.copy(p.z, b_s.at[0], b_r.at[turn], 2 - half)
        self.on = [self.copy(self.zs[j + 1], f_s.at[j], b_r.at[j], beside) for j in range(2)]

    @staticmethod
    def sems():
        return dma_sems(1, 1, 1, 2, 2, 1)

    def block(self, z):
        rows = rows_of(2 * z + self.row, self.T)
        return self.full.at[rows] if self.cols is None else self.full.at[rows, self.cols]

    def copy(self, z, send, recv, to):
        return to_shard(self.block(z), self.block(z), send, recv, 2 * to + self.p.y)

    def start(self):
        self.near.start()
        self.over.start()

    def push(self, then=(None, None, None)):
        self.near.wait_recv()
        if then[0] is not None:
            then[0].start()

        @pl.when(self.inner)
        def _():
            for j in range(2):
                self.on[j].wait_recv()
                self.on[j].start()
                if then[j + 1] is not None:
                    then[j + 1].start()

    def pull(self, then=(None, None, None)):
        @pl.when(self.outer)
        def _():
            for j in range(2):
                self.on[j].wait_recv()
                if then[j + 1] is not None:
                    then[j + 1].start()

    def drain(self):
        self.near.wait_send()
        self.over.wait_send()

        @pl.when(self.inner)
        def _():
            for copy in self.on:
                copy.wait_send()


class RowGather:
    def __init__(self, p, full, T, sems, cols=None):
        self.line = LineGather(p, full, T, p.y, sems[:6], cols)
        ys, yr = sems[6:]
        self.side = []
        for i, z in enumerate([p.z] + self.line.zs):
            block = self.line.block(z)
            self.side.append(to_shard(block, block, ys.at[i], yr.at[i], p.across))

    @staticmethod
    def sems(Z):
        return LineGather.sems() + dma_sems(Z, Z)

    def start(self):
        self.line.start()
        self.side[0].start()

    def push(self):
        self.line.push(self.side[1:])

    def pull(self):
        self.line.pull(self.side[1:])

    def finish(self):
        for copy in self.side:
            copy.wait_recv()

    def drain(self):
        self.line.drain()
        drain(self.side)


class SideGather:
    def __init__(self, p, full, T, sems, cols=None):
        self.lines = [
            LineGather(p, full, T, row, sems[6 * i : 6 * i + 6], cols)
            for i, row in enumerate((p.y, 1 - p.y))
        ]
        block = self.lines[0].block(p.z)
        self.side = to_shard(block, block, sems[12].at[0], sems[13].at[0], p.across)

    @staticmethod
    def sems(Z):
        return LineGather.sems() * 2 + dma_sems(1, 1)

    def begin(self):
        self.side.start()

    def start(self):
        self.lines[0].start()
        self.side.wait_recv()
        self.lines[1].start()

    def push(self):
        for line in self.lines:
            line.push()

    def pull(self):
        for line in self.lines:
            line.pull()

    def finish(self):
        pass

    def drain(self):
        for line in self.lines:
            line.drain()
        self.side.wait_send()


class PlaneGather:
    def __init__(self, p, full, T, sems):
        self.p = p
        self.zs, self.zr, self.ys, self.yr = sems
        rows = full.at[rows_of(p.y, T)]
        self.far = {
            k: to_shard(rows, rows, self.zs.at[k - 1], self.zr.at[0], p.up(k))
            for k in range(1, p.Z)
        }
        self.near = to_shard(rows, rows, self.ys.at[0], self.yr.at[0], p.across)
        self.mine = p.z == p.me

    @staticmethod
    def sems(Z):
        return dma_sems(Z - 1, 1, 1, 1)

    def start(self):
        @pl.when(self.mine)
        def _():
            for k in range(1, self.p.Z):
                self.far[k].start()
            self.near.start()

    def forward(self):
        @pl.when(jnp.logical_not(self.mine))
        def _():
            self.far[1].wait_recv()
            self.near.start()

    def finish(self):
        self.near.wait_recv()

    def drain(self):
        @pl.when(self.mine)
        def _():
            for k in range(1, self.p.Z):
                self.far[k].wait_send()

        self.near.wait_send()


class LineScatter:
    def __init__(self, p, part, T, row, bufs, sems, cols, close=None):
        self.p, self.part, self.T, self.row, self.cols = p, part, T, row, cols
        self.out, self.ain, self.bin, self.fin = bufs
        self.close = close
        a_s, a_r, f_s, f_r, b_s, b_r = sems
        half = lax.div(p.z, 2)
        self.inner = p.z == 1 + half
        self.outer = jnp.logical_not(self.inner)
        beside = 4 * half + 1 - p.z
        self.zs = [beside, 3 - 3 * half, 2 - half, p.z]

        def to(z, src, dst, send, recv):
            return to_shard(src, dst, send, recv, 2 * z + p.y)

        src = [self.block(z) if close is None else self.out.at[j] for j, z in enumerate(self.zs[:3])]
        self.near = to(beside, src[0], self.ain, a_s.at[0], a_r.at[0])
        self.up = [
            to(beside, src[j + 1], self.fin.at[j], f_s.at[j], f_r.at[j]) for j in range(2)
        ]
        self.over = [
            to(self.zs[j + 1], self.out.at[j + 1], self.bin, b_s.at[j], b_r.at[0])
            for j in range(2)
        ]

    @staticmethod
    def bufs(T, C, dtype):
        return [pltpu.VMEM(n + (T, C), dtype) for n in ((3,), (), (), (2,))]

    @staticmethod
    def sems():
        return dma_sems(1, 1, 2, 2, 2, 1)

    def block(self, z):
        return self.part.at[rows_of(2 * z + self.row, self.T), self.cols]

    def terms(self, j, i):
        base = (2 * self.zs[j] + self.row) * self.T
        total = self.part[chunk_rows(i, base), self.cols].astype(F32)
        if self.close is not None:
            total = total + self.close[j, chunk_rows(i), :].astype(F32)
        return total

    def each(self, put):
        def step(i, _):
            put(i)
            return 0

        lax.fori_loop(0, self.T // CHUNK, step, 0)

    def lift(self, j):
        if self.close is not None:

            def put(i):
                self.out[j, chunk_rows(i), :] = self.terms(j, i).astype(self.out.dtype)

            self.each(put)
        if j == 0:
            self.near.start()
        else:
            self.up[j - 1].start()

    def relay(self, j):
        self.up[j - 1].wait_recv()

        def put(i):
            total = self.terms(j, i) + self.fin[j - 1, chunk_rows(i), :].astype(F32)
            self.out[j, chunk_rows(i), :] = total.astype(self.out.dtype)

        self.each(put)
        self.over[j - 1].start()

    def wait(self):
        self.near.wait_recv()
        self.over[0].wait_recv()

    def read(self, i):
        total = self.terms(3, i) + self.ain[chunk_rows(i), :].astype(F32)
        return total + self.bin[chunk_rows(i), :].astype(F32)

    def drain(self):
        self.near.wait_send()

        @pl.when(self.outer)
        def _():
            drain(self.up)

        @pl.when(self.inner)
        def _():
            drain(self.over)


class RowScatter:
    def __init__(self, p, part, T, bufs, sems, cols=None):
        self.p, self.T = p, T
        self.cols = pl.ds(0, part.shape[1]) if cols is None else cols
        close = bufs[4]
        self.line = LineScatter(p, part, T, p.y, bufs[:4], sems[:6], self.cols, close)
        ys, yr = sems[6:]
        self.side = [
            to_shard(
                part.at[rows_of(2 * z + 1 - p.y, T), self.cols],
                close.at[j],
                ys.at[j],
                yr.at[j],
                p.across,
            )
            for j, z in enumerate(self.line.zs)
        ]

    @staticmethod
    def bufs(T, C, dtype):
        return LineScatter.bufs(T, C, dtype) + [pltpu.VMEM((4, T, C), dtype)]

    @staticmethod
    def sems():
        return LineScatter.sems() + dma_sems(4, 4)

    def launch(self, j):
        self.side[j].start()

    def start(self):
        for j in (1, 2, 0, 3):
            self.launch(j)

    def lift(self, j):
        if j == 0:
            self.side[0].wait_recv()
            self.line.lift(0)
        else:

            @pl.when(self.line.outer)
            def _():
                self.side[j].wait_recv()
                self.line.lift(j)

    def relay(self, j):
        @pl.when(self.line.inner)
        def _():
            self.side[j].wait_recv()
            self.line.relay(j)

    def total(self, dst):
        self.side[3].wait_recv()
        self.line.wait()

        def put(i):
            dst[self.p.me, chunk_rows(i), self.cols] = self.line.read(i).astype(dst.dtype)

        self.line.each(put)

    def drain(self):
        self.line.drain()
        drain(self.side)


class SideScatter:
    def __init__(self, p, part, T, bufs, sems, cols):
        self.p, self.cols = p, cols
        self.lines = [
            LineScatter(p, part, T, row, bufs[4 * i : 4 * i + 4], sems[6 * i : 6 * i + 6], cols)
            for i, row in enumerate((1 - p.y, p.y))
        ]
        self.sent, self.got = bufs[8:]
        self.side = to_shard(self.sent, self.got, sems[12].at[0], sems[13].at[0], p.across)

    @staticmethod
    def bufs(T, C, dtype):
        return LineScatter.bufs(T, C, dtype) * 2 + [pltpu.VMEM((T, C), dtype)] * 2

    @staticmethod
    def sems():
        return LineScatter.sems() * 2 + dma_sems(1, 1)

    def launch(self, j):
        if j == 0:
            for line in self.lines:
                line.lift(0)
        elif j < 3:

            @pl.when(self.lines[0].outer)
            def _():
                for line in self.lines:
                    line.lift(j)

    def relay(self, j):
        @pl.when(self.lines[0].inner)
        def _():
            for line in self.lines:
                line.relay(j)

    def cross(self):
        line = self.lines[0]
        line.wait()

        def put(i):
            self.sent[chunk_rows(i), :] = line.read(i).astype(self.sent.dtype)

        line.each(put)
        self.side.start()

    def total(self, dst):
        line = self.lines[1]
        line.wait()
        self.side.wait_recv()

        def put(i):
            total = line.read(i) + self.got[chunk_rows(i), :].astype(F32)
            dst[self.p.me, chunk_rows(i), self.cols] = total.astype(dst.dtype)

        line.each(put)

    def drain(self):
        for line in self.lines:
            line.drain()
        self.side.wait_send()


class PlaneScatter:
    def __init__(self, p, part, T, bufs, sems):
        self.p, self.part, self.T = p, part, T
        self.close, self.out, self.far = bufs
        ys, yr, zs, zr = sems
        self.first = to_shard(
            part.at[rows_of(1 - p.y, T)], self.close, ys.at[0], yr.at[0], p.across
        )
        self.mine = p.z == p.me
        self.hop = lax.rem(p.z + p.Z - p.me, p.Z)
        self.sends = to_shard(
            self.out,
            self.far.at[jnp.maximum(self.hop - 1, 0)],
            zs.at[0],
            zr.at[jnp.maximum(self.hop - 1, 0)],
            2 * p.me + p.y,
        )
        self.gets = [
            to_shard(self.out, self.far.at[k], zs.at[0], zr.at[k], p.up(k + 1))
            for k in range(p.Z - 1)
        ]

    @staticmethod
    def bufs(Z, T, C, dtype):
        return [pltpu.VMEM((T, C), dtype), pltpu.VMEM((T, C), dtype), pltpu.VMEM((Z - 1, T, C), dtype)]

    @staticmethod
    def sems(Z):
        return dma_sems(1, 1, 1, Z - 1)

    def start(self):
        self.first.start()

    def pass_on(self):
        self.first.wait_recv()

        def add(i, _):
            mine = self.part[chunk_rows(i, self.p.y * self.T), :].astype(F32)
            self.out[chunk_rows(i), :] = (mine + self.close[chunk_rows(i), :].astype(F32)).astype(BF)
            return 0

        lax.fori_loop(0, self.T // CHUNK, add, 0)

        @pl.when(jnp.logical_not(self.mine))
        def _():
            self.sends.start()

    def total(self, dst):
        @pl.when(self.mine)
        def _():
            for copy in self.gets:
                copy.wait_recv()

            def add(i, _):
                total = self.part[chunk_rows(i, self.p.y * self.T), :].astype(F32)
                total = total + self.close[chunk_rows(i), :].astype(F32)
                for k in range(self.p.Z - 1):
                    total = total + self.far[k, chunk_rows(i), :].astype(F32)
                dst[chunk_rows(i), :] = total.astype(BF)
                return 0

            lax.fori_loop(0, self.T // CHUNK, add, 0)

    def drain(self):
        self.first.wait_send()

        @pl.when(jnp.logical_not(self.mine))
        def _():
            self.sends.wait_send()


class RepSpread:
    def __init__(self, p, full, sems):
        self.p = p
        dir_s, dir_r, fwd_s, fwd_r = sems
        own = full.at[p.me]
        self.direct = {0: remote(own, own, dir_s.at[0], dir_r.at[0], p.partner)}
        self.passed = {}
        for k in range(1, p.A):
            self.direct[k] = remote(own, own, dir_s.at[k], dir_r.at[k], p.same(k))
            block = full.at[p.same(p.A - k)]
            self.passed[k] = remote(block, block, fwd_s.at[k - 1], fwd_r.at[k - 1], p.partner)

    @staticmethod
    def sems(A):
        return dma_sems(A, A, A - 1, A - 1)

    def start(self):
        for k in list(range(1, self.p.A)) + [0]:
            self.direct[k].start()

    def forward(self):
        for k in range(1, self.p.A):
            self.direct[k].wait_recv()
            self.passed[k].start()

    def finish(self):
        self.direct[0].wait_recv()
        for copy in self.passed.values():
            copy.wait_recv()

    def drain(self):
        drain(list(self.direct.values()) + list(self.passed.values()))


class OwnerSpread:
    def __init__(self, p, block, sems):
        self.p = p
        s0, s1, rx, rp = sems
        self.across = remote(block, block, s0.at[0], rx.at[0], p.same(1))
        self.beside = remote(block, block, s1.at[0], rp.at[0], p.partner)
        self.mine = p.z == p.me
        self.relay = p.z == p.same(1)
        self.other = jnp.logical_not(jnp.logical_or(self.mine, self.relay))

    @staticmethod
    def sems():
        return dma_sems(1, 1, 1, 1)

    def start(self):
        @pl.when(self.mine)
        def _():
            self.across.start()
            self.beside.start()

    def forward(self):
        @pl.when(self.relay)
        def _():
            self.across.wait_recv()
            self.beside.start()

    def finish(self):
        @pl.when(self.other)
        def _():
            self.beside.wait_recv()

    def drain(self):
        @pl.when(self.mine)
        def _():
            self.across.wait_send()

        @pl.when(jnp.logical_not(self.other))
        def _():
            self.beside.wait_send()

class RepScatter:
    def __init__(self, p, part, T, bufs, sems):
        self.p, self.part, self.T = p, part, T
        self.near, self.out, self.far = bufs
        near_s, near_r, far_s, far_r = sems
        self.first = {
            k: remote(
                part.at[rows_of(p.other(k), T)],
                self.near.at[k],
                near_s.at[k],
                near_r.at[k],
                p.partner,
            )
            for k in range(p.A)
        }
        self.second = {
            k: remote(
                self.out.at[k - 1], self.far.at[k - 1], far_s.at[k - 1], far_r.at[k - 1], p.same(k)
            )
            for k in range(1, p.A)
        }

    @staticmethod
    def bufs(A, T, D):
        return [pltpu.VMEM((n, T, D), BF) for n in (A, A - 1, A - 1)]

    @staticmethod
    def sems(A):
        return dma_sems(A, A, A - 1, A - 1)

    def start_far(self):
        for k in range(1, self.p.A):
            self.first[k].start()

    def start_near(self):
        self.first[0].start()

    def pass_on(self):
        for k in range(1, self.p.A):
            self.first[k].wait_recv()
            base = self.p.same(k) * self.T

            def add(i, _, k=k, base=base):
                mine = self.part[step_rows(i, base), :].astype(F32)
                near = self.near[k, step_rows(i), :].astype(F32)
                self.out[k - 1, step_rows(i), :] = (mine + near).astype(BF)
                return 0

            lax.fori_loop(0, self.T // STEP, add, 0)
            self.second[k].start()

    def finish(self):
        self.first[0].wait_recv()
        for copy in self.second.values():
            copy.wait_recv()

    def read(self, i):
        total = self.part[step_rows(i, self.p.me * self.T), :].astype(F32)
        total = total + self.near[0, step_rows(i), :].astype(F32)
        for k in range(1, self.p.A):
            total = total + self.far[k - 1, step_rows(i), :].astype(F32)
        return total

    def drain(self):
        drain(list(self.first.values()) + list(self.second.values()))


STEP = 32


def step_rows(i, base=None):
    start = i * STEP if base is None else base + i * STEP
    return pl.ds(pl.multiple_of(start, STEP), STEP)


class TokenSpread:
    def __init__(self, p, full, T, sems):
        self.p = p
        dir_s, dir_r, fwd_s, fwd_r = sems
        own = full.at[rows_of(p.me, T)]
        self.direct = {0: remote(own, own, dir_s.at[0], dir_r.at[0], p.partner)}
        self.passed = {}
        for k in range(1, p.A):
            self.direct[k] = remote(own, own, dir_s.at[k], dir_r.at[k], p.same(k))
            block = full.at[rows_of(p.same(p.A - k), T)]
            self.passed[k] = remote(block, block, fwd_s.at[k - 1], fwd_r.at[k - 1], p.partner)

    @staticmethod
    def sems(A):
        return dma_sems(A, A, A - 1, A - 1)

    def start(self):
        for k in list(range(1, self.p.A)) + [0]:
            self.direct[k].start()

    def beside(self):
        self.direct[0].wait_recv()

    def across(self):
        for k in range(1, self.p.A):
            self.direct[k].wait_recv()
            self.passed[k].start()
        for copy in self.passed.values():
            copy.wait_recv()

    def drain(self):
        drain(list(self.direct.values()) + list(self.passed.values()))


class Bag:
    def __init__(self):
        self.names, self.specs = [], []

    def want(self, name, specs):
        specs = specs if isinstance(specs, list) else [specs]
        self.names.append((name, len(specs)))
        self.specs += specs

    def hand_out(self, refs):
        got, at = {}, 0
        for name, n in self.names:
            got[name] = refs[at] if n == 1 else list(refs[at : at + n])
            at += n
        return got


def fold(v):
    return jnp.sum(v.reshape(v.shape[0] // 8, 8, v.shape[1]), axis=0)


TILE = 256
QUARTERS = 4


def tiles(n, body):
    def step(i, _):
        body(pl.ds(pl.multiple_of(i * TILE, TILE), TILE))
        return 0

    lax.fori_loop(0, n // TILE, step, 0)


def layer(x, cot, wq, wk, wv, wo, wi, wd, vectors, S, R):
    T, D = x.shape
    ds, fs = wq.shape[0], wd.shape[0]
    dr, fr = D // R, fs // R
    V = S * fr
    W = 3 * dr
    Z, A = S // 2, R // 2
    nv = len(vectors)
    N = R * T
    C = N // A
    pairs = dr // 128
    half = V // 2
    wide = D // QUARTERS

    bag = Bag()
    bag.want("here", pltpu.SemaphoreType.DMA((S + 6,)))
    bag.want("small", pltpu.VMEM((S * NVEC, ds), F32))
    bag.want("flat", pltpu.VMEM((NVEC, D), F32))
    for name, shape, t in (
        ("x_all", (N, D), BF),
        ("wqkv", (D, W), BF),
        ("wor", (dr, D), BF),
        ("wir", (D, V), BF),
        ("wdr", (V, D), BF),
        ("qkv", (N, W), BF),
        ("probs", (N * dr // HEAD_DIM, SEQ), F32),
        ("ctx", (N, dr), BF),
        ("part", (N, D), BF),
        ("normed", (T, D), F32),
        ("rstd", (T, 128), F32),
        ("hidden", (T, D), F32),
        ("hid_all", (N, D), BF),
        ("acted", (N, V), BF),
        ("slope", (N, V), F32),
        ("d_two", (T, D), F32),
        ("d2_all", (N, D), BF),
        ("d_in", (N, V), BF),
        ("d_one", (T, D), F32),
        ("d1_all", (N, D), BF),
        ("dctx", (N, dr), BF),
        ("dqkv", (N, W), BF),
        ("sums", (48, D), F32),
        ("gbi8", (8, V), F32),
        ("gqv8", (8, 2 * dr), F32),
        ("gflat", (NVEC, D), F32),
        ("gs", (S * NVEC, ds), F32),
        ("gwd", (V, D), BF),
        ("gwi", (D, V), BF),
        ("gqkv", (D, W), BF),
        ("gwo", (dr, D), BF),
    ):
        bag.want(name, pltpu.VMEM(shape, t))
    for name in ("smalls", "g_qkv", "g_wia", "g_wib", "g_wd0", "g_wd1"):
        bag.want(name, RowGather.sems(Z))
    bag.want("g_wd2", SideGather.sems(Z))
    bag.want("g_wo", PlaneGather.sems(Z))
    for name in ("ax", "a1", "a2", "a3"):
        bag.want(name, TokenSpread.sems(A))
    for name in ("t1", "t2", "t3", "t4"):
        bag.want(name + "b", RepScatter.bufs(A, T, D))
        bag.want(name + "s", RepScatter.sems(A))
    for name, n, c, t in (
        ("rwd", fr, D // 2, BF),
        ("rwi", ds, V, BF),
        ("rqkv", ds, W, BF),
        ("rsm", NVEC, ds, F32),
    ):
        bag.want(name + "b", RowScatter.bufs(n, c, t))
        bag.want(name + "s", RowScatter.sems())
        bag.want(name + "p", RepSpread.sems(A))
    bag.want("rwxb", SideScatter.bufs(fr, D // 2, BF))
    bag.want("rwxs", SideScatter.sems())
    bag.want("rwob", PlaneScatter.bufs(Z, ds, D, BF))
    bag.want("rwos", PlaneScatter.sems(Z))
    bag.want("rwop", OwnerSpread.sems())

    def kernel(*refs):
        x, cot, wq, wk, wv, wo, wi, wd = refs[:8]
        vecs = refs[8 : 8 + nv]
        at = 8 + nv
        out_o, gin_o, tq, ti, td, to, ts = refs[at : at + 7]
        b = bag.hand_out(refs[at + 7 :])
        x_all, wqkv, wor, wir, wdr = b["x_all"], b["wqkv"], b["wor"], b["wir"], b["wdr"]
        qkv, probs, ctx, part = b["qkv"], b["probs"], b["ctx"], b["part"]
        flat, small, here = b["flat"], b["small"], b["here"]
        normed_r, rstd_r, hidden_r = b["normed"], b["rstd"], b["hidden"]
        hid_all, acted, slope, d_two_r, d2_all = (
            b["hid_all"],
            b["acted"],
            b["slope"],
            b["d_two"],
            b["d2_all"],
        )
        d_in, d_one_r, d1_all, dctx, dqkv = b["d_in"], b["d_one"], b["d1_all"], b["dctx"], b["dqkv"]
        sums, gbi8, gqv8, gflat, gs = b["sums"], b["gbi8"], b["gqv8"], b["gflat"], b["gs"]
        gwd, gwi, gqkv, gwo = b["gwd"], b["gwi"], b["gqkv"], b["gwo"]

        p = Place(S, R)
        mine = rows_of(p.s, ds)
        own_tok = rows_of(p.me, T)
        own_chip = rows_of(p.a, C)
        far_chip = rows_of(p.chip(1), C)
        cols = pl.ds(pl.multiple_of(p.me * dr, dr), dr)
        local = []

        def bring(src, dst):
            copy = pltpu.make_async_copy(src, dst, here.at[len(local)])
            copy.start()
            local.append(copy)

        for i, w in enumerate((wq, wk, wv)):
            bring(w.at[:, cols], wqkv.at[mine, pl.ds(i * dr, dr)])
        for c in range(S):
            piece = pl.ds(pl.multiple_of(c * fs + p.me * fr, fr), fr)
            bring(wi.at[:, piece], wir.at[mine, pl.ds(c * fr, fr)])
        bring(wd.at[rows_of(p.me, fr)], wdr.at[mine])
        own_wo = pltpu.make_async_copy(wo, wor.at[rows_of(p.y, ds)], here.at[len(local)])

        @pl.when(p.z == p.me)
        def _():
            own_wo.start()

        piece = pl.ds(pl.multiple_of(p.me * fr, fr), fr)
        pieces = [v[...] for v in vecs[:-1]] + [vecs[-1][:, piece]]
        pieces.append(jnp.zeros((NVEC - nv, ds), F32))
        small[rows_of(p.s, NVEC), :] = jnp.concatenate(pieces, 0)
        x_all[own_tok, :] = x[...]
        p.meet_all()

        smalls = RowGather(p, small, NVEC, b["smalls"])
        g_qkv = RowGather(p, wqkv, ds, b["g_qkv"])
        left, right = pl.ds(0, half), pl.ds(half, half)
        g_wia = RowGather(p, wir, ds, b["g_wia"], left)
        g_wib = RowGather(p, wir, ds, b["g_wib"], right)
        g_wd0 = RowGather(p, wdr, fr, b["g_wd0"], pl.ds(0, wide))
        g_wd1 = RowGather(p, wdr, fr, b["g_wd1"], pl.ds(wide, wide))
        g_wd2 = SideGather(p, wdr, fr, b["g_wd2"], pl.ds(2 * wide, 2 * wide))
        g_wo = PlaneGather(p, wor, ds, b["g_wo"])
        ax = TokenSpread(p, x_all, T, b["ax"])
        a1 = TokenSpread(p, hid_all, T, b["a1"])
        a2 = TokenSpread(p, d2_all, T, b["a2"])
        a3 = TokenSpread(p, d1_all, T, b["a3"])
        t1 = RepScatter(p, part, T, b["t1b"], b["t1s"])
        t2 = RepScatter(p, part, T, b["t2b"], b["t2s"])
        t3 = RepScatter(p, part, T, b["t3b"], b["t3s"])
        t4 = RepScatter(p, part, T, b["t4b"], b["t4s"])
        rwd = RowScatter(p, gwd, fr, b["rwdb"], b["rwds"], pl.ds(0, D // 2))
        rwx = SideScatter(p, gwd, fr, b["rwxb"], b["rwxs"], pl.ds(D // 2, D // 2))
        rwi = RowScatter(p, gwi, ds, b["rwib"], b["rwis"])
        rqkv = RowScatter(p, gqkv, ds, b["rqkvb"], b["rqkvs"])
        rsm = RowScatter(p, gs, NVEC, b["rsmb"], b["rsms"])
        rwo = PlaneScatter(p, gwo, ds, b["rwob"], b["rwos"])
        sd = RepSpread(p, td, b["rwdp"])
        si = RepSpread(p, ti, b["rwip"])
        sq = RepSpread(p, tq, b["rqkvp"])
        ss = RepSpread(p, ts, b["rsmp"])
        so = OwnerSpread(p, to, b["rwop"])

        smalls.start()
        for copy in local[:3]:
            copy.wait()
        g_qkv.start()
        ax.start()
        for copy in local[3:]:
            copy.wait()

        @pl.when(p.z == p.me)
        def _():
            own_wo.wait()

        g_wo.start()
        g_wia.start()
        sums[...] = jnp.zeros_like(sums)
        gbi8[...] = jnp.zeros_like(gbi8)
        gqv8[...] = jnp.zeros_like(gqv8)
        gflat[...] = jnp.zeros_like(gflat)
        smalls.push()
        g_qkv.push()
        smalls.pull()
        g_wo.forward()
        g_qkv.pull()
        g_wib.start()
        g_wd2.begin()
        g_wd0.start()
        g_wd1.start()
        smalls.finish()
        for i in range(nv):
            row = [small[s * NVEC + i : s * NVEC + i + 1, :] for s in range(S)]
            flat[i : i + 1, :] = jnp.concatenate(row, 1)
        ax.beside()
        ax.across()
        g_wia.push()
        g_qkv.finish()

        low = lax.broadcasted_iota(jnp.int32, (SEQ, 128), 1) < HEAD_DIM
        keep = (low, jnp.logical_not(low))

        def project(rows):
            for n in range(3):
                c = pl.ds(n * dr, dr)
                z = mm(x_all[rows, :], wqkv[:, c])
                if n == 0:
                    z = z + flat[0:1, cols]
                if n == 2:
                    z = z + flat[1:2, cols]
                qkv[rows, c] = z.astype(BF)

        def pick(v, h):
            return jnp.where(keep[h], v, jnp.zeros_like(v))

        def attend(chip):
            def one(j, _):
                seq = chip * (C // SEQ) + j
                rows = rows_of(seq, SEQ)
                for n in range(pairs):
                    q2 = qkv[rows, n * 128 : n * 128 + 128]
                    k2 = qkv[rows, dr + n * 128 : dr + n * 128 + 128]
                    v2 = qkv[rows, 2 * dr + n * 128 : 2 * dr + n * 128 + 128]
                    got = []
                    for h in range(2):
                        scores = mm_nt(pick(q2, h), k2) * 0.125
                        e = jnp.exp(scores - jnp.max(scores, axis=-1, keepdims=True))
                        pr = e / jnp.sum(e, axis=-1, keepdims=True)
                        probs[rows_of(seq * 2 * pairs + 2 * n + h, SEQ), :] = pr
                        got.append(mm(pr.astype(BF), v2))
                    ctx[rows, n * 128 : n * 128 + 128] = jnp.where(low, got[0], got[1]).astype(BF)
                return 0

            lax.fori_loop(0, C // SEQ, one, 0)

        def attn_part(rows):
            def tile(c):
                part[rows, c] = mm(ctx[rows, :], wor[:, c]).astype(BF)

            tiles(D, tile)

        def inner(rows):
            def tile(c):
                z = mm(hid_all[rows, :], wir[:, c]) + flat[8:9, c]
                phi = 0.5 * (1.0 + lax.erf(z * INV_ROOT_TWO))
                acted[rows, c] = (z * phi).astype(BF)
                slope[rows, c] = phi + z * jnp.exp(-0.5 * z * z) * INV_ROOT_TWO_PI

            tiles(V, tile)

        def down(rows, q):
            c = pl.ds(q * wide, wide)
            part[rows, c] = mm(acted[rows, :], wdr[:, c]).astype(BF)

        def d_inner(rows):
            def tile(c):
                d = mm_nt(d2_all[rows, :], wdr[c, :]) * slope[rows, c]
                gbi8[:, c] += fold(d)
                d_in[rows, c] = d.astype(BF)

            tiles(V, tile)

        def hid_part(rows):
            def tile(c):
                part[rows, c] = mm_nt(d_in[rows, :], wir[c, :]).astype(BF)

            tiles(D, tile)

        def d_attend(chip):
            rows = rows_of(chip, C)
            dctx[rows, :] = mm_nt(d1_all[rows, :], wor[...]).astype(BF)

            def one(j, _):
                seq = chip * (C // SEQ) + j
                rows = rows_of(seq, SEQ)
                for n in range(pairs):
                    lanes = [slice(m * dr + n * 128, m * dr + n * 128 + 128) for m in range(3)]
                    q2, k2, v2 = (qkv[rows, c] for c in lanes)
                    dc2 = dctx[rows, lanes[0]]
                    got = []
                    for h in range(2):
                        pr = probs[rows_of(seq * 2 * pairs + 2 * n + h, SEQ), :]
                        dp = mm_nt(pick(dc2, h), v2)
                        delta = jnp.sum(pr * dp, axis=-1, keepdims=True)
                        dsc = (pr * (dp - delta) * 0.125).astype(BF)
                        got.append((mm(dsc, k2), mm_tn(dsc, q2), mm_tn(pr.astype(BF), dc2)))
                    dq, dk, dv = (jnp.where(low, u, w) for u, w in zip(*got))
                    gqv8[:, lanes[0]] += fold(dq)
                    gqv8[:, lanes[1]] += fold(dv)
                    for v, c in zip((dq, dk, dv), lanes):
                        dqkv[rows, c] = v.astype(BF)
                return 0

            lax.fori_loop(0, C // SEQ, one, 0)

        def in_part(rows):
            def tile(c):
                part[rows, c] = mm_nt(dqkv[rows, :], wqkv[c, :]).astype(BF)

            tiles(D, tile)

        def grad_plane(lhs, rhs, dst, z):
            both = pl.ds(pl.multiple_of(z * 2 * ds, 2 * ds), 2 * ds)
            dst[both, :] = mm_tn(lhs[:, both], rhs[...]).astype(BF)

        def grad_all(lhs, rhs, dst, *scatters):
            for j in (1, 2, 0, 3):
                grad_plane(lhs, rhs, dst, rwi.line.zs[j])
                for g in scatters:
                    g.launch(j)

        project(far_chip)
        project(own_chip)
        attend(p.chip(1))
        g_wia.pull()
        g_wo.finish()
        attn_part(far_chip)
        t1.start_far()
        g_wib.push()
        attend(p.a)
        attn_part(own_chip)
        t1.start_near()
        t1.pass_on()
        g_wib.pull()
        g_wd0.push()
        g_wd2.start()
        t1.finish()

        def norm_one(i, _):
            at = step_rows(i)
            normed, rstd = norm_parts(x[at, :].astype(F32) + t1.read(i) + flat[2:3, :])
            hidden = normed * flat[3:4, :] + flat[4:5, :]
            normed_r[at, :] = normed
            rstd_r[at, :] = jnp.broadcast_to(rstd, (STEP, 128))
            hidden_r[at, :] = hidden
            hid_all[step_rows(i, p.me * T), :] = hidden.astype(BF)
            return 0

        lax.fori_loop(0, T // STEP, norm_one, 0)
        a1.start()
        t1.drain()
        g_wd0.pull()
        g_wd1.push()
        a1.beside()
        a1.across()
        g_wd1.pull()
        g_wd2.push()
        g_wia.finish()
        g_wib.finish()
        inner(own_chip)
        inner(far_chip)
        g_wd0.finish()
        down(far_chip, 0)
        down(own_chip, 0)
        g_wd1.finish()
        down(far_chip, 1)
        down(own_chip, 1)
        g_wd2.pull()
        down(far_chip, 2)
        down(far_chip, 3)
        t2.start_far()
        down(own_chip, 2)
        down(own_chip, 3)
        t2.start_near()
        t2.pass_on()
        t2.finish()

        def norm_two(i, _):
            at = step_rows(i)
            normed, rstd = norm_parts(hidden_r[at, :] + t2.read(i) + flat[5:6, :])
            out_o[at, :] = (normed * flat[6:7, :] + flat[7:8, :]).astype(BF)
            dout = cot[at, :].astype(F32)
            d_two = norm_back(dout * flat[6:7, :], normed, rstd)
            sums[24:32, :] += fold(d_two)
            sums[32:40, :] += fold(dout * normed)
            sums[40:48, :] += fold(dout)
            d_two_r[at, :] = d_two
            d2_all[step_rows(i, p.me * T), :] = d_two.astype(BF)
            return 0

        lax.fori_loop(0, T // STEP, norm_two, 0)
        a2.start()
        t2.drain()
        a2.beside()
        d_inner(own_chip)
        a2.across()
        grad_all(acted, d2_all, gwd, rwd, rwx)
        d_inner(far_chip)
        hid_part(far_chip)
        t3.start_far()
        hid_part(own_chip)
        t3.start_near()
        t3.pass_on()
        grad_all(hid_all, d_in, gwi, rwi)
        for j in (1, 2, 0):
            rwd.lift(j)
        rwx.relay(1)
        rwx.relay(2)
        t3.finish()

        def back_one(i, _):
            at = step_rows(i)
            d_hidden = d_two_r[at, :] + t3.read(i)
            normed = normed_r[at, :]
            d_one = norm_back(d_hidden * flat[3:4, :], normed, rstd_r[at, 0:1])
            sums[0:8, :] += fold(d_one)
            sums[8:16, :] += fold(d_hidden * normed)
            sums[16:24, :] += fold(d_hidden)
            d_one_r[at, :] = d_one
            d1_all[step_rows(i, p.me * T), :] = d_one.astype(BF)
            return 0

        lax.fori_loop(0, T // STEP, back_one, 0)
        a3.start()
        t3.drain()
        rwd.relay(1)
        rwd.relay(2)
        a3.beside()
        d_attend(p.a)
        a3.across()
        gwo[...] = mm_tn(ctx[...], d1_all[...]).astype(BF)
        rwo.start()
        rwi.lift(1)
        d_attend(p.chip(1))
        gflat[0:1, cols] = jnp.sum(gqv8[:, :dr], axis=0, keepdims=True)
        gflat[1:2, cols] = jnp.sum(gqv8[:, dr:], axis=0, keepdims=True)
        for i in range(6):
            gflat[i + 2 : i + 3, :] = jnp.sum(sums[8 * i : 8 * i + 8, :], axis=0, keepdims=True)
        gflat[8:9, :] = jnp.sum(gbi8[...], axis=0, keepdims=True)
        for s in range(S):
            gs[s * NVEC : (s + 1) * NVEC, :] = gflat[:, s * ds : (s + 1) * ds]
        rsm.start()
        rwi.lift(2)
        rwx.cross()
        grad_all(x_all, dqkv, gqkv, rqkv)
        rwi.lift(0)
        rwi.relay(1)
        in_part(far_chip)
        t4.start_far()
        in_part(own_chip)
        t4.start_near()
        t4.pass_on()
        rwi.relay(2)
        rwd.total(td)
        t4.finish()

        def last(i, _):
            at = step_rows(i)
            gin_o[at, :] = (d_one_r[at, :] + t4.read(i)).astype(BF)
            return 0

        lax.fori_loop(0, T // STEP, last, 0)
        rwo.pass_on()
        for j in (1, 2, 0):
            rsm.lift(j)
        rwx.total(td)
        sd.start()
        rqkv.lift(1)
        rsm.relay(1)
        rsm.relay(2)
        rqkv.lift(2)
        rqkv.relay(1)
        rwi.total(ti)
        si.start()
        sd.forward()
        rqkv.lift(0)
        rqkv.relay(2)
        rwo.total(to)
        so.start()
        rsm.total(ts)
        ss.start()
        si.forward()
        so.forward()
        rqkv.total(tq)
        sq.start()
        ss.forward()
        sd.finish()
        si.finish()
        so.finish()
        sq.forward()
        sq.finish()
        ss.finish()
        for g in (smalls, g_qkv, g_wo, g_wia, g_wib, g_wd0, g_wd1, g_wd2, ax, a1, a2, a3, t4):
            g.drain()
        for g in (rwd, rwx, rwi, rqkv, rsm, rwo, sd, si, sq, ss, so):
            g.drain()

    ins = [x, cot, wq, wk, wv, wo, wi, wd] + [v[None] for v in vectors]
    outs = [((T, D), BF)] * 2
    outs += [((R, ds, W), BF), ((R, ds, V), BF), ((R, fr, D), BF), ((ds, D), BF)]
    outs += [((R, NVEC, ds), F32)]
    return pl.pallas_call(
        kernel,
        out_shape=[jax.ShapeDtypeStruct(*o) for o in outs],
        in_specs=[VMEM_SPEC] * 2 + [ANY_SPEC] * 6 + [VMEM_SPEC] * nv,
        out_specs=[VMEM_SPEC] * len(outs),
        scratch_shapes=bag.specs,
        compiler_params=pltpu.CompilerParams(
            collective_id=12, has_side_effects=True, vmem_limit_bytes=LIMIT
        ),
        cost_estimate=pl.CostEstimate(
            flops=10 * 10**9, bytes_accessed=24 << 20, transcendentals=4 << 20
        ),
    )(*ins)


def widen(out, gin, tq, ti, td, to, ts, S):
    R, ds, W = tq.shape
    D, dr = R * W // 3, W // 3
    fr, V = td.shape[1], ti.shape[2]
    fs = fr * R
    T = out.shape[0]
    few, tok = ds // R, T // R

    def kernel(out, gin, tq, ti, td, to, ts, out_o, gin_o, oq, ok, ov, oo, oi, od, *vec_o):
        out_o[...] = out[...]
        gin_o[...] = gin[...]
        od[...] = td[0].astype(F32)
        oo[...] = to[...].astype(F32)
        for r in range(R):
            for n, o in enumerate((oq, ok, ov)):
                o[:, r * dr : (r + 1) * dr] = tq[r, :, n * dr : (n + 1) * dr].astype(F32)
            for c in range(S):
                lo = c * fs + r * fr
                oi[:, lo : lo + fr] = ti[r, :, c * fr : (c + 1) * fr].astype(F32)

        @pl.when(pl.program_id(0) == 0)
        def _():
            total = ts[0]
            for r in range(1, R):
                total = total + ts[r]
            for i in range(8):
                vec_o[i][...] = total[i : i + 1, :]
            for r in range(R):
                vec_o[8][:, r * fr : (r + 1) * fr] = ts[r, 8:9, :]

    def rows(n, c):
        return pl.BlockSpec((n, c), lambda i: (i, 0))

    def slab(n, c):
        return pl.BlockSpec((R, n, c), lambda i: (0, i, 0))

    def whole(*shape):
        return pl.BlockSpec(shape, lambda i: (0,) * len(shape))

    outs = [((T, D), BF)] * 2 + [((ds, D), F32)] * 4 + [((ds, S * fs), F32), ((fs, D), F32)]
    outs += [((1, ds), F32)] * 8 + [((1, fs), F32)]
    return pl.pallas_call(
        kernel,
        grid=(R,),
        out_shape=[jax.ShapeDtypeStruct(*o) for o in outs],
        in_specs=[
            rows(tok, D),
            rows(tok, D),
            slab(few, W),
            slab(few, V),
            pl.BlockSpec((1, fr, D), lambda i: (i, 0, 0)),
            rows(few, D),
            whole(R, NVEC, ds),
        ],
        out_specs=[rows(tok, D)] * 2
        + [rows(few, D)] * 4
        + [rows(few, S * fs), rows(fr, D)]
        + [whole(1, ds)] * 8
        + [whole(1, fs)],
        compiler_params=pltpu.CompilerParams(vmem_limit_bytes=LIMIT),
    )(out, gin, tq, ti, td, to, ts)


def fast_body(
    block_input,
    out_cotangent,
    w_query,
    w_key,
    w_value,
    w_output,
    bias_query,
    bias_value,
    bias_output,
    gain_first,
    shift_first,
    w_inner,
    bias_inner,
    w_down,
    bias_down,
    gain_second,
    shift_second,
):
    vectors = (
        bias_query,
        bias_value,
        bias_output,
        gain_first,
        shift_first,
        bias_down,
        gain_second,
        shift_second,
        bias_inner,
    )
    S = lax.axis_size("shard")
    got = layer(
        block_input,
        out_cotangent,
        w_query,
        w_key,
        w_value,
        w_output,
        w_inner,
        w_down,
        vectors,
        S,
        lax.axis_size("rep"),
    )
    got = widen(*got, S)
    output, grad_input, gq, gk, gv, go, gi, gd = got[:8]
    gbq, gbv, gbo, ggone, gsone, gbd, ggtwo, gstwo, gbi = (v.reshape(-1) for v in got[8:])
    return (
        output,
        grad_input,
        gq,
        gk,
        gv,
        go,
        gbq,
        gbv,
        gbo,
        ggone,
        gsone,
        gi,
        gbi,
        gd,
        gbd,
        ggtwo,
        gstwo,
    )


def fits_fast(mesh):
    S, R = mesh.shape["shard"], mesh.shape["rep"]
    return R == 4 and S == 8


def solution(mesh):
    tokens = P(("shard", "rep"), None)
    mat = P("shard", None)
    vec = P("shard")
    params = (mat, mat, mat, mat, vec, vec, vec, vec, vec, mat, vec, mat, vec, vec, vec)
    return jax.shard_map(
        fast_body if fits_fast(mesh) else body,
        mesh=mesh,
        in_specs=(tokens, tokens) + params,
        out_specs=(tokens, tokens) + params,
        check_vma=False,
    )
```

```python
import jax
import jax.numpy as jnp
from jax import lax
from jax.experimental import pallas as pl
from jax.experimental.pallas import tpu as pltpu
from jax.sharding import PartitionSpec as P

HEAD_DIM = 64
SEQ = 128
PAD = 16


EPS = 1e-06
INV_ROOT_TWO = 0.7071067811865476
INV_ROOT_TWO_PI = 0.3989422804014327
BF = jnp.bfloat16
F32 = jnp.float32


def norm_parts(resid):
    centre = resid - jnp.mean(resid, axis=-1, keepdims=True)
    variance = jnp.mean(centre * centre, axis=-1, keepdims=True)
    rstd = lax.rsqrt(variance + EPS)
    return (centre * rstd, rstd)


def norm_back(upstream, normed, rstd):
    return rstd * (
        upstream
        - jnp.mean(upstream, axis=-1, keepdims=True)
        - normed * jnp.mean(upstream * normed, axis=-1, keepdims=True)
    )


def mm(a, b):
    return jnp.dot(a, b, preferred_element_type=F32)


def mm_nt(a, b):
    return lax.dot_general(a, b, (((1,), (1,)), ((), ())), preferred_element_type=F32)


def mm_tn(a, b):
    return lax.dot_general(a, b, (((0,), (0,)), ((), ())), preferred_element_type=F32)


def ein(spec, a, b):
    return jnp.einsum(spec, a, b, preferred_element_type=F32)


MESH = pl.DeviceIdType.MESH
CHUNK = 16


class Peers:
    def __init__(self, R):
        self.R, self.A = R, R // 2
        self.me = lax.axis_index("rep")
        self.c = lax.rem(self.me, 2)
        self.a = lax.div(self.me, 2)
        self.partner = self.me + 1 - 2 * self.c

    def chip(self, k):
        return lax.rem(self.a + k, self.A)

    def same(self, k):
        return 2 * self.chip(k) + self.c

    def other(self, k):
        return 2 * self.chip(k) + 1 - self.c

    def meet(self):
        barrier = pltpu.get_barrier_semaphore()
        for dev in [self.partner] + [self.same(k) for k in range(1, self.A)]:
            pl.semaphore_signal(barrier, inc=1, device_id={"rep": dev}, device_id_type=MESH)
        pl.semaphore_wait(barrier, self.A)


def rows_of(index, T):
    return pl.ds(pl.multiple_of(index * T, T), T)


def chunk_rows(i, base=None):
    start = i * CHUNK if base is None else base + i * CHUNK
    return pl.ds(pl.multiple_of(start, CHUNK), CHUNK)


def remote(src, dst, send, recv, dev):
    return pltpu.make_async_remote_copy(
        src_ref=src,
        dst_ref=dst,
        send_sem=send,
        recv_sem=recv,
        device_id={"rep": dev},
        device_id_type=MESH,
    )


def scatter_sum(p, part, T, near, far, out, sems):
    near_s, near_r, far_s, far_r = sems
    order = list(range(1, p.A)) + [0]
    first = {
        k: remote(
            part.at[rows_of(p.other(k), T)], near.at[k], near_s.at[k], near_r.at[k], p.partner
        )
        for k in order
    }
    for k in order:
        first[k].start()
    second = []
    for k in range(1, p.A):
        first[k].wait_recv()
        base = p.same(k) * T

        def add(i, _, k=k, base=base):
            mine = part[chunk_rows(i, base), :].astype(F32)
            out[k - 1, chunk_rows(i), :] = (mine + near[k, chunk_rows(i), :].astype(F32)).astype(BF)
            return 0

        lax.fori_loop(0, T // CHUNK, add, 0)
        copy = remote(out.at[k - 1], far.at[k - 1], far_s.at[k - 1], far_r.at[k - 1], p.same(k))
        copy.start()
        second.append(copy)
    first[0].wait_recv()
    for copy in second:
        copy.wait_recv()

    def read(i):
        total = part[chunk_rows(i, p.me * T), :].astype(F32) + near[0, chunk_rows(i), :].astype(F32)
        for k in range(1, p.A):
            total = total + far[k - 1, chunk_rows(i), :].astype(F32)
        return total

    return read, list(first.values()) + second


def spread(p, src, full, T, sems):
    dir_s, dir_r, fwd_s, fwd_r = sems
    mine = full.at[rows_of(p.me, T)]
    direct = {}
    for k in list(range(1, p.A)) + [0]:
        dev = p.partner if k == 0 else p.same(k)
        direct[k] = remote(src, mine, dir_s.at[k], dir_r.at[k], dev)
        direct[k].start()
    passed = []
    for k in range(1, p.A):
        direct[k].wait_recv()
        block = full.at[rows_of(p.same(p.A - k), T)]
        copy = remote(block, block, fwd_s.at[k - 1], fwd_r.at[k - 1], p.partner)
        copy.start()
        passed.append(copy)
    direct[0].wait_recv()
    for copy in passed:
        copy.wait_recv()
    return list(direct.values()) + passed


def drain(copies):
    for copy in copies:
        copy.wait_send()


def run_kernel(kernel, cid, T, D, R, ins, outs, scatter, gather):
    A = R // 2
    few = max(A - 1, 1)
    scratch = []
    if scatter:
        scratch += [
            pltpu.VMEM((A, T, D), BF),
            pltpu.VMEM((few, T, D), BF),
            pltpu.VMEM((few, T, D), BF),
        ]
        scratch += [pltpu.SemaphoreType.DMA((n,)) for n in (A, A, few, few)]
    if gather:
        scratch += [pltpu.SemaphoreType.DMA((n,)) for n in (A, A, few, few)]
    vmem = pl.BlockSpec(memory_space=pltpu.VMEM)
    return pl.pallas_call(
        kernel,
        out_shape=[jax.ShapeDtypeStruct(*o) for o in outs],
        in_specs=[vmem] * len(ins),
        out_specs=[vmem] * len(outs),
        scratch_shapes=scratch,
        compiler_params=pltpu.CompilerParams(collective_id=cid, has_side_effects=True),
        cost_estimate=pl.CostEstimate(flops=0, bytes_accessed=24 << 20, transcendentals=0),
    )(*ins)


def gather_kernel(block, R, cid):
    T, D = block.shape

    def kernel(src, full, *sems):
        p = Peers(R)
        p.meet()

        def put(i, _):
            full[chunk_rows(i, p.me * T), :] = src[chunk_rows(i), :]
            return 0

        lax.fori_loop(0, T // CHUNK, put, 0)
        drain(spread(p, src, full, T, sems))

    return run_kernel(kernel, cid, T, D, R, [block], [((R * T, D), BF)], False, True)[0]


def norm_one_step(partial, x, bo, gone, sone):
    T, D = x.shape
    R = partial.shape[0] // T

    def kernel(part, xr, bor, gr, sr, normed_o, rstd_o, hidden_o, full, near, far, out, *sems):
        p = Peers(R)
        p.meet()
        read, sent = scatter_sum(p, part, T, near, far, out, sems[:4])

        def step(i, _):
            normed, rstd = norm_parts(xr[chunk_rows(i), :].astype(F32) + read(i) + bor[...])
            hidden = normed * gr[...] + sr[...]
            normed_o[chunk_rows(i), :] = normed
            rstd_o[chunk_rows(i), :] = rstd
            hidden_o[chunk_rows(i), :] = hidden
            full[chunk_rows(i, p.me * T), :] = hidden.astype(BF)
            return 0

        lax.fori_loop(0, T // CHUNK, step, 0)
        drain(sent + spread(p, full.at[rows_of(p.me, T)], full, T, sems[4:]))

    ins = [partial, x, bo[None], gone[None], sone[None]]
    outs = [((T, D), F32), ((T, 1), F32), ((T, D), F32), ((R * T, D), BF)]
    return run_kernel(kernel, 1, T, D, R, ins, outs, True, True)


def add_sums(ref, values):
    for n, v in enumerate(values):
        ref[n : n + 1, :] += jnp.sum(v, axis=0, keepdims=True)


def norm_two_step(partial, hidden, bd, gtwo, stwo, cot):
    T, D = hidden.shape
    R = partial.shape[0] // T

    def kernel(part, hr, br, gr, sr, cr, out_o, d_o, sums, full, near, far, out, *sems):
        p = Peers(R)
        p.meet()
        sums[...] = jnp.zeros_like(sums)
        read, sent = scatter_sum(p, part, T, near, far, out, sems[:4])

        def step(i, _):
            normed, rstd = norm_parts(hr[chunk_rows(i), :] + read(i) + br[...])
            out_o[chunk_rows(i), :] = (normed * gr[...] + sr[...]).astype(BF)
            dout = cr[chunk_rows(i), :].astype(F32)
            d_two = norm_back(dout * gr[...], normed, rstd)
            add_sums(sums, (d_two, dout * normed, dout))
            d_o[chunk_rows(i), :] = d_two
            full[chunk_rows(i, p.me * T), :] = d_two.astype(BF)
            return 0

        lax.fori_loop(0, T // CHUNK, step, 0)
        drain(sent + spread(p, full.at[rows_of(p.me, T)], full, T, sems[4:]))

    ins = [partial, hidden, bd[None], gtwo[None], stwo[None], cot]
    outs = [((T, D), BF), ((T, D), F32), ((8, D), F32), ((R * T, D), BF)]
    return run_kernel(kernel, 2, T, D, R, ins, outs, True, True)


def back_one_step(partial, d_two, normed, rstd, gone):
    T, D = d_two.shape
    R = partial.shape[0] // T

    def kernel(part, dr, nr, rr, gr, d_o, sums, full, near, far, out, *sems):
        p = Peers(R)
        p.meet()
        sums[...] = jnp.zeros_like(sums)
        read, sent = scatter_sum(p, part, T, near, far, out, sems[:4])

        def step(i, _):
            d_hidden = dr[chunk_rows(i), :] + read(i)
            normed = nr[chunk_rows(i), :]
            d_one = norm_back(d_hidden * gr[...], normed, rr[chunk_rows(i), :])
            add_sums(sums, (d_one, d_hidden * normed, d_hidden))
            d_o[chunk_rows(i), :] = d_one
            full[chunk_rows(i, p.me * T), :] = d_one.astype(BF)
            return 0

        lax.fori_loop(0, T // CHUNK, step, 0)
        drain(sent + spread(p, full.at[rows_of(p.me, T)], full, T, sems[4:]))

    ins = [partial, d_two, normed, rstd, gone[None]]
    outs = [((T, D), F32), ((8, D), F32), ((R * T, D), BF)]
    return run_kernel(kernel, 3, T, D, R, ins, outs, True, True)


def input_step(partial, d_one):
    T, D = d_one.shape
    R = partial.shape[0] // T

    def kernel(part, dr, grad, near, far, out, *sems):
        p = Peers(R)
        p.meet()
        read, sent = scatter_sum(p, part, T, near, far, out, sems)

        def step(i, _):
            grad[chunk_rows(i), :] = (dr[chunk_rows(i), :] + read(i)).astype(BF)
            return 0

        lax.fori_loop(0, T // CHUNK, step, 0)
        drain(sent)

    return run_kernel(kernel, 4, T, D, R, [partial, d_one], [((T, D), BF)], True, False)[0]


def body(
    block_input,
    out_cotangent,
    w_query,
    w_key,
    w_value,
    w_output,
    bias_query,
    bias_value,
    bias_output,
    gain_first,
    shift_first,
    w_inner,
    bias_inner,
    w_down,
    bias_down,
    gain_second,
    shift_second,
):
    S = lax.axis_size("shard")
    R = lax.axis_size("rep")
    r = lax.axis_index("rep")
    T = block_input.shape[0]
    D = w_query.shape[1]
    ds = w_query.shape[0]
    dr = D // R
    fs = w_down.shape[0]
    fr = fs // R
    W = 4 * dr

    def cols(w):
        return lax.dynamic_slice(w, (0, r * dr), (ds, dr))

    small = jnp.concatenate(
        [
            v.astype(BF)
            for v in (
                bias_query,
                bias_value,
                bias_output,
                gain_first,
                shift_first,
                bias_down,
                gain_second,
                shift_second,
                bias_inner,
            )
        ]
    )
    n_small = small.shape[0]
    small = jnp.pad(small, (0, PAD * W - n_small)).reshape(PAD, W)
    pack = jnp.concatenate(
        [jnp.concatenate([cols(w_query), cols(w_key), cols(w_value), cols(w_output)], 1), small], 0
    )
    got = lax.all_gather(pack, "shard", axis=0)
    x_all = gather_kernel(block_input, R, 0)
    wi_r = lax.dynamic_index_in_dim(w_inner.reshape(ds, S, R, fr), r, 2, keepdims=False)
    V = S * fr
    dv = fr * D // V
    wd_r = lax.dynamic_slice(w_down, (r * fr, 0), (fr, D)).reshape(dv, V)
    mlp = lax.all_gather(jnp.concatenate([wi_r.reshape(ds, V), wd_r], 0), "shard", axis=0)
    wi = mlp[:, :ds].reshape(D, V)
    wd = mlp[:, ds:].reshape(V, D)
    wqkv = got[:, :ds, : 3 * dr].reshape(D, 3 * dr)
    wo = lax.all_to_all(
        got[:, :ds, 3 * dr :].reshape(D, dr), "rep", split_axis=0, concat_axis=1, tiled=True
    )
    flat = got[:, ds:, :].reshape(S, PAD * W)[:, :n_small].astype(F32)
    bq, bv, bo, gone, sone, bd, gtwo, stwo = (
        flat[:, i * ds : (i + 1) * ds].reshape(D) for i in range(8)
    )
    bi = lax.dynamic_index_in_dim(flat[:, 8 * ds :].reshape(S, R, fr), r, 1, keepdims=False)
    bi = bi.reshape(S * fr)
    bq = lax.dynamic_slice(bq, (r * dr,), (dr,))
    bv = lax.dynamic_slice(bv, (r * dr,), (dr,))

    N = R * T
    shape4 = (N // SEQ, SEQ, dr // HEAD_DIM, HEAD_DIM)
    qkv = mm(x_all, wqkv)
    query = (qkv[:, :dr] + bq).astype(BF).reshape(shape4)
    keyed = qkv[:, dr : 2 * dr].astype(BF).reshape(shape4)
    valued = (qkv[:, 2 * dr :] + bv).astype(BF).reshape(shape4)
    scores = ein("bqhe,bkhe->bhqk", query, keyed) * 0.125
    top = jnp.max(scores, axis=-1, keepdims=True)
    logsum = top + jnp.log(jnp.sum(jnp.exp(scores - top), axis=-1, keepdims=True))
    probs = jnp.exp(scores - logsum)
    probs_b = probs.astype(BF)
    context = ein("bhqk,bkhe->bqhe", probs_b, valued).astype(BF).reshape(N, dr)
    attn_part = mm(context, wo).astype(BF)

    normed_one, rstd_one, hidden, hidden_all = norm_one_step(attn_part, block_input, bo, gone, sone)
    inner = mm(hidden_all, wi) + bi
    phi = 0.5 * (1.0 + lax.erf(inner * INV_ROOT_TWO))
    acted = (inner * phi).astype(BF)
    slope = phi + inner * jnp.exp(-0.5 * inner * inner) * INV_ROOT_TWO_PI
    down_part = mm(acted, wd).astype(BF)

    output, d_two, sums_two, d_two_all = norm_two_step(
        down_part, hidden, bd, gtwo, stwo, out_cotangent
    )
    d_inner = mm_nt(d_two_all, wd) * slope
    g_bias_inner = jnp.sum(d_inner, axis=0)
    d_inner_b = d_inner.astype(BF)
    hid_part = mm_nt(d_inner_b, wi).astype(BF)
    g_wd = mm_tn(acted, d_two_all).astype(BF).reshape(S, dv, V)
    g_wi = mm_tn(hidden_all, d_inner_b).astype(BF).reshape(S, ds, V)
    g_mlp = lax.psum_scatter(
        jnp.concatenate([g_wi, g_wd], 1), "shard", scatter_dimension=0, tiled=True
    )[0]

    d_one, sums_one, d_one_all = back_one_step(hid_part, d_two, normed_one, rstd_one, gone)
    g_wo = mm_tn(context, d_one_all).astype(BF)
    g_wo = lax.all_to_all(g_wo, "rep", split_axis=1, concat_axis=0, tiled=True)
    d_context = mm_nt(d_one_all, wo).astype(BF).reshape(shape4)
    d_probs = ein("bqhe,bkhe->bhqk", d_context, valued)
    delta = jnp.sum(probs * d_probs, axis=-1, keepdims=True)
    d_scores = (probs * (d_probs - delta) * 0.125).astype(BF)
    d_query = ein("bhqk,bkhe->bqhe", d_scores, keyed).reshape(N, dr)
    d_keyed = ein("bhqk,bqhe->bkhe", d_scores, query).reshape(N, dr)
    d_valued = ein("bhqk,bqhe->bkhe", probs_b, d_context).reshape(N, dr)
    g_bias_query = jnp.sum(d_query, axis=0)
    g_bias_value = jnp.sum(d_valued, axis=0)
    d_qkv = jnp.concatenate([d_query.astype(BF), d_keyed.astype(BF), d_valued.astype(BF)], 1)
    in_part = mm_nt(d_qkv, wqkv).astype(BF)

    def placed(v):
        return lax.dynamic_update_slice(jnp.zeros((D,), F32), v, (r * dr,)).reshape(S, ds)

    g_small = jnp.concatenate(
        [
            placed(g_bias_query),
            placed(g_bias_value),
            sums_one[0].reshape(S, ds),
            sums_one[1].reshape(S, ds),
            sums_one[2].reshape(S, ds),
            sums_two[0].reshape(S, ds),
            sums_two[1].reshape(S, ds),
            sums_two[2].reshape(S, ds),
            g_bias_inner.reshape(S, fr),
        ],
        1,
    ).astype(BF)
    n_g = g_small.shape[1]
    g_small = jnp.pad(g_small, ((0, 0), (0, PAD * W - n_g))).reshape(S, PAD, W)
    g_pack = jnp.concatenate([mm_tn(x_all, d_qkv).astype(BF), g_wo], 1).reshape(S, ds, W)
    g_pack = jnp.concatenate([g_pack, g_small], 1)
    g_pack = lax.psum_scatter(g_pack, "shard", scatter_dimension=0, tiled=True)[0]

    grad_input = input_step(in_part, d_one)

    mlps = gather_kernel(g_mlp, R, 5).reshape(R, ds + dv, V).astype(F32)
    wd_out = mlps[:, ds:].reshape(R * fr, D)
    wi_out = mlps[:, :ds].reshape(R, ds, S, fr).transpose(1, 2, 0, 3).reshape(ds, S * R * fr)
    packs = gather_kernel(g_pack, R, 6).reshape(R, ds + PAD, W).astype(F32)
    main = packs[:, :ds].reshape(R, ds, 4, dr).transpose(2, 1, 0, 3).reshape(4, ds, D)
    tail = packs[:, ds:].reshape(R, PAD * W)
    summed = jnp.sum(tail[:, : 8 * ds], axis=0)
    gbq, gbv, gbo, ggone, gsone, gbd, ggtwo, gstwo = (
        summed[i * ds : (i + 1) * ds] for i in range(8)
    )
    gbi = tail[:, 8 * ds : n_g].reshape(fs)
    return (
        output,
        grad_input,
        main[0],
        main[1],
        main[2],
        main[3],
        gbq,
        gbv,
        gbo,
        ggone,
        gsone,
        wi_out,
        gbi,
        wd_out,
        gbd,
        ggtwo,
        gstwo,
    )

VMEM_SPEC = pl.BlockSpec(memory_space=pltpu.VMEM)
ANY_SPEC = pl.BlockSpec(memory_space=pl.ANY)
LIMIT = 56 << 20
NVEC = 16


def dma_sems(*counts):
    return [pltpu.SemaphoreType.DMA((n,)) for n in counts]


class Place(Peers):
    def __init__(self, S, R):
        super().__init__(R)
        self.S, self.Z = S, S // 2
        self.s = lax.axis_index("shard")
        self.z = lax.div(self.s, 2)
        self.y = lax.rem(self.s, 2)
        self.across = self.s + 1 - 2 * self.y

    def up(self, k):
        return 2 * lax.rem(self.z + k, self.Z) + self.y

    def down(self, k):
        return 2 * lax.rem(self.z + self.Z - k, self.Z) + self.y

    def flip(self, s):
        return s + 1 - 2 * self.y

    def meet_all(self):
        barrier = pltpu.get_barrier_semaphore()
        for dev in [self.partner] + [self.same(k) for k in range(1, self.A)]:
            pl.semaphore_signal(barrier, inc=1, device_id={"rep": dev}, device_id_type=MESH)
        for dev in [self.across] + [self.up(k) for k in range(1, self.Z)]:
            pl.semaphore_signal(barrier, inc=1, device_id={"shard": dev}, device_id_type=MESH)
        pl.semaphore_wait(barrier, self.A + self.Z)


def to_shard(src, dst, send, recv, dev):
    return pltpu.make_async_remote_copy(
        src_ref=src,
        dst_ref=dst,
        send_sem=send,
        recv_sem=recv,
        device_id={"shard": dev},
        device_id_type=MESH,
    )


class LineGather:
    def __init__(self, p, full, T, row, sems, cols=None):
        self.p, self.full, self.T, self.row, self.cols = p, full, T, row, cols
        a_s, a_r, b_s, b_r, f_s, f_r = sems
        half = lax.div(p.z, 2)
        self.inner = p.z == 1 + half
        self.outer = jnp.logical_not(self.inner)
        beside = 4 * half + 1 - p.z
        turn = jnp.where(self.inner, 1, 0)
        self.zs = [beside, 3 - 3 * half, 2 - half]
        self.near = self.copy(p.z, a_s.at[0], a_r.at[0], beside)
        self.over = self.copy(p.z, b_s.at[0], b_r.at[turn], 2 - half)
        self.on = [self.copy(self.zs[j + 1], f_s.at[j], b_r.at[j], beside) for j in range(2)]

    @staticmethod
    def sems():
        return dma_sems(1, 1, 1, 2, 2, 1)

    def block(self, z):
        rows = rows_of(2 * z + self.row, self.T)
        return self.full.at[rows] if self.cols is None else self.full.at[rows, self.cols]

    def copy(self, z, send, recv, to):
        return to_shard(self.block(z), self.block(z), send, recv, 2 * to + self.p.y)

    def start(self):
        self.near.start()
        self.over.start()

    def push(self, then=(None, None, None)):
        self.near.wait_recv()
        if then[0] is not None:
            then[0].start()

        @pl.when(self.inner)
        def _():
            for j in range(2):
                self.on[j].wait_recv()
                self.on[j].start()
                if then[j + 1] is not None:
                    then[j + 1].start()

    def pull(self, then=(None, None, None)):
        @pl.when(self.outer)
        def _():
            for j in range(2):
                self.on[j].wait_recv()
                if then[j + 1] is not None:
                    then[j + 1].start()

    def drain(self):
        self.near.wait_send()
        self.over.wait_send()

        @pl.when(self.inner)
        def _():
            for copy in self.on:
                copy.wait_send()


class RowGather:
    def __init__(self, p, full, T, sems, cols=None):
        self.line = LineGather(p, full, T, p.y, sems[:6], cols)
        ys, yr = sems[6:]
        self.side = []
        for i, z in enumerate([p.z] + self.line.zs):
            block = self.line.block(z)
            self.side.append(to_shard(block, block, ys.at[i], yr.at[i], p.across))

    @staticmethod
    def sems(Z):
        return LineGather.sems() + dma_sems(Z, Z)

    def start(self):
        self.line.start()
        self.side[0].start()

    def push(self):
        self.line.push(self.side[1:])

    def pull(self):
        self.line.pull(self.side[1:])

    def finish(self):
        for copy in self.side:
            copy.wait_recv()

    def drain(self):
        self.line.drain()
        drain(self.side)


class SideGather:
    def __init__(self, p, full, T, sems, cols=None):
        self.lines = [
            LineGather(p, full, T, row, sems[6 * i : 6 * i + 6], cols)
            for i, row in enumerate((p.y, 1 - p.y))
        ]
        block = self.lines[0].block(p.z)
        self.side = to_shard(block, block, sems[12].at[0], sems[13].at[0], p.across)

    @staticmethod
    def sems(Z):
        return LineGather.sems() * 2 + dma_sems(1, 1)

    def begin(self):
        self.side.start()

    def start(self):
        self.lines[0].start()

    def follow(self):
        self.side.wait_recv()
        self.lines[1].start()

    def push(self):
        for line in self.lines:
            line.push()

    def pull(self):
        for line in self.lines:
            line.pull()

    def finish(self):
        pass

    def drain(self):
        for line in self.lines:
            line.drain()
        self.side.wait_send()


class PlaneGather:
    def __init__(self, p, full, T, sems):
        self.p = p
        self.zs, self.zr, self.ys, self.yr = sems
        rows = full.at[rows_of(p.y, T)]
        self.far = {
            k: to_shard(rows, rows, self.zs.at[k - 1], self.zr.at[0], p.up(k))
            for k in range(1, p.Z)
        }
        self.near = to_shard(rows, rows, self.ys.at[0], self.yr.at[0], p.across)
        self.mine = p.z == p.me

    @staticmethod
    def sems(Z):
        return dma_sems(Z - 1, 1, 1, 1)

    def start(self):
        @pl.when(self.mine)
        def _():
            for k in range(1, self.p.Z):
                self.far[k].start()
            self.near.start()

    def forward(self):
        @pl.when(jnp.logical_not(self.mine))
        def _():
            self.far[1].wait_recv()
            self.near.start()

    def finish(self):
        self.near.wait_recv()

    def drain(self):
        @pl.when(self.mine)
        def _():
            for k in range(1, self.p.Z):
                self.far[k].wait_send()

        self.near.wait_send()


class LineScatter:
    def __init__(self, p, part, T, row, bufs, sems, cols, close=None):
        self.p, self.part, self.T, self.row, self.cols = p, part, T, row, cols
        self.out, self.ain, self.bin, self.fin = bufs
        self.close = close
        a_s, a_r, f_s, f_r, b_s, b_r = sems
        half = lax.div(p.z, 2)
        self.inner = p.z == 1 + half
        self.outer = jnp.logical_not(self.inner)
        beside = 4 * half + 1 - p.z
        self.zs = [beside, 3 - 3 * half, 2 - half, p.z]

        def to(z, src, dst, send, recv):
            return to_shard(src, dst, send, recv, 2 * z + p.y)

        src = [self.block(z) if close is None else self.out.at[j] for j, z in enumerate(self.zs[:3])]
        self.near = to(beside, src[0], self.ain, a_s.at[0], a_r.at[0])
        self.up = [
            to(beside, src[j + 1], self.fin.at[j], f_s.at[j], f_r.at[j]) for j in range(2)
        ]
        self.over = [
            to(self.zs[j + 1], self.out.at[j + 1], self.bin, b_s.at[j], b_r.at[0])
            for j in range(2)
        ]

    @staticmethod
    def bufs(T, C, dtype):
        return [pltpu.VMEM(n + (T, C), dtype) for n in ((3,), (), (), (2,))]

    @staticmethod
    def sems():
        return dma_sems(1, 1, 2, 2, 2, 1)

    def block(self, z):
        return self.part.at[rows_of(2 * z + self.row, self.T), self.cols]

    def terms(self, j, i):
        base = (2 * self.zs[j] + self.row) * self.T
        total = self.part[chunk_rows(i, base), self.cols].astype(F32)
        if self.close is not None:
            total = total + self.close[j, chunk_rows(i), :].astype(F32)
        return total

    def each(self, put):
        def step(i, _):
            put(i)
            return 0

        lax.fori_loop(0, self.T // CHUNK, step, 0)

    def lift(self, j):
        if self.close is not None:

            def put(i):
                self.out[j, chunk_rows(i), :] = self.terms(j, i).astype(self.out.dtype)

            self.each(put)
        if j == 0:
            self.near.start()
        else:
            self.up[j - 1].start()

    def relay(self, j):
        self.up[j - 1].wait_recv()

        def put(i):
            total = self.terms(j, i) + self.fin[j - 1, chunk_rows(i), :].astype(F32)
            self.out[j, chunk_rows(i), :] = total.astype(self.out.dtype)

        self.each(put)
        self.over[j - 1].start()

    def wait(self):
        self.near.wait_recv()
        self.over[0].wait_recv()

    def read(self, i):
        total = self.terms(3, i) + self.ain[chunk_rows(i), :].astype(F32)
        return total + self.bin[chunk_rows(i), :].astype(F32)

    def drain(self):
        self.near.wait_send()

        @pl.when(self.outer)
        def _():
            drain(self.up)

        @pl.when(self.inner)
        def _():
            drain(self.over)


class RowScatter:
    def __init__(self, p, part, T, bufs, sems, cols=None):
        self.p, self.T = p, T
        self.cols = pl.ds(0, part.shape[1]) if cols is None else cols
        close = bufs[4]
        self.line = LineScatter(p, part, T, p.y, bufs[:4], sems[:6], self.cols, close)
        ys, yr = sems[6:]
        self.side = [
            to_shard(
                part.at[rows_of(2 * z + 1 - p.y, T), self.cols],
                close.at[j],
                ys.at[j],
                yr.at[j],
                p.across,
            )
            for j, z in enumerate(self.line.zs)
        ]

    @staticmethod
    def bufs(T, C, dtype):
        return LineScatter.bufs(T, C, dtype) + [pltpu.VMEM((4, T, C), dtype)]

    @staticmethod
    def sems():
        return LineScatter.sems() + dma_sems(4, 4)

    def launch(self, j):
        self.side[j].start()

    def start(self):
        for j in (1, 2, 0, 3):
            self.launch(j)

    def lift(self, j):
        if j == 0:
            self.side[0].wait_recv()
            self.line.lift(0)
        else:

            @pl.when(self.line.outer)
            def _():
                self.side[j].wait_recv()
                self.line.lift(j)

    def relay(self, j):
        @pl.when(self.line.inner)
        def _():
            self.side[j].wait_recv()
            self.line.relay(j)

    def total(self, dst):
        self.side[3].wait_recv()
        self.line.wait()

        def put(i):
            dst[self.p.me, chunk_rows(i), self.cols] = self.line.read(i).astype(dst.dtype)

        self.line.each(put)

    def drain(self):
        self.line.drain()
        drain(self.side)


class SideScatter:
    def __init__(self, p, part, T, bufs, sems, cols):
        self.p, self.cols = p, cols
        self.lines = [
            LineScatter(p, part, T, row, bufs[4 * i : 4 * i + 4], sems[6 * i : 6 * i + 6], cols)
            for i, row in enumerate((1 - p.y, p.y))
        ]
        self.sent, self.got = bufs[8:]
        self.side = to_shard(self.sent, self.got, sems[12].at[0], sems[13].at[0], p.across)

    @staticmethod
    def bufs(T, C, dtype):
        return LineScatter.bufs(T, C, dtype) * 2 + [pltpu.VMEM((T, C), dtype)] * 2

    @staticmethod
    def sems():
        return LineScatter.sems() * 2 + dma_sems(1, 1)

    def launch(self, j):
        if j == 0:
            for line in self.lines:
                line.lift(0)
        elif j < 3:

            @pl.when(self.lines[0].outer)
            def _():
                for line in self.lines:
                    line.lift(j)

    def relay(self, j):
        @pl.when(self.lines[0].inner)
        def _():
            for line in self.lines:
                line.relay(j)

    def cross(self):
        line = self.lines[0]
        line.wait()

        def put(i):
            self.sent[chunk_rows(i), :] = line.read(i).astype(self.sent.dtype)

        line.each(put)
        self.side.start()

    def total(self, dst):
        line = self.lines[1]
        line.wait()
        self.side.wait_recv()

        def put(i):
            total = line.read(i) + self.got[chunk_rows(i), :].astype(F32)
            dst[self.p.me, chunk_rows(i), self.cols] = total.astype(dst.dtype)

        line.each(put)

    def drain(self):
        for line in self.lines:
            line.drain()
        self.side.wait_send()


class PlaneScatter:
    def __init__(self, p, part, T, bufs, sems):
        self.p, self.part, self.T = p, part, T
        self.close, self.out, self.far = bufs
        ys, yr, zs, zr = sems
        self.first = to_shard(
            part.at[rows_of(1 - p.y, T)], self.close, ys.at[0], yr.at[0], p.across
        )
        self.mine = p.z == p.me
        self.hop = lax.rem(p.z + p.Z - p.me, p.Z)
        self.sends = to_shard(
            self.out,
            self.far.at[jnp.maximum(self.hop - 1, 0)],
            zs.at[0],
            zr.at[jnp.maximum(self.hop - 1, 0)],
            2 * p.me + p.y,
        )
        self.gets = [
            to_shard(self.out, self.far.at[k], zs.at[0], zr.at[k], p.up(k + 1))
            for k in range(p.Z - 1)
        ]

    @staticmethod
    def bufs(Z, T, C, dtype):
        return [pltpu.VMEM((T, C), dtype), pltpu.VMEM((T, C), dtype), pltpu.VMEM((Z - 1, T, C), dtype)]

    @staticmethod
    def sems(Z):
        return dma_sems(1, 1, 1, Z - 1)

    def start(self):
        self.first.start()

    def pass_on(self):
        self.first.wait_recv()

        def add(i, _):
            mine = self.part[chunk_rows(i, self.p.y * self.T), :].astype(F32)
            self.out[chunk_rows(i), :] = (mine + self.close[chunk_rows(i), :].astype(F32)).astype(BF)
            return 0

        lax.fori_loop(0, self.T // CHUNK, add, 0)

        @pl.when(jnp.logical_not(self.mine))
        def _():
            self.sends.start()

    def total(self, dst):
        @pl.when(self.mine)
        def _():
            for copy in self.gets:
                copy.wait_recv()

            def add(i, _):
                total = self.part[chunk_rows(i, self.p.y * self.T), :].astype(F32)
                total = total + self.close[chunk_rows(i), :].astype(F32)
                for k in range(self.p.Z - 1):
                    total = total + self.far[k, chunk_rows(i), :].astype(F32)
                dst[chunk_rows(i), :] = total.astype(BF)
                return 0

            lax.fori_loop(0, self.T // CHUNK, add, 0)

    def drain(self):
        self.first.wait_send()

        @pl.when(jnp.logical_not(self.mine))
        def _():
            self.sends.wait_send()


class RepSpread:
    def __init__(self, p, full, sems, cols=None):
        self.p = p
        dir_s, dir_r, fwd_s, fwd_r = sems
        cols = pl.ds(0, full.shape[2]) if cols is None else cols
        own = full.at[p.me, :, cols]
        self.direct = {0: remote(own, own, dir_s.at[0], dir_r.at[0], p.partner)}
        self.passed = {}
        for k in range(1, p.A):
            self.direct[k] = remote(own, own, dir_s.at[k], dir_r.at[k], p.same(k))
            block = full.at[p.same(p.A - k), :, cols]
            self.passed[k] = remote(block, block, fwd_s.at[k - 1], fwd_r.at[k - 1], p.partner)

    @staticmethod
    def sems(A):
        return dma_sems(A, A, A - 1, A - 1)

    def start(self):
        for k in list(range(1, self.p.A)) + [0]:
            self.direct[k].start()

    def forward(self):
        for k in range(1, self.p.A):
            self.direct[k].wait_recv()
            self.passed[k].start()

    def finish(self):
        self.direct[0].wait_recv()
        for copy in self.passed.values():
            copy.wait_recv()

    def drain(self):
        drain(list(self.direct.values()) + list(self.passed.values()))


class OwnerSpread:
    def __init__(self, p, block, sems):
        self.p = p
        s0, s1, rx, rp = sems
        self.across = remote(block, block, s0.at[0], rx.at[0], p.same(1))
        self.beside = remote(block, block, s1.at[0], rp.at[0], p.partner)
        self.mine = p.z == p.me
        self.relay = p.z == p.same(1)
        self.other = jnp.logical_not(jnp.logical_or(self.mine, self.relay))

    @staticmethod
    def sems():
        return dma_sems(1, 1, 1, 1)

    def start(self):
        @pl.when(self.mine)
        def _():
            self.across.start()
            self.beside.start()

    def forward(self):
        @pl.when(self.relay)
        def _():
            self.across.wait_recv()
            self.beside.start()

    def finish(self):
        @pl.when(self.other)
        def _():
            self.beside.wait_recv()

    def drain(self):
        @pl.when(self.mine)
        def _():
            self.across.wait_send()

        @pl.when(jnp.logical_not(self.other))
        def _():
            self.beside.wait_send()

class RepScatter:
    def __init__(self, p, part, T, bufs, sems, cols=None):
        self.p, self.part, self.T = p, part, T
        cols = pl.ds(0, part.shape[1]) if cols is None else cols
        self.cols = cols
        self.near, self.out, self.far = bufs
        near_s, near_r, far_s, far_r = sems
        self.first = {
            k: remote(
                part.at[rows_of(p.other(k), T), cols],
                self.near.at[k, :, cols],
                near_s.at[k],
                near_r.at[k],
                p.partner,
            )
            for k in range(p.A)
        }
        self.second = {
            k: remote(
                self.out.at[k - 1, :, cols],
                self.far.at[k - 1, :, cols],
                far_s.at[k - 1],
                far_r.at[k - 1],
                p.same(k),
            )
            for k in range(1, p.A)
        }

    @staticmethod
    def bufs(A, T, D):
        return [pltpu.VMEM((n, T, D), BF) for n in (A, A - 1, A - 1)]

    @staticmethod
    def sems(A):
        return dma_sems(A, A, A - 1, A - 1)

    def start_far(self):
        for k in range(1, self.p.A):
            self.first[k].start()

    def start_near(self):
        self.first[0].start()

    def pass_on(self):
        for k in range(1, self.p.A):
            self.first[k].wait_recv()
            base = self.p.same(k) * self.T

            def add(i, _, k=k, base=base):
                mine = self.part[step_rows(i, base), self.cols].astype(F32)
                near = self.near[k, step_rows(i), self.cols].astype(F32)
                self.out[k - 1, step_rows(i), self.cols] = (mine + near).astype(BF)
                return 0

            lax.fori_loop(0, self.T // STEP, add, 0)
            self.second[k].start()

    def finish(self):
        self.first[0].wait_recv()
        for copy in self.second.values():
            copy.wait_recv()

    def read(self, i):
        total = self.part[step_rows(i, self.p.me * self.T), :].astype(F32)
        total = total + self.near[0, step_rows(i), :].astype(F32)
        for k in range(1, self.p.A):
            total = total + self.far[k - 1, step_rows(i), :].astype(F32)
        return total

    def drain(self):
        drain(list(self.first.values()) + list(self.second.values()))


STEP = 32


def step_rows(i, base=None):
    start = i * STEP if base is None else base + i * STEP
    return pl.ds(pl.multiple_of(start, STEP), STEP)


class TokenSpread:
    def __init__(self, p, full, T, sems):
        self.p = p
        dir_s, dir_r, fwd_s, fwd_r = sems
        own = full.at[rows_of(p.me, T)]
        self.direct = {0: remote(own, own, dir_s.at[0], dir_r.at[0], p.partner)}
        self.passed = {}
        for k in range(1, p.A):
            self.direct[k] = remote(own, own, dir_s.at[k], dir_r.at[k], p.same(k))
            block = full.at[rows_of(p.same(p.A - k), T)]
            self.passed[k] = remote(block, block, fwd_s.at[k - 1], fwd_r.at[k - 1], p.partner)

    @staticmethod
    def sems(A):
        return dma_sems(A, A, A - 1, A - 1)

    def start(self):
        for k in list(range(1, self.p.A)) + [0]:
            self.direct[k].start()

    def beside(self):
        self.direct[0].wait_recv()

    def across(self):
        for k in range(1, self.p.A):
            self.direct[k].wait_recv()
            self.passed[k].start()
        for copy in self.passed.values():
            copy.wait_recv()

    def drain(self):
        drain(list(self.direct.values()) + list(self.passed.values()))


class Bag:
    def __init__(self):
        self.names, self.specs = [], []

    def want(self, name, specs):
        specs = specs if isinstance(specs, list) else [specs]
        self.names.append((name, len(specs)))
        self.specs += specs

    def hand_out(self, refs):
        got, at = {}, 0
        for name, n in self.names:
            got[name] = refs[at] if n == 1 else list(refs[at : at + n])
            at += n
        return got


def fold(v):
    return jnp.sum(v.reshape(v.shape[0] // 8, 8, v.shape[1]), axis=0)


TILE = 256
QUARTERS = 4


def tiles(n, body):
    def step(i, _):
        body(pl.ds(pl.multiple_of(i * TILE, TILE), TILE))
        return 0

    lax.fori_loop(0, n // TILE, step, 0)


def layer(x, cot, wq, wk, wv, wo, wi, wd, vectors, S, R):
    T, D = x.shape
    ds, fs = wq.shape[0], wd.shape[0]
    dr, fr = D // R, fs // R
    V = S * fr
    W = 3 * dr
    Z, A = S // 2, R // 2
    nv = len(vectors)
    N = R * T
    C = N // A
    pairs = dr // 128
    half = V // 2
    wide = D // QUARTERS

    bag = Bag()
    bag.want("here", pltpu.SemaphoreType.DMA((S + 6,)))
    bag.want("small", pltpu.VMEM((S * NVEC, ds), F32))
    bag.want("flat", pltpu.VMEM((NVEC, D), F32))
    for name, shape, t in (
        ("x_all", (N, D), BF),
        ("wqkv", (D, W), BF),
        ("wor", (dr, D), BF),
        ("wir", (D, V), BF),
        ("wdr", (V, D), BF),
        ("qkv", (N, W), BF),
        ("probs", (N * dr // HEAD_DIM, SEQ), F32),
        ("ctx", (N, dr), BF),
        ("part", (N, D), BF),
        ("normed", (T, D), F32),
        ("rstd", (T, 128), F32),
        ("hidden", (T, D), F32),
        ("hid_all", (N, D), BF),
        ("acted", (N, V), BF),
        ("slope", (N, V), F32),
        ("d_two", (T, D), F32),
        ("d2_all", (N, D), BF),
        ("d_in", (N, V), BF),
        ("d_one", (T, D), F32),
        ("d1_all", (N, D), BF),
        ("dctx", (N, dr), BF),
        ("dqkv", (N, W), BF),
        ("sums", (48, D), F32),
        ("gbi8", (8, V), F32),
        ("gqv8", (8, 2 * dr), F32),
        ("gflat", (NVEC, D), F32),
        ("gs", (S * NVEC, ds), F32),
        ("gwd", (V, D), BF),
        ("gwi", (D, V), BF),
        ("gqkv", (D, W), BF),
        ("gwo", (dr, D), BF),
    ):
        bag.want(name, pltpu.VMEM(shape, t))
    for name in ("smalls", "g_qkv", "g_wia", "g_wib", "g_wd0", "g_wd1"):
        bag.want(name, RowGather.sems(Z))
    bag.want("g_wd2", SideGather.sems(Z))
    bag.want("g_wo", PlaneGather.sems(Z))
    for name in ("ax", "a1", "a2", "a3"):
        bag.want(name, TokenSpread.sems(A))
    for name in ("t1", "t2", "t3", "t4"):
        bag.want(name + "b", RepScatter.bufs(A, T, D))
        bag.want(name + "s", RepScatter.sems(A))
    bag.want("t2z", RepScatter.sems(A))
    for name, n, c, t in (
        ("rwd", fr, D // 2, BF),
        ("rwi", ds, V, BF),
        ("rqk", ds, 2 * dr, BF),
        ("rv", ds, dr, BF),
        ("rsm", NVEC, ds, F32),
    ):
        bag.want(name + "b", RowScatter.bufs(n, c, t))
        bag.want(name + "s", RowScatter.sems())
        bag.want(name + "p", RepSpread.sems(A))
    bag.want("rwxb", SideScatter.bufs(fr, D // 2, BF))
    bag.want("rwxs", SideScatter.sems())
    bag.want("rwob", PlaneScatter.bufs(Z, ds, D, BF))
    bag.want("rwos", PlaneScatter.sems(Z))
    bag.want("rwop", OwnerSpread.sems())

    def kernel(*refs):
        x, cot, wq, wk, wv, wo, wi, wd = refs[:8]
        vecs = refs[8 : 8 + nv]
        at = 8 + nv
        out_o, gin_o, tq, ti, td, to, ts = refs[at : at + 7]
        b = bag.hand_out(refs[at + 7 :])
        x_all, wqkv, wor, wir, wdr = b["x_all"], b["wqkv"], b["wor"], b["wir"], b["wdr"]
        qkv, probs, ctx, part = b["qkv"], b["probs"], b["ctx"], b["part"]
        flat, small, here = b["flat"], b["small"], b["here"]
        normed_r, rstd_r, hidden_r = b["normed"], b["rstd"], b["hidden"]
        hid_all, acted, slope, d_two_r, d2_all = (
            b["hid_all"],
            b["acted"],
            b["slope"],
            b["d_two"],
            b["d2_all"],
        )
        d_in, d_one_r, d1_all, dctx, dqkv = b["d_in"], b["d_one"], b["d1_all"], b["dctx"], b["dqkv"]
        sums, gbi8, gqv8, gflat, gs = b["sums"], b["gbi8"], b["gqv8"], b["gflat"], b["gs"]
        gwd, gwi, gqkv, gwo = b["gwd"], b["gwi"], b["gqkv"], b["gwo"]

        p = Place(S, R)
        mine = rows_of(p.s, ds)
        own_tok = rows_of(p.me, T)
        own_chip = rows_of(p.a, C)
        far_chip = rows_of(p.chip(1), C)
        cols = pl.ds(pl.multiple_of(p.me * dr, dr), dr)
        local = []

        def bring(src, dst):
            copy = pltpu.make_async_copy(src, dst, here.at[len(local)])
            copy.start()
            local.append(copy)

        for i, w in enumerate((wq, wk, wv)):
            bring(w.at[:, cols], wqkv.at[mine, pl.ds(i * dr, dr)])
        for c in range(S):
            piece = pl.ds(pl.multiple_of(c * fs + p.me * fr, fr), fr)
            bring(wi.at[:, piece], wir.at[mine, pl.ds(c * fr, fr)])
        bring(wd.at[rows_of(p.me, fr)], wdr.at[mine])
        own_wo = pltpu.make_async_copy(wo, wor.at[rows_of(p.y, ds)], here.at[len(local)])

        @pl.when(p.z == p.me)
        def _():
            own_wo.start()

        piece = pl.ds(pl.multiple_of(p.me * fr, fr), fr)
        pieces = [v[...] for v in vecs[:-1]] + [vecs[-1][:, piece]]
        pieces.append(jnp.zeros((NVEC - nv, ds), F32))
        small[rows_of(p.s, NVEC), :] = jnp.concatenate(pieces, 0)
        x_all[own_tok, :] = x[...]
        p.meet_all()

        smalls = RowGather(p, small, NVEC, b["smalls"])
        g_qkv = RowGather(p, wqkv, ds, b["g_qkv"])
        left, right = pl.ds(0, half), pl.ds(half, half)
        g_wia = RowGather(p, wir, ds, b["g_wia"], left)
        g_wib = RowGather(p, wir, ds, b["g_wib"], right)
        g_wd0 = RowGather(p, wdr, fr, b["g_wd0"], pl.ds(0, wide))
        g_wd1 = RowGather(p, wdr, fr, b["g_wd1"], pl.ds(wide, wide))
        g_wd2 = SideGather(p, wdr, fr, b["g_wd2"], pl.ds(2 * wide, 2 * wide))
        g_wo = PlaneGather(p, wor, ds, b["g_wo"])
        ax = TokenSpread(p, x_all, T, b["ax"])
        a1 = TokenSpread(p, hid_all, T, b["a1"])
        a2 = TokenSpread(p, d2_all, T, b["a2"])
        a3 = TokenSpread(p, d1_all, T, b["a3"])
        t1 = RepScatter(p, part, T, b["t1b"], b["t1s"])
        t2 = RepScatter(p, part, T, b["t2b"], b["t2s"], pl.ds(0, D // 2))
        t2z = RepScatter(p, part, T, b["t2b"], b["t2z"], pl.ds(D // 2, D // 2))
        t3 = RepScatter(p, part, T, b["t3b"], b["t3s"])
        t4 = RepScatter(p, part, T, b["t4b"], b["t4s"])
        rwd = RowScatter(p, gwd, fr, b["rwdb"], b["rwds"], pl.ds(0, D // 2))
        rwx = SideScatter(p, gwd, fr, b["rwxb"], b["rwxs"], pl.ds(D // 2, D // 2))
        rwi = RowScatter(p, gwi, ds, b["rwib"], b["rwis"])
        qk_cols, v_cols = pl.ds(0, 2 * dr), pl.ds(2 * dr, dr)
        rqk = RowScatter(p, gqkv, ds, b["rqkb"], b["rqks"], qk_cols)
        rv = RowScatter(p, gqkv, ds, b["rvb"], b["rvs"], v_cols)
        rsm = RowScatter(p, gs, NVEC, b["rsmb"], b["rsms"])
        rwo = PlaneScatter(p, gwo, ds, b["rwob"], b["rwos"])
        sd = RepSpread(p, td, b["rwdp"])
        si = RepSpread(p, ti, b["rwip"])
        sq = RepSpread(p, tq, b["rqkp"], qk_cols)
        sv = RepSpread(p, tq, b["rvp"], v_cols)
        ss = RepSpread(p, ts, b["rsmp"])
        so = OwnerSpread(p, to, b["rwop"])

        smalls.start()
        for copy in local[:3]:
            copy.wait()
        g_qkv.start()
        ax.start()
        for copy in local[3:]:
            copy.wait()

        @pl.when(p.z == p.me)
        def _():
            own_wo.wait()

        g_wo.start()
        g_wia.start()
        sums[...] = jnp.zeros_like(sums)
        gbi8[...] = jnp.zeros_like(gbi8)
        gqv8[...] = jnp.zeros_like(gqv8)
        gflat[...] = jnp.zeros_like(gflat)
        smalls.push()
        g_qkv.push()
        smalls.pull()
        g_qkv.pull()
        g_wib.start()
        g_wd2.begin()
        g_wd0.start()
        g_wd1.start()
        g_wd2.start()
        smalls.finish()
        for i in range(nv):
            row = [small[s * NVEC + i : s * NVEC + i + 1, :] for s in range(S)]
            flat[i : i + 1, :] = jnp.concatenate(row, 1)
        ax.beside()
        ax.across()
        g_qkv.finish()

        low = lax.broadcasted_iota(jnp.int32, (SEQ, 128), 1) < HEAD_DIM
        keep = (low, jnp.logical_not(low))

        def project(rows):
            for n in range(3):
                c = pl.ds(n * dr, dr)
                z = mm(x_all[rows, :], wqkv[:, c])
                if n == 0:
                    z = z + flat[0:1, cols]
                if n == 2:
                    z = z + flat[1:2, cols]
                qkv[rows, c] = z.astype(BF)

        def pick(v, h):
            return jnp.where(keep[h], v, jnp.zeros_like(v))

        def attend(chip):
            def one(j, _):
                seq = chip * (C // SEQ) + j
                rows = rows_of(seq, SEQ)
                for n in range(pairs):
                    q2 = qkv[rows, n * 128 : n * 128 + 128]
                    k2 = qkv[rows, dr + n * 128 : dr + n * 128 + 128]
                    v2 = qkv[rows, 2 * dr + n * 128 : 2 * dr + n * 128 + 128]
                    got = []
                    for h in range(2):
                        scores = mm_nt(pick(q2, h), k2) * 0.125
                        e = jnp.exp(scores - jnp.max(scores, axis=-1, keepdims=True))
                        pr = e / jnp.sum(e, axis=-1, keepdims=True)
                        probs[rows_of(seq * 2 * pairs + 2 * n + h, SEQ), :] = pr
                        got.append(mm(pr.astype(BF), v2))
                    ctx[rows, n * 128 : n * 128 + 128] = jnp.where(low, got[0], got[1]).astype(BF)
                return 0

            lax.fori_loop(0, C // SEQ, one, 0)

        def attn_part(rows):
            def tile(c):
                part[rows, c] = mm(ctx[rows, :], wor[:, c]).astype(BF)

            tiles(D, tile)

        def inner(rows):
            def tile(c):
                z = mm(hid_all[rows, :], wir[:, c]) + flat[8:9, c]
                phi = 0.5 * (1.0 + lax.erf(z * INV_ROOT_TWO))
                acted[rows, c] = (z * phi).astype(BF)
                slope[rows, c] = phi + z * jnp.exp(-0.5 * z * z) * INV_ROOT_TWO_PI

            tiles(V, tile)

        def down(rows, q):
            c = pl.ds(q * wide, wide)
            part[rows, c] = mm(acted[rows, :], wdr[:, c]).astype(BF)

        def d_inner(rows):
            def tile(c):
                d = mm_nt(d2_all[rows, :], wdr[c, :]) * slope[rows, c]
                gbi8[:, c] += fold(d)
                d_in[rows, c] = d.astype(BF)

            tiles(V, tile)

        def hid_part(rows):
            def tile(c):
                part[rows, c] = mm_nt(d_in[rows, :], wir[c, :]).astype(BF)

            tiles(D, tile)

        def d_attend(chip):
            rows = rows_of(chip, C)
            dctx[rows, :] = mm_nt(d1_all[rows, :], wor[...]).astype(BF)

            def one(j, _):
                seq = chip * (C // SEQ) + j
                rows = rows_of(seq, SEQ)
                for n in range(pairs):
                    lanes = [slice(m * dr + n * 128, m * dr + n * 128 + 128) for m in range(3)]
                    q2, k2, v2 = (qkv[rows, c] for c in lanes)
                    dc2 = dctx[rows, lanes[0]]
                    got = []
                    for h in range(2):
                        pr = probs[rows_of(seq * 2 * pairs + 2 * n + h, SEQ), :]
                        dp = mm_nt(pick(dc2, h), v2)
                        delta = jnp.sum(pr * dp, axis=-1, keepdims=True)
                        dsc = (pr * (dp - delta) * 0.125).astype(BF)
                        got.append((mm(dsc, k2), mm_tn(dsc, q2), mm_tn(pr.astype(BF), dc2)))
                    dq, dk, dv = (jnp.where(low, u, w) for u, w in zip(*got))
                    gqv8[:, lanes[0]] += fold(dq)
                    gqv8[:, lanes[1]] += fold(dv)
                    for v, c in zip((dq, dk, dv), lanes):
                        dqkv[rows, c] = v.astype(BF)
                return 0

            lax.fori_loop(0, C // SEQ, one, 0)

        def in_part(rows):
            def tile(c):
                part[rows, c] = mm_nt(dqkv[rows, :], wqkv[c, :]).astype(BF)

            tiles(D, tile)

        def grad_plane(lhs, rhs, dst, z):
            both = pl.ds(pl.multiple_of(z * 2 * ds, 2 * ds), 2 * ds)
            dst[both, :] = mm_tn(lhs[:, both], rhs[...]).astype(BF)

        def grad_all(lhs, rhs, dst, *scatters):
            for j in (1, 2, 0, 3):
                grad_plane(lhs, rhs, dst, rwi.line.zs[j])
                for g in scatters:
                    g.launch(j)

        project(far_chip)
        g_wo.forward()
        g_wia.push()
        project(own_chip)
        attend(p.chip(1))
        g_wo.finish()
        attn_part(far_chip)
        t1.start_far()
        g_wd2.follow()
        attend(p.a)
        g_wib.push()
        g_wd0.push()
        attn_part(own_chip)
        t1.start_near()
        t1.pass_on()
        g_wia.pull()
        t1.finish()

        def norm_one(i, _):
            at = step_rows(i)
            normed, rstd = norm_parts(x[at, :].astype(F32) + t1.read(i) + flat[2:3, :])
            hidden = normed * flat[3:4, :] + flat[4:5, :]
            normed_r[at, :] = normed
            rstd_r[at, :] = jnp.broadcast_to(rstd, (STEP, 128))
            hidden_r[at, :] = hidden
            hid_all[step_rows(i, p.me * T), :] = hidden.astype(BF)
            return 0

        lax.fori_loop(0, T // STEP, norm_one, 0)
        a1.start()
        t1.drain()
        g_wd1.push()
        g_wib.pull()
        a1.beside()
        a1.across()
        g_wd2.push()
        g_wia.finish()
        g_wib.finish()
        inner(own_chip)
        g_wd0.pull()
        g_wd1.pull()
        inner(far_chip)
        g_wd0.finish()
        down(far_chip, 0)
        g_wd1.finish()
        down(far_chip, 1)
        t2.start_far()
        down(own_chip, 0)
        down(own_chip, 1)
        t2.start_near()
        t2.pass_on()
        g_wd2.pull()
        down(far_chip, 2)
        down(far_chip, 3)
        t2z.start_far()
        down(own_chip, 2)
        down(own_chip, 3)
        t2z.start_near()
        t2z.pass_on()
        t2.finish()
        t2z.finish()

        def norm_two(i, _):
            at = step_rows(i)
            normed, rstd = norm_parts(hidden_r[at, :] + t2.read(i) + flat[5:6, :])
            out_o[at, :] = (normed * flat[6:7, :] + flat[7:8, :]).astype(BF)
            dout = cot[at, :].astype(F32)
            d_two = norm_back(dout * flat[6:7, :], normed, rstd)
            sums[24:32, :] += fold(d_two)
            sums[32:40, :] += fold(dout * normed)
            sums[40:48, :] += fold(dout)
            d_two_r[at, :] = d_two
            d2_all[step_rows(i, p.me * T), :] = d_two.astype(BF)
            return 0

        lax.fori_loop(0, T // STEP, norm_two, 0)
        a2.start()
        t2.drain()
        t2z.drain()
        a2.beside()
        d_inner(own_chip)
        a2.across()
        grad_all(acted, d2_all, gwd, rwd, rwx)
        d_inner(far_chip)
        hid_part(far_chip)
        t3.start_far()
        hid_part(own_chip)
        t3.start_near()
        t3.pass_on()
        grad_all(hid_all, d_in, gwi, rwi)
        for j in (1, 2, 0):
            rwd.lift(j)
        rwx.relay(1)
        rwx.relay(2)
        t3.finish()

        def back_one(i, _):
            at = step_rows(i)
            d_hidden = d_two_r[at, :] + t3.read(i)
            normed = normed_r[at, :]
            d_one = norm_back(d_hidden * flat[3:4, :], normed, rstd_r[at, 0:1])
            sums[0:8, :] += fold(d_one)
            sums[8:16, :] += fold(d_hidden * normed)
            sums[16:24, :] += fold(d_hidden)
            d_one_r[at, :] = d_one
            d1_all[step_rows(i, p.me * T), :] = d_one.astype(BF)
            return 0

        lax.fori_loop(0, T // STEP, back_one, 0)
        a3.start()
        t3.drain()
        rwd.relay(1)
        rwd.relay(2)
        a3.beside()
        d_attend(p.a)
        a3.across()
        gwo[...] = mm_tn(ctx[...], d1_all[...]).astype(BF)
        rwo.start()
        rwi.lift(1)
        d_attend(p.chip(1))
        gflat[0:1, cols] = jnp.sum(gqv8[:, :dr], axis=0, keepdims=True)
        gflat[1:2, cols] = jnp.sum(gqv8[:, dr:], axis=0, keepdims=True)
        for i in range(6):
            gflat[i + 2 : i + 3, :] = jnp.sum(sums[8 * i : 8 * i + 8, :], axis=0, keepdims=True)
        gflat[8:9, :] = jnp.sum(gbi8[...], axis=0, keepdims=True)
        for s in range(S):
            gs[s * NVEC : (s + 1) * NVEC, :] = gflat[:, s * ds : (s + 1) * ds]
        rsm.start()
        rwi.lift(2)
        rwx.cross()
        grad_all(x_all, dqkv, gqkv, rqk, rv)
        rwi.lift(0)
        rwi.relay(1)
        in_part(far_chip)
        t4.start_far()
        in_part(own_chip)
        t4.start_near()
        t4.pass_on()
        rwi.relay(2)
        rwd.total(td)
        t4.finish()

        def last(i, _):
            at = step_rows(i)
            gin_o[at, :] = (d_one_r[at, :] + t4.read(i)).astype(BF)
            return 0

        lax.fori_loop(0, T // STEP, last, 0)
        rwo.pass_on()
        for j in (1, 2, 0):
            rsm.lift(j)
        rwx.total(td)
        sd.start()
        for g in (rqk, rv):
            g.lift(1)
        rsm.relay(1)
        rsm.relay(2)
        for g in (rqk, rv):
            g.lift(2)
        rqk.relay(1)
        rwi.total(ti)
        si.start()
        rv.relay(1)
        sd.forward()
        for g in (rqk, rv):
            g.lift(0)
        rqk.relay(2)
        rv.relay(2)
        rwo.total(to)
        so.start()
        rsm.total(ts)
        ss.start()
        si.forward()
        rqk.total(tq)
        sq.start()
        so.forward()
        rv.total(tq)
        sv.start()
        ss.forward()
        sd.finish()
        si.finish()
        so.finish()
        sq.forward()
        sv.forward()
        sq.finish()
        sv.finish()
        ss.finish()
        for g in (smalls, g_qkv, g_wo, g_wia, g_wib, g_wd0, g_wd1, g_wd2, ax, a1, a2, a3, t4):
            g.drain()
        for g in (rwd, rwx, rwi, rqk, rv, rsm, rwo, sd, si, sq, sv, ss, so):
            g.drain()

    ins = [x, cot, wq, wk, wv, wo, wi, wd] + [v[None] for v in vectors]
    outs = [((T, D), BF)] * 2
    outs += [((R, ds, W), BF), ((R, ds, V), BF), ((R, fr, D), BF), ((ds, D), BF)]
    outs += [((R, NVEC, ds), F32)]
    return pl.pallas_call(
        kernel,
        out_shape=[jax.ShapeDtypeStruct(*o) for o in outs],
        in_specs=[VMEM_SPEC] * 2 + [ANY_SPEC] * 6 + [VMEM_SPEC] * nv,
        out_specs=[VMEM_SPEC] * len(outs),
        scratch_shapes=bag.specs,
        compiler_params=pltpu.CompilerParams(
            collective_id=12, has_side_effects=True, vmem_limit_bytes=LIMIT
        ),
        cost_estimate=pl.CostEstimate(
            flops=10 * 10**9, bytes_accessed=24 << 20, transcendentals=4 << 20
        ),
    )(*ins)


def widen(out, gin, tq, ti, td, to, ts, S):
    R, ds, W = tq.shape
    D, dr = R * W // 3, W // 3
    fr, V = td.shape[1], ti.shape[2]
    fs = fr * R
    T = out.shape[0]
    few, tok = ds // R, T // R

    def kernel(out, gin, tq, ti, td, to, ts, out_o, gin_o, oq, ok, ov, oo, oi, od, *vec_o):
        out_o[...] = out[...]
        gin_o[...] = gin[...]
        od[...] = td[0].astype(F32)
        oo[...] = to[...].astype(F32)
        for r in range(R):
            for n, o in enumerate((oq, ok, ov)):
                o[:, r * dr : (r + 1) * dr] = tq[r, :, n * dr : (n + 1) * dr].astype(F32)
            for c in range(S):
                lo = c * fs + r * fr
                oi[:, lo : lo + fr] = ti[r, :, c * fr : (c + 1) * fr].astype(F32)

        @pl.when(pl.program_id(0) == 0)
        def _():
            total = ts[0]
            for r in range(1, R):
                total = total + ts[r]
            for i in range(8):
                vec_o[i][...] = total[i : i + 1, :]
            for r in range(R):
                vec_o[8][:, r * fr : (r + 1) * fr] = ts[r, 8:9, :]

    def rows(n, c):
        return pl.BlockSpec((n, c), lambda i: (i, 0))

    def slab(n, c):
        return pl.BlockSpec((R, n, c), lambda i: (0, i, 0))

    def whole(*shape):
        return pl.BlockSpec(shape, lambda i: (0,) * len(shape))

    outs = [((T, D), BF)] * 2 + [((ds, D), F32)] * 4 + [((ds, S * fs), F32), ((fs, D), F32)]
    outs += [((1, ds), F32)] * 8 + [((1, fs), F32)]
    return pl.pallas_call(
        kernel,
        grid=(R,),
        out_shape=[jax.ShapeDtypeStruct(*o) for o in outs],
        in_specs=[
            rows(tok, D),
            rows(tok, D),
            slab(few, W),
            slab(few, V),
            pl.BlockSpec((1, fr, D), lambda i: (i, 0, 0)),
            rows(few, D),
            whole(R, NVEC, ds),
        ],
        out_specs=[rows(tok, D)] * 2
        + [rows(few, D)] * 4
        + [rows(few, S * fs), rows(fr, D)]
        + [whole(1, ds)] * 8
        + [whole(1, fs)],
        compiler_params=pltpu.CompilerParams(vmem_limit_bytes=LIMIT),
    )(out, gin, tq, ti, td, to, ts)


def fast_body(
    block_input,
    out_cotangent,
    w_query,
    w_key,
    w_value,
    w_output,
    bias_query,
    bias_value,
    bias_output,
    gain_first,
    shift_first,
    w_inner,
    bias_inner,
    w_down,
    bias_down,
    gain_second,
    shift_second,
):
    vectors = (
        bias_query,
        bias_value,
        bias_output,
        gain_first,
        shift_first,
        bias_down,
        gain_second,
        shift_second,
        bias_inner,
    )
    S = lax.axis_size("shard")
    got = layer(
        block_input,
        out_cotangent,
        w_query,
        w_key,
        w_value,
        w_output,
        w_inner,
        w_down,
        vectors,
        S,
        lax.axis_size("rep"),
    )
    got = widen(*got, S)
    output, grad_input, gq, gk, gv, go, gi, gd = got[:8]
    gbq, gbv, gbo, ggone, gsone, gbd, ggtwo, gstwo, gbi = (v.reshape(-1) for v in got[8:])
    return (
        output,
        grad_input,
        gq,
        gk,
        gv,
        go,
        gbq,
        gbv,
        gbo,
        ggone,
        gsone,
        gi,
        gbi,
        gd,
        gbd,
        ggtwo,
        gstwo,
    )


def fits_fast(mesh):
    S, R = mesh.shape["shard"], mesh.shape["rep"]
    return R == 4 and S == 8


def solution(mesh):
    tokens = P(("shard", "rep"), None)
    mat = P("shard", None)
    vec = P("shard")
    params = (mat, mat, mat, mat, vec, vec, vec, vec, vec, mat, vec, mat, vec, vec, vec)
    return jax.shard_map(
        fast_body if fits_fast(mesh) else body,
        mesh=mesh,
        in_specs=(tokens, tokens) + params,
        out_specs=(tokens, tokens) + params,
        check_vma=False,
    )
```

```python
import jax
import jax.numpy as jnp
from jax import lax
from jax.experimental import pallas as pl
from jax.experimental.pallas import tpu as pltpu
from jax.sharding import PartitionSpec as P

HEAD_DIM = 64
SEQ = 128
PAD = 16


EPS = 1e-06
INV_ROOT_TWO = 0.7071067811865476
INV_ROOT_TWO_PI = 0.3989422804014327
BF = jnp.bfloat16
F32 = jnp.float32


def norm_parts(resid):
    centre = resid - jnp.mean(resid, axis=-1, keepdims=True)
    variance = jnp.mean(centre * centre, axis=-1, keepdims=True)
    rstd = lax.rsqrt(variance + EPS)
    return (centre * rstd, rstd)


def norm_back(upstream, normed, rstd):
    return rstd * (
        upstream
        - jnp.mean(upstream, axis=-1, keepdims=True)
        - normed * jnp.mean(upstream * normed, axis=-1, keepdims=True)
    )


def mm(a, b):
    return jnp.dot(a, b, preferred_element_type=F32)


def mm_nt(a, b):
    return lax.dot_general(a, b, (((1,), (1,)), ((), ())), preferred_element_type=F32)


def mm_tn(a, b):
    return lax.dot_general(a, b, (((0,), (0,)), ((), ())), preferred_element_type=F32)


def ein(spec, a, b):
    return jnp.einsum(spec, a, b, preferred_element_type=F32)


MESH = pl.DeviceIdType.MESH
CHUNK = 16


class Peers:
    def __init__(self, R):
        self.R, self.A = R, R // 2
        self.me = lax.axis_index("rep")
        self.c = lax.rem(self.me, 2)
        self.a = lax.div(self.me, 2)
        self.partner = self.me + 1 - 2 * self.c

    def chip(self, k):
        return lax.rem(self.a + k, self.A)

    def same(self, k):
        return 2 * self.chip(k) + self.c

    def other(self, k):
        return 2 * self.chip(k) + 1 - self.c

    def meet(self):
        barrier = pltpu.get_barrier_semaphore()
        for dev in [self.partner] + [self.same(k) for k in range(1, self.A)]:
            pl.semaphore_signal(barrier, inc=1, device_id={"rep": dev}, device_id_type=MESH)
        pl.semaphore_wait(barrier, self.A)


def rows_of(index, T):
    return pl.ds(pl.multiple_of(index * T, T), T)


def chunk_rows(i, base=None):
    start = i * CHUNK if base is None else base + i * CHUNK
    return pl.ds(pl.multiple_of(start, CHUNK), CHUNK)


def remote(src, dst, send, recv, dev):
    return pltpu.make_async_remote_copy(
        src_ref=src,
        dst_ref=dst,
        send_sem=send,
        recv_sem=recv,
        device_id={"rep": dev},
        device_id_type=MESH,
    )


def scatter_sum(p, part, T, near, far, out, sems):
    near_s, near_r, far_s, far_r = sems
    order = list(range(1, p.A)) + [0]
    first = {
        k: remote(
            part.at[rows_of(p.other(k), T)], near.at[k], near_s.at[k], near_r.at[k], p.partner
        )
        for k in order
    }
    for k in order:
        first[k].start()
    second = []
    for k in range(1, p.A):
        first[k].wait_recv()
        base = p.same(k) * T

        def add(i, _, k=k, base=base):
            mine = part[chunk_rows(i, base), :].astype(F32)
            out[k - 1, chunk_rows(i), :] = (mine + near[k, chunk_rows(i), :].astype(F32)).astype(BF)
            return 0

        lax.fori_loop(0, T // CHUNK, add, 0)
        copy = remote(out.at[k - 1], far.at[k - 1], far_s.at[k - 1], far_r.at[k - 1], p.same(k))
        copy.start()
        second.append(copy)
    first[0].wait_recv()
    for copy in second:
        copy.wait_recv()

    def read(i):
        total = part[chunk_rows(i, p.me * T), :].astype(F32) + near[0, chunk_rows(i), :].astype(F32)
        for k in range(1, p.A):
            total = total + far[k - 1, chunk_rows(i), :].astype(F32)
        return total

    return read, list(first.values()) + second


def spread(p, src, full, T, sems):
    dir_s, dir_r, fwd_s, fwd_r = sems
    mine = full.at[rows_of(p.me, T)]
    direct = {}
    for k in list(range(1, p.A)) + [0]:
        dev = p.partner if k == 0 else p.same(k)
        direct[k] = remote(src, mine, dir_s.at[k], dir_r.at[k], dev)
        direct[k].start()
    passed = []
    for k in range(1, p.A):
        direct[k].wait_recv()
        block = full.at[rows_of(p.same(p.A - k), T)]
        copy = remote(block, block, fwd_s.at[k - 1], fwd_r.at[k - 1], p.partner)
        copy.start()
        passed.append(copy)
    direct[0].wait_recv()
    for copy in passed:
        copy.wait_recv()
    return list(direct.values()) + passed


def drain(copies):
    for copy in copies:
        copy.wait_send()


def run_kernel(kernel, cid, T, D, R, ins, outs, scatter, gather):
    A = R // 2
    few = max(A - 1, 1)
    scratch = []
    if scatter:
        scratch += [
            pltpu.VMEM((A, T, D), BF),
            pltpu.VMEM((few, T, D), BF),
            pltpu.VMEM((few, T, D), BF),
        ]
        scratch += [pltpu.SemaphoreType.DMA((n,)) for n in (A, A, few, few)]
    if gather:
        scratch += [pltpu.SemaphoreType.DMA((n,)) for n in (A, A, few, few)]
    vmem = pl.BlockSpec(memory_space=pltpu.VMEM)
    return pl.pallas_call(
        kernel,
        out_shape=[jax.ShapeDtypeStruct(*o) for o in outs],
        in_specs=[vmem] * len(ins),
        out_specs=[vmem] * len(outs),
        scratch_shapes=scratch,
        compiler_params=pltpu.CompilerParams(collective_id=cid, has_side_effects=True),
        cost_estimate=pl.CostEstimate(flops=0, bytes_accessed=24 << 20, transcendentals=0),
    )(*ins)


def gather_kernel(block, R, cid):
    T, D = block.shape

    def kernel(src, full, *sems):
        p = Peers(R)
        p.meet()

        def put(i, _):
            full[chunk_rows(i, p.me * T), :] = src[chunk_rows(i), :]
            return 0

        lax.fori_loop(0, T // CHUNK, put, 0)
        drain(spread(p, src, full, T, sems))

    return run_kernel(kernel, cid, T, D, R, [block], [((R * T, D), BF)], False, True)[0]


def norm_one_step(partial, x, bo, gone, sone):
    T, D = x.shape
    R = partial.shape[0] // T

    def kernel(part, xr, bor, gr, sr, normed_o, rstd_o, hidden_o, full, near, far, out, *sems):
        p = Peers(R)
        p.meet()
        read, sent = scatter_sum(p, part, T, near, far, out, sems[:4])

        def step(i, _):
            normed, rstd = norm_parts(xr[chunk_rows(i), :].astype(F32) + read(i) + bor[...])
            hidden = normed * gr[...] + sr[...]
            normed_o[chunk_rows(i), :] = normed
            rstd_o[chunk_rows(i), :] = rstd
            hidden_o[chunk_rows(i), :] = hidden
            full[chunk_rows(i, p.me * T), :] = hidden.astype(BF)
            return 0

        lax.fori_loop(0, T // CHUNK, step, 0)
        drain(sent + spread(p, full.at[rows_of(p.me, T)], full, T, sems[4:]))

    ins = [partial, x, bo[None], gone[None], sone[None]]
    outs = [((T, D), F32), ((T, 1), F32), ((T, D), F32), ((R * T, D), BF)]
    return run_kernel(kernel, 1, T, D, R, ins, outs, True, True)


def add_sums(ref, values):
    for n, v in enumerate(values):
        ref[n : n + 1, :] += jnp.sum(v, axis=0, keepdims=True)


def norm_two_step(partial, hidden, bd, gtwo, stwo, cot):
    T, D = hidden.shape
    R = partial.shape[0] // T

    def kernel(part, hr, br, gr, sr, cr, out_o, d_o, sums, full, near, far, out, *sems):
        p = Peers(R)
        p.meet()
        sums[...] = jnp.zeros_like(sums)
        read, sent = scatter_sum(p, part, T, near, far, out, sems[:4])

        def step(i, _):
            normed, rstd = norm_parts(hr[chunk_rows(i), :] + read(i) + br[...])
            out_o[chunk_rows(i), :] = (normed * gr[...] + sr[...]).astype(BF)
            dout = cr[chunk_rows(i), :].astype(F32)
            d_two = norm_back(dout * gr[...], normed, rstd)
            add_sums(sums, (d_two, dout * normed, dout))
            d_o[chunk_rows(i), :] = d_two
            full[chunk_rows(i, p.me * T), :] = d_two.astype(BF)
            return 0

        lax.fori_loop(0, T // CHUNK, step, 0)
        drain(sent + spread(p, full.at[rows_of(p.me, T)], full, T, sems[4:]))

    ins = [partial, hidden, bd[None], gtwo[None], stwo[None], cot]
    outs = [((T, D), BF), ((T, D), F32), ((8, D), F32), ((R * T, D), BF)]
    return run_kernel(kernel, 2, T, D, R, ins, outs, True, True)


def back_one_step(partial, d_two, normed, rstd, gone):
    T, D = d_two.shape
    R = partial.shape[0] // T

    def kernel(part, dr, nr, rr, gr, d_o, sums, full, near, far, out, *sems):
        p = Peers(R)
        p.meet()
        sums[...] = jnp.zeros_like(sums)
        read, sent = scatter_sum(p, part, T, near, far, out, sems[:4])

        def step(i, _):
            d_hidden = dr[chunk_rows(i), :] + read(i)
            normed = nr[chunk_rows(i), :]
            d_one = norm_back(d_hidden * gr[...], normed, rr[chunk_rows(i), :])
            add_sums(sums, (d_one, d_hidden * normed, d_hidden))
            d_o[chunk_rows(i), :] = d_one
            full[chunk_rows(i, p.me * T), :] = d_one.astype(BF)
            return 0

        lax.fori_loop(0, T // CHUNK, step, 0)
        drain(sent + spread(p, full.at[rows_of(p.me, T)], full, T, sems[4:]))

    ins = [partial, d_two, normed, rstd, gone[None]]
    outs = [((T, D), F32), ((8, D), F32), ((R * T, D), BF)]
    return run_kernel(kernel, 3, T, D, R, ins, outs, True, True)


def input_step(partial, d_one):
    T, D = d_one.shape
    R = partial.shape[0] // T

    def kernel(part, dr, grad, near, far, out, *sems):
        p = Peers(R)
        p.meet()
        read, sent = scatter_sum(p, part, T, near, far, out, sems)

        def step(i, _):
            grad[chunk_rows(i), :] = (dr[chunk_rows(i), :] + read(i)).astype(BF)
            return 0

        lax.fori_loop(0, T // CHUNK, step, 0)
        drain(sent)

    return run_kernel(kernel, 4, T, D, R, [partial, d_one], [((T, D), BF)], True, False)[0]


def body(
    block_input,
    out_cotangent,
    w_query,
    w_key,
    w_value,
    w_output,
    bias_query,
    bias_value,
    bias_output,
    gain_first,
    shift_first,
    w_inner,
    bias_inner,
    w_down,
    bias_down,
    gain_second,
    shift_second,
):
    S = lax.axis_size("shard")
    R = lax.axis_size("rep")
    r = lax.axis_index("rep")
    T = block_input.shape[0]
    D = w_query.shape[1]
    ds = w_query.shape[0]
    dr = D // R
    fs = w_down.shape[0]
    fr = fs // R
    W = 4 * dr

    def cols(w):
        return lax.dynamic_slice(w, (0, r * dr), (ds, dr))

    small = jnp.concatenate(
        [
            v.astype(BF)
            for v in (
                bias_query,
                bias_value,
                bias_output,
                gain_first,
                shift_first,
                bias_down,
                gain_second,
                shift_second,
                bias_inner,
            )
        ]
    )
    n_small = small.shape[0]
    small = jnp.pad(small, (0, PAD * W - n_small)).reshape(PAD, W)
    pack = jnp.concatenate(
        [jnp.concatenate([cols(w_query), cols(w_key), cols(w_value), cols(w_output)], 1), small], 0
    )
    got = lax.all_gather(pack, "shard", axis=0)
    x_all = gather_kernel(block_input, R, 0)
    wi_r = lax.dynamic_index_in_dim(w_inner.reshape(ds, S, R, fr), r, 2, keepdims=False)
    V = S * fr
    dv = fr * D // V
    wd_r = lax.dynamic_slice(w_down, (r * fr, 0), (fr, D)).reshape(dv, V)
    mlp = lax.all_gather(jnp.concatenate([wi_r.reshape(ds, V), wd_r], 0), "shard", axis=0)
    wi = mlp[:, :ds].reshape(D, V)
    wd = mlp[:, ds:].reshape(V, D)
    wqkv = got[:, :ds, : 3 * dr].reshape(D, 3 * dr)
    wo = lax.all_to_all(
        got[:, :ds, 3 * dr :].reshape(D, dr), "rep", split_axis=0, concat_axis=1, tiled=True
    )
    flat = got[:, ds:, :].reshape(S, PAD * W)[:, :n_small].astype(F32)
    bq, bv, bo, gone, sone, bd, gtwo, stwo = (
        flat[:, i * ds : (i + 1) * ds].reshape(D) for i in range(8)
    )
    bi = lax.dynamic_index_in_dim(flat[:, 8 * ds :].reshape(S, R, fr), r, 1, keepdims=False)
    bi = bi.reshape(S * fr)
    bq = lax.dynamic_slice(bq, (r * dr,), (dr,))
    bv = lax.dynamic_slice(bv, (r * dr,), (dr,))

    N = R * T
    shape4 = (N // SEQ, SEQ, dr // HEAD_DIM, HEAD_DIM)
    qkv = mm(x_all, wqkv)
    query = (qkv[:, :dr] + bq).astype(BF).reshape(shape4)
    keyed = qkv[:, dr : 2 * dr].astype(BF).reshape(shape4)
    valued = (qkv[:, 2 * dr :] + bv).astype(BF).reshape(shape4)
    scores = ein("bqhe,bkhe->bhqk", query, keyed) * 0.125
    top = jnp.max(scores, axis=-1, keepdims=True)
    logsum = top + jnp.log(jnp.sum(jnp.exp(scores - top), axis=-1, keepdims=True))
    probs = jnp.exp(scores - logsum)
    probs_b = probs.astype(BF)
    context = ein("bhqk,bkhe->bqhe", probs_b, valued).astype(BF).reshape(N, dr)
    attn_part = mm(context, wo).astype(BF)

    normed_one, rstd_one, hidden, hidden_all = norm_one_step(attn_part, block_input, bo, gone, sone)
    inner = mm(hidden_all, wi) + bi
    phi = 0.5 * (1.0 + lax.erf(inner * INV_ROOT_TWO))
    acted = (inner * phi).astype(BF)
    slope = phi + inner * jnp.exp(-0.5 * inner * inner) * INV_ROOT_TWO_PI
    down_part = mm(acted, wd).astype(BF)

    output, d_two, sums_two, d_two_all = norm_two_step(
        down_part, hidden, bd, gtwo, stwo, out_cotangent
    )
    d_inner = mm_nt(d_two_all, wd) * slope
    g_bias_inner = jnp.sum(d_inner, axis=0)
    d_inner_b = d_inner.astype(BF)
    hid_part = mm_nt(d_inner_b, wi).astype(BF)
    g_wd = mm_tn(acted, d_two_all).astype(BF).reshape(S, dv, V)
    g_wi = mm_tn(hidden_all, d_inner_b).astype(BF).reshape(S, ds, V)
    g_mlp = lax.psum_scatter(
        jnp.concatenate([g_wi, g_wd], 1), "shard", scatter_dimension=0, tiled=True
    )[0]

    d_one, sums_one, d_one_all = back_one_step(hid_part, d_two, normed_one, rstd_one, gone)
    g_wo = mm_tn(context, d_one_all).astype(BF)
    g_wo = lax.all_to_all(g_wo, "rep", split_axis=1, concat_axis=0, tiled=True)
    d_context = mm_nt(d_one_all, wo).astype(BF).reshape(shape4)
    d_probs = ein("bqhe,bkhe->bhqk", d_context, valued)
    delta = jnp.sum(probs * d_probs, axis=-1, keepdims=True)
    d_scores = (probs * (d_probs - delta) * 0.125).astype(BF)
    d_query = ein("bhqk,bkhe->bqhe", d_scores, keyed).reshape(N, dr)
    d_keyed = ein("bhqk,bqhe->bkhe", d_scores, query).reshape(N, dr)
    d_valued = ein("bhqk,bqhe->bkhe", probs_b, d_context).reshape(N, dr)
    g_bias_query = jnp.sum(d_query, axis=0)
    g_bias_value = jnp.sum(d_valued, axis=0)
    d_qkv = jnp.concatenate([d_query.astype(BF), d_keyed.astype(BF), d_valued.astype(BF)], 1)
    in_part = mm_nt(d_qkv, wqkv).astype(BF)

    def placed(v):
        return lax.dynamic_update_slice(jnp.zeros((D,), F32), v, (r * dr,)).reshape(S, ds)

    g_small = jnp.concatenate(
        [
            placed(g_bias_query),
            placed(g_bias_value),
            sums_one[0].reshape(S, ds),
            sums_one[1].reshape(S, ds),
            sums_one[2].reshape(S, ds),
            sums_two[0].reshape(S, ds),
            sums_two[1].reshape(S, ds),
            sums_two[2].reshape(S, ds),
            g_bias_inner.reshape(S, fr),
        ],
        1,
    ).astype(BF)
    n_g = g_small.shape[1]
    g_small = jnp.pad(g_small, ((0, 0), (0, PAD * W - n_g))).reshape(S, PAD, W)
    g_pack = jnp.concatenate([mm_tn(x_all, d_qkv).astype(BF), g_wo], 1).reshape(S, ds, W)
    g_pack = jnp.concatenate([g_pack, g_small], 1)
    g_pack = lax.psum_scatter(g_pack, "shard", scatter_dimension=0, tiled=True)[0]

    grad_input = input_step(in_part, d_one)

    mlps = gather_kernel(g_mlp, R, 5).reshape(R, ds + dv, V).astype(F32)
    wd_out = mlps[:, ds:].reshape(R * fr, D)
    wi_out = mlps[:, :ds].reshape(R, ds, S, fr).transpose(1, 2, 0, 3).reshape(ds, S * R * fr)
    packs = gather_kernel(g_pack, R, 6).reshape(R, ds + PAD, W).astype(F32)
    main = packs[:, :ds].reshape(R, ds, 4, dr).transpose(2, 1, 0, 3).reshape(4, ds, D)
    tail = packs[:, ds:].reshape(R, PAD * W)
    summed = jnp.sum(tail[:, : 8 * ds], axis=0)
    gbq, gbv, gbo, ggone, gsone, gbd, ggtwo, gstwo = (
        summed[i * ds : (i + 1) * ds] for i in range(8)
    )
    gbi = tail[:, 8 * ds : n_g].reshape(fs)
    return (
        output,
        grad_input,
        main[0],
        main[1],
        main[2],
        main[3],
        gbq,
        gbv,
        gbo,
        ggone,
        gsone,
        wi_out,
        gbi,
        wd_out,
        gbd,
        ggtwo,
        gstwo,
    )

VMEM_SPEC = pl.BlockSpec(memory_space=pltpu.VMEM)
ANY_SPEC = pl.BlockSpec(memory_space=pl.ANY)
LIMIT = 56 << 20
NVEC = 16


def dma_sems(*counts):
    return [pltpu.SemaphoreType.DMA((n,)) for n in counts]


class Place(Peers):
    def __init__(self, S, R):
        super().__init__(R)
        self.S, self.Z = S, S // 2
        self.s = lax.axis_index("shard")
        self.z = lax.div(self.s, 2)
        self.y = lax.rem(self.s, 2)
        self.across = self.s + 1 - 2 * self.y

    def up(self, k):
        return 2 * lax.rem(self.z + k, self.Z) + self.y

    def down(self, k):
        return 2 * lax.rem(self.z + self.Z - k, self.Z) + self.y

    def flip(self, s):
        return s + 1 - 2 * self.y

    def meet_all(self):
        barrier = pltpu.get_barrier_semaphore()
        for dev in [self.partner] + [self.same(k) for k in range(1, self.A)]:
            pl.semaphore_signal(barrier, inc=1, device_id={"rep": dev}, device_id_type=MESH)
        for dev in [self.across] + [self.up(k) for k in range(1, self.Z)]:
            pl.semaphore_signal(barrier, inc=1, device_id={"shard": dev}, device_id_type=MESH)
        pl.semaphore_wait(barrier, self.A + self.Z)


def to_shard(src, dst, send, recv, dev):
    return pltpu.make_async_remote_copy(
        src_ref=src,
        dst_ref=dst,
        send_sem=send,
        recv_sem=recv,
        device_id={"shard": dev},
        device_id_type=MESH,
    )


class LineGather:
    def __init__(self, p, full, T, row, sems, cols=None):
        self.p, self.full, self.T, self.row, self.cols = p, full, T, row, cols
        a_s, a_r, b_s, b_r, f_s, f_r = sems
        half = lax.div(p.z, 2)
        self.inner = p.z == 1 + half
        self.outer = jnp.logical_not(self.inner)
        beside = 4 * half + 1 - p.z
        turn = jnp.where(self.inner, 1, 0)
        self.zs = [beside, 3 - 3 * half, 2 - half]
        self.near = self.copy(p.z, a_s.at[0], a_r.at[0], beside)
        self.over = self.copy(p.z, b_s.at[0], b_r.at[turn], 2 - half)
        self.on = [self.copy(self.zs[j + 1], f_s.at[j], b_r.at[j], beside) for j in range(2)]

    @staticmethod
    def sems():
        return dma_sems(1, 1, 1, 2, 2, 1)

    def block(self, z):
        rows = rows_of(2 * z + self.row, self.T)
        return self.full.at[rows] if self.cols is None else self.full.at[rows, self.cols]

    def copy(self, z, send, recv, to):
        return to_shard(self.block(z), self.block(z), send, recv, 2 * to + self.p.y)

    def start(self):
        self.near.start()
        self.over.start()

    def push(self, then=(None, None, None)):
        self.near.wait_recv()
        if then[0] is not None:
            then[0].start()

        @pl.when(self.inner)
        def _():
            for j in range(2):
                self.on[j].wait_recv()
                self.on[j].start()
                if then[j + 1] is not None:
                    then[j + 1].start()

    def pull(self, then=(None, None, None)):
        @pl.when(self.outer)
        def _():
            for j in range(2):
                self.on[j].wait_recv()
                if then[j + 1] is not None:
                    then[j + 1].start()

    def drain(self):
        self.near.wait_send()
        self.over.wait_send()

        @pl.when(self.inner)
        def _():
            for copy in self.on:
                copy.wait_send()


class RowGather:
    def __init__(self, p, full, T, sems, cols=None):
        self.line = LineGather(p, full, T, p.y, sems[:6], cols)
        ys, yr = sems[6:]
        self.side = []
        for i, z in enumerate([p.z] + self.line.zs):
            block = self.line.block(z)
            self.side.append(to_shard(block, block, ys.at[i], yr.at[i], p.across))

    @staticmethod
    def sems(Z):
        return LineGather.sems() + dma_sems(Z, Z)

    def start(self):
        self.line.start()
        self.side[0].start()

    def push(self):
        self.line.push(self.side[1:])

    def pull(self):
        self.line.pull(self.side[1:])

    def finish(self):
        for copy in self.side:
            copy.wait_recv()

    def drain(self):
        self.line.drain()
        drain(self.side)


class SideGather:
    def __init__(self, p, full, T, sems, cols=None):
        self.lines = [
            LineGather(p, full, T, row, sems[6 * i : 6 * i + 6], cols)
            for i, row in enumerate((p.y, 1 - p.y))
        ]
        block = self.lines[0].block(p.z)
        self.side = to_shard(block, block, sems[12].at[0], sems[13].at[0], p.across)

    @staticmethod
    def sems(Z):
        return LineGather.sems() * 2 + dma_sems(1, 1)

    def begin(self):
        self.side.start()

    def start(self):
        self.lines[0].start()

    def follow(self):
        self.side.wait_recv()
        self.lines[1].start()

    def push(self):
        for line in self.lines:
            line.push()

    def pull(self):
        for line in self.lines:
            line.pull()

    def finish(self):
        pass

    def drain(self):
        for line in self.lines:
            line.drain()
        self.side.wait_send()


class PlaneGather:
    def __init__(self, p, full, T, sems):
        self.p = p
        self.zs, self.zr, self.ys, self.yr = sems
        rows = full.at[rows_of(p.y, T)]
        self.far = {
            k: to_shard(rows, rows, self.zs.at[k - 1], self.zr.at[0], p.up(k))
            for k in range(1, p.Z)
        }
        self.near = to_shard(rows, rows, self.ys.at[0], self.yr.at[0], p.across)
        self.mine = p.z == p.me

    @staticmethod
    def sems(Z):
        return dma_sems(Z - 1, 1, 1, 1)

    def start(self):
        @pl.when(self.mine)
        def _():
            for k in range(1, self.p.Z):
                self.far[k].start()
            self.near.start()

    def forward(self):
        @pl.when(jnp.logical_not(self.mine))
        def _():
            self.far[1].wait_recv()
            self.near.start()

    def finish(self):
        self.near.wait_recv()

    def drain(self):
        @pl.when(self.mine)
        def _():
            for k in range(1, self.p.Z):
                self.far[k].wait_send()

        self.near.wait_send()


class LineScatter:
    def __init__(self, p, part, T, row, bufs, sems, cols, close=None):
        self.p, self.part, self.T, self.row, self.cols = p, part, T, row, cols
        self.out, self.ain, self.bin, self.fin = bufs
        self.close = close
        a_s, a_r, f_s, f_r, b_s, b_r = sems
        half = lax.div(p.z, 2)
        self.inner = p.z == 1 + half
        self.outer = jnp.logical_not(self.inner)
        beside = 4 * half + 1 - p.z
        self.zs = [beside, 3 - 3 * half, 2 - half, p.z]

        def to(z, src, dst, send, recv):
            return to_shard(src, dst, send, recv, 2 * z + p.y)

        src = [self.block(z) if close is None else self.out.at[j] for j, z in enumerate(self.zs[:3])]
        self.near = to(beside, src[0], self.ain, a_s.at[0], a_r.at[0])
        self.up = [
            to(beside, src[j + 1], self.fin.at[j], f_s.at[j], f_r.at[j]) for j in range(2)
        ]
        self.over = [
            to(self.zs[j + 1], self.out.at[j + 1], self.bin, b_s.at[j], b_r.at[0])
            for j in range(2)
        ]

    @staticmethod
    def bufs(T, C, dtype):
        return [pltpu.VMEM(n + (T, C), dtype) for n in ((3,), (), (), (2,))]

    @staticmethod
    def sems():
        return dma_sems(1, 1, 2, 2, 2, 1)

    def block(self, z):
        return self.part.at[rows_of(2 * z + self.row, self.T), self.cols]

    def terms(self, j, i):
        base = (2 * self.zs[j] + self.row) * self.T
        total = self.part[chunk_rows(i, base), self.cols].astype(F32)
        if self.close is not None:
            total = total + self.close[j, chunk_rows(i), :].astype(F32)
        return total

    def each(self, put):
        def step(i, _):
            put(i)
            return 0

        lax.fori_loop(0, self.T // CHUNK, step, 0)

    def lift(self, j):
        if self.close is not None:

            def put(i):
                self.out[j, chunk_rows(i), :] = self.terms(j, i).astype(self.out.dtype)

            self.each(put)
        if j == 0:
            self.near.start()
        else:
            self.up[j - 1].start()

    def relay(self, j):
        self.up[j - 1].wait_recv()

        def put(i):
            total = self.terms(j, i) + self.fin[j - 1, chunk_rows(i), :].astype(F32)
            self.out[j, chunk_rows(i), :] = total.astype(self.out.dtype)

        self.each(put)
        self.over[j - 1].start()

    def wait(self):
        self.near.wait_recv()
        self.over[0].wait_recv()

    def read(self, i):
        total = self.terms(3, i) + self.ain[chunk_rows(i), :].astype(F32)
        return total + self.bin[chunk_rows(i), :].astype(F32)

    def drain(self):
        self.near.wait_send()

        @pl.when(self.outer)
        def _():
            drain(self.up)

        @pl.when(self.inner)
        def _():
            drain(self.over)


class RowScatter:
    def __init__(self, p, part, T, bufs, sems, cols=None):
        self.p, self.T = p, T
        self.cols = pl.ds(0, part.shape[1]) if cols is None else cols
        close = bufs[4]
        self.line = LineScatter(p, part, T, p.y, bufs[:4], sems[:6], self.cols, close)
        ys, yr = sems[6:]
        self.side = [
            to_shard(
                part.at[rows_of(2 * z + 1 - p.y, T), self.cols],
                close.at[j],
                ys.at[j],
                yr.at[j],
                p.across,
            )
            for j, z in enumerate(self.line.zs)
        ]

    @staticmethod
    def bufs(T, C, dtype):
        return LineScatter.bufs(T, C, dtype) + [pltpu.VMEM((4, T, C), dtype)]

    @staticmethod
    def sems():
        return LineScatter.sems() + dma_sems(4, 4)

    def launch(self, j):
        self.side[j].start()

    def start(self):
        for j in (1, 2, 0, 3):
            self.launch(j)

    def lift(self, j):
        if j == 0:
            self.side[0].wait_recv()
            self.line.lift(0)
        else:

            @pl.when(self.line.outer)
            def _():
                self.side[j].wait_recv()
                self.line.lift(j)

    def relay(self, j):
        @pl.when(self.line.inner)
        def _():
            self.side[j].wait_recv()
            self.line.relay(j)

    def total(self, dst):
        self.side[3].wait_recv()
        self.line.wait()

        def put(i):
            dst[self.p.me, chunk_rows(i), self.cols] = self.line.read(i).astype(dst.dtype)

        self.line.each(put)

    def drain(self):
        self.line.drain()
        drain(self.side)


class SideScatter:
    def __init__(self, p, part, T, bufs, sems, cols):
        self.p, self.cols = p, cols
        self.lines = [
            LineScatter(p, part, T, row, bufs[4 * i : 4 * i + 4], sems[6 * i : 6 * i + 6], cols)
            for i, row in enumerate((1 - p.y, p.y))
        ]
        self.sent, self.got = bufs[8:]
        self.side = to_shard(self.sent, self.got, sems[12].at[0], sems[13].at[0], p.across)

    @staticmethod
    def bufs(T, C, dtype):
        return LineScatter.bufs(T, C, dtype) * 2 + [pltpu.VMEM((T, C), dtype)] * 2

    @staticmethod
    def sems():
        return LineScatter.sems() * 2 + dma_sems(1, 1)

    def launch(self, j):
        if j == 0:
            for line in self.lines:
                line.lift(0)
        elif j < 3:

            @pl.when(self.lines[0].outer)
            def _():
                for line in self.lines:
                    line.lift(j)

    def relay(self, j):
        @pl.when(self.lines[0].inner)
        def _():
            for line in self.lines:
                line.relay(j)

    def cross(self):
        line = self.lines[0]
        line.wait()

        def put(i):
            self.sent[chunk_rows(i), :] = line.read(i).astype(self.sent.dtype)

        line.each(put)
        self.side.start()

    def total(self, dst):
        line = self.lines[1]
        line.wait()
        self.side.wait_recv()

        def put(i):
            total = line.read(i) + self.got[chunk_rows(i), :].astype(F32)
            dst[self.p.me, chunk_rows(i), self.cols] = total.astype(dst.dtype)

        line.each(put)

    def drain(self):
        for line in self.lines:
            line.drain()
        self.side.wait_send()


class PlaneScatter:
    def __init__(self, p, part, T, bufs, sems):
        self.p, self.part, self.T = p, part, T
        self.close, self.out, self.far = bufs
        ys, yr, zs, zr = sems
        self.first = to_shard(
            part.at[rows_of(1 - p.y, T)], self.close, ys.at[0], yr.at[0], p.across
        )
        self.mine = p.z == p.me
        self.hop = lax.rem(p.z + p.Z - p.me, p.Z)
        self.sends = to_shard(
            self.out,
            self.far.at[jnp.maximum(self.hop - 1, 0)],
            zs.at[0],
            zr.at[jnp.maximum(self.hop - 1, 0)],
            2 * p.me + p.y,
        )
        self.gets = [
            to_shard(self.out, self.far.at[k], zs.at[0], zr.at[k], p.up(k + 1))
            for k in range(p.Z - 1)
        ]

    @staticmethod
    def bufs(Z, T, C, dtype):
        return [pltpu.VMEM((T, C), dtype), pltpu.VMEM((T, C), dtype), pltpu.VMEM((Z - 1, T, C), dtype)]

    @staticmethod
    def sems(Z):
        return dma_sems(1, 1, 1, Z - 1)

    def start(self):
        self.first.start()

    def pass_on(self):
        self.first.wait_recv()

        def add(i, _):
            mine = self.part[chunk_rows(i, self.p.y * self.T), :].astype(F32)
            self.out[chunk_rows(i), :] = (mine + self.close[chunk_rows(i), :].astype(F32)).astype(BF)
            return 0

        lax.fori_loop(0, self.T // CHUNK, add, 0)

        @pl.when(jnp.logical_not(self.mine))
        def _():
            self.sends.start()

    def total(self, dst):
        @pl.when(self.mine)
        def _():
            for copy in self.gets:
                copy.wait_recv()

            def add(i, _):
                total = self.part[chunk_rows(i, self.p.y * self.T), :].astype(F32)
                total = total + self.close[chunk_rows(i), :].astype(F32)
                for k in range(self.p.Z - 1):
                    total = total + self.far[k, chunk_rows(i), :].astype(F32)
                dst[chunk_rows(i), :] = total.astype(BF)
                return 0

            lax.fori_loop(0, self.T // CHUNK, add, 0)

    def drain(self):
        self.first.wait_send()

        @pl.when(jnp.logical_not(self.mine))
        def _():
            self.sends.wait_send()


class RepSpread:
    def __init__(self, p, full, sems, cols=None):
        self.p = p
        dir_s, dir_r, fwd_s, fwd_r = sems
        cols = pl.ds(0, full.shape[2]) if cols is None else cols
        own = full.at[p.me, :, cols]
        self.direct = {0: remote(own, own, dir_s.at[0], dir_r.at[0], p.partner)}
        self.passed = {}
        for k in range(1, p.A):
            self.direct[k] = remote(own, own, dir_s.at[k], dir_r.at[k], p.same(k))
            block = full.at[p.same(p.A - k), :, cols]
            self.passed[k] = remote(block, block, fwd_s.at[k - 1], fwd_r.at[k - 1], p.partner)

    @staticmethod
    def sems(A):
        return dma_sems(A, A, A - 1, A - 1)

    def start(self):
        for k in list(range(1, self.p.A)) + [0]:
            self.direct[k].start()

    def forward(self):
        for k in range(1, self.p.A):
            self.direct[k].wait_recv()
            self.passed[k].start()

    def finish(self):
        self.direct[0].wait_recv()
        for copy in self.passed.values():
            copy.wait_recv()

    def drain(self):
        drain(list(self.direct.values()) + list(self.passed.values()))


class OwnerSpread:
    def __init__(self, p, block, sems):
        self.p = p
        s0, s1, rx, rp = sems
        self.across = remote(block, block, s0.at[0], rx.at[0], p.same(1))
        self.beside = remote(block, block, s1.at[0], rp.at[0], p.partner)
        self.mine = p.z == p.me
        self.relay = p.z == p.same(1)
        self.other = jnp.logical_not(jnp.logical_or(self.mine, self.relay))

    @staticmethod
    def sems():
        return dma_sems(1, 1, 1, 1)

    def start(self):
        @pl.when(self.mine)
        def _():
            self.across.start()
            self.beside.start()

    def forward(self):
        @pl.when(self.relay)
        def _():
            self.across.wait_recv()
            self.beside.start()

    def finish(self):
        @pl.when(self.other)
        def _():
            self.beside.wait_recv()

    def drain(self):
        @pl.when(self.mine)
        def _():
            self.across.wait_send()

        @pl.when(jnp.logical_not(self.other))
        def _():
            self.beside.wait_send()

class RepScatter:
    def __init__(self, p, part, T, bufs, sems, cols=None):
        self.p, self.part, self.T = p, part, T
        cols = pl.ds(0, part.shape[1]) if cols is None else cols
        self.cols = cols
        self.near, self.out, self.far = bufs
        near_s, near_r, far_s, far_r = sems
        self.first = {
            k: remote(
                part.at[rows_of(p.other(k), T), cols],
                self.near.at[k, :, cols],
                near_s.at[k],
                near_r.at[k],
                p.partner,
            )
            for k in range(p.A)
        }
        self.second = {
            k: remote(
                self.out.at[k - 1, :, cols],
                self.far.at[k - 1, :, cols],
                far_s.at[k - 1],
                far_r.at[k - 1],
                p.same(k),
            )
            for k in range(1, p.A)
        }

    @staticmethod
    def bufs(A, T, D):
        return [pltpu.VMEM((n, T, D), BF) for n in (A, A - 1, A - 1)]

    @staticmethod
    def sems(A):
        return dma_sems(A, A, A - 1, A - 1)

    def start_far(self):
        for k in range(1, self.p.A):
            self.first[k].start()

    def start_near(self):
        self.first[0].start()

    def pass_on(self):
        for k in range(1, self.p.A):
            self.first[k].wait_recv()
            base = self.p.same(k) * self.T

            def add(i, _, k=k, base=base):
                mine = self.part[step_rows(i, base), self.cols].astype(F32)
                near = self.near[k, step_rows(i), self.cols].astype(F32)
                self.out[k - 1, step_rows(i), self.cols] = (mine + near).astype(BF)
                return 0

            lax.fori_loop(0, self.T // STEP, add, 0)
            self.second[k].start()

    def finish(self):
        self.first[0].wait_recv()
        for copy in self.second.values():
            copy.wait_recv()

    def read(self, i):
        total = self.part[step_rows(i, self.p.me * self.T), :].astype(F32)
        total = total + self.near[0, step_rows(i), :].astype(F32)
        for k in range(1, self.p.A):
            total = total + self.far[k - 1, step_rows(i), :].astype(F32)
        return total

    def drain(self):
        drain(list(self.first.values()) + list(self.second.values()))


STEP = 32


def step_rows(i, base=None):
    start = i * STEP if base is None else base + i * STEP
    return pl.ds(pl.multiple_of(start, STEP), STEP)


class TokenSpread:
    def __init__(self, p, full, T, sems, piece=0, pieces=1):
        self.p = p
        n = T // pieces

        def rows(r):
            return pl.ds(pl.multiple_of(r * T + piece * n, n), n)

        dir_s, dir_r, fwd_s, fwd_r = sems
        own = full.at[rows(p.me)]
        self.direct = {0: remote(own, own, dir_s.at[0], dir_r.at[0], p.partner)}
        self.passed = {}
        for k in range(1, p.A):
            self.direct[k] = remote(own, own, dir_s.at[k], dir_r.at[k], p.same(k))
            block = full.at[rows(p.same(p.A - k))]
            self.passed[k] = remote(block, block, fwd_s.at[k - 1], fwd_r.at[k - 1], p.partner)

    @staticmethod
    def sems(A):
        return dma_sems(A, A, A - 1, A - 1)

    def start(self):
        for k in list(range(1, self.p.A)) + [0]:
            self.direct[k].start()

    def beside(self):
        self.direct[0].wait_recv()

    def across(self):
        self.hop()
        self.land()

    def hop(self):
        for k in range(1, self.p.A):
            self.direct[k].wait_recv()
            self.passed[k].start()

    def land(self):
        for copy in self.passed.values():
            copy.wait_recv()

    def drain(self):
        drain(list(self.direct.values()) + list(self.passed.values()))


class Bag:
    def __init__(self):
        self.names, self.specs = [], []

    def want(self, name, specs):
        specs = specs if isinstance(specs, list) else [specs]
        self.names.append((name, len(specs)))
        self.specs += specs

    def hand_out(self, refs):
        got, at = {}, 0
        for name, n in self.names:
            got[name] = refs[at] if n == 1 else list(refs[at : at + n])
            at += n
        return got


def fold(v):
    return jnp.sum(v.reshape(v.shape[0] // 8, 8, v.shape[1]), axis=0)


TILE = 256
QUARTERS = 4


def tiles(n, body):
    def step(i, _):
        body(pl.ds(pl.multiple_of(i * TILE, TILE), TILE))
        return 0

    lax.fori_loop(0, n // TILE, step, 0)


def layer(x, cot, wq, wk, wv, wo, wi, wd, vectors, S, R):
    T, D = x.shape
    ds, fs = wq.shape[0], wd.shape[0]
    dr, fr = D // R, fs // R
    V = S * fr
    W = 3 * dr
    Z, A = S // 2, R // 2
    nv = len(vectors)
    N = R * T
    C = N // A
    pairs = dr // 128
    half = V // 2
    wide = D // QUARTERS

    bag = Bag()
    bag.want("here", pltpu.SemaphoreType.DMA((S + 6,)))
    bag.want("small", pltpu.VMEM((S * NVEC, ds), F32))
    bag.want("flat", pltpu.VMEM((NVEC, D), F32))
    for name, shape, t in (
        ("x_all", (N, D), BF),
        ("wqkv", (D, W), BF),
        ("wor", (dr, D), BF),
        ("wir", (D, V), BF),
        ("wdr", (V, D), BF),
        ("qkv", (N, W), BF),
        ("probs", (N * dr // HEAD_DIM, SEQ), F32),
        ("ctx", (N, dr), BF),
        ("part", (N, D), BF),
        ("normed", (T, D), F32),
        ("rstd", (T, 128), F32),
        ("hidden", (T, D), F32),
        ("hid_all", (N, D), BF),
        ("acted", (N, V), BF),
        ("slope", (N, V), F32),
        ("d_two", (T, D), F32),
        ("d2_all", (N, D), BF),
        ("d_in", (N, V), BF),
        ("d_one", (T, D), F32),
        ("d1_all", (N, D), BF),
        ("dctx", (N, dr), BF),
        ("dqkv", (N, W), BF),
        ("sums", (48, D), F32),
        ("gbi8", (8, V), F32),
        ("gqv8", (8, 2 * dr), F32),
        ("gflat", (NVEC, D), F32),
        ("gs", (S * NVEC, ds), F32),
        ("gwd", (V, D), BF),
        ("gwi", (D, V), BF),
        ("gqkv", (D, W), BF),
        ("gwo", (dr, D), BF),
    ):
        bag.want(name, pltpu.VMEM(shape, t))
    for name in ("smalls", "g_qkv", "g_wia", "g_wib", "g_wd0", "g_wd1"):
        bag.want(name, RowGather.sems(Z))
    bag.want("g_wd2", SideGather.sems(Z))
    bag.want("g_wo", PlaneGather.sems(Z))
    for name in ("ax", "a1", "a2", "a2z", "a3"):
        bag.want(name, TokenSpread.sems(A))
    for name in ("t1", "t2", "t3", "t4"):
        bag.want(name + "b", RepScatter.bufs(A, T, D))
        bag.want(name + "s", RepScatter.sems(A))
    bag.want("t2z", RepScatter.sems(A))
    for name, n, c, t in (
        ("rwd", fr, D // 2, BF),
        ("rwi", ds, V, BF),
        ("rqk", ds, 2 * dr, BF),
        ("rv", ds, dr, BF),
        ("rsm", NVEC, ds, F32),
    ):
        bag.want(name + "b", RowScatter.bufs(n, c, t))
        bag.want(name + "s", RowScatter.sems())
        bag.want(name + "p", RepSpread.sems(A))
    bag.want("rwxb", SideScatter.bufs(fr, D // 2, BF))
    bag.want("rwxs", SideScatter.sems())
    bag.want("rwob", PlaneScatter.bufs(Z, ds, D, BF))
    bag.want("rwos", PlaneScatter.sems(Z))
    bag.want("rwop", OwnerSpread.sems())

    def kernel(*refs):
        x, cot, wq, wk, wv, wo, wi, wd = refs[:8]
        vecs = refs[8 : 8 + nv]
        at = 8 + nv
        out_o, gin_o, tq, ti, td, to, ts = refs[at : at + 7]
        b = bag.hand_out(refs[at + 7 :])
        x_all, wqkv, wor, wir, wdr = b["x_all"], b["wqkv"], b["wor"], b["wir"], b["wdr"]
        qkv, probs, ctx, part = b["qkv"], b["probs"], b["ctx"], b["part"]
        flat, small, here = b["flat"], b["small"], b["here"]
        normed_r, rstd_r, hidden_r = b["normed"], b["rstd"], b["hidden"]
        hid_all, acted, slope, d_two_r, d2_all = (
            b["hid_all"],
            b["acted"],
            b["slope"],
            b["d_two"],
            b["d2_all"],
        )
        d_in, d_one_r, d1_all, dctx, dqkv = b["d_in"], b["d_one"], b["d1_all"], b["dctx"], b["dqkv"]
        sums, gbi8, gqv8, gflat, gs = b["sums"], b["gbi8"], b["gqv8"], b["gflat"], b["gs"]
        gwd, gwi, gqkv, gwo = b["gwd"], b["gwi"], b["gqkv"], b["gwo"]

        p = Place(S, R)
        mine = rows_of(p.s, ds)
        own_tok = rows_of(p.me, T)
        own_chip = rows_of(p.a, C)
        far_chip = rows_of(p.chip(1), C)
        cols = pl.ds(pl.multiple_of(p.me * dr, dr), dr)
        local = []

        def bring(src, dst):
            copy = pltpu.make_async_copy(src, dst, here.at[len(local)])
            copy.start()
            local.append(copy)

        for i, w in enumerate((wq, wk, wv)):
            bring(w.at[:, cols], wqkv.at[mine, pl.ds(i * dr, dr)])
        for c in range(S):
            piece = pl.ds(pl.multiple_of(c * fs + p.me * fr, fr), fr)
            bring(wi.at[:, piece], wir.at[mine, pl.ds(c * fr, fr)])
        bring(wd.at[rows_of(p.me, fr)], wdr.at[mine])
        own_wo = pltpu.make_async_copy(wo, wor.at[rows_of(p.y, ds)], here.at[len(local)])

        @pl.when(p.z == p.me)
        def _():
            own_wo.start()

        piece = pl.ds(pl.multiple_of(p.me * fr, fr), fr)
        pieces = [v[...] for v in vecs[:-1]] + [vecs[-1][:, piece]]
        pieces.append(jnp.zeros((NVEC - nv, ds), F32))
        small[rows_of(p.s, NVEC), :] = jnp.concatenate(pieces, 0)
        x_all[own_tok, :] = x[...]
        p.meet_all()

        smalls = RowGather(p, small, NVEC, b["smalls"])
        g_qkv = RowGather(p, wqkv, ds, b["g_qkv"])
        left, right = pl.ds(0, half), pl.ds(half, half)
        g_wia = RowGather(p, wir, ds, b["g_wia"], left)
        g_wib = RowGather(p, wir, ds, b["g_wib"], right)
        g_wd0 = RowGather(p, wdr, fr, b["g_wd0"], pl.ds(0, wide))
        g_wd1 = RowGather(p, wdr, fr, b["g_wd1"], pl.ds(wide, wide))
        g_wd2 = SideGather(p, wdr, fr, b["g_wd2"], pl.ds(2 * wide, 2 * wide))
        g_wo = PlaneGather(p, wor, ds, b["g_wo"])
        ax = TokenSpread(p, x_all, T, b["ax"])
        a1 = TokenSpread(p, hid_all, T, b["a1"])
        a2 = TokenSpread(p, d2_all, T, b["a2"], 0, 2)
        a2z = TokenSpread(p, d2_all, T, b["a2z"], 1, 2)
        a3 = TokenSpread(p, d1_all, T, b["a3"])
        t1 = RepScatter(p, part, T, b["t1b"], b["t1s"])
        t2 = RepScatter(p, part, T, b["t2b"], b["t2s"], pl.ds(0, D // 2))
        t2z = RepScatter(p, part, T, b["t2b"], b["t2z"], pl.ds(D // 2, D // 2))
        t3 = RepScatter(p, part, T, b["t3b"], b["t3s"])
        t4 = RepScatter(p, part, T, b["t4b"], b["t4s"])
        rwd = RowScatter(p, gwd, fr, b["rwdb"], b["rwds"], pl.ds(0, D // 2))
        rwx = SideScatter(p, gwd, fr, b["rwxb"], b["rwxs"], pl.ds(D // 2, D // 2))
        rwi = RowScatter(p, gwi, ds, b["rwib"], b["rwis"])
        qk_cols, v_cols = pl.ds(0, 2 * dr), pl.ds(2 * dr, dr)
        rqk = RowScatter(p, gqkv, ds, b["rqkb"], b["rqks"], qk_cols)
        rv = RowScatter(p, gqkv, ds, b["rvb"], b["rvs"], v_cols)
        rsm = RowScatter(p, gs, NVEC, b["rsmb"], b["rsms"])
        rwo = PlaneScatter(p, gwo, ds, b["rwob"], b["rwos"])
        sd = RepSpread(p, td, b["rwdp"])
        si = RepSpread(p, ti, b["rwip"])
        sq = RepSpread(p, tq, b["rqkp"], qk_cols)
        sv = RepSpread(p, tq, b["rvp"], v_cols)
        ss = RepSpread(p, ts, b["rsmp"])
        so = OwnerSpread(p, to, b["rwop"])

        smalls.start()
        for copy in local[:3]:
            copy.wait()
        g_qkv.start()
        ax.start()
        for copy in local[3:]:
            copy.wait()

        @pl.when(p.z == p.me)
        def _():
            own_wo.wait()

        g_wo.start()
        g_wia.start()
        sums[...] = jnp.zeros_like(sums)
        gbi8[...] = jnp.zeros_like(gbi8)
        gqv8[...] = jnp.zeros_like(gqv8)
        gflat[...] = jnp.zeros_like(gflat)
        smalls.push()
        g_qkv.push()
        smalls.pull()
        g_qkv.pull()
        g_wib.start()
        g_wd2.begin()
        g_wd0.start()
        g_wd1.start()
        g_wd2.start()
        smalls.finish()
        for i in range(nv):
            row = [small[s * NVEC + i : s * NVEC + i + 1, :] for s in range(S)]
            flat[i : i + 1, :] = jnp.concatenate(row, 1)
        ax.beside()
        ax.across()
        g_qkv.finish()

        low = lax.broadcasted_iota(jnp.int32, (SEQ, 128), 1) < HEAD_DIM
        keep = (low, jnp.logical_not(low))

        def project(rows):
            for n in range(3):
                c = pl.ds(n * dr, dr)
                z = mm(x_all[rows, :], wqkv[:, c])
                if n == 0:
                    z = z + flat[0:1, cols]
                if n == 2:
                    z = z + flat[1:2, cols]
                qkv[rows, c] = z.astype(BF)

        def pick(v, h):
            return jnp.where(keep[h], v, jnp.zeros_like(v))

        def attend(chip):
            def one(j, _):
                seq = chip * (C // SEQ) + j
                rows = rows_of(seq, SEQ)
                for n in range(pairs):
                    q2 = qkv[rows, n * 128 : n * 128 + 128]
                    k2 = qkv[rows, dr + n * 128 : dr + n * 128 + 128]
                    v2 = qkv[rows, 2 * dr + n * 128 : 2 * dr + n * 128 + 128]
                    got = []
                    for h in range(2):
                        scores = mm_nt(pick(q2, h), k2) * 0.125
                        e = jnp.exp(scores - jnp.max(scores, axis=-1, keepdims=True))
                        pr = e / jnp.sum(e, axis=-1, keepdims=True)
                        probs[rows_of(seq * 2 * pairs + 2 * n + h, SEQ), :] = pr
                        got.append(mm(pr.astype(BF), v2))
                    ctx[rows, n * 128 : n * 128 + 128] = jnp.where(low, got[0], got[1]).astype(BF)
                return 0

            lax.fori_loop(0, C // SEQ, one, 0)

        def attn_part(rows):
            def tile(c):
                part[rows, c] = mm(ctx[rows, :], wor[:, c]).astype(BF)

            tiles(D, tile)

        def inner(rows):
            def tile(c):
                z = mm(hid_all[rows, :], wir[:, c]) + flat[8:9, c]
                phi = 0.5 * (1.0 + lax.erf(z * INV_ROOT_TWO))
                acted[rows, c] = (z * phi).astype(BF)
                slope[rows, c] = phi + z * jnp.exp(-0.5 * z * z) * INV_ROOT_TWO_PI

            tiles(V, tile)

        def down(rows, q):
            c = pl.ds(q * wide, wide)
            part[rows, c] = mm(acted[rows, :], wdr[:, c]).astype(BF)

        def d_inner(rows):
            def tile(c):
                d = mm_nt(d2_all[rows, :], wdr[c, :]) * slope[rows, c]
                gbi8[:, c] += fold(d)
                d_in[rows, c] = d.astype(BF)

            tiles(V, tile)

        def hid_part(rows):
            def tile(c):
                part[rows, c] = mm_nt(d_in[rows, :], wir[c, :]).astype(BF)

            tiles(D, tile)

        def d_attend(chip):
            rows = rows_of(chip, C)
            dctx[rows, :] = mm_nt(d1_all[rows, :], wor[...]).astype(BF)

            def one(j, _):
                seq = chip * (C // SEQ) + j
                rows = rows_of(seq, SEQ)
                for n in range(pairs):
                    lanes = [slice(m * dr + n * 128, m * dr + n * 128 + 128) for m in range(3)]
                    q2, k2, v2 = (qkv[rows, c] for c in lanes)
                    dc2 = dctx[rows, lanes[0]]
                    got = []
                    for h in range(2):
                        pr = probs[rows_of(seq * 2 * pairs + 2 * n + h, SEQ), :]
                        dp = mm_nt(pick(dc2, h), v2)
                        delta = jnp.sum(pr * dp, axis=-1, keepdims=True)
                        dsc = (pr * (dp - delta) * 0.125).astype(BF)
                        got.append((mm(dsc, k2), mm_tn(dsc, q2), mm_tn(pr.astype(BF), dc2)))
                    dq, dk, dv = (jnp.where(low, u, w) for u, w in zip(*got))
                    gqv8[:, lanes[0]] += fold(dq)
                    gqv8[:, lanes[1]] += fold(dv)
                    for v, c in zip((dq, dk, dv), lanes):
                        dqkv[rows, c] = v.astype(BF)
                return 0

            lax.fori_loop(0, C // SEQ, one, 0)

        def in_part(rows):
            def tile(c):
                part[rows, c] = mm_nt(dqkv[rows, :], wqkv[c, :]).astype(BF)

            tiles(D, tile)

        def grad_plane(lhs, rhs, dst, z):
            both = pl.ds(pl.multiple_of(z * 2 * ds, 2 * ds), 2 * ds)
            dst[both, :] = mm_tn(lhs[:, both], rhs[...]).astype(BF)

        def grad_all(lhs, rhs, dst, *scatters):
            for j in (1, 2, 0, 3):
                grad_plane(lhs, rhs, dst, rwi.line.zs[j])
                for g in scatters:
                    g.launch(j)

        project(far_chip)
        g_wo.forward()
        g_wia.push()
        project(own_chip)
        attend(p.chip(1))
        g_wo.finish()
        attn_part(far_chip)
        t1.start_far()
        g_wd2.follow()
        attend(p.a)
        g_wib.push()
        g_wd0.push()
        attn_part(own_chip)
        t1.start_near()
        t1.pass_on()
        g_wia.pull()
        t1.finish()

        def norm_one(i, _):
            at = step_rows(i)
            normed, rstd = norm_parts(x[at, :].astype(F32) + t1.read(i) + flat[2:3, :])
            hidden = normed * flat[3:4, :] + flat[4:5, :]
            normed_r[at, :] = normed
            rstd_r[at, :] = jnp.broadcast_to(rstd, (STEP, 128))
            hidden_r[at, :] = hidden
            hid_all[step_rows(i, p.me * T), :] = hidden.astype(BF)
            return 0

        lax.fori_loop(0, T // STEP, norm_one, 0)
        a1.start()
        t1.drain()
        g_wd1.push()
        g_wib.pull()
        a1.beside()
        a1.across()
        g_wd2.push()
        g_wia.finish()
        g_wib.finish()
        inner(own_chip)
        g_wd0.pull()
        g_wd1.pull()
        inner(far_chip)
        g_wd0.finish()
        down(far_chip, 0)
        g_wd1.finish()
        down(far_chip, 1)
        t2.start_far()
        down(own_chip, 0)
        down(own_chip, 1)
        t2.start_near()
        t2.pass_on()
        g_wd2.pull()
        down(far_chip, 2)
        down(far_chip, 3)
        t2z.start_far()
        down(own_chip, 2)
        down(own_chip, 3)
        t2z.start_near()
        t2z.pass_on()
        t2.finish()
        t2z.finish()

        def norm_two(i, _):
            at = step_rows(i)
            normed, rstd = norm_parts(hidden_r[at, :] + t2.read(i) + flat[5:6, :])
            out_o[at, :] = (normed * flat[6:7, :] + flat[7:8, :]).astype(BF)
            dout = cot[at, :].astype(F32)
            d_two = norm_back(dout * flat[6:7, :], normed, rstd)
            sums[24:32, :] += fold(d_two)
            sums[32:40, :] += fold(dout * normed)
            sums[40:48, :] += fold(dout)
            d_two_r[at, :] = d_two
            d2_all[step_rows(i, p.me * T), :] = d_two.astype(BF)
            return 0

        lax.fori_loop(0, T // STEP // 2, norm_two, 0)
        a2.start()
        lax.fori_loop(T // STEP // 2, T // STEP, norm_two, 0)
        a2z.start()
        t2.drain()
        t2z.drain()
        a2.beside()
        a2z.beside()
        d_inner(own_chip)
        a2.hop()
        a2z.hop()
        a2.land()
        a2z.land()
        grad_all(acted, d2_all, gwd, rwd, rwx)
        d_inner(far_chip)
        hid_part(far_chip)
        t3.start_far()
        hid_part(own_chip)
        t3.start_near()
        t3.pass_on()
        grad_all(hid_all, d_in, gwi, rwi)
        for j in (1, 2, 0):
            rwd.lift(j)
        rwx.relay(1)
        rwx.relay(2)
        t3.finish()

        def back_one(i, _):
            at = step_rows(i)
            d_hidden = d_two_r[at, :] + t3.read(i)
            normed = normed_r[at, :]
            d_one = norm_back(d_hidden * flat[3:4, :], normed, rstd_r[at, 0:1])
            sums[0:8, :] += fold(d_one)
            sums[8:16, :] += fold(d_hidden * normed)
            sums[16:24, :] += fold(d_hidden)
            d_one_r[at, :] = d_one
            d1_all[step_rows(i, p.me * T), :] = d_one.astype(BF)
            return 0

        lax.fori_loop(0, T // STEP, back_one, 0)
        a3.start()
        t3.drain()
        rwd.relay(1)
        rwd.relay(2)
        a3.beside()
        d_attend(p.a)
        a3.across()
        gwo[...] = mm_tn(ctx[...], d1_all[...]).astype(BF)
        rwo.start()
        rwi.lift(1)
        d_attend(p.chip(1))
        gflat[0:1, cols] = jnp.sum(gqv8[:, :dr], axis=0, keepdims=True)
        gflat[1:2, cols] = jnp.sum(gqv8[:, dr:], axis=0, keepdims=True)
        for i in range(6):
            gflat[i + 2 : i + 3, :] = jnp.sum(sums[8 * i : 8 * i + 8, :], axis=0, keepdims=True)
        gflat[8:9, :] = jnp.sum(gbi8[...], axis=0, keepdims=True)
        for s in range(S):
            gs[s * NVEC : (s + 1) * NVEC, :] = gflat[:, s * ds : (s + 1) * ds]
        rsm.start()
        rwi.lift(2)
        rwx.cross()
        grad_all(x_all, dqkv, gqkv, rqk, rv)
        rwi.lift(0)
        rwi.relay(1)
        in_part(far_chip)
        t4.start_far()
        in_part(own_chip)
        t4.start_near()
        t4.pass_on()
        rwi.relay(2)
        rwd.total(td)
        t4.finish()

        def last(i, _):
            at = step_rows(i)
            gin_o[at, :] = (d_one_r[at, :] + t4.read(i)).astype(BF)
            return 0

        lax.fori_loop(0, T // STEP, last, 0)
        rwo.pass_on()
        for j in (1, 2, 0):
            rsm.lift(j)
        rwx.total(td)
        sd.start()
        for g in (rqk, rv):
            g.lift(1)
        rsm.relay(1)
        rsm.relay(2)
        for g in (rqk, rv):
            g.lift(2)
        rqk.relay(1)
        rwi.total(ti)
        si.start()
        rv.relay(1)
        sd.forward()
        for g in (rqk, rv):
            g.lift(0)
        rqk.relay(2)
        rv.relay(2)
        rwo.total(to)
        so.start()
        rsm.total(ts)
        ss.start()
        si.forward()
        rqk.total(tq)
        sq.start()
        so.forward()
        rv.total(tq)
        sv.start()
        ss.forward()
        sd.finish()
        si.finish()
        so.finish()
        sq.forward()
        sv.forward()
        sq.finish()
        sv.finish()
        ss.finish()
        for g in (smalls, g_qkv, g_wo, g_wia, g_wib, g_wd0, g_wd1, g_wd2, ax, a1, a2, a2z, a3, t4):
            g.drain()
        for g in (rwd, rwx, rwi, rqk, rv, rsm, rwo, sd, si, sq, sv, ss, so):
            g.drain()

    ins = [x, cot, wq, wk, wv, wo, wi, wd] + [v[None] for v in vectors]
    outs = [((T, D), BF)] * 2
    outs += [((R, ds, W), BF), ((R, ds, V), BF), ((R, fr, D), BF), ((ds, D), BF)]
    outs += [((R, NVEC, ds), F32)]
    return pl.pallas_call(
        kernel,
        out_shape=[jax.ShapeDtypeStruct(*o) for o in outs],
        in_specs=[VMEM_SPEC] * 2 + [ANY_SPEC] * 6 + [VMEM_SPEC] * nv,
        out_specs=[VMEM_SPEC] * len(outs),
        scratch_shapes=bag.specs,
        compiler_params=pltpu.CompilerParams(
            collective_id=12, has_side_effects=True, vmem_limit_bytes=LIMIT
        ),
        cost_estimate=pl.CostEstimate(
            flops=10 * 10**9, bytes_accessed=24 << 20, transcendentals=4 << 20
        ),
    )(*ins)


def widen(out, gin, tq, ti, td, to, ts, S):
    R, ds, W = tq.shape
    D, dr = R * W // 3, W // 3
    fr, V = td.shape[1], ti.shape[2]
    fs = fr * R
    T = out.shape[0]
    few, tok = ds // R, T // R

    def kernel(out, gin, tq, ti, td, to, ts, out_o, gin_o, oq, ok, ov, oo, oi, od, *vec_o):
        out_o[...] = out[...]
        gin_o[...] = gin[...]
        od[...] = td[0].astype(F32)
        oo[...] = to[...].astype(F32)
        for r in range(R):
            for n, o in enumerate((oq, ok, ov)):
                o[:, r * dr : (r + 1) * dr] = tq[r, :, n * dr : (n + 1) * dr].astype(F32)
            for c in range(S):
                lo = c * fs + r * fr
                oi[:, lo : lo + fr] = ti[r, :, c * fr : (c + 1) * fr].astype(F32)

        @pl.when(pl.program_id(0) == 0)
        def _():
            total = ts[0]
            for r in range(1, R):
                total = total + ts[r]
            for i in range(8):
                vec_o[i][...] = total[i : i + 1, :]
            for r in range(R):
                vec_o[8][:, r * fr : (r + 1) * fr] = ts[r, 8:9, :]

    def rows(n, c):
        return pl.BlockSpec((n, c), lambda i: (i, 0))

    def slab(n, c):
        return pl.BlockSpec((R, n, c), lambda i: (0, i, 0))

    def whole(*shape):
        return pl.BlockSpec(shape, lambda i: (0,) * len(shape))

    outs = [((T, D), BF)] * 2 + [((ds, D), F32)] * 4 + [((ds, S * fs), F32), ((fs, D), F32)]
    outs += [((1, ds), F32)] * 8 + [((1, fs), F32)]
    return pl.pallas_call(
        kernel,
        grid=(R,),
        out_shape=[jax.ShapeDtypeStruct(*o) for o in outs],
        in_specs=[
            rows(tok, D),
            rows(tok, D),
            slab(few, W),
            slab(few, V),
            pl.BlockSpec((1, fr, D), lambda i: (i, 0, 0)),
            rows(few, D),
            whole(R, NVEC, ds),
        ],
        out_specs=[rows(tok, D)] * 2
        + [rows(few, D)] * 4
        + [rows(few, S * fs), rows(fr, D)]
        + [whole(1, ds)] * 8
        + [whole(1, fs)],
        compiler_params=pltpu.CompilerParams(vmem_limit_bytes=LIMIT),
    )(out, gin, tq, ti, td, to, ts)


def fast_body(
    block_input,
    out_cotangent,
    w_query,
    w_key,
    w_value,
    w_output,
    bias_query,
    bias_value,
    bias_output,
    gain_first,
    shift_first,
    w_inner,
    bias_inner,
    w_down,
    bias_down,
    gain_second,
    shift_second,
):
    vectors = (
        bias_query,
        bias_value,
        bias_output,
        gain_first,
        shift_first,
        bias_down,
        gain_second,
        shift_second,
        bias_inner,
    )
    S = lax.axis_size("shard")
    got = layer(
        block_input,
        out_cotangent,
        w_query,
        w_key,
        w_value,
        w_output,
        w_inner,
        w_down,
        vectors,
        S,
        lax.axis_size("rep"),
    )
    got = widen(*got, S)
    output, grad_input, gq, gk, gv, go, gi, gd = got[:8]
    gbq, gbv, gbo, ggone, gsone, gbd, ggtwo, gstwo, gbi = (v.reshape(-1) for v in got[8:])
    return (
        output,
        grad_input,
        gq,
        gk,
        gv,
        go,
        gbq,
        gbv,
        gbo,
        ggone,
        gsone,
        gi,
        gbi,
        gd,
        gbd,
        ggtwo,
        gstwo,
    )


def fits_fast(mesh):
    S, R = mesh.shape["shard"], mesh.shape["rep"]
    return R == 4 and S == 8


def solution(mesh):
    tokens = P(("shard", "rep"), None)
    mat = P("shard", None)
    vec = P("shard")
    params = (mat, mat, mat, mat, vec, vec, vec, vec, vec, mat, vec, mat, vec, vec, vec)
    return jax.shard_map(
        fast_body if fits_fast(mesh) else body,
        mesh=mesh,
        in_specs=(tokens, tokens) + params,
        out_specs=(tokens, tokens) + params,
        check_vma=False,
    )
```
